128 devices in a mesh: grp: 4 (over x), dom: 32 (over y, z, core).
Axes of the slice: x: 4, y: 4, z: 4, core: 2. Of those that a mesh axis runs over, the one named last changes fastest.
Arguments:
- forcing: float32 [3, 8192, 512], P(None, 'dom'), may hold values from -144 to 144
- viscosity: float32 [8192], P('dom'), may hold values from 0.3 to 3
- mass_coef: float32 [8192], P('dom'), may hold values from 8 to 80
- element_order: int32 [32, 256], P('dom'), may hold values from 0 to 255, each once within a row
- owner: int32 [32, 256], P('dom'), may hold values from -1 to 31, as said below
Outputs:
- fields: float32 [4, 8192, 512], P('grp', 'dom')
The draws below stay inside these ranges and needn't reach their ends.
Inputs may be any that keep to these rules, and one draw needn't show every extreme that they name: `element_order`: row d gives each element slot of partition d its cell in the partition's brick of 8 x 8 x 4 elements, every cell once. -1 marks an element that is not analysed; at most 8 elements of one partition have the same owner, and some owner gets exactly 8 from every partition.
All inputs are finite; a program needn't handle non-finite values.
Results may differ from the reference program's by a relative error of at most 0.00037.
Values may be sent and summed in bfloat16 or wider, within the bound.
A program may use at most 64 MiB of HBM per device.

```python
import math
import jax
import jax.numpy as jnp
import numpy as np
from jax import lax

NP = 8
NODES = 512
BX = 8
BY = 8
BZ = 4
ITERS = 4
SWEEPS = 4
E_DEV = 256
ELEMS = 8192
CAP = 8
N_DOM = 32


def draw_owner(key, part):
    levels = jax.random.randint(jax.random.fold_in(key, 11), (N_DOM,), 1, 5)
    full_owner = jax.random.randint(jax.random.fold_in(key, 12), (), 0, N_DOM)
    levels = jnp.where(jnp.arange(N_DOM) == full_owner, 8, levels)
    tickets = jnp.arange(E_DEV) // CAP

    def one_partition(part_key):
        ordering = jax.random.permutation(part_key, E_DEV)
        keeping = jax.random.randint(jax.random.fold_in(part_key, 1), (E_DEV,), 0, 8) < levels[tickets]
        kept_owner = jnp.where(keeping, tickets, -1)
        return kept_owner[ordering]
    part_keys = jax.random.split(jax.random.fold_in(key, 13), N_DOM)
    return jax.vmap(one_partition)(part_keys).astype(jnp.int32)


def block_levels(stream_key, dims, pieces, low, top_value):
    def one(axis_at, shards_of):
        steps = jax.random.uniform(jax.random.fold_in(jax.random.fold_in(stream_key, 6), axis_at), (shards_of,), jnp.float32, low / len(pieces), top_value / len(pieces))
        return jnp.repeat(jnp.exp(steps), dims[axis_at] // shards_of).reshape((-1,) + (1,) * (len(dims) - axis_at - 1))

    factor_of = one(*pieces[0])
    for cut in pieces[1:]:
        factor_of = factor_of * one(*cut)
    return factor_of


def scatter_about(stream_key, shape, scale, limit, cuts=(), kind=jnp.bfloat16):
    values = jax.random.normal(stream_key, shape, jnp.float32) * scale
    if len(cuts) > 0:
        values = block_levels(stream_key, shape, cuts, -0.22, 0.18) * values
    return jnp.clip(values, min=-limit, max=limit).astype(kind)


def setup_inputs(seed: int = 0) -> dict:
    arg_keys = jax.random.split(jax.random.key(seed), 6)
    forcing = scatter_about(arg_keys[0], (3, ELEMS, NODES), 24.0, 144.0, ((1, 32),), jnp.float32)
    viscosity = jnp.clip(jnp.exp(math.log(3.0) - 2.3025851 * jax.random.uniform(arg_keys[1], (ELEMS,), jnp.float32) ** block_levels(arg_keys[1], (ELEMS,), ((0, 32),), -0.2, 0.2)), 0.3, 3.0)
    mass_coef = jnp.clip(jnp.exp(math.log(80.0) - 2.3025851 * jax.random.uniform(arg_keys[2], (ELEMS,), jnp.float32) ** block_levels(arg_keys[2], (ELEMS,), ((0, 32),), -0.2, 0.2)), 8.0, 80.0)
    element_order = jax.vmap(lambda own: jax.random.permutation(own, E_DEV))(jax.random.split(arg_keys[3], N_DOM)).reshape((N_DOM, E_DEV)).astype(jnp.int32)
    owner = draw_owner(jax.random.fold_in(arg_keys[5], 71), 0)
    return dict(forcing=forcing, viscosity=viscosity, mass_coef=mass_coef, element_order=element_order, owner=owner)


def legendre_values(points, node_count):
    legendre = np.zeros((points.shape[0], node_count))
    legendre[:, 0] = 1.0
    legendre[:, 1] = points
    for poly_order in range(2, node_count):
        legendre[:, poly_order] = ((2 * poly_order - 1) * points * legendre[:, poly_order - 1] - (poly_order - 1) * legendre[:, poly_order - 2]) / poly_order
    return legendre


def lobatto_table(node_count):
    degree = node_count - 1
    points = np.cos(np.pi * np.arange(node_count) / degree)
    for attempt in range(60):
        legendre = legendre_values(points, node_count)
        points = points - (points * legendre[:, degree] - legendre[:, degree - 1]) / (node_count * legendre[:, degree])
    points = points[::-1].copy()
    end_values = legendre_values(points, node_count)[:, degree]
    weights = 2.0 / (degree * node_count * end_values * end_values)
    spacing = points[:, None] - points[None, :] + np.eye(node_count)
    diff_matrix = end_values[:, None] / end_values[None, :] / spacing
    diff_matrix = diff_matrix * (1.0 - np.eye(node_count))
    diff_matrix[0, 0] = -degree * node_count / 4.0
    diff_matrix[-1, -1] = degree * node_count / 4.0
    return weights, diff_matrix


def operator_tables(node_count):
    weights, diff_matrix = lobatto_table(node_count)
    identity = np.eye(node_count)
    weight_cube = (weights[:, None, None] * weights[None, :, None] * weights[None, None, :]).reshape(-1)
    directional = [np.kron(identity, np.kron(identity, diff_matrix)), np.kron(identity, np.kron(diff_matrix, identity)), np.kron(diff_matrix, np.kron(identity, identity))]
    stiffness = np.zeros((node_count ** 3, node_count ** 3))
    for direction_matrix in directional:
        stiffness = stiffness + direction_matrix.T @ (weight_cube[:, None] * direction_matrix)
    return diff_matrix, weight_cube, stiffness


def lambda_two(jacobian):
    strain = [[0.5 * (jacobian[first_index][second_index] + jacobian[second_index][first_index]) for second_index in range(3)] for first_index in range(3)]
    rotation_rate = [[0.5 * (jacobian[first_index][second_index] - jacobian[second_index][first_index]) for second_index in range(3)] for first_index in range(3)]
    matrix = [[None, None, None], [None, None, None], [None, None, None]]
    for first_index in range(3):
        for second_index in range(first_index, 3):
            entry_value = strain[first_index][0] * strain[0][second_index] + rotation_rate[first_index][0] * rotation_rate[0][second_index]
            for middle_index in (1, 2):
                entry_value = entry_value + strain[first_index][middle_index] * strain[middle_index][second_index] + rotation_rate[first_index][middle_index] * rotation_rate[middle_index][second_index]
            matrix[first_index][second_index] = entry_value
            matrix[second_index][first_index] = entry_value
    for sweep_index in range(SWEEPS):
        for first_index, second_index, third_index in ((0, 1, 2), (0, 2, 1), (1, 2, 0)):
            pivot_entry = matrix[first_index][second_index]
            first_diag = matrix[first_index][first_index]
            second_diag = matrix[second_index][second_index]
            rotation = 0.5 * jnp.arctan2(2.0 * pivot_entry, first_diag - second_diag)
            cosine = jnp.cos(rotation)
            sine_part = jnp.sin(rotation)
            new_first_diag = cosine * cosine * first_diag + 2.0 * cosine * sine_part * pivot_entry + sine_part * sine_part * second_diag
            new_second_diag = sine_part * sine_part * first_diag - 2.0 * cosine * sine_part * pivot_entry + cosine * cosine * second_diag
            side_first = matrix[third_index][first_index]
            side_second = matrix[third_index][second_index]
            new_side_first = cosine * side_first + sine_part * side_second
            new_side_second = cosine * side_second - sine_part * side_first
            matrix[first_index][first_index] = new_first_diag
            matrix[second_index][second_index] = new_second_diag
            matrix[first_index][second_index] = jnp.zeros_like(pivot_entry)
            matrix[second_index][first_index] = jnp.zeros_like(pivot_entry)
            matrix[third_index][first_index] = new_side_first
            matrix[first_index][third_index] = new_side_first
            matrix[third_index][second_index] = new_side_second
            matrix[second_index][third_index] = new_side_second
    diagonal = [matrix[0][0], matrix[1][1], matrix[2][2]]
    trace_sum = diagonal[0] + diagonal[1] + diagonal[2]
    largest = jnp.maximum(jnp.maximum(diagonal[0], diagonal[1]), diagonal[2])
    smallest = jnp.minimum(jnp.minimum(diagonal[0], diagonal[1]), diagonal[2])
    return trace_sum - largest - smallest


def reference(forcing, viscosity, mass_coef, element_order, owner):
    highest = lax.Precision.HIGHEST
    diff_np, weight_np, stiff_np = operator_tables(NP)
    diff_matrix = jnp.asarray(diff_np, jnp.float32)
    weight_cube = jnp.asarray(weight_np, jnp.float32)
    weight_block = weight_cube.reshape(NP, NP, NP)
    diag_ids = np.arange(NP ** 3)
    stiff_diag = jnp.asarray(stiff_np[diag_ids, diag_ids], jnp.float32)
    cell_index = (jnp.arange(N_DOM, dtype=jnp.int32)[:, None] * E_DEV + element_order.astype(jnp.int32)).reshape(-1).astype(jnp.int32)
    layer_total = N_DOM * BZ

    def shared(values):
        leading = values.shape[:-2]
        brick_values = jnp.zeros_like(values).at[..., cell_index, :].set(values)
        brick_values = brick_values.reshape(leading + (layer_total, BY, BX, NP, NP, NP))
        pair_sum = brick_values[..., :-1, :, :, -1] + brick_values[..., 1:, :, :, 0]
        brick_values = brick_values.at[..., :-1, :, :, -1].set(pair_sum).at[..., 1:, :, :, 0].set(pair_sum)
        pair_sum = brick_values[..., :-1, :, :, -1, :] + brick_values[..., 1:, :, :, 0, :]
        brick_values = brick_values.at[..., :-1, :, :, -1, :].set(pair_sum).at[..., 1:, :, :, 0, :].set(pair_sum)
        pair_sum = brick_values[..., :-1, :, :, -1, :, :] + brick_values[..., 1:, :, :, 0, :, :]
        brick_values = brick_values.at[..., :-1, :, :, -1, :, :].set(pair_sum).at[..., 1:, :, :, 0, :, :].set(pair_sum)
        return brick_values.reshape(leading + (ELEMS, NODES))[..., cell_index, :]

    def derivatives(values):
        node_cube = values.reshape(ELEMS, NP, NP, NP)
        first_dir = jnp.einsum("ai,ekji->ekja", diff_matrix, node_cube, precision=highest)
        second_dir = jnp.einsum("aj,ekji->ekai", diff_matrix, node_cube, precision=highest)
        third_dir = jnp.einsum("ak,ekji->eaji", diff_matrix, node_cube, precision=highest)
        return [first_dir, second_dir, third_dir]

    def stiffness_apply(values):
        parts_list = derivatives(values)
        stiff_total = jnp.einsum("ai,ekja->ekji", diff_matrix, weight_block * parts_list[0], precision=highest)
        stiff_total = stiff_total + jnp.einsum("aj,ekai->ekji", diff_matrix, weight_block * parts_list[1], precision=highest)
        stiff_total = stiff_total + jnp.einsum("ak,eaji->ekji", diff_matrix, weight_block * parts_list[2], precision=highest)
        return stiff_total.reshape(ELEMS, NODES)

    def operate(values):
        return shared(viscosity[:, None] * stiffness_apply(values) + mass_coef[:, None] * (weight_cube * values))

    multiplicity = shared(jnp.ones((ELEMS, NODES), jnp.float32))
    inverse_mult = 1.0 / multiplicity

    def weighted_dot(first_vec, second_vec):
        return jnp.sum(first_vec * second_vec * inverse_mult)

    rhs_all = shared(weight_cube * forcing)
    jacobi = shared(viscosity[:, None] * stiff_diag + mass_coef[:, None] * weight_cube)
    velocity = []
    gradient_rows = []
    for component in range(3):
        solution = jnp.zeros((ELEMS, NODES), jnp.float32)
        residual = rhs_all[component]
        precond = residual / jacobi
        direction = precond
        energy_now = weighted_dot(residual, precond)
        for iteration in range(ITERS):
            image = operate(direction)
            step_size = energy_now / weighted_dot(direction, image)
            solution = solution + step_size * direction
            residual = residual - step_size * image
            precond = residual / jacobi
            energy_next = weighted_dot(residual, precond)
            direction = precond + (energy_next / energy_now) * direction
            energy_now = energy_next
        velocity.append(solution)
        grads = shared(jnp.stack([cube_values.reshape(ELEMS, NODES) for cube_values in derivatives(solution)])) * inverse_mult / NP
        rounded = lax.optimization_barrier(grads.astype(jnp.bfloat16)).astype(jnp.float32)
        gradient_rows.append([rounded[0], rounded[1], rounded[2]])
    vortex_value = lambda_two(gradient_rows)
    owner_ids = owner.astype(jnp.int32)
    matches = (owner_ids[:, :, None] == jnp.arange(N_DOM, dtype=jnp.int32)[None, None, :]).astype(jnp.int32)
    running = jnp.cumsum(matches, axis=1)
    slot_rank = jnp.sum(matches * running, axis=2) - 1
    partition = jnp.arange(N_DOM, dtype=jnp.int32)[:, None]
    dest_row = jnp.where(owner_ids >= 0, owner_ids * E_DEV + partition * CAP + slot_rank, ELEMS).reshape(-1).astype(jnp.int32)
    analysis = jnp.zeros((ELEMS, NODES), jnp.float32).at[dest_row].set(vortex_value, mode="drop")
    return jnp.concatenate([jnp.stack(velocity), analysis[None]], 0)
```

```python
import functools

import jax
import jax.numpy as jnp
import ml_dtypes
import numpy as np
from jax import lax
from jax.experimental import pallas as pl
from jax.experimental.pallas import tpu as pltpu
from jax.sharding import PartitionSpec as P

NP = 8
ITERS = 4
SWEEPS = 4
LAYER = 64
CELLS = 256
NODES = 512
DOMS = 32
BASIS_LOW = 0.3
BASIS_HIGH = 2.0
THETA = 0.5 * (BASIS_LOW + BASIS_HIGH)
DELTA = 0.5 * (BASIS_HIGH - BASIS_LOW)
MESH = pl.DeviceIdType.MESH
F32 = jnp.float32
BF16 = jnp.bfloat16


def legendre_values(points, node_count):
    legendre = np.zeros((points.shape[0], node_count))
    legendre[:, 0] = 1.0
    legendre[:, 1] = points
    for poly_order in range(2, node_count):
        legendre[:, poly_order] = (
            (2 * poly_order - 1) * points * legendre[:, poly_order - 1]
            - (poly_order - 1) * legendre[:, poly_order - 2]
        ) / poly_order
    return legendre


def lobatto_table(node_count):
    degree = node_count - 1
    points = np.cos(np.pi * np.arange(node_count) / degree)
    for attempt in range(60):
        legendre = legendre_values(points, node_count)
        points = points - (points * legendre[:, degree] - legendre[:, degree - 1]) / (
            node_count * legendre[:, degree]
        )
    points = points[::-1].copy()
    end_values = legendre_values(points, node_count)[:, degree]
    weights = 2.0 / (degree * node_count * end_values * end_values)
    spacing = points[:, None] - points[None, :] + np.eye(node_count)
    diff_matrix = end_values[:, None] / end_values[None, :] / spacing
    diff_matrix = diff_matrix * (1.0 - np.eye(node_count))
    diff_matrix[0, 0] = -degree * node_count / 4.0
    diff_matrix[-1, -1] = degree * node_count / 4.0
    return (weights, diff_matrix)


def split_rows(matrix):
    high = matrix.astype(np.float32).astype(ml_dtypes.bfloat16)
    low = (matrix - high.astype(np.float64)).astype(np.float32).astype(ml_dtypes.bfloat16)
    return high, low


def tables():
    weights, diff = lobatto_table(NP)
    eye = np.eye(NP)
    cube = (
        weights[:, None, None] * weights[None, :, None] * weights[None, None, :]
    ).reshape(-1)
    directional = [
        np.kron(eye, np.kron(eye, diff)),
        np.kron(eye, np.kron(diff, eye)),
        np.kron(diff, np.kron(eye, eye)),
    ]
    stiff = np.zeros((NODES, NODES))
    for matrix in directional:
        stiff = stiff + matrix.T @ (cube[:, None] * matrix)
    mats = np.stack([np.stack(split_rows(m)) for m in (stiff, directional[2].T)])
    flat = np.concatenate([directional[0].T[:128, :128], directional[1].T[:128, :128]], 1)
    high, low = split_rows(flat)
    flat = np.concatenate([high, high, low], 0)
    lanes = np.zeros((8, NODES), np.float32)
    lanes[0] = cube
    lanes[1] = np.diag(stiff)
    lanes[2] = np.repeat(diff[NP - 1], LAYER)
    lanes[3] = np.repeat(diff[0], LAYER)
    return mats, flat, lanes


def rotated(value, shift, axis):
    return pltpu.roll(value, shift % value.shape[axis], axis)


def kernel(
    forcing, par_in, owner_in, lanes, flat, mats,
    out,
    fsc, weights, par, parn, pone, ptr, visc, mass, raw, tmp, inv, lhs, v0, v1, v2, v3,
    xs, xlhs, gx, gy, gz, gpack, fbuf, fsend, frecv, moments, red, packed, recv, lam, lamrecv,
    wsem, fsem, psend, precv, gsend, grecv, f3send, f3recv, rsend, rrecv, asend, arecv,
    osend, orecv,
):
    grp = lax.axis_index("grp")
    dom = lax.axis_index("dom")
    comp = jnp.minimum(grp, 2)
    up = lax.rem(dom + 1, DOMS)
    down = lax.rem(dom + DOMS - 1, DOMS)
    barrier = pltpu.get_barrier_semaphore()

    for step in range(1, DOMS):
        pl.semaphore_signal(
            barrier, inc=1, device_id=(grp, lax.rem(dom + step, DOMS)), device_id_type=MESH
        )
    for step in range(1, 4):
        pl.semaphore_signal(
            barrier, inc=1, device_id=(lax.rem(grp + step, 4), dom), device_id_type=MESH
        )

    load_force = pltpu.make_async_copy(forcing.at[comp], fsc, fsem)
    load_force.start()
    load_mats = []
    for which in range(2):
        for part, source in enumerate((0, 0, 1)):
            copy = pltpu.make_async_copy(
                mats.at[which, source],
                weights.at[which, part * NODES : (part + 1) * NODES],
                wsem.at[3 * which + part],
            )
            copy.start()
            load_mats.append(copy)

    lane = lax.broadcasted_iota(jnp.int32, (8, 8, 128), 2)
    sub = lax.broadcasted_iota(jnp.int32, (8, 8, 128), 1)
    node_i = lax.rem(lane, 8)
    node_j = lax.rem(lane // 8, 8)
    x_high = (node_i == 7) & (sub < 7)
    x_low = (node_i == 0) & (sub > 0)
    y_high = node_j == 7
    y_low = node_j == 0
    half_low = lane < LAYER
    has_up = jnp.where(dom < DOMS - 1, 1.0, 0.0).astype(F32)
    has_down = jnp.where(dom > 0, 1.0, 0.0).astype(F32)

    def x_neighbours(a):
        above = rotated(rotated(a, 7, 2), -1, 1)
        below = rotated(rotated(a, -7, 2), 1, 1)
        return jnp.where(x_high, above, jnp.where(x_low, below, 0.0))

    def y_neighbours(a):
        blank = jnp.zeros((1, 8, 128), F32)
        above = jnp.concatenate([rotated(a, 56, 2)[1:], blank], 0)
        below = jnp.concatenate([blank, rotated(a, -56, 2)[:-1]], 0)
        return jnp.where(y_high, above, jnp.where(y_low, below, 0.0))

    def xy_sum(a):
        a = a + x_neighbours(a)
        return a + y_neighbours(a)

    def rows_of(layer):
        return pl.ds(pl.multiple_of(layer * LAYER, LAYER), LAYER)

    def load(ref, layer, tile):
        return ref[rows_of(layer), tile * 128 : tile * 128 + 128].reshape(8, 8, 128)

    def store(ref, layer, tile, value):
        ref[rows_of(layer), tile * 128 : tile * 128 + 128] = value.reshape(LAYER, 128)

    def column(ref, layer):
        return ref[rows_of(layer), :].reshape(8, 8, 128)

    def table(row, tile):
        return lanes[row : row + 1, tile * 128 : tile * 128 + 128].reshape(1, 1, 128)

    def split3(value):
        high = value.astype(BF16)
        rest = value - high.astype(F32)
        middle = rest.astype(BF16)
        low = (rest - middle.astype(F32)).astype(BF16)
        return high, middle, low

    def store_lhs(ref, layer, tile, value):
        value = value.reshape(LAYER, 128)
        high = value.astype(BF16)
        low = (value - high.astype(F32)).astype(BF16)
        ref[rows_of(layer), tile * 128 : tile * 128 + 128] = high
        ref[rows_of(layer), NODES + tile * 128 : NODES + tile * 128 + 128] = low
        ref[rows_of(layer), 2 * NODES + tile * 128 : 2 * NODES + tile * 128 + 128] = high

    cell_sub = lax.broadcasted_iota(jnp.int32, (CELLS, CELLS), 0).astype(F32)
    cell_lane = lax.broadcasted_iota(jnp.int32, (CELLS, CELLS), 1).astype(F32)
    par[...] = par_in[...]

    def coefficients(ref, base, scale):
        hit = ref[2:3, :] == cell_sub
        for row, target in ((0, visc), (1, mass)):
            col = jnp.sum(jnp.where(hit, ref[row : row + 1, :], 0.0), axis=1, keepdims=True)
            target[base : base + CELLS, :] = jnp.broadcast_to(col * scale, (CELLS, 128))
        return hit

    hit = coefficients(par, CELLS, 1.0)
    pone[...] = jnp.where(hit, 1.0, 0.0).astype(BF16)
    order_col = jnp.sum(
        jnp.where(cell_sub == cell_lane, par[2:3, :], 0.0), axis=1, keepdims=True
    )
    ptr[...] = jnp.where(order_col == cell_lane, 1.0, 0.0).astype(BF16)

    load_force.wait()

    def gather_own(tile, carry):
        cols = pl.ds(pl.multiple_of(tile * 128, 128), 128)
        parts = split3(fsc[:, cols])
        total = jnp.zeros((CELLS, 128), F32)
        for part in parts:
            total = total + jnp.dot(pone[...], part, preferred_element_type=F32)
        raw[CELLS : 2 * CELLS, cols] = total * lanes[0:1, cols]
        return carry

    lax.fori_loop(0, 4, gather_own, 0)

    pl.semaphore_wait(barrier, DOMS - 1 + 3)

    def remote(src, dst, send, recv_sem, device):
        return pltpu.make_async_remote_copy(
            src_ref=src, dst_ref=dst, send_sem=send, recv_sem=recv_sem,
            device_id=device, device_id_type=MESH,
        )

    par_copies = [
        remote(par, parn.at[0], psend.at[0], precv.at[0], (grp, up)),
        remote(par, parn.at[1], psend.at[1], precv.at[1], (grp, down)),
    ]
    ghost_copies = [
        remote(
            raw.at[5 * LAYER : 8 * LAYER], raw.at[1 * LAYER : 4 * LAYER],
            gsend.at[0], grecv.at[0], (grp, up),
        ),
        remote(
            raw.at[4 * LAYER : 7 * LAYER], raw.at[8 * LAYER : 11 * LAYER],
            gsend.at[1], grecv.at[1], (grp, down),
        ),
        remote(
            raw.at[4 * LAYER : 5 * LAYER, 384:512], raw.at[0:LAYER, 384:512],
            gsend.at[2], grecv.at[2], (grp, up),
        ),
        remote(
            raw.at[7 * LAYER : 8 * LAYER, 0:128], raw.at[11 * LAYER : 12 * LAYER, 0:128],
            gsend.at[3], grecv.at[3], (grp, down),
        ),
    ]
    for copy in par_copies + ghost_copies:
        copy.start()

    def assemble_xy(layer, tiles, scale):
        coef_v = column(visc, layer)
        coef_m = column(mass, layer)
        for tile in tiles:
            force = load(raw, layer, tile)
            if scale is not None:
                force = force * scale
            store(tmp, layer, tile, xy_sum(force))
            diag = coef_v * table(1, tile) + coef_m * table(0, tile)
            store(inv, layer, tile, xy_sum(diag))

    def over(low, high, body):
        lax.fori_loop(low, high, lambda layer, carry: (body(layer), carry)[1], 0)

    every = (0, 1, 2, 3)
    over(4, 8, lambda layer: assemble_xy(layer, every, None))

    owner_row = owner_in[...].astype(F32)
    owner_col = jnp.sum(
        jnp.where(cell_sub == cell_lane, owner_row, 0.0), axis=1, keepdims=True
    )
    same = (owner_col == owner_row) & (cell_sub < cell_lane)
    rank_row = jnp.sum(jnp.where(same, 1.0, 0.0), axis=0, keepdims=True)
    dest_row = jnp.where(owner_row >= 0.0, owner_row * 8.0 + rank_row, -1.0)
    slot_of = jnp.where(dest_row == cell_sub, 1.0, 0.0).astype(BF16)
    gpack[...] = jnp.dot(slot_of, ptr[...], preferred_element_type=F32).astype(BF16)

    for copy in par_copies:
        copy.wait()
    coefficients(parn.at[0], 0, has_down)
    coefficients(parn.at[1], 2 * CELLS, has_up)
    for copy in ghost_copies:
        copy.wait()

    assemble_xy(0, (3,), has_down)
    over(1, 4, lambda layer: assemble_xy(layer, every, has_down))
    over(8, 11, lambda layer: assemble_xy(layer, every, has_up))
    assemble_xy(11, (0,), has_up)

    def z_sum(ref, layer, tile):
        value = load(ref, layer, tile)
        if tile == 0:
            value = value + jnp.where(half_low, rotated(load(ref, layer - 1, 3), 64, 2), 0.0)
        if tile == 3:
            value = value + jnp.where(half_low, 0.0, rotated(load(ref, layer + 1, 0), 64, 2))
        return value

    def assemble_z(layer):
        for tile in every:
            diag = z_sum(inv, layer, tile)
            force = z_sum(tmp, layer, tile)
            inverse = jnp.where(diag > 0.0, 1.0 / jnp.where(diag > 0.0, diag, 1.0), 0.0)
            store(v1, layer, tile, inverse)
            value = force * inverse
            store(v0, layer, tile, value)
            store_lhs(lhs, layer, tile, value)

    over(1, 11, assemble_z)

    def copy_inverse(layer):
        for tile in every:
            store(inv, layer, tile, load(v1, layer, tile) * (1.0 / DELTA))

    over(2, 10, copy_inverse)

    for copy in load_mats:
        copy.wait()

    def multiply(left, low, high, which, target, target_low):
        def body(half, carry):
            cols = pl.ds(pl.multiple_of(half * 256, 256), 256)
            target[target_low * LAYER : (target_low + high - low) * LAYER, cols] = jnp.dot(
                left[low * LAYER : high * LAYER, :],
                weights[which, :, cols],
                preferred_element_type=F32,
            )
            return carry

        lax.fori_loop(0, 2, body, 0)

    def apply_xy(vec, layer, sums):
        coef_v = column(visc, layer)
        coef_m = column(mass, layer)
        for tile in every:
            value = load(vec, layer, tile)
            image = coef_v * load(tmp, layer, tile) + coef_m * (table(0, tile) * value)
            if sums is not None:
                diag = coef_v * table(1, tile) + coef_m * table(0, tile)
                sums = (
                    sums[0] + jnp.sum(value * image, axis=0),
                    sums[1] + jnp.sum(value * value * diag, axis=0),
                )
            store(tmp, layer, tile, xy_sum(image))
        return sums

    def last_sums(vec, layer, sums):
        coef_v = column(visc, layer)
        coef_m = column(mass, layer)
        for tile in every:
            value = load(vec, layer, tile)
            image = coef_v * load(tmp, layer, tile) + coef_m * (table(0, tile) * value)
            diag = coef_v * table(1, tile) + coef_m * table(0, tile)
            sums = (
                sums[0] + jnp.sum(value * image, axis=0),
                sums[1] + jnp.sum(value * value * diag, axis=0),
            )
        return sums

    def advance(layer, current, previous, following):
        for tile in every:
            value = z_sum(tmp, layer, tile) * load(inv, layer, tile)
            value = value - (THETA / DELTA) * load(current, layer, tile)
            if previous is not None:
                value = 2.0 * value - load(previous, layer, tile)
            store(following, layer, tile, value)
            store_lhs(lhs, layer, tile, value)

    blank = (jnp.zeros((8, 128), F32), jnp.zeros((8, 128), F32))
    basis = (v0, v1, v2, v3)
    for step in range(ITERS):
        low, high = 1 + step, 11 - step
        multiply(lhs, low, high, 0, tmp, low)
        if step + 1 < ITERS:
            over(low, 4, lambda layer: apply_xy(basis[step], layer, None))
            sums = lax.fori_loop(
                4, 8, lambda layer, carry: apply_xy(basis[step], layer, carry), blank
            )
            over(8, high, lambda layer: apply_xy(basis[step], layer, None))
        else:
            sums = lax.fori_loop(
                4, 8, lambda layer, carry: last_sums(basis[step], layer, carry), blank
            )
        moments[step : step + 1, :] = jnp.sum(sums[0], axis=0, keepdims=True)
        moments[4 + step : 5 + step, :] = jnp.sum(sums[1], axis=0, keepdims=True)
        if step + 1 < ITERS:
            over(
                low + 1,
                high - 1,
                lambda layer: advance(
                    layer, basis[step], basis[step - 1] if step else None, basis[step + 1]
                ),
            )

    red[0] = moments[...]
    sum_copies = []
    for step in range(1, DOMS):
        copy = remote(
            moments, red.at[step], rsend, rrecv, (grp, lax.rem(dom + step, DOMS))
        )
        copy.start()

    def end_face(ref, layer, row):
        total = load(ref, layer, 0) * table(row, 0)
        for tile in (1, 2, 3):
            total = total + load(ref, layer, tile) * table(row, tile)
        return total + rotated(total, 64, 2)

    fsend[0] = end_face(v3, 7, 2).reshape(LAYER, 128)
    fsend[1] = end_face(v3, 4, 3).reshape(LAYER, 128)
    face_copies = [
        remote(fsend.at[0], frecv.at[0], f3send.at[0], f3recv.at[0], (grp, up)),
        remote(fsend.at[1], frecv.at[1], f3send.at[1], f3recv.at[1], (grp, down)),
    ]
    for copy in face_copies:
        copy.start()

    whole = remote(red.at[1:DOMS], red.at[1:DOMS], rsend, rrecv, (grp, up))
    whole.wait_send()
    whole.wait_recv()

    total = jnp.sum(red[...], axis=0)
    total = jnp.broadcast_to(jnp.sum(total, axis=1, keepdims=True), (8, 128))
    moments[...] = total

    def scalar(row):
        return jnp.broadcast_to(moments[row : row + 1, :], (8, 128))

    alpha = [scalar(row) for row in range(4)]
    beta = [scalar(4 + row) for row in range(4)]
    gamma = [(alpha[k] - THETA * beta[k]) * (1.0 / DELTA) for k in range(4)]
    mu = [beta[0], gamma[0]]
    ahead = gamma[0]
    for k in range(1, 4):
        ahead = 2.0 * gamma[k] - ahead
        mu.append(2.0 * beta[k] - mu[0])
        mu.append(2.0 * ahead - mu[1])

    def inner(i, j):
        return 0.5 * (mu[i + j] + mu[abs(i - j)])

    gram = [
        [
            DELTA * 0.5 * (inner(i, j + 1) + inner(i, abs(j - 1))) + THETA * inner(i, j)
            for j in range(4)
        ]
        for i in range(4)
    ]
    right = [mu[k] for k in range(4)]
    pivots = []
    for k in range(4):
        original = DELTA * 0.5 * (inner(k, k + 1) + inner(k, abs(k - 1))) + THETA * inner(k, k)
        pivot = gram[k][k]
        good = pivot > 1e-7 * original
        inverse = jnp.where(good, 1.0 / jnp.where(good, pivot, 1.0), 0.0)
        pivots.append(inverse)
        for i in range(k + 1, 4):
            factor = gram[i][k] * inverse
            for j in range(k + 1, 4):
                gram[i][j] = gram[i][j] - factor * gram[k][j]
            right[i] = right[i] - factor * right[k]
    coef = [None] * 4
    for k in (3, 2, 1, 0):
        value = right[k]
        for j in range(k + 1, 4):
            value = value - gram[k][j] * coef[j]
        coef[k] = value * pivots[k]
    wide = [value.reshape(1, 8, 128) for value in coef]

    for copy in face_copies:
        copy.wait()

    def combine(layer, tile, count):
        value = wide[0] * load(v0, layer, tile)
        for k in range(1, count):
            value = value + wide[k] * load(basis[k], layer, tile)
        return value

    def solve_layer(layer):
        for tile in every:
            value = combine(layer, tile, 4)
            store(xs, layer - 4, tile, value)
            store_lhs(xlhs, layer - 4, tile, value)

    over(4, 8, solve_layer)

    def neighbour_face(layer, row, extra):
        total = combine(layer, 0, 3) * table(row, 0)
        for tile in (1, 2, 3):
            total = total + combine(layer, tile, 3) * table(row, tile)
        total = total + rotated(total, 64, 2)
        return total + wide[3] * extra.reshape(8, 8, 128)

    fbuf[0] = neighbour_face(3, 2, frecv[0]).reshape(LAYER, 128)
    fbuf[1] = neighbour_face(8, 3, frecv[1]).reshape(LAYER, 128)

    def in_plane(tile, carry):
        start = pl.multiple_of(tile * 128, 128)
        left = jnp.concatenate(
            [xlhs[:, pl.ds(part * NODES + start, 128)] for part in range(3)], 1
        )
        both = jnp.dot(left, flat[...], preferred_element_type=F32)
        gx[:, pl.ds(start, 128)] = both[:, 0:128]
        gy[:, pl.ds(start, 128)] = both[:, 128:256]
        return carry

    lax.fori_loop(0, 4, in_plane, 0)
    multiply(xlhs, 0, 4, 1, gz, 0)

    def put_grad(layer, direction, tile, value):
        base = direction * NODES + tile * 128
        packed_in[rows_of(layer), base : base + 128] = (
            (value * 0.125).reshape(LAYER, 128).astype(BF16)
        )

    packed_in = lhs
    x_face = x_high | x_low
    y_row = lax.broadcasted_iota(jnp.int32, (8, 8, 128), 0)
    y_face = (y_high & (y_row < 7)) | (y_low & (y_row > 0))

    def grad_layer(layer, z_low, z_high):
        for tile in every:
            value = load(gx, layer, tile)
            value = jnp.where(x_face, 0.5, 1.0) * (value + x_neighbours(value))
            put_grad(layer, 0, tile, value)
            value = load(gy, layer, tile)
            value = jnp.where(y_face, 0.5, 1.0) * (value + y_neighbours(value))
            put_grad(layer, 1, tile, value)
            value = load(gz, layer, tile)
            if tile == 0:
                if z_low is None:
                    other, there = load(gz, layer - 1, 3), 1.0
                    other = rotated(other, 64, 2)
                else:
                    other, there = z_low
                mixed = value + (0.5 * there) * (other - value)
                value = jnp.where(half_low, mixed, value)
            if tile == 3:
                if z_high is None:
                    other, there = load(gz, layer + 1, 0), 1.0
                    other = rotated(other, 64, 2)
                else:
                    other, there = z_high
                mixed = value + (0.5 * there) * (other - value)
                value = jnp.where(half_low, value, mixed)
            put_grad(layer, 2, tile, value)

    grad_layer(0, (fbuf[0].reshape(8, 8, 128), has_down), None)
    over(1, 3, lambda layer: grad_layer(layer, None, None))
    grad_layer(3, None, (fbuf[1].reshape(8, 8, 128), has_up))

    def pack(part, carry):
        cols = pl.ds(pl.multiple_of(part * 256, 256), 256)
        packed[:, cols] = jnp.dot(
            gpack[...], packed_in[0:CELLS, cols], preferred_element_type=F32
        ).astype(BF16)
        return carry

    lax.fori_loop(0, 6, pack, 0)

    def to_group(target, slot):
        start = pl.multiple_of(target * LAYER, LAYER)
        return remote(
            packed.at[pl.ds(start, LAYER)], recv.at[comp],
            asend.at[slot], arecv.at[comp], (target, dom),
        )

    def each_send(action):
        @pl.when(grp < 2)
        def _():
            for step in range(1, 4):
                action(to_group(lax.rem(grp + step, 4), step - 1))

        @pl.when(grp >= 2)
        def _():
            action(to_group(3 - grp, 0))

    each_send(lambda copy: copy.start())
    recv[comp] = packed[pl.ds(pl.multiple_of(grp * LAYER, LAYER), LAYER), :]

    def velocity_out(tile, carry):
        cols = pl.ds(pl.multiple_of(tile * 128, 128), 128)
        total = jnp.zeros((CELLS, 128), F32)
        for part in split3(xs[:, cols]):
            total = total + jnp.dot(ptr[...], part, preferred_element_type=F32)
        out[:, cols] = total
        return carry

    @pl.when(grp < 3)
    def _():
        lax.fori_loop(0, 4, velocity_out, 0)

    each_send(lambda copy: copy.wait_send())
    for step in (1, 2):
        other = lax.rem(comp + step, 3)
        remote(recv.at[other], recv.at[other], asend.at[0], arecv.at[other], (grp, up)).wait_recv()

    def lambda_rows(block, carry):
        rows = pl.ds(pl.multiple_of(block * 16, 16), 16)
        for part in range(2):
            jac = [
                [
                    recv[c, rows, d * NODES + part * 256 : d * NODES + part * 256 + 256].astype(F32)
                    for d in range(3)
                ]
                for c in range(3)
            ]
            lam[rows, part * 256 : part * 256 + 256] = lambda_two(jac)
        return carry

    lax.fori_loop(0, 4, lambda_rows, 0)

    base = grp * 8
    here = pl.ds(pl.multiple_of(dom * 8, 8), 8)

    def to_owner(k):
        return remote(
            lam.at[8 * k : 8 * k + 8], lamrecv.at[here], osend.at[k], orecv, (3, base + k)
        )

    def each_owner(action):
        for k in range(8):
            own = (grp == 3) & (base + k == dom)

            @pl.when(jnp.logical_not(own))
            def _():
                action(to_owner(k))

    each_owner(lambda copy: copy.start())
    for k in range(8):

        @pl.when((grp == 3) & (base + k == dom))
        def _():
            lamrecv[here, :] = lam[8 * k : 8 * k + 8, :]

    each_owner(lambda copy: copy.wait_send())

    def wait_rows(count):
        piece = lamrecv.at[0 : 8 * count]
        remote(piece, piece, osend.at[0], orecv, (grp, up)).wait_recv()

    @pl.when((grp == 3) & (dom >= 24))
    def _():
        wait_rows(31)

    @pl.when((grp == 3) & (dom < 24))
    def _():
        wait_rows(32)

    @pl.when(grp == 3)
    def _():
        out[...] = lamrecv[...]


def lambda_two(jac):
    strain = [[0.5 * (jac[a][b] + jac[b][a]) for b in range(3)] for a in range(3)]
    spin = [[0.5 * (jac[a][b] - jac[b][a]) for b in range(3)] for a in range(3)]
    m = [[None] * 3 for _ in range(3)]
    for a in range(3):
        for b in range(a, 3):
            value = strain[a][0] * strain[0][b] + spin[a][0] * spin[0][b]
            for k in (1, 2):
                value = value + strain[a][k] * strain[k][b] + spin[a][k] * spin[k][b]
            m[a][b] = value
            m[b][a] = value
    for sweep in range(SWEEPS):
        for p, q, r in ((0, 1, 2), (0, 2, 1), (1, 2, 0)):
            last = sweep == SWEEPS - 1
            twice = 2.0 * m[p][q]
            gap = m[p][p] - m[q][q]
            square = twice * twice + gap * gap
            inverse = lax.rsqrt(jnp.maximum(square, 1e-36))
            length = square * inverse
            mean = 0.5 * (m[p][p] + m[q][q])
            m[p][p] = mean + 0.5 * length
            m[q][q] = mean - 0.5 * length
            if last and (p, q) == (1, 2):
                continue
            none = square < 1e-36
            cosine2 = jnp.where(none, 1.0, jnp.abs(gap) * inverse)
            sine2 = jnp.where(none, 0.0, twice * inverse)
            larger = 0.5 + 0.5 * cosine2
            root = lax.rsqrt(larger)
            big = larger * root
            small = 0.5 * sine2 * root
            flip = gap < 0.0
            sine_big = jnp.where(sine2 < 0.0, -big, big)
            cosine = jnp.where(flip, jnp.abs(small), big)
            sine = jnp.where(flip, sine_big, small)
            side_p = m[r][p]
            side_q = m[r][q]
            m[r][p] = m[p][r] = cosine * side_p + sine * side_q
            m[r][q] = m[q][r] = cosine * side_q - sine * side_p
            m[p][q] = m[q][p] = jnp.zeros_like(side_p)
    diagonal = [m[0][0], m[1][1], m[2][2]]
    largest = jnp.maximum(jnp.maximum(diagonal[0], diagonal[1]), diagonal[2])
    smallest = jnp.minimum(jnp.minimum(diagonal[0], diagonal[1]), diagonal[2])
    return diagonal[0] + diagonal[1] + diagonal[2] - largest - smallest


def per_device(forcing, viscosity, mass_coef, element_order, owner):
    mats, flat, lanes = tables()
    par_in = jnp.concatenate(
        [
            viscosity[None],
            mass_coef[None],
            element_order.astype(F32),
            jnp.zeros((5, CELLS), F32),
        ],
        0,
    )
    vmem = pl.BlockSpec(memory_space=pltpu.VMEM)
    anywhere = pl.BlockSpec(memory_space=pl.ANY)
    wide = (12 * LAYER, NODES)
    own = (CELLS, NODES)
    dma = pltpu.SemaphoreType.DMA
    result = pl.pallas_call(
        kernel,
        out_shape=jax.ShapeDtypeStruct(own, F32),
        in_specs=[anywhere, vmem, vmem, vmem, vmem, anywhere],
        out_specs=vmem,
        scratch_shapes=[
            pltpu.VMEM(own, F32),
            pltpu.VMEM((2, 3 * NODES, NODES), BF16),
            pltpu.VMEM((8, CELLS), F32),
            pltpu.VMEM((2, 8, CELLS), F32),
            pltpu.VMEM((CELLS, CELLS), BF16),
            pltpu.VMEM((CELLS, CELLS), BF16),
            pltpu.VMEM((12 * LAYER, 128), F32),
            pltpu.VMEM((12 * LAYER, 128), F32),
            pltpu.VMEM(wide, F32),
            pltpu.VMEM(wide, F32),
            pltpu.VMEM(wide, F32),
            pltpu.VMEM((12 * LAYER, 3 * NODES), BF16),
            pltpu.VMEM(wide, F32),
            pltpu.VMEM(wide, F32),
            pltpu.VMEM(wide, F32),
            pltpu.VMEM(wide, F32),
            pltpu.VMEM(own, F32),
            pltpu.VMEM((CELLS, 3 * NODES), BF16),
            pltpu.VMEM(own, F32),
            pltpu.VMEM(own, F32),
            pltpu.VMEM(own, F32),
            pltpu.VMEM((CELLS, CELLS), BF16),
            pltpu.VMEM((2, LAYER, 128), F32),
            pltpu.VMEM((2, LAYER, 128), F32),
            pltpu.VMEM((2, LAYER, 128), F32),
            pltpu.VMEM((8, 128), F32),
            pltpu.VMEM((DOMS, 8, 128), F32),
            pltpu.VMEM((CELLS, 3 * NODES), BF16),
            pltpu.VMEM((3, LAYER, 3 * NODES), BF16),
            pltpu.VMEM((LAYER, NODES), F32),
            pltpu.VMEM(own, F32),
            dma((6,)), dma, dma((2,)), dma((2,)), dma((4,)), dma((4,)), dma((2,)), dma((2,)),
            dma, dma, dma((3,)), dma((3,)), dma((8,)), dma,
        ],
        compiler_params=pltpu.CompilerParams(
            collective_id=0, has_side_effects=True, vmem_limit_bytes=48 * 1024 * 1024
        ),
        name="solve_and_analyse",
    )(forcing, par_in, owner, jnp.asarray(lanes), jnp.asarray(flat), jnp.asarray(mats))
    return result[None]


def solution(mesh):
    in_specs = (P(None, "dom", None), P("dom"), P("dom"), P("dom", None), P("dom", None))
    out_specs = P("grp", "dom", None)
    return jax.shard_map(
        per_device, mesh=mesh, in_specs=in_specs, out_specs=out_specs, check_vma=False
    )
```

```python
import functools

import jax
import jax.numpy as jnp
import ml_dtypes
import numpy as np
from jax import lax
from jax.experimental import pallas as pl
from jax.experimental.pallas import tpu as pltpu
from jax.sharding import PartitionSpec as P

NP = 8
ITERS = 4
SWEEPS = 4
LAYER = 64
CELLS = 256
NODES = 512
DOMS = 32
BASIS_LOW = 0.3
BASIS_HIGH = 2.0
THETA = 0.5 * (BASIS_LOW + BASIS_HIGH)
DELTA = 0.5 * (BASIS_HIGH - BASIS_LOW)
MESH = pl.DeviceIdType.MESH
F32 = jnp.float32
BF16 = jnp.bfloat16


def legendre_values(points, node_count):
    legendre = np.zeros((points.shape[0], node_count))
    legendre[:, 0] = 1.0
    legendre[:, 1] = points
    for poly_order in range(2, node_count):
        legendre[:, poly_order] = (
            (2 * poly_order - 1) * points * legendre[:, poly_order - 1]
            - (poly_order - 1) * legendre[:, poly_order - 2]
        ) / poly_order
    return legendre


def lobatto_table(node_count):
    degree = node_count - 1
    points = np.cos(np.pi * np.arange(node_count) / degree)
    for attempt in range(60):
        legendre = legendre_values(points, node_count)
        points = points - (points * legendre[:, degree] - legendre[:, degree - 1]) / (
            node_count * legendre[:, degree]
        )
    points = points[::-1].copy()
    end_values = legendre_values(points, node_count)[:, degree]
    weights = 2.0 / (degree * node_count * end_values * end_values)
    spacing = points[:, None] - points[None, :] + np.eye(node_count)
    diff_matrix = end_values[:, None] / end_values[None, :] / spacing
    diff_matrix = diff_matrix * (1.0 - np.eye(node_count))
    diff_matrix[0, 0] = -degree * node_count / 4.0
    diff_matrix[-1, -1] = degree * node_count / 4.0
    return (weights, diff_matrix)


def split_rows(matrix):
    high = matrix.astype(np.float32).astype(ml_dtypes.bfloat16)
    low = (matrix - high.astype(np.float64)).astype(np.float32).astype(ml_dtypes.bfloat16)
    return high, low


def tables():
    weights, diff = lobatto_table(NP)
    eye = np.eye(NP)
    cube = (
        weights[:, None, None] * weights[None, :, None] * weights[None, None, :]
    ).reshape(-1)
    directional = [
        np.kron(eye, np.kron(eye, diff)),
        np.kron(eye, np.kron(diff, eye)),
        np.kron(diff, np.kron(eye, eye)),
    ]
    stiff = np.zeros((NODES, NODES))
    for matrix in directional:
        stiff = stiff + matrix.T @ (cube[:, None] * matrix)
    mats = np.stack([np.stack(split_rows(m)) for m in (stiff, directional[2].T)])
    flat = np.concatenate([directional[0].T[:128, :128], directional[1].T[:128, :128]], 1)
    high, low = split_rows(flat)
    flat = np.concatenate([high, high, low], 0)
    lanes = np.zeros((8, NODES), np.float32)
    lanes[0] = cube
    lanes[1] = np.diag(stiff)
    lanes[2] = np.repeat(diff[NP - 1], LAYER)
    lanes[3] = np.repeat(diff[0], LAYER)
    return mats, flat, lanes


def rotated(value, shift, axis):
    return pltpu.roll(value, shift % value.shape[axis], axis)


def kernel(
    forcing, visc_in, mass_in, order_in, owner_in, lanes_in, flat_in, mats,
    out,
    fsc, lanes, flat, order_sc, owner_sc, weights, par, parn, pone, ptr, visc, mass, raw, tmp, inv, lhs, v0, v1, v2, v3,
    xs, xlhs, gx, gy, gz, gpack, fbuf, fsend, frecv, moments, red, packed, recv, lam, lamrecv,
    ssem, wsem, fsem, psend, precv, gsend, grecv, f3send, f3recv, rsend, rrecv, asend, arecv,
    osend, orecv,
):
    grp = lax.axis_index("grp")
    dom = lax.axis_index("dom")
    comp = jnp.minimum(grp, 2)
    up = lax.rem(dom + 1, DOMS)
    down = lax.rem(dom + DOMS - 1, DOMS)
    barrier = pltpu.get_barrier_semaphore()

    for step in range(1, DOMS):
        pl.semaphore_signal(
            barrier, inc=1, device_id=(grp, lax.rem(dom + step, DOMS)), device_id_type=MESH
        )
    for step in range(1, 4):
        pl.semaphore_signal(
            barrier, inc=1, device_id=(lax.rem(grp + step, 4), dom), device_id_type=MESH
        )

    load_small = [
        pltpu.make_async_copy(source, target, ssem.at[k])
        for k, (source, target) in enumerate(
            (
                (visc_in, par.at[0:1]),
                (mass_in, par.at[1:2]),
                (order_in, order_sc),
                (owner_in, owner_sc),
                (lanes_in, lanes),
            )
        )
    ]
    for copy in load_small:
        copy.start()
    load_force = pltpu.make_async_copy(forcing.at[comp], fsc, fsem)
    load_force.start()
    load_mats = [pltpu.make_async_copy(flat_in, flat, wsem.at[6])]
    load_mats[0].start()
    for which in range(2):
        for part, source in enumerate((0, 0, 1)):
            copy = pltpu.make_async_copy(
                mats.at[which, source],
                weights.at[which, part * NODES : (part + 1) * NODES],
                wsem.at[3 * which + part],
            )
            copy.start()
            load_mats.append(copy)

    lane = lax.broadcasted_iota(jnp.int32, (8, 8, 128), 2)
    sub = lax.broadcasted_iota(jnp.int32, (8, 8, 128), 1)
    node_i = lax.rem(lane, 8)
    node_j = lax.rem(lane // 8, 8)
    x_high = (node_i == 7) & (sub < 7)
    x_low = (node_i == 0) & (sub > 0)
    y_high = node_j == 7
    y_low = node_j == 0
    half_low = lane < LAYER
    has_up = jnp.where(dom < DOMS - 1, 1.0, 0.0).astype(F32)
    has_down = jnp.where(dom > 0, 1.0, 0.0).astype(F32)

    def x_neighbours(a):
        above = rotated(rotated(a, 7, 2), -1, 1)
        below = rotated(rotated(a, -7, 2), 1, 1)
        return jnp.where(x_high, above, jnp.where(x_low, below, 0.0))

    def y_neighbours(a):
        blank = jnp.zeros((1, 8, 128), F32)
        above = jnp.concatenate([rotated(a, 56, 2)[1:], blank], 0)
        below = jnp.concatenate([blank, rotated(a, -56, 2)[:-1]], 0)
        return jnp.where(y_high, above, jnp.where(y_low, below, 0.0))

    def xy_sum(a):
        a = a + x_neighbours(a)
        return a + y_neighbours(a)

    def rows_of(layer):
        return pl.ds(pl.multiple_of(layer * LAYER, LAYER), LAYER)

    def load(ref, layer, tile):
        return ref[rows_of(layer), tile * 128 : tile * 128 + 128].reshape(8, 8, 128)

    def store(ref, layer, tile, value):
        ref[rows_of(layer), tile * 128 : tile * 128 + 128] = value.reshape(LAYER, 128)

    def column(ref, layer):
        return ref[rows_of(layer), :].reshape(8, 8, 128)

    def table(row, tile):
        return lanes[row : row + 1, tile * 128 : tile * 128 + 128].reshape(1, 1, 128)

    def split3(value):
        high = value.astype(BF16)
        rest = value - high.astype(F32)
        middle = rest.astype(BF16)
        low = (rest - middle.astype(F32)).astype(BF16)
        return high, middle, low

    def store_lhs(ref, layer, tile, value):
        value = value.reshape(LAYER, 128)
        high = value.astype(BF16)
        low = (value - high.astype(F32)).astype(BF16)
        ref[rows_of(layer), tile * 128 : tile * 128 + 128] = high
        ref[rows_of(layer), NODES + tile * 128 : NODES + tile * 128 + 128] = low
        ref[rows_of(layer), 2 * NODES + tile * 128 : 2 * NODES + tile * 128 + 128] = high

    cell_sub = lax.broadcasted_iota(jnp.int32, (CELLS, CELLS), 0).astype(F32)
    cell_lane = lax.broadcasted_iota(jnp.int32, (CELLS, CELLS), 1).astype(F32)
    for copy in load_small:
        copy.wait()
    par[2:3, :] = order_sc[...].astype(F32)
    par[3:8, :] = jnp.zeros((5, CELLS), F32)

    def coefficients(ref, base, scale):
        hit = ref[2:3, :] == cell_sub
        for row, target in ((0, visc), (1, mass)):
            col = jnp.sum(jnp.where(hit, ref[row : row + 1, :], 0.0), axis=1, keepdims=True)
            target[base : base + CELLS, :] = jnp.broadcast_to(col * scale, (CELLS, 128))
        return hit

    hit = coefficients(par, CELLS, 1.0)
    pone[...] = jnp.where(hit, 1.0, 0.0).astype(BF16)
    order_col = jnp.sum(
        jnp.where(cell_sub == cell_lane, par[2:3, :], 0.0), axis=1, keepdims=True
    )
    ptr[...] = jnp.where(order_col == cell_lane, 1.0, 0.0).astype(BF16)

    load_force.wait()

    def gather_own(tile, carry):
        cols = pl.ds(pl.multiple_of(tile * 128, 128), 128)
        parts = split3(fsc[:, cols])
        total = jnp.zeros((CELLS, 128), F32)
        for part in parts:
            total = total + jnp.dot(pone[...], part, preferred_element_type=F32)
        raw[CELLS : 2 * CELLS, cols] = total * lanes[0:1, cols]
        return carry

    lax.fori_loop(0, 4, gather_own, 0)

    pl.semaphore_wait(barrier, DOMS - 1 + 3)

    def remote(src, dst, send, recv_sem, device):
        return pltpu.make_async_remote_copy(
            src_ref=src, dst_ref=dst, send_sem=send, recv_sem=recv_sem,
            device_id=device, device_id_type=MESH,
        )

    par_copies = [
        remote(par, parn.at[0], psend.at[0], precv.at[0], (grp, up)),
        remote(par, parn.at[1], psend.at[1], precv.at[1], (grp, down)),
    ]
    ghost_copies = [
        remote(
            raw.at[5 * LAYER : 8 * LAYER], raw.at[1 * LAYER : 4 * LAYER],
            gsend.at[0], grecv.at[0], (grp, up),
        ),
        remote(
            raw.at[4 * LAYER : 7 * LAYER], raw.at[8 * LAYER : 11 * LAYER],
            gsend.at[1], grecv.at[1], (grp, down),
        ),
        remote(
            raw.at[4 * LAYER : 5 * LAYER, 384:512], raw.at[0:LAYER, 384:512],
            gsend.at[2], grecv.at[2], (grp, up),
        ),
        remote(
            raw.at[7 * LAYER : 8 * LAYER, 0:128], raw.at[11 * LAYER : 12 * LAYER, 0:128],
            gsend.at[3], grecv.at[3], (grp, down),
        ),
    ]
    for copy in par_copies + ghost_copies:
        copy.start()

    def assemble_xy(layer, tiles, scale):
        coef_v = column(visc, layer)
        coef_m = column(mass, layer)
        for tile in tiles:
            force = load(raw, layer, tile)
            if scale is not None:
                force = force * scale
            store(tmp, layer, tile, xy_sum(force))
            diag = coef_v * table(1, tile) + coef_m * table(0, tile)
            store(inv, layer, tile, xy_sum(diag))

    def over(low, high, body):
        lax.fori_loop(low, high, lambda layer, carry: (body(layer), carry)[1], 0)

    every = (0, 1, 2, 3)
    over(4, 8, lambda layer: assemble_xy(layer, every, None))

    owner_row = owner_sc[...].astype(F32)
    owner_col = jnp.sum(
        jnp.where(cell_sub == cell_lane, owner_row, 0.0), axis=1, keepdims=True
    )
    same = (owner_col == owner_row) & (cell_sub < cell_lane)
    rank_row = jnp.sum(jnp.where(same, 1.0, 0.0), axis=0, keepdims=True)
    dest_row = jnp.where(owner_row >= 0.0, owner_row * 8.0 + rank_row, -1.0)
    slot_of = jnp.where(dest_row == cell_sub, 1.0, 0.0).astype(BF16)
    gpack[...] = jnp.dot(slot_of, ptr[...], preferred_element_type=F32).astype(BF16)

    for copy in par_copies:
        copy.wait()
    coefficients(parn.at[0], 0, has_down)
    coefficients(parn.at[1], 2 * CELLS, has_up)
    for copy in ghost_copies:
        copy.wait()

    assemble_xy(0, (3,), has_down)
    over(1, 4, lambda layer: assemble_xy(layer, every, has_down))
    over(8, 11, lambda layer: assemble_xy(layer, every, has_up))
    assemble_xy(11, (0,), has_up)

    def z_sum(ref, layer, tile):
        value = load(ref, layer, tile)
        if tile == 0:
            value = value + jnp.where(half_low, rotated(load(ref, layer - 1, 3), 64, 2), 0.0)
        if tile == 3:
            value = value + jnp.where(half_low, 0.0, rotated(load(ref, layer + 1, 0), 64, 2))
        return value

    def assemble_z(layer):
        for tile in every:
            diag = z_sum(inv, layer, tile)
            force = z_sum(tmp, layer, tile)
            inverse = jnp.where(diag > 0.0, 1.0 / jnp.where(diag > 0.0, diag, 1.0), 0.0)
            store(v1, layer, tile, inverse)
            value = force * inverse
            store(v0, layer, tile, value)
            store_lhs(lhs, layer, tile, value)

    over(1, 11, assemble_z)

    def copy_inverse(layer):
        for tile in every:
            store(inv, layer, tile, load(v1, layer, tile) * (1.0 / DELTA))

    over(2, 10, copy_inverse)

    for copy in load_mats:
        copy.wait()

    def multiply(left, low, high, which, target, target_low):
        def body(half, carry):
            cols = pl.ds(pl.multiple_of(half * 256, 256), 256)
            target[target_low * LAYER : (target_low + high - low) * LAYER, cols] = jnp.dot(
                left[low * LAYER : high * LAYER, :],
                weights[which, :, cols],
                preferred_element_type=F32,
            )
            return carry

        lax.fori_loop(0, 2, body, 0)

    def apply_xy(vec, layer, sums):
        coef_v = column(visc, layer)
        coef_m = column(mass, layer)
        for tile in every:
            value = load(vec, layer, tile)
            image = coef_v * load(tmp, layer, tile) + coef_m * (table(0, tile) * value)
            if sums is not None:
                diag = coef_v * table(1, tile) + coef_m * table(0, tile)
                sums = (
                    sums[0] + jnp.sum(value * image, axis=0),
                    sums[1] + jnp.sum(value * value * diag, axis=0),
                )
            store(tmp, layer, tile, xy_sum(image))
        return sums

    def last_sums(vec, layer, sums):
        coef_v = column(visc, layer)
        coef_m = column(mass, layer)
        for tile in every:
            value = load(vec, layer, tile)
            image = coef_v * load(tmp, layer, tile) + coef_m * (table(0, tile) * value)
            diag = coef_v * table(1, tile) + coef_m * table(0, tile)
            sums = (
                sums[0] + jnp.sum(value * image, axis=0),
                sums[1] + jnp.sum(value * value * diag, axis=0),
            )
        return sums

    def advance(layer, current, previous, following):
        for tile in every:
            value = z_sum(tmp, layer, tile) * load(inv, layer, tile)
            value = value - (THETA / DELTA) * load(current, layer, tile)
            if previous is not None:
                value = 2.0 * value - load(previous, layer, tile)
            store(following, layer, tile, value)
            store_lhs(lhs, layer, tile, value)

    blank = (jnp.zeros((8, 128), F32), jnp.zeros((8, 128), F32))
    basis = (v0, v1, v2, v3)
    for step in range(ITERS):
        low, high = 1 + step, 11 - step
        multiply(lhs, low, high, 0, tmp, low)
        if step + 1 < ITERS:
            over(low, 4, lambda layer: apply_xy(basis[step], layer, None))
            sums = lax.fori_loop(
                4, 8, lambda layer, carry: apply_xy(basis[step], layer, carry), blank
            )
            over(8, high, lambda layer: apply_xy(basis[step], layer, None))
        else:
            sums = lax.fori_loop(
                4, 8, lambda layer, carry: last_sums(basis[step], layer, carry), blank
            )
        moments[step : step + 1, :] = jnp.sum(sums[0], axis=0, keepdims=True)
        moments[4 + step : 5 + step, :] = jnp.sum(sums[1], axis=0, keepdims=True)
        if step + 1 < ITERS:
            over(
                low + 1,
                high - 1,
                lambda layer: advance(
                    layer, basis[step], basis[step - 1] if step else None, basis[step + 1]
                ),
            )

    red[0] = moments[...]
    sum_copies = []
    for step in range(1, DOMS):
        copy = remote(
            moments, red.at[step], rsend, rrecv, (grp, lax.rem(dom + step, DOMS))
        )
        copy.start()

    def end_face(ref, layer, row):
        total = load(ref, layer, 0) * table(row, 0)
        for tile in (1, 2, 3):
            total = total + load(ref, layer, tile) * table(row, tile)
        return total + rotated(total, 64, 2)

    fsend[0] = end_face(v3, 7, 2).reshape(LAYER, 128)
    fsend[1] = end_face(v3, 4, 3).reshape(LAYER, 128)
    face_copies = [
        remote(fsend.at[0], frecv.at[0], f3send.at[0], f3recv.at[0], (grp, up)),
        remote(fsend.at[1], frecv.at[1], f3send.at[1], f3recv.at[1], (grp, down)),
    ]
    for copy in face_copies:
        copy.start()

    whole = remote(red.at[1:DOMS], red.at[1:DOMS], rsend, rrecv, (grp, up))
    whole.wait_send()
    whole.wait_recv()

    total = jnp.sum(red[...], axis=0)
    total = jnp.broadcast_to(jnp.sum(total, axis=1, keepdims=True), (8, 128))
    moments[...] = total

    def scalar(row):
        return jnp.broadcast_to(moments[row : row + 1, :], (8, 128))

    alpha = [scalar(row) for row in range(4)]
    beta = [scalar(4 + row) for row in range(4)]
    gamma = [(alpha[k] - THETA * beta[k]) * (1.0 / DELTA) for k in range(4)]
    mu = [beta[0], gamma[0]]
    ahead = gamma[0]
    for k in range(1, 4):
        ahead = 2.0 * gamma[k] - ahead
        mu.append(2.0 * beta[k] - mu[0])
        mu.append(2.0 * ahead - mu[1])

    def inner(i, j):
        return 0.5 * (mu[i + j] + mu[abs(i - j)])

    gram = [
        [
            DELTA * 0.5 * (inner(i, j + 1) + inner(i, abs(j - 1))) + THETA * inner(i, j)
            for j in range(4)
        ]
        for i in range(4)
    ]
    right = [mu[k] for k in range(4)]
    pivots = []
    for k in range(4):
        original = DELTA * 0.5 * (inner(k, k + 1) + inner(k, abs(k - 1))) + THETA * inner(k, k)
        pivot = gram[k][k]
        good = pivot > 1e-7 * original
        inverse = jnp.where(good, 1.0 / jnp.where(good, pivot, 1.0), 0.0)
        pivots.append(inverse)
        for i in range(k + 1, 4):
            factor = gram[i][k] * inverse
            for j in range(k + 1, 4):
                gram[i][j] = gram[i][j] - factor * gram[k][j]
            right[i] = right[i] - factor * right[k]
    coef = [None] * 4
    for k in (3, 2, 1, 0):
        value = right[k]
        for j in range(k + 1, 4):
            value = value - gram[k][j] * coef[j]
        coef[k] = value * pivots[k]
    wide = [value.reshape(1, 8, 128) for value in coef]

    for copy in face_copies:
        copy.wait()

    def combine(layer, tile, count):
        value = wide[0] * load(v0, layer, tile)
        for k in range(1, count):
            value = value + wide[k] * load(basis[k], layer, tile)
        return value

    def solve_layer(layer):
        for tile in every:
            value = combine(layer, tile, 4)
            store(xs, layer - 4, tile, value)
            store_lhs(xlhs, layer - 4, tile, value)

    over(4, 8, solve_layer)

    def neighbour_face(layer, row, extra):
        total = combine(layer, 0, 3) * table(row, 0)
        for tile in (1, 2, 3):
            total = total + combine(layer, tile, 3) * table(row, tile)
        total = total + rotated(total, 64, 2)
        return total + wide[3] * extra.reshape(8, 8, 128)

    fbuf[0] = neighbour_face(3, 2, frecv[0]).reshape(LAYER, 128)
    fbuf[1] = neighbour_face(8, 3, frecv[1]).reshape(LAYER, 128)

    def in_plane(tile, carry):
        start = pl.multiple_of(tile * 128, 128)
        left = jnp.concatenate(
            [xlhs[:, pl.ds(part * NODES + start, 128)] for part in range(3)], 1
        )
        both = jnp.dot(left, flat[...], preferred_element_type=F32)
        gx[:, pl.ds(start, 128)] = both[:, 0:128]
        gy[:, pl.ds(start, 128)] = both[:, 128:256]
        return carry

    lax.fori_loop(0, 4, in_plane, 0)
    multiply(xlhs, 0, 4, 1, gz, 0)

    def put_grad(layer, direction, tile, value):
        base = direction * NODES + tile * 128
        packed_in[rows_of(layer), base : base + 128] = (
            (value * 0.125).reshape(LAYER, 128).astype(BF16)
        )

    packed_in = lhs
    x_face = x_high | x_low
    y_row = lax.broadcasted_iota(jnp.int32, (8, 8, 128), 0)
    y_face = (y_high & (y_row < 7)) | (y_low & (y_row > 0))

    def grad_layer(layer, z_low, z_high):
        for tile in every:
            value = load(gx, layer, tile)
            value = jnp.where(x_face, 0.5, 1.0) * (value + x_neighbours(value))
            put_grad(layer, 0, tile, value)
            value = load(gy, layer, tile)
            value = jnp.where(y_face, 0.5, 1.0) * (value + y_neighbours(value))
            put_grad(layer, 1, tile, value)
            value = load(gz, layer, tile)
            if tile == 0:
                if z_low is None:
                    other, there = load(gz, layer - 1, 3), 1.0
                    other = rotated(other, 64, 2)
                else:
                    other, there = z_low
                mixed = value + (0.5 * there) * (other - value)
                value = jnp.where(half_low, mixed, value)
            if tile == 3:
                if z_high is None:
                    other, there = load(gz, layer + 1, 0), 1.0
                    other = rotated(other, 64, 2)
                else:
                    other, there = z_high
                mixed = value + (0.5 * there) * (other - value)
                value = jnp.where(half_low, value, mixed)
            put_grad(layer, 2, tile, value)

    grad_layer(0, (fbuf[0].reshape(8, 8, 128), has_down), None)
    over(1, 3, lambda layer: grad_layer(layer, None, None))
    grad_layer(3, None, (fbuf[1].reshape(8, 8, 128), has_up))

    def pack(part, carry):
        cols = pl.ds(pl.multiple_of(part * 256, 256), 256)
        packed[:, cols] = jnp.dot(
            gpack[...], packed_in[0:CELLS, cols], preferred_element_type=F32
        ).astype(BF16)
        return carry

    lax.fori_loop(0, 6, pack, 0)

    def to_group(target, slot):
        start = pl.multiple_of(target * LAYER, LAYER)
        return remote(
            packed.at[pl.ds(start, LAYER)], recv.at[comp],
            asend.at[slot], arecv.at[comp], (target, dom),
        )

    def each_send(action):
        @pl.when(grp < 2)
        def _():
            for step in range(1, 4):
                action(to_group(lax.rem(grp + step, 4), step - 1))

        @pl.when(grp >= 2)
        def _():
            action(to_group(3 - grp, 0))

    each_send(lambda copy: copy.start())
    recv[comp] = packed[pl.ds(pl.multiple_of(grp * LAYER, LAYER), LAYER), :]

    def velocity_out(tile, carry):
        cols = pl.ds(pl.multiple_of(tile * 128, 128), 128)
        total = jnp.zeros((CELLS, 128), F32)
        for part in split3(xs[:, cols]):
            total = total + jnp.dot(ptr[...], part, preferred_element_type=F32)
        out[:, cols] = total
        return carry

    @pl.when(grp < 3)
    def _():
        lax.fori_loop(0, 4, velocity_out, 0)

    each_send(lambda copy: copy.wait_send())
    for step in (1, 2):
        other = lax.rem(comp + step, 3)
        remote(recv.at[other], recv.at[other], asend.at[0], arecv.at[other], (grp, up)).wait_recv()

    def lambda_rows(block, carry):
        rows = pl.ds(pl.multiple_of(block * 16, 16), 16)
        for part in range(2):
            jac = [
                [
                    recv[c, rows, d * NODES + part * 256 : d * NODES + part * 256 + 256].astype(F32)
                    for d in range(3)
                ]
                for c in range(3)
            ]
            lam[rows, part * 256 : part * 256 + 256] = lambda_two(jac)
        return carry

    lax.fori_loop(0, 4, lambda_rows, 0)

    base = grp * 8
    here = pl.ds(pl.multiple_of(dom * 8, 8), 8)

    def to_owner(k):
        return remote(
            lam.at[8 * k : 8 * k + 8], lamrecv.at[here], osend.at[k], orecv, (3, base + k)
        )

    def each_owner(action):
        for k in range(8):
            own = (grp == 3) & (base + k == dom)

            @pl.when(jnp.logical_not(own))
            def _():
                action(to_owner(k))

    each_owner(lambda copy: copy.start())
    for k in range(8):

        @pl.when((grp == 3) & (base + k == dom))
        def _():
            lamrecv[here, :] = lam[8 * k : 8 * k + 8, :]

    each_owner(lambda copy: copy.wait_send())

    def wait_rows(count):
        piece = lamrecv.at[0 : 8 * count]
        remote(piece, piece, osend.at[0], orecv, (grp, up)).wait_recv()

    @pl.when((grp == 3) & (dom >= 24))
    def _():
        wait_rows(31)

    @pl.when((grp == 3) & (dom < 24))
    def _():
        wait_rows(32)

    @pl.when(grp == 3)
    def _():
        out[...] = lamrecv[...]


def lambda_two(jac):
    strain = [[0.5 * (jac[a][b] + jac[b][a]) for b in range(3)] for a in range(3)]
    spin = [[0.5 * (jac[a][b] - jac[b][a]) for b in range(3)] for a in range(3)]
    m = [[None] * 3 for _ in range(3)]
    for a in range(3):
        for b in range(a, 3):
            value = strain[a][0] * strain[0][b] + spin[a][0] * spin[0][b]
            for k in (1, 2):
                value = value + strain[a][k] * strain[k][b] + spin[a][k] * spin[k][b]
            m[a][b] = value
            m[b][a] = value
    for sweep in range(SWEEPS):
        for p, q, r in ((0, 1, 2), (0, 2, 1), (1, 2, 0)):
            last = sweep == SWEEPS - 1
            twice = 2.0 * m[p][q]
            gap = m[p][p] - m[q][q]
            square = twice * twice + gap * gap
            inverse = lax.rsqrt(jnp.maximum(square, 1e-36))
            length = square * inverse
            mean = 0.5 * (m[p][p] + m[q][q])
            m[p][p] = mean + 0.5 * length
            m[q][q] = mean - 0.5 * length
            if last and (p, q) == (1, 2):
                continue
            none = square < 1e-36
            cosine2 = jnp.where(none, 1.0, jnp.abs(gap) * inverse)
            sine2 = jnp.where(none, 0.0, twice * inverse)
            larger = 0.5 + 0.5 * cosine2
            root = lax.rsqrt(larger)
            big = larger * root
            small = 0.5 * sine2 * root
            flip = gap < 0.0
            sine_big = jnp.where(sine2 < 0.0, -big, big)
            cosine = jnp.where(flip, jnp.abs(small), big)
            sine = jnp.where(flip, sine_big, small)
            side_p = m[r][p]
            side_q = m[r][q]
            m[r][p] = m[p][r] = cosine * side_p + sine * side_q
            m[r][q] = m[q][r] = cosine * side_q - sine * side_p
            m[p][q] = m[q][p] = jnp.zeros_like(side_p)
    diagonal = [m[0][0], m[1][1], m[2][2]]
    largest = jnp.maximum(jnp.maximum(diagonal[0], diagonal[1]), diagonal[2])
    smallest = jnp.minimum(jnp.minimum(diagonal[0], diagonal[1]), diagonal[2])
    return diagonal[0] + diagonal[1] + diagonal[2] - largest - smallest


def per_device(forcing, viscosity, mass_coef, element_order, owner):
    mats, flat, lanes = tables()
    vmem = pl.BlockSpec(memory_space=pltpu.VMEM)
    hbm = pl.BlockSpec(memory_space=pltpu.HBM)
    wide = (12 * LAYER, NODES)
    own = (CELLS, NODES)
    dma = pltpu.SemaphoreType.DMA
    result = pl.pallas_call(
        kernel,
        out_shape=jax.ShapeDtypeStruct(own, F32),
        in_specs=[hbm] * 8,
        out_specs=vmem,
        scratch_shapes=[
            pltpu.VMEM(own, F32),
            pltpu.VMEM((8, NODES), F32),
            pltpu.VMEM((384, 256), BF16),
            pltpu.VMEM((1, CELLS), jnp.int32),
            pltpu.VMEM((1, CELLS), jnp.int32),
            pltpu.VMEM((2, 3 * NODES, NODES), BF16),
            pltpu.VMEM((8, CELLS), F32),
            pltpu.VMEM((2, 8, CELLS), F32),
            pltpu.VMEM((CELLS, CELLS), BF16),
            pltpu.VMEM((CELLS, CELLS), BF16),
            pltpu.VMEM((12 * LAYER, 128), F32),
            pltpu.VMEM((12 * LAYER, 128), F32),
            pltpu.VMEM(wide, F32),
            pltpu.VMEM(wide, F32),
            pltpu.VMEM(wide, F32),
            pltpu.VMEM((12 * LAYER, 3 * NODES), BF16),
            pltpu.VMEM(wide, F32),
            pltpu.VMEM(wide, F32),
            pltpu.VMEM(wide, F32),
            pltpu.VMEM(wide, F32),
            pltpu.VMEM(own, F32),
            pltpu.VMEM((CELLS, 3 * NODES), BF16),
            pltpu.VMEM(own, F32),
            pltpu.VMEM(own, F32),
            pltpu.VMEM(own, F32),
            pltpu.VMEM((CELLS, CELLS), BF16),
            pltpu.VMEM((2, LAYER, 128), F32),
            pltpu.VMEM((2, LAYER, 128), F32),
            pltpu.VMEM((2, LAYER, 128), F32),
            pltpu.VMEM((8, 128), F32),
            pltpu.VMEM((DOMS, 8, 128), F32),
            pltpu.VMEM((CELLS, 3 * NODES), BF16),
            pltpu.VMEM((3, LAYER, 3 * NODES), BF16),
            pltpu.VMEM((LAYER, NODES), F32),
            pltpu.VMEM(own, F32),
            dma((5,)), dma((7,)), dma, dma((2,)), dma((2,)), dma((4,)), dma((4,)), dma((2,)), dma((2,)),
            dma, dma, dma((3,)), dma((3,)), dma((8,)), dma,
        ],
        compiler_params=pltpu.CompilerParams(
            collective_id=0, has_side_effects=True, vmem_limit_bytes=60 * 1024 * 1024
        ),
        name="solve_and_analyse",
    )(
        forcing, viscosity[None], mass_coef[None], element_order, owner,
        jnp.asarray(lanes), jnp.asarray(flat), jnp.asarray(mats),
    )
    return result[None]


def solution(mesh):
    in_specs = (P(None, "dom", None), P("dom"), P("dom"), P("dom", None), P("dom", None))
    out_specs = P("grp", "dom", None)
    return jax.shard_map(
        per_device, mesh=mesh, in_specs=in_specs, out_specs=out_specs, check_vma=False
    )
```

```python
import functools

import jax
import jax.numpy as jnp
import ml_dtypes
import numpy as np
from jax import lax
from jax.experimental import pallas as pl
from jax.experimental.pallas import tpu as pltpu
from jax.sharding import PartitionSpec as P

NP = 8
ITERS = 4
SWEEPS = 4
LAYER = 64
CELLS = 256
NODES = 512
DOMS = 32
BASIS_LOW = 0.3
BASIS_HIGH = 2.0
THETA = 0.5 * (BASIS_LOW + BASIS_HIGH)
DELTA = 0.5 * (BASIS_HIGH - BASIS_LOW)
MESH = pl.DeviceIdType.MESH
F32 = jnp.float32
BF16 = jnp.bfloat16


def legendre_values(points, node_count):
    legendre = np.zeros((points.shape[0], node_count))
    legendre[:, 0] = 1.0
    legendre[:, 1] = points
    for poly_order in range(2, node_count):
        legendre[:, poly_order] = (
            (2 * poly_order - 1) * points * legendre[:, poly_order - 1]
            - (poly_order - 1) * legendre[:, poly_order - 2]
        ) / poly_order
    return legendre


def lobatto_table(node_count):
    degree = node_count - 1
    points = np.cos(np.pi * np.arange(node_count) / degree)
    for attempt in range(60):
        legendre = legendre_values(points, node_count)
        points = points - (points * legendre[:, degree] - legendre[:, degree - 1]) / (
            node_count * legendre[:, degree]
        )
    points = points[::-1].copy()
    end_values = legendre_values(points, node_count)[:, degree]
    weights = 2.0 / (degree * node_count * end_values * end_values)
    spacing = points[:, None] - points[None, :] + np.eye(node_count)
    diff_matrix = end_values[:, None] / end_values[None, :] / spacing
    diff_matrix = diff_matrix * (1.0 - np.eye(node_count))
    diff_matrix[0, 0] = -degree * node_count / 4.0
    diff_matrix[-1, -1] = degree * node_count / 4.0
    return (weights, diff_matrix)


def split_rows(matrix):
    high = matrix.astype(np.float32).astype(ml_dtypes.bfloat16)
    low = (matrix - high.astype(np.float64)).astype(np.float32).astype(ml_dtypes.bfloat16)
    return high, low


def tables():
    weights, diff = lobatto_table(NP)
    eye = np.eye(NP)
    cube = (
        weights[:, None, None] * weights[None, :, None] * weights[None, None, :]
    ).reshape(-1)
    directional = [
        np.kron(eye, np.kron(eye, diff)),
        np.kron(eye, np.kron(diff, eye)),
        np.kron(diff, np.kron(eye, eye)),
    ]
    stiff = np.zeros((NODES, NODES))
    for matrix in directional:
        stiff = stiff + matrix.T @ (cube[:, None] * matrix)
    mats = np.stack([np.stack(split_rows(m)) for m in (stiff, directional[2].T)])
    flat = np.concatenate([directional[0].T[:128, :128], directional[1].T[:128, :128]], 1)
    high, low = split_rows(flat)
    flat = np.concatenate([high, high, low], 0)
    lanes = np.zeros((8, NODES), np.float32)
    lanes[0] = cube
    lanes[1] = np.diag(stiff)
    lanes[2] = np.repeat(diff[0], LAYER)
    back = eye[::-1]
    half = np.eye(2)
    mirror = np.concatenate(
        [
            np.kron(half, np.kron(eye, back)),
            np.kron(half, np.kron(back, eye)),
            np.kron(half, np.kron(back, back)),
        ],
        1,
    ).astype(ml_dtypes.bfloat16)
    return mats, np.concatenate([np.concatenate([flat, np.zeros((384, 128), flat.dtype)], 1), mirror], 0), lanes


def rotated(value, shift, axis):
    return pltpu.roll(value, shift % value.shape[axis], axis)


def kernel(
    forcing, visc_in, mass_in, order_in, owner_in, lanes_in, flat_in, mats,
    out,
    fsc, lanes, flat, order_sc, owner_sc, weights, par, parn, pone, ptr, visc, mass, raw, tmp,
    inv, lhs, v0, v1, v2, v3, xs, xstd, grads, gz, gpack, classes, gcells, fsend, frecv, moments,
    red, packed, recv, lam, lamrecv,
    ssem, wsem, fsem, psend, precv, gsend, grecv, f3send, f3recv, rsend, rrecv, asend, arecv,
    osend, orecv,
):
    grp = lax.axis_index("grp")
    dom = lax.axis_index("dom")
    comp = jnp.minimum(grp, 2)
    up = lax.rem(dom + 1, DOMS)
    down = lax.rem(dom + DOMS - 1, DOMS)
    barrier = pltpu.get_barrier_semaphore()
    basis = (v0, v1, v2, v3)
    every = (0, 1, 2, 3)

    for step in range(1, DOMS):
        pl.semaphore_signal(
            barrier, inc=1, device_id=(grp, lax.rem(dom + step, DOMS)), device_id_type=MESH
        )
    for step in range(1, 4):
        pl.semaphore_signal(
            barrier, inc=1, device_id=(lax.rem(grp + step, 4), dom), device_id_type=MESH
        )

    load_small = [
        pltpu.make_async_copy(source, target, ssem.at[k])
        for k, (source, target) in enumerate(
            (
                (visc_in, par.at[0:1]),
                (mass_in, par.at[1:2]),
                (order_in, order_sc),
                (owner_in, owner_sc),
                (lanes_in, lanes),
                (flat_in, flat),
            )
        )
    ]
    for copy in load_small:
        copy.start()
    load_force = pltpu.make_async_copy(forcing.at[comp], fsc, fsem)
    load_force.start()
    load_mats = []
    for which in range(2):
        for part, source in enumerate((0, 0, 1)):
            copy = pltpu.make_async_copy(
                mats.at[which, source],
                weights.at[which, part * NODES : (part + 1) * NODES],
                wsem.at[3 * which + part],
            )
            copy.start()
            load_mats.append(copy)

    lane = lax.broadcasted_iota(jnp.int32, (8, 128), 1)
    sub = lax.broadcasted_iota(jnp.int32, (8, 128), 0)
    node_i = lax.rem(lane, 8)
    node_j = lax.rem(lane // 8, 8)
    odd = lax.rem(sub, 2) == 1
    first_i = node_i == 0
    last_i = node_i == 7
    take_up = ((last_i & jnp.logical_not(odd)) | (first_i & odd & (sub < 7)))
    take_down = ((last_i & odd) | (first_i & jnp.logical_not(odd) & (sub > 0)))
    has_up = jnp.where(dom < DOMS - 1, 1.0, 0.0).astype(F32)
    has_down = jnp.where(dom > 0, 1.0, 0.0).astype(F32)

    def wide(mask):
        return jnp.broadcast_to(mask[None], (8, 8, 128))

    x_up = wide(take_up)
    x_down = wide(take_down)
    x_odd = wide(odd)
    y_last = wide(node_j == 7)
    y_first = wide(node_j == 0)
    low_half = wide(lane < LAYER)

    def x_others(a):
        above = rotated(a, -1, 1)
        below = rotated(a, 1, 1)
        return jnp.where(x_up, above, jnp.where(x_down, below, 0.0))

    def y_others(a):
        blank = jnp.zeros((1, 8, 128), F32)
        last = jnp.concatenate([a[k ^ 1 : (k ^ 1) + 1] for k in range(8)], 0)
        first = jnp.concatenate(
            [blank] + [a[k : k + 1] for k in (2, 1, 4, 3, 6, 5)] + [blank], 0
        )
        return jnp.where(y_last, last, jnp.where(y_first, first, 0.0))

    def xy_sum(a):
        a = a + x_others(a)
        return a + y_others(a)

    def rows_of(layer):
        if isinstance(layer, int):
            return slice(layer * LAYER, layer * LAYER + LAYER)
        return pl.ds(pl.multiple_of(layer * LAYER, LAYER), LAYER)

    def load(ref, layer, tile):
        return ref[rows_of(layer), tile * 128 : tile * 128 + 128].reshape(8, 8, 128)

    def store(ref, layer, tile, value):
        ref[rows_of(layer), tile * 128 : tile * 128 + 128] = value.reshape(LAYER, 128)

    def column(ref, layer):
        return ref[rows_of(layer), :].reshape(8, 8, 128)

    def table(row, tile):
        return lanes[row : row + 1, tile * 128 : tile * 128 + 128].reshape(1, 1, 128)

    def split3(value):
        high = value.astype(BF16)
        rest = value - high.astype(F32)
        middle = rest.astype(BF16)
        low = (rest - middle.astype(F32)).astype(BF16)
        return high, middle, low

    def store_lhs(layer, tile, value):
        value = value.reshape(LAYER, 128)
        high = value.astype(BF16)
        low = (value - high.astype(F32)).astype(BF16)
        lhs[rows_of(layer), tile * 128 : tile * 128 + 128] = high
        lhs[rows_of(layer), NODES + tile * 128 : NODES + tile * 128 + 128] = low
        lhs[rows_of(layer), 2 * NODES + tile * 128 : 2 * NODES + tile * 128 + 128] = high

    def reversals(value):
        total = None
        for part in split3(value):
            term = jnp.dot(part, flat[384:512, :], preferred_element_type=F32)
            total = term if total is None else total + term
        return total[:, 0:128], total[:, 128:256], total[:, 256:384]

    def mirror_layers(value, tile, target, base):
        flipped = reversals(value)
        for layer in range(4):
            rows = slice(layer * LAYER, layer * LAYER + LAYER)
            plain, rev_x, rev_y, rev_xy = [
                part[rows].reshape(8, 8, 128) for part in (value,) + flipped
            ]
            even_y = jnp.where(x_odd, rev_x, plain)
            odd_y = jnp.where(x_odd, rev_xy, rev_y)
            mixed = jnp.concatenate(
                [(odd_y if k % 2 else even_y)[k : k + 1] for k in range(8)], 0
            )
            if layer % 2:
                store(target, base + layer, 3 - tile, rotated(mixed, 64, 2))
            else:
                store(target, base + layer, tile, mixed)

    def over(low, high, body):
        lax.fori_loop(low, high, lambda layer, carry: (body(layer), carry)[1], 0)

    cell_sub = lax.broadcasted_iota(jnp.int32, (CELLS, CELLS), 0).astype(F32)
    cell_lane = lax.broadcasted_iota(jnp.int32, (CELLS, CELLS), 1).astype(F32)
    for copy in load_small:
        copy.wait()
    par[2:3, :] = order_sc[...].astype(F32)
    par[3:8, :] = jnp.zeros((5, CELLS), F32)

    def coefficients(ref, base, scale):
        hit = ref[2:3, :] == cell_sub
        for row, target in ((0, visc), (1, mass)):
            col = jnp.sum(jnp.where(hit, ref[row : row + 1, :], 0.0), axis=1, keepdims=True)
            target[base : base + CELLS, :] = jnp.broadcast_to(col * scale, (CELLS, 128))
        return hit

    pone[...] = jnp.where(par[2:3, :] == cell_sub, 1.0, 0.0).astype(BF16)
    load_force.wait()
    for tile in every:
        cols = slice(tile * 128, tile * 128 + 128)
        total = None
        for part in split3(fsc[:, cols]):
            term = jnp.dot(pone[...], part, preferred_element_type=F32)
            total = term if total is None else total + term
        mirror_layers(total * lanes[0:1, cols], tile, raw, 4)

    pl.semaphore_wait(barrier, DOMS - 1 + 3)

    def remote(src, dst, send, recv_sem, device):
        return pltpu.make_async_remote_copy(
            src_ref=src, dst_ref=dst, send_sem=send, recv_sem=recv_sem,
            device_id=device, device_id_type=MESH,
        )

    par_copies = [
        remote(par, parn.at[0], psend.at[0], precv.at[0], (grp, up)),
        remote(par, parn.at[1], psend.at[1], precv.at[1], (grp, down)),
    ]
    ghost_copies = [
        remote(
            raw.at[5 * LAYER : 8 * LAYER], raw.at[1 * LAYER : 4 * LAYER],
            gsend.at[0], grecv.at[0], (grp, up),
        ),
        remote(
            raw.at[4 * LAYER : 7 * LAYER], raw.at[8 * LAYER : 11 * LAYER],
            gsend.at[1], grecv.at[1], (grp, down),
        ),
        remote(
            raw.at[4 * LAYER : 5 * LAYER, 384:512], raw.at[0:LAYER, 384:512],
            gsend.at[2], grecv.at[2], (grp, up),
        ),
        remote(
            raw.at[7 * LAYER : 8 * LAYER, 384:512], raw.at[11 * LAYER : 12 * LAYER, 384:512],
            gsend.at[3], grecv.at[3], (grp, down),
        ),
    ]
    for copy in par_copies + ghost_copies:
        copy.start()

    coefficients(par, CELLS, 1.0)
    order_col = jnp.sum(
        jnp.where(cell_sub == cell_lane, par[2:3, :], 0.0), axis=1, keepdims=True
    )
    ptr[...] = jnp.where(order_col == cell_lane, 1.0, 0.0).astype(BF16)
    owner_row = owner_sc[...].astype(F32)
    owner_col = jnp.sum(
        jnp.where(cell_sub == cell_lane, owner_row, 0.0), axis=1, keepdims=True
    )
    same = (owner_col == owner_row) & (cell_sub < cell_lane)
    rank_row = jnp.sum(jnp.where(same, 1.0, 0.0), axis=0, keepdims=True)
    dest_row = jnp.where(owner_row >= 0.0, owner_row * 8.0 + rank_row, -1.0)
    slot_of = jnp.where(dest_row == cell_sub, 1.0, 0.0).astype(BF16)
    gpack[...] = jnp.dot(slot_of, ptr[...], preferred_element_type=F32).astype(BF16)
    cell_id = lax.broadcasted_iota(jnp.int32, (CELLS, 128), 0)
    for k, width in enumerate((1, 8, 64)):
        parity = lax.rem(cell_id // width, 2).astype(F32).astype(BF16)
        classes[:, k * 128 : k * 128 + 128] = jnp.dot(
            gpack[...], parity, preferred_element_type=F32
        )

    for copy in par_copies:
        copy.wait()
    coefficients(parn.at[0], 0, has_down)
    coefficients(parn.at[1], 2 * CELLS, has_up)

    def partners(layer):
        parity = layer % 2 if isinstance(layer, int) else lax.rem(layer, 2)
        return {0: layer - 1 + 2 * parity, 3: layer + 1 - 2 * parity}

    def face_sum(ref, layer, tile):
        value = load(ref, layer, tile)
        other = load(ref, partners(layer)[tile], tile)
        if tile == 0:
            return value + jnp.where(low_half, other, 0.0)
        return value + jnp.where(low_half, 0.0, other)

    def put_inverse(layer, tile, diag):
        store(inv, layer, tile, jnp.where(diag > 0.0, (2.0 / DELTA) / diag, 0.0))

    def diagonal(layer, tiles):
        coef_v = column(visc, layer)
        coef_m = column(mass, layer)
        for tile in tiles:
            diag = xy_sum(coef_v * table(1, tile) + coef_m * table(0, tile))
            if tile in (0, 3):
                store(tmp, layer, tile, diag)
            else:
                put_inverse(layer, tile, diag)

    diagonal(0, (3,))
    over(1, 11, lambda layer: diagonal(layer, every))
    diagonal(11, (3,))

    def diagonal_faces(layer):
        for tile in (0, 3):
            put_inverse(layer, tile, face_sum(tmp, layer, tile))

    over(1, 11, diagonal_faces)

    def put_first(layer, tile, force):
        value = force * load(inv, layer, tile) * (0.5 * DELTA)
        store(v0, layer, tile, value)
        store_lhs(layer, tile, value)

    def assemble(layer, tiles, scale):
        for tile in tiles:
            force = load(raw, layer, tile)
            if scale is not None:
                force = force * scale
            force = xy_sum(force)
            if tile in (0, 3):
                store(tmp, layer, tile, force)
            else:
                put_first(layer, tile, force)

    over(4, 8, lambda layer: assemble(layer, every, None))
    for copy in load_mats:
        copy.wait()
    for copy in ghost_copies:
        copy.wait()
    assemble(0, (3,), has_down)
    over(1, 4, lambda layer: assemble(layer, every, has_down))
    over(8, 11, lambda layer: assemble(layer, every, has_up))
    assemble(11, (3,), has_up)

    def first_faces(layer):
        for tile in (0, 3):
            put_first(layer, tile, face_sum(tmp, layer, tile))

    over(1, 11, first_faces)

    def multiply(low, high, which, target, target_low):
        def body(half, carry):
            cols = pl.ds(pl.multiple_of(half * 256, 256), 256)
            target[target_low * LAYER : (target_low + high - low) * LAYER, cols] = jnp.dot(
                lhs[low * LAYER : high * LAYER, :],
                weights[which, :, cols],
                preferred_element_type=F32,
            )
            return carry

        lax.fori_loop(0, 2, body, 0)

    def advance(step, layer, tile, total):
        value = total * load(inv, layer, tile)
        current = load(basis[step], layer, tile)
        if step == 0:
            value = 0.5 * value - (THETA / DELTA) * current
        else:
            value = value - (2.0 * THETA / DELTA) * current - load(basis[step - 1], layer, tile)
        store(basis[step + 1], layer, tile, value)
        store_lhs(layer, tile, value)

    def apply(step, layer, tiles, sums, going):
        coef_v = column(visc, layer)
        coef_m = column(mass, layer)
        for tile in tiles:
            value = load(basis[step], layer, tile)
            weighted = coef_m * table(0, tile)
            image = coef_v * load(tmp, layer, tile) + weighted * value
            if sums is not None:
                diag = coef_v * table(1, tile) + weighted
                sums = (
                    sums[0] + jnp.sum(value * image, axis=0),
                    sums[1] + jnp.sum(value * value * diag, axis=0),
                )
            if going:
                image = xy_sum(image)
                if tile in (0, 3):
                    store(tmp, layer, tile, image)
                else:
                    advance(step, layer, tile, image)
        return sums

    def faces(step, layer):
        for tile in (0, 3):
            advance(step, layer, tile, face_sum(tmp, layer, tile))

    blank_sums = (jnp.zeros((8, 128), F32), jnp.zeros((8, 128), F32))
    for step in range(ITERS):
        low, high = 1 + step, 11 - step
        going = step + 1 < ITERS
        multiply(low, high, 0, tmp, low)
        if going:
            inward = 0 if low % 2 else 3
            apply(step, low, (inward,), None, True)
            over(low + 1, 4, lambda layer: apply(step, layer, every, None, True))
        sums = lax.fori_loop(
            4, 8, lambda layer, carry: apply(step, layer, every, carry, going), blank_sums
        )
        if going:
            over(8, high - 1, lambda layer: apply(step, layer, every, None, True))
            apply(step, high - 1, (inward,), None, True)
        moments[step : step + 1, :] = jnp.sum(sums[0], axis=0, keepdims=True)
        moments[4 + step : 5 + step, :] = jnp.sum(sums[1], axis=0, keepdims=True)
        if going:
            over(low + 1, high - 1, lambda layer: faces(step, layer))

    red[0] = moments[...]
    for step in range(1, DOMS):
        remote(
            moments, red.at[step], rsend, rrecv, (grp, lax.rem(dom + step, DOMS))
        ).start()

    def end_face(ref, layer):
        total = load(ref, layer, 0) * table(2, 0)
        for tile in (1, 2, 3):
            total = total + load(ref, layer, tile) * table(2, tile)
        total = total + rotated(total, 64, 2)
        return -total if layer % 2 else total

    fsend[0] = end_face(v3, 7).reshape(LAYER, 128)
    fsend[1] = end_face(v3, 4).reshape(LAYER, 128)
    face_copies = [
        remote(fsend.at[0], frecv.at[0], f3send.at[0], f3recv.at[0], (grp, up)),
        remote(fsend.at[1], frecv.at[1], f3send.at[1], f3recv.at[1], (grp, down)),
    ]
    for copy in face_copies:
        copy.start()

    x_sign = jnp.where(odd, -1.0, 1.0).reshape(1, 8, 128)
    x_scale = jnp.where(take_up | take_down, 0.5, 1.0).reshape(1, 8, 128) * x_sign
    y_half = jnp.where((node_j == 7) | (node_j == 0), 0.5, 1.0).reshape(1, 8, 128)
    y_end = jnp.where(node_j == 7, 0.5, 1.0).reshape(1, 8, 128)
    y_scale = jnp.concatenate(
        [y_end, -y_half, y_half, -y_half, y_half, -y_half, y_half, -y_end], 0
    )

    def refill(ref):
        def body(layer):
            for tile in every:
                store_lhs(layer, tile, load(ref, layer, tile))

        over(4, 8, body)

    for index in range(ITERS):
        vec = basis[index]
        if index < ITERS - 1:
            refill_needed = True
        else:
            refill_needed = True
        if refill_needed:
            refill(vec)
        own_rows = slice(4 * LAYER, 8 * LAYER)

        def in_plane(tile, carry, index=index):
            start = pl.multiple_of(tile * 128, 128)
            left = jnp.concatenate(
                [lhs[own_rows, pl.ds(part * NODES + start, 128)] for part in range(3)], 1
            )
            both = jnp.dot(left, flat[0:384, 0:256], preferred_element_type=F32)
            for layer in range(4):
                rows = slice(layer * LAYER, layer * LAYER + LAYER)
                value = both[rows, 0:128].reshape(8, 8, 128)
                value = x_scale * (value - x_others(value))
                grads[index, rows, pl.ds(start, 128)] = value.reshape(LAYER, 128)
                value = both[rows, 128:256].reshape(8, 8, 128)
                value = y_scale * (value - y_others(value))
                grads[index, rows, pl.ds(NODES + start, 128)] = value.reshape(LAYER, 128)
            return carry

        lax.fori_loop(0, 4, in_plane, 0)
        multiply(4, 8, 1, gz, 0)
        if index == ITERS - 1:
            for copy in face_copies:
                copy.wait()
        for layer in range(4):
            sign = -1.0 if layer % 2 else 1.0
            for tile in every:
                value = load(gz, layer, tile) * sign
                if tile == 0:
                    if layer in (0, 3):
                        side = 0 if layer == 0 else 1
                        if index == ITERS - 1:
                            other = frecv[side].reshape(8, 8, 128)
                        else:
                            other = end_face(vec, 3 if side == 0 else 8)
                        there = 0.5 * (has_down if side == 0 else has_up)
                    else:
                        other = load(gz, 3 - layer, 0) * -sign
                        there = 0.5
                    value = value + jnp.where(low_half, there * (other - value), 0.0)
                if tile == 3:
                    other = load(gz, layer ^ 1, 3) * -sign
                    value = value + jnp.where(low_half, 0.0, 0.5 * (other - value))
                base = 2 * NODES + tile * 128
                grads[index, layer * LAYER : layer * LAYER + LAYER, base : base + 128] = (
                    value.reshape(LAYER, 128)
                )

    whole = remote(red.at[1:DOMS], red.at[1:DOMS], rsend, rrecv, (grp, up))
    whole.wait_send()
    whole.wait_recv()

    total = jnp.sum(red[...], axis=0)
    total = jnp.broadcast_to(jnp.sum(total, axis=1, keepdims=True), (8, 128))
    moments[...] = total

    def scalar(row):
        return jnp.broadcast_to(moments[row : row + 1, :], (8, 128))

    alpha = [scalar(row) for row in range(4)]
    beta = [scalar(4 + row) for row in range(4)]
    gamma = [(alpha[k] - THETA * beta[k]) * (1.0 / DELTA) for k in range(4)]
    mu = [beta[0], gamma[0]]
    ahead = gamma[0]
    for k in range(1, 4):
        ahead = 2.0 * gamma[k] - ahead
        mu.append(2.0 * beta[k] - mu[0])
        mu.append(2.0 * ahead - mu[1])

    def inner(i, j):
        return 0.5 * (mu[i + j] + mu[abs(i - j)])

    gram = [
        [
            DELTA * 0.5 * (inner(i, j + 1) + inner(i, abs(j - 1))) + THETA * inner(i, j)
            for j in range(4)
        ]
        for i in range(4)
    ]
    right = [mu[k] for k in range(4)]
    pivots = []
    for k in range(4):
        original = DELTA * 0.5 * (inner(k, k + 1) + inner(k, abs(k - 1))) + THETA * inner(k, k)
        pivot = gram[k][k]
        good = pivot > 1e-7 * original
        inverse = jnp.where(good, 1.0 / jnp.where(good, pivot, 1.0), 0.0)
        pivots.append(inverse)
        for i in range(k + 1, 4):
            factor = gram[i][k] * inverse
            for j in range(k + 1, 4):
                gram[i][j] = gram[i][j] - factor * gram[k][j]
            right[i] = right[i] - factor * right[k]
    coef = [None] * 4
    for k in (3, 2, 1, 0):
        value = right[k]
        for j in range(k + 1, 4):
            value = value - gram[k][j] * coef[j]
        coef[k] = value * pivots[k]

    wide16 = [
        jnp.concatenate([value * (1.0 / NP)] * 2, 0).reshape(1, 16, 128) for value in coef
    ]

    def combine_grads(block, carry):
        rows = pl.ds(pl.multiple_of(block * 32, 32), 32)
        for tile in range(12):
            cols = slice(tile * 128, tile * 128 + 128)
            value = wide16[0] * grads[0, rows, cols].reshape(2, 16, 128)
            for k in range(1, 4):
                value = value + wide16[k] * grads[k, rows, cols].reshape(2, 16, 128)
            gcells[rows, cols] = value.reshape(32, 128).astype(BF16)
        return carry

    lax.fori_loop(0, 8, combine_grads, 0)

    def pack(part, carry):
        cols = pl.ds(pl.multiple_of(part * 256, 256), 256)
        packed[:, cols] = jnp.dot(
            gpack[...], gcells[:, cols], preferred_element_type=F32
        ).astype(BF16)
        return carry

    lax.fori_loop(0, 6, pack, 0)

    def to_group(target, slot):
        start = pl.multiple_of(target * LAYER, LAYER)
        return remote(
            packed.at[pl.ds(start, LAYER)], recv.at[comp],
            asend.at[slot], arecv.at[comp], (target, dom),
        )

    def each_send(action):
        @pl.when(grp < 2)
        def _():
            for step in range(1, 4):
                action(to_group(lax.rem(grp + step, 4), step - 1))

        @pl.when(grp >= 2)
        def _():
            action(to_group(3 - grp, 0))

    each_send(lambda copy: copy.start())
    own_slots = pl.ds(pl.multiple_of(grp * LAYER, LAYER), LAYER)
    recv[comp] = packed[own_slots, :]

    wide8 = [value.reshape(1, 8, 128) for value in coef]

    @pl.when(grp < 3)
    def _():
        def solve_layer(layer):
            for tile in every:
                value = wide8[0] * load(v0, layer, tile)
                for k in range(1, 4):
                    value = value + wide8[k] * load(basis[k], layer, tile)
                store(xs, layer - 4, tile, value)

        over(4, 8, solve_layer)
        for tile in every:
            mirror_layers(xs[:, tile * 128 : tile * 128 + 128], tile, xstd, 0)

        def velocity_out(tile, carry):
            cols = pl.ds(pl.multiple_of(tile * 128, 128), 128)
            total = jnp.zeros((CELLS, 128), F32)
            for part in split3(xstd[:, cols]):
                total = total + jnp.dot(ptr[...], part, preferred_element_type=F32)
            out[:, cols] = total
            return carry

        lax.fori_loop(0, 4, velocity_out, 0)

    each_send(lambda copy: copy.wait_send())
    for step in (1, 2):
        other = lax.rem(comp + step, 3)
        remote(recv.at[other], recv.at[other], asend.at[0], arecv.at[other], (grp, up)).wait_recv()

    def lambda_rows(block, carry):
        rows = pl.ds(pl.multiple_of(block * 16, 16), 16)
        for part in range(2):
            jac = [
                [
                    recv[c, rows, d * NODES + part * 256 : d * NODES + part * 256 + 256].astype(F32)
                    for d in range(3)
                ]
                for c in range(3)
            ]
            lam[rows, part * 256 : part * 256 + 256] = lambda_two(jac)
        return carry

    lax.fori_loop(0, 4, lambda_rows, 0)

    odd_x, odd_y, odd_z = [
        classes[own_slots, k * 128 : k * 128 + 128] > 0.5 for k in range(3)
    ]
    turned = []
    for tile in every:
        value = lam[:, tile * 128 : tile * 128 + 128]
        rev_x, rev_y, rev_xy = reversals(value)
        turned.append(
            jnp.where(odd_x, jnp.where(odd_y, rev_xy, rev_x), jnp.where(odd_y, rev_y, value))
        )
    for tile in every:
        lam[:, tile * 128 : tile * 128 + 128] = jnp.where(
            odd_z, rotated(turned[3 - tile], 64, 1), turned[tile]
        )

    base = grp * 8
    here = pl.ds(pl.multiple_of(dom * 8, 8), 8)

    def to_owner(k):
        return remote(
            lam.at[8 * k : 8 * k + 8], lamrecv.at[here], osend.at[k], orecv, (3, base + k)
        )

    def each_owner(action):
        for k in range(8):
            own = (grp == 3) & (base + k == dom)

            @pl.when(jnp.logical_not(own))
            def _():
                action(to_owner(k))

    each_owner(lambda copy: copy.start())
    for k in range(8):

        @pl.when((grp == 3) & (base + k == dom))
        def _():
            lamrecv[here, :] = lam[8 * k : 8 * k + 8, :]

    each_owner(lambda copy: copy.wait_send())

    def wait_rows(count):
        piece = lamrecv.at[0 : 8 * count]
        remote(piece, piece, osend.at[0], orecv, (grp, up)).wait_recv()

    @pl.when((grp == 3) & (dom >= 24))
    def _():
        wait_rows(31)

    @pl.when((grp == 3) & (dom < 24))
    def _():
        wait_rows(32)

    @pl.when(grp == 3)
    def _():
        out[...] = lamrecv[...]


def lambda_two(jac):
    strain = [[0.5 * (jac[a][b] + jac[b][a]) for b in range(3)] for a in range(3)]
    spin = [[0.5 * (jac[a][b] - jac[b][a]) for b in range(3)] for a in range(3)]
    m = [[None] * 3 for _ in range(3)]
    for a in range(3):
        for b in range(a, 3):
            value = strain[a][0] * strain[0][b] + spin[a][0] * spin[0][b]
            for k in (1, 2):
                value = value + strain[a][k] * strain[k][b] + spin[a][k] * spin[k][b]
            m[a][b] = value
            m[b][a] = value
    for sweep in range(SWEEPS):
        for p, q, r in ((0, 1, 2), (0, 2, 1), (1, 2, 0)):
            last = sweep == SWEEPS - 1
            twice = 2.0 * m[p][q]
            gap = m[p][p] - m[q][q]
            square = twice * twice + gap * gap
            inverse = lax.rsqrt(jnp.maximum(square, 1e-36))
            length = square * inverse
            mean = 0.5 * (m[p][p] + m[q][q])
            m[p][p] = mean + 0.5 * length
            m[q][q] = mean - 0.5 * length
            if last and (p, q) == (1, 2):
                continue
            none = square < 1e-36
            cosine2 = jnp.where(none, 1.0, jnp.abs(gap) * inverse)
            sine2 = jnp.where(none, 0.0, twice * inverse)
            larger = 0.5 + 0.5 * cosine2
            root = lax.rsqrt(larger)
            big = larger * root
            small = 0.5 * sine2 * root
            flip = gap < 0.0
            sine_big = jnp.where(sine2 < 0.0, -big, big)
            cosine = jnp.where(flip, jnp.abs(small), big)
            sine = jnp.where(flip, sine_big, small)
            side_p = m[r][p]
            side_q = m[r][q]
            m[r][p] = m[p][r] = cosine * side_p + sine * side_q
            m[r][q] = m[q][r] = cosine * side_q - sine * side_p
            m[p][q] = m[q][p] = jnp.zeros_like(side_p)
    diagonal = [m[0][0], m[1][1], m[2][2]]
    largest = jnp.maximum(jnp.maximum(diagonal[0], diagonal[1]), diagonal[2])
    smallest = jnp.minimum(jnp.minimum(diagonal[0], diagonal[1]), diagonal[2])
    return diagonal[0] + diagonal[1] + diagonal[2] - largest - smallest


def per_device(forcing, viscosity, mass_coef, element_order, owner):
    mats, flat, lanes = tables()
    vmem = pl.BlockSpec(memory_space=pltpu.VMEM)
    hbm = pl.BlockSpec(memory_space=pltpu.HBM)
    wide = (12 * LAYER, NODES)
    own = (CELLS, NODES)
    dma = pltpu.SemaphoreType.DMA
    result = pl.pallas_call(
        kernel,
        out_shape=jax.ShapeDtypeStruct(own, F32),
        in_specs=[hbm] * 8,
        out_specs=vmem,
        scratch_shapes=[
            pltpu.VMEM(own, F32),
            pltpu.VMEM((8, NODES), F32),
            pltpu.VMEM((512, 384), BF16),
            pltpu.VMEM((1, CELLS), jnp.int32),
            pltpu.VMEM((1, CELLS), jnp.int32),
            pltpu.VMEM((2, 3 * NODES, NODES), BF16),
            pltpu.VMEM((8, CELLS), F32),
            pltpu.VMEM((2, 8, CELLS), F32),
            pltpu.VMEM((CELLS, CELLS), BF16),
            pltpu.VMEM((CELLS, CELLS), BF16),
            pltpu.VMEM((12 * LAYER, 128), F32),
            pltpu.VMEM((12 * LAYER, 128), F32),
            pltpu.VMEM(wide, F32),
            pltpu.VMEM(wide, F32),
            pltpu.VMEM(wide, F32),
            pltpu.VMEM((12 * LAYER, 3 * NODES), BF16),
            pltpu.VMEM(wide, F32),
            pltpu.VMEM(wide, F32),
            pltpu.VMEM(wide, F32),
            pltpu.VMEM(wide, F32),
            pltpu.VMEM(own, F32),
            pltpu.VMEM(own, F32),
            pltpu.VMEM((4, CELLS, 3 * NODES), F32),
            pltpu.VMEM(own, F32),
            pltpu.VMEM((CELLS, CELLS), BF16),
            pltpu.VMEM((CELLS, 384), F32),
            pltpu.VMEM((CELLS, 3 * NODES), BF16),
            pltpu.VMEM((2, LAYER, 128), F32),
            pltpu.VMEM((2, LAYER, 128), F32),
            pltpu.VMEM((8, 128), F32),
            pltpu.VMEM((DOMS, 8, 128), F32),
            pltpu.VMEM((CELLS, 3 * NODES), BF16),
            pltpu.VMEM((3, LAYER, 3 * NODES), BF16),
            pltpu.VMEM((LAYER, NODES), F32),
            pltpu.VMEM(own, F32),
            dma((6,)), dma((6,)), dma, dma((2,)), dma((2,)), dma((4,)), dma((4,)), dma((2,)),
            dma((2,)), dma, dma, dma((3,)), dma((3,)), dma((8,)), dma,
        ],
        compiler_params=pltpu.CompilerParams(
            collective_id=0, has_side_effects=True, vmem_limit_bytes=60 * 1024 * 1024
        ),
        name="solve_and_analyse",
    )(
        forcing, viscosity[None], mass_coef[None], element_order, owner,
        jnp.asarray(lanes), jnp.asarray(flat), jnp.asarray(mats),
    )
    return result[None]


def solution(mesh):
    in_specs = (P(None, "dom", None), P("dom"), P("dom"), P("dom", None), P("dom", None))
    out_specs = P("grp", "dom", None)
    return jax.shard_map(
        per_device, mesh=mesh, in_specs=in_specs, out_specs=out_specs, check_vma=False
    )
```

```python
import functools

import jax
import jax.numpy as jnp
import ml_dtypes
import numpy as np
from jax import lax
from jax.experimental import pallas as pl
from jax.experimental.pallas import tpu as pltpu
from jax.sharding import PartitionSpec as P

NP = 8
ITERS = 4
SWEEPS = 4
LAYER = 64
CELLS = 256
NODES = 512
DOMS = 32
HALF = 128
CHUNK = 32
BASIS_LOW = 0.3
BASIS_HIGH = 2.0
THETA = 0.5 * (BASIS_LOW + BASIS_HIGH)
DELTA = 0.5 * (BASIS_HIGH - BASIS_LOW)
MESH = pl.DeviceIdType.MESH
F32 = jnp.float32
BF16 = jnp.bfloat16


def legendre_values(points, node_count):
    legendre = np.zeros((points.shape[0], node_count))
    legendre[:, 0] = 1.0
    legendre[:, 1] = points
    for poly_order in range(2, node_count):
        legendre[:, poly_order] = (
            (2 * poly_order - 1) * points * legendre[:, poly_order - 1]
            - (poly_order - 1) * legendre[:, poly_order - 2]
        ) / poly_order
    return legendre


def lobatto_table(node_count):
    degree = node_count - 1
    points = np.cos(np.pi * np.arange(node_count) / degree)
    for attempt in range(60):
        legendre = legendre_values(points, node_count)
        points = points - (points * legendre[:, degree] - legendre[:, degree - 1]) / (
            node_count * legendre[:, degree]
        )
    points = points[::-1].copy()
    end_values = legendre_values(points, node_count)[:, degree]
    weights = 2.0 / (degree * node_count * end_values * end_values)
    spacing = points[:, None] - points[None, :] + np.eye(node_count)
    diff_matrix = end_values[:, None] / end_values[None, :] / spacing
    diff_matrix = diff_matrix * (1.0 - np.eye(node_count))
    diff_matrix[0, 0] = -degree * node_count / 4.0
    diff_matrix[-1, -1] = degree * node_count / 4.0
    return (weights, diff_matrix)


def split_rows(matrix):
    high = matrix.astype(np.float32).astype(ml_dtypes.bfloat16)
    low = (matrix - high.astype(np.float64)).astype(np.float32).astype(ml_dtypes.bfloat16)
    return high, low


def tables():
    weights, diff = lobatto_table(NP)
    eye = np.eye(NP)
    cube = (
        weights[:, None, None] * weights[None, :, None] * weights[None, None, :]
    ).reshape(-1)
    directional = [
        np.kron(eye, np.kron(eye, diff)),
        np.kron(eye, np.kron(diff, eye)),
        np.kron(diff, np.kron(eye, eye)),
    ]
    stiff = np.zeros((NODES, NODES))
    for matrix in directional:
        stiff = stiff + matrix.T @ (cube[:, None] * matrix)
    flip = np.arange(NODES).reshape(NP, LAYER)[::-1][: NP // 2].reshape(-1)
    mats = []
    for matrix in (stiff, directional[2]):
        near, far = matrix[:256, :256], matrix[:256, flip]
        for block in (0.5 * (near + far), 0.5 * (near - far)):
            mats.append(np.stack(split_rows(block.T)))
    mats = np.stack(mats)
    flat = np.concatenate([directional[0].T[:128, :128], directional[1].T[:128, :128]], 1)
    high, low = split_rows(flat)
    flat = np.concatenate([high, high, low], 0)
    lanes = np.zeros((8, NODES), np.float32)
    lanes[0] = cube
    lanes[1] = np.diag(stiff)
    lanes[2] = np.repeat(diff[0], LAYER)
    order = [0, 1, 2, 3, 5, 4, 7, 6]
    lanes = lanes.reshape(8, NP, LAYER)[:, order].reshape(8, NODES)
    natural = cube.reshape(NP, LAYER).astype(np.float32).reshape(-1)
    lanes[3] = natural
    back = eye[::-1]
    half = np.eye(2)
    mirror = np.concatenate(
        [
            np.kron(half, np.kron(eye, back)),
            np.kron(half, np.kron(back, eye)),
            np.kron(half, np.kron(back, back)),
        ],
        1,
    ).astype(ml_dtypes.bfloat16)
    wide = np.concatenate([flat, np.zeros((384, 128), flat.dtype)], 1)
    return mats, np.concatenate([wide, mirror, mirror], 0), lanes


def rotated(value, shift, axis):
    return pltpu.roll(value, shift % value.shape[axis], axis)


def kernel(
    forcing, visc_in, mass_in, order_in, owner_in, lanes_in, flat_in, mats,
    out,
    fsc, lanes, flat, order_sc, owner_sc, weights, par, parn, pone, ptr, parts, visc, mass, raw, tmp,
    inv, lhs, v0, v1, v2, v3, xs, xstd, grads, gpack, classes, gcells, fsend, frecv, fghost, moments,
    red, packed, recv, lam, lamrecv,
    ssem, wsem, fsem, psend, precv, gsend, grecv, f3send, f3recv, rsend, rrecv, asend, arecv,
    osend, orecv,
):
    grp = lax.axis_index("grp")
    dom = lax.axis_index("dom")
    comp = jnp.minimum(grp, 2)
    up = lax.rem(dom + 1, DOMS)
    down = lax.rem(dom + DOMS - 1, DOMS)
    barrier = pltpu.get_barrier_semaphore()
    basis = (v0, v1, v2, v3)
    every = (0, 1, 2, 3)

    for step in range(1, DOMS):
        pl.semaphore_signal(
            barrier, inc=1, device_id=(grp, lax.rem(dom + step, DOMS)), device_id_type=MESH
        )
    for step in range(1, 4):
        pl.semaphore_signal(
            barrier, inc=1, device_id=(lax.rem(grp + step, 4), dom), device_id_type=MESH
        )

    load_small = [
        pltpu.make_async_copy(source, target, ssem.at[k])
        for k, (source, target) in enumerate(
            (
                (visc_in, par.at[0:1]),
                (mass_in, par.at[1:2]),
                (order_in, order_sc),
                (owner_in, owner_sc),
                (lanes_in, lanes),
                (flat_in, flat),
            )
        )
    ]
    for copy in load_small:
        copy.start()
    load_force = pltpu.make_async_copy(forcing.at[comp], fsc, fsem)
    load_force.start()
    load_mats = []
    for which in range(4):
        for part, source in enumerate((0, 0, 1)):
            copy = pltpu.make_async_copy(
                mats.at[which, source],
                weights.at[which, part * 256 : part * 256 + 256],
                wsem.at[3 * which + part],
            )
            copy.start()
            load_mats.append(copy)

    lane = lax.broadcasted_iota(jnp.int32, (8, 128), 1)
    sub = lax.broadcasted_iota(jnp.int32, (8, 128), 0)
    node_i = lax.rem(lane, 8)
    node_j = lax.rem(lane // 8, 8)
    odd = lax.rem(sub, 2) == 1
    first_i = node_i == 0
    last_i = node_i == 7
    take_up = ((last_i & jnp.logical_not(odd)) | (first_i & odd & (sub < 7)))
    take_down = ((last_i & odd) | (first_i & jnp.logical_not(odd) & (sub > 0)))
    has_up = jnp.where(dom < DOMS - 1, 1.0, 0.0).astype(F32)
    has_down = jnp.where(dom > 0, 1.0, 0.0).astype(F32)

    def wide(mask):
        return jnp.broadcast_to(mask[None], (8, 8, 128))

    x_up = wide(take_up)
    x_down = wide(take_down)
    x_odd = wide(odd)
    y_last = wide(node_j == 7)
    y_first = wide(node_j == 0)
    low_half = wide(lane < LAYER)

    def x_others(a):
        above = rotated(a, -1, 1)
        below = rotated(a, 1, 1)
        return jnp.where(x_up, above, jnp.where(x_down, below, 0.0))

    def y_others(a):
        blank = jnp.zeros((1, 8, 128), F32)
        last = jnp.concatenate([a[k ^ 1 : (k ^ 1) + 1] for k in range(8)], 0)
        first = jnp.concatenate(
            [blank] + [a[k : k + 1] for k in (2, 1, 4, 3, 6, 5)] + [blank], 0
        )
        return jnp.where(y_last, last, jnp.where(y_first, first, 0.0))

    def xy_sum(a):
        a = a + x_others(a)
        return a + y_others(a)

    def rows_of(layer):
        if isinstance(layer, int):
            return slice(layer * LAYER, layer * LAYER + LAYER)
        return pl.ds(pl.multiple_of(layer * LAYER, LAYER), LAYER)

    def load(ref, layer, tile):
        return ref[rows_of(layer), tile * 128 : tile * 128 + 128].reshape(8, 8, 128)

    def store(ref, layer, tile, value):
        ref[rows_of(layer), tile * 128 : tile * 128 + 128] = value.reshape(LAYER, 128)

    def column(ref, layer):
        return ref[rows_of(layer), :].reshape(8, 8, 128)

    def table(row, tile):
        return lanes[row : row + 1, tile * 128 : tile * 128 + 128].reshape(1, 1, 128)

    def split(value):
        high = value.astype(BF16)
        return high, (value - high.astype(F32)).astype(BF16)

    def store_lhs(layer, pair, first, second):
        for start, value in ((0, first + second), (768, first - second)):
            start = start + pair * 128
            high, low = split(value.reshape(LAYER, 128))
            lhs[rows_of(layer), start : start + 128] = high
            lhs[rows_of(layer), start + 256 : start + 384] = low
            lhs[rows_of(layer), start + 512 : start + 640] = high

    def reversals(value):
        total = jnp.dot(
            jnp.concatenate(split(value), 1), flat[384:640, :], preferred_element_type=F32
        )
        return total[:, 0:128], total[:, 128:256], total[:, 256:384]

    def mirror_layers(value, tile, target, base, back):
        flipped = reversals(value)
        for layer in range(4):
            rows = slice(layer * LAYER, layer * LAYER + LAYER)
            plain, rev_x, rev_y, rev_xy = [
                part[rows].reshape(8, 8, 128) for part in (value,) + flipped
            ]
            even_y = jnp.where(x_odd, rev_x, plain)
            odd_y = jnp.where(x_odd, rev_xy, rev_y)
            mixed = jnp.concatenate(
                [(odd_y if k % 2 else even_y)[k : k + 1] for k in range(8)], 0
            )
            place = 3 - tile if layer % 2 else tile
            if (place if back else tile) >= 2:
                mixed = rotated(mixed, 64, 2)
            store(target, base + layer, place, mixed)

    def over(low, high, body):
        lax.fori_loop(low, high, lambda layer, carry: (body(layer), carry)[1], 0)

    cell_sub = lax.broadcasted_iota(jnp.int32, (CELLS, CELLS), 0).astype(F32)
    cell_lane = lax.broadcasted_iota(jnp.int32, (CELLS, CELLS), 1).astype(F32)
    for copy in load_small:
        copy.wait()
    par[2:3, :] = order_sc[...].astype(F32)
    par[3:8, :] = jnp.zeros((5, CELLS), F32)

    def coefficients(ref, base, scale):
        hit = ref[2:3, :] == cell_sub
        for row, target in ((0, visc), (1, mass)):
            col = jnp.sum(jnp.where(hit, ref[row : row + 1, :], 0.0), axis=1, keepdims=True)
            target[base : base + CELLS, :] = jnp.broadcast_to(col * scale, (CELLS, 128))
        return hit

    one_hot = jnp.where(par[2:3, :] == cell_sub, 1.0, 0.0).astype(BF16)
    pone[:, 0:CELLS] = one_hot
    pone[:, CELLS : 2 * CELLS] = one_hot
    load_force.wait()
    high, low = split(fsc[...])
    parts[0:CELLS, :] = high
    parts[CELLS : 2 * CELLS, :] = low
    fsc[...] = jnp.dot(pone[...], parts[...], preferred_element_type=F32) * lanes[3:4, :]
    for tile in every:
        mirror_layers(fsc[:, tile * 128 : tile * 128 + 128], tile, raw, 4, False)

    pl.semaphore_wait(barrier, DOMS - 1 + 3)

    def remote(src, dst, send, recv_sem, device):
        return pltpu.make_async_remote_copy(
            src_ref=src, dst_ref=dst, send_sem=send, recv_sem=recv_sem,
            device_id=device, device_id_type=MESH,
        )

    par_copies = [
        remote(par, parn.at[0], psend.at[0], precv.at[0], (grp, up)),
        remote(par, parn.at[1], psend.at[1], precv.at[1], (grp, down)),
    ]
    ghost_copies = [
        remote(
            raw.at[5 * LAYER : 8 * LAYER], raw.at[1 * LAYER : 4 * LAYER],
            gsend.at[0], grecv.at[0], (grp, up),
        ),
        remote(
            raw.at[4 * LAYER : 7 * LAYER], raw.at[8 * LAYER : 11 * LAYER],
            gsend.at[1], grecv.at[1], (grp, down),
        ),
        remote(
            raw.at[4 * LAYER : 5 * LAYER, 384:512], raw.at[0:LAYER, 384:512],
            gsend.at[2], grecv.at[2], (grp, up),
        ),
        remote(
            raw.at[7 * LAYER : 8 * LAYER, 384:512], raw.at[11 * LAYER : 12 * LAYER, 384:512],
            gsend.at[3], grecv.at[3], (grp, down),
        ),
    ]
    for copy in par_copies + ghost_copies:
        copy.start()

    coefficients(par, CELLS, 1.0)
    order_col = jnp.sum(
        jnp.where(cell_sub == cell_lane, par[2:3, :], 0.0), axis=1, keepdims=True
    )
    one_hot = jnp.where(order_col == cell_lane, 1.0, 0.0).astype(BF16)
    ptr[:, 0:CELLS] = one_hot
    ptr[:, CELLS : 2 * CELLS] = one_hot
    owner_row = owner_sc[...].astype(F32)
    owner_col = jnp.sum(
        jnp.where(cell_sub == cell_lane, owner_row, 0.0), axis=1, keepdims=True
    )
    same = (owner_col == owner_row) & (cell_sub < cell_lane)
    rank_row = jnp.sum(jnp.where(same, 1.0, 0.0), axis=0, keepdims=True)
    dest_row = jnp.where(owner_row >= 0.0, owner_row * 8.0 + rank_row, -1.0)
    slot_of = jnp.where(dest_row == cell_sub, 1.0, 0.0).astype(BF16)
    gpack[...] = jnp.dot(slot_of, one_hot, preferred_element_type=F32).astype(BF16)
    cell_id = lax.broadcasted_iota(jnp.int32, (CELLS, 128), 0)
    for k, width in enumerate((1, 8, 64)):
        parity = lax.rem(cell_id // width, 2).astype(F32).astype(BF16)
        classes[:, k * 128 : k * 128 + 128] = jnp.dot(
            gpack[...], parity, preferred_element_type=F32
        )

    for copy in par_copies:
        copy.wait()
    coefficients(parn.at[0], 0, has_down)
    coefficients(parn.at[1], 2 * CELLS, has_up)

    def partners(layer):
        parity = layer % 2 if isinstance(layer, int) else lax.rem(layer, 2)
        return {0: layer - 1 + 2 * parity, 3: layer + 1 - 2 * parity}

    def face_sum(ref, layer, tile):
        value = load(ref, layer, tile)
        other = load(ref, partners(layer)[tile], tile)
        return value + jnp.where(low_half, other, 0.0)

    def put_inverse(layer, tile, diag):
        store(inv, layer, tile, jnp.where(diag > 0.0, (2.0 / DELTA) / diag, 0.0))

    def diagonal(layer, tiles):
        coef_v = column(visc, layer)
        coef_m = column(mass, layer)
        for tile in tiles:
            diag = xy_sum(coef_v * table(1, tile) + coef_m * table(0, tile))
            if tile in (0, 3):
                store(tmp, layer, tile, diag)
            else:
                put_inverse(layer, tile, diag)

    diagonal(0, (3,))
    over(1, 11, lambda layer: diagonal(layer, every))
    diagonal(11, (3,))

    def diagonal_faces(layer):
        for tile in (0, 3):
            put_inverse(layer, tile, face_sum(tmp, layer, tile))

    over(1, 11, diagonal_faces)

    def put_first(layer, pair, forces):
        values = []
        for tile, force in zip((pair, 3 - pair), forces):
            value = force * load(inv, layer, tile) * (0.5 * DELTA)
            store(v0, layer, tile, value)
            values.append(value)
        store_lhs(layer, pair, *values)

    def assemble(layer, tiles, scale):
        sums = []
        for tile in tiles:
            force = load(raw, layer, tile)
            if scale is not None:
                force = force * scale
            force = xy_sum(force)
            if tile in (0, 3):
                store(tmp, layer, tile, force)
            else:
                sums.append(force)
        if sums:
            put_first(layer, 1, sums)

    over(4, 8, lambda layer: assemble(layer, every, None))
    for copy in load_mats:
        copy.wait()
    for copy in ghost_copies:
        copy.wait()
    assemble(0, (3,), has_down)
    over(1, 4, lambda layer: assemble(layer, every, has_down))
    over(8, 11, lambda layer: assemble(layer, every, has_up))
    assemble(11, (3,), has_up)

    def first_faces(layer):
        put_first(layer, 0, [face_sum(tmp, layer, tile) for tile in (0, 3)])

    over(1, 11, first_faces)

    def multiply(low, high, which, target, first=0):
        for part in range(2):
            target[:, first + part * 256 : first + part * 256 + 256] = jnp.dot(
                lhs[low * LAYER : high * LAYER, part * 768 : part * 768 + 768],
                weights[2 * which + part],
                preferred_element_type=F32,
            )

    def advance(step, layer, pair, totals):
        values = []
        for tile, total in zip((pair, 3 - pair), totals):
            value = total * load(inv, layer, tile)
            current = load(basis[step], layer, tile)
            if step == 0:
                value = 0.5 * value - (THETA / DELTA) * current
            else:
                value = value - (2.0 * THETA / DELTA) * current
                value = value - load(basis[step - 1], layer, tile)
            store(basis[step + 1], layer, tile, value)
            values.append(value)
        store_lhs(layer, pair, *values)

    def apply(step, layer, tiles, sums, going):
        coef_v = column(visc, layer)
        coef_m = column(mass, layer)
        for pair in (1, 0):
            if pair not in tiles and 3 - pair not in tiles:
                continue
            even = load(tmp, layer, pair)
            uneven = load(tmp, layer, 2 + pair)
            images = []
            for tile, product in ((pair, even + uneven), (3 - pair, even - uneven)):
                if tile not in tiles:
                    continue
                value = load(basis[step], layer, tile)
                weighted = coef_m * table(0, tile)
                image = coef_v * product + weighted * value
                if sums is not None:
                    diag = coef_v * table(1, tile) + weighted
                    sums = (
                        sums[0] + jnp.sum(value * image, axis=0),
                        sums[1] + jnp.sum(value * value * diag, axis=0),
                    )
                if going:
                    image = xy_sum(image)
                    if pair == 0:
                        store(tmp, layer, tile, image)
                    else:
                        images.append(image)
            if images:
                advance(step, layer, 1, images)
        return sums

    def faces(step, layer):
        advance(step, layer, 0, [face_sum(tmp, layer, tile) for tile in (0, 3)])

    blank_sums = (jnp.zeros((8, 128), F32), jnp.zeros((8, 128), F32))
    for step in range(ITERS):
        low, high = 1 + step, 11 - step
        going = step + 1 < ITERS
        multiply(low, high, 0, tmp.at[low * LAYER : high * LAYER])
        if going:
            inward = 0 if low % 2 else 3
            apply(step, low, (inward,), None, True)
            over(low + 1, 4, lambda layer: apply(step, layer, every, None, True))
        sums = lax.fori_loop(
            4, 8, lambda layer, carry: apply(step, layer, every, carry, going), blank_sums
        )
        if going:
            over(8, high - 1, lambda layer: apply(step, layer, every, None, True))
            apply(step, high - 1, (inward,), None, True)
        moments[step : step + 1, :] = jnp.sum(sums[0], axis=0, keepdims=True)
        moments[4 + step : 5 + step, :] = jnp.sum(sums[1], axis=0, keepdims=True)
        if going:
            over(low + 1, high - 1, lambda layer: faces(step, layer))

    red[0] = moments[...]
    for step in range(1, DOMS):
        remote(
            moments, red.at[step], rsend, rrecv, (grp, lax.rem(dom + step, DOMS))
        ).start()

    def end_face(ref, layer):
        total = load(ref, layer, 0) * table(2, 0)
        for tile in (1, 2, 3):
            total = total + load(ref, layer, tile) * table(2, tile)
        total = total + rotated(total, 64, 2)
        return -total if layer % 2 else total

    fsend[0] = end_face(v3, 7).reshape(LAYER, 128)
    fsend[1] = end_face(v3, 4).reshape(LAYER, 128)
    face_copies = [
        remote(fsend.at[0], frecv.at[0], f3send.at[0], f3recv.at[0], (grp, up)),
        remote(fsend.at[1], frecv.at[1], f3send.at[1], f3recv.at[1], (grp, down)),
    ]
    for copy in face_copies:
        copy.start()

    own_rows = slice(4 * LAYER, 8 * LAYER)
    for index in (3, 0, 1, 2):
        if index < 3:
            over(
                4,
                8,
                lambda layer: [
                    store_lhs(
                        layer,
                        pair,
                        load(basis[index], layer, pair),
                        load(basis[index], layer, 3 - pair),
                    )
                    for pair in (0, 1)
                ],
            )

        left = jnp.concatenate(
            [
                jnp.concatenate(
                    [
                        lhs[own_rows, start + part * 256 : start + part * 256 + 128]
                        for part in range(3)
                    ],
                    1,
                )
                for start in (0, 128, 768, 896)
            ],
            0,
        )
        both = jnp.dot(left, flat[0:384, 0:256], preferred_element_type=F32)
        for part in range(4):
            rows = slice(part * CELLS, part * CELLS + CELLS)
            grads[index, :, part * 128 : part * 128 + 128] = both[rows, 0:128]
            grads[index, :, NODES + part * 128 : NODES + part * 128 + 128] = both[rows, 128:256]
        multiply(4, 8, 1, grads.at[index], 2 * NODES)
        if index < 3:
            fghost[index, 0] = end_face(basis[index], 3).reshape(LAYER, 128)
            fghost[index, 1] = end_face(basis[index], 8).reshape(LAYER, 128)

    for copy in face_copies:
        copy.wait()
    for side in range(2):
        fghost[3, side] = frecv[side]

    whole = remote(red.at[1:DOMS], red.at[1:DOMS], rsend, rrecv, (grp, up))
    whole.wait_send()
    whole.wait_recv()

    total = jnp.sum(red[...], axis=0)
    total = jnp.broadcast_to(jnp.sum(total, axis=1, keepdims=True), (8, 128))
    moments[...] = total

    def scalar(row):
        return jnp.broadcast_to(moments[row : row + 1, :], (8, 128))

    alpha = [scalar(row) for row in range(4)]
    beta = [scalar(4 + row) for row in range(4)]
    gamma = [(alpha[k] - THETA * beta[k]) * (1.0 / DELTA) for k in range(4)]
    mu = [beta[0], gamma[0]]
    ahead = gamma[0]
    for k in range(1, 4):
        ahead = 2.0 * gamma[k] - ahead
        mu.append(2.0 * beta[k] - mu[0])
        mu.append(2.0 * ahead - mu[1])

    def inner(i, j):
        return 0.5 * (mu[i + j] + mu[abs(i - j)])

    gram = [
        [
            DELTA * 0.5 * (inner(i, j + 1) + inner(i, abs(j - 1))) + THETA * inner(i, j)
            for j in range(4)
        ]
        for i in range(4)
    ]
    right = [mu[k] for k in range(4)]
    pivots = []
    for k in range(4):
        original = DELTA * 0.5 * (inner(k, k + 1) + inner(k, abs(k - 1))) + THETA * inner(k, k)
        pivot = gram[k][k]
        good = pivot > 1e-7 * original
        inverse = jnp.where(good, 1.0 / jnp.where(good, pivot, 1.0), 0.0)
        pivots.append(inverse)
        for i in range(k + 1, 4):
            factor = gram[i][k] * inverse
            for j in range(k + 1, 4):
                gram[i][j] = gram[i][j] - factor * gram[k][j]
            right[i] = right[i] - factor * right[k]
    coef = [None] * 4
    for k in (3, 2, 1, 0):
        value = right[k]
        for j in range(k + 1, 4):
            value = value - gram[k][j] * coef[j]
        coef[k] = value * pivots[k]

    coef8 = [(value * (1.0 / NP)).reshape(1, 8, 128) for value in coef]
    coef16 = [0.5 * value for value in coef8]
    x_sign = jnp.where(odd, -1.0, 1.0).reshape(1, 8, 128)
    x_scale = jnp.where(take_up | take_down, 0.5, 1.0).reshape(1, 8, 128) * x_sign
    y_half = jnp.where((node_j == 7) | (node_j == 0), 0.5, 1.0).reshape(1, 8, 128)
    y_end = jnp.where(node_j == 7, 0.5, 1.0).reshape(1, 8, 128)
    y_scale = jnp.concatenate(
        [y_end, -y_half, y_half, -y_half, y_half, -y_half, y_half, -y_end], 0
    )

    def combined(layer, direction, pair):
        parts_of = []
        scale = coef8 if direction == 2 else coef16
        for start in (0, 256):
            start = start + direction * NODES + pair * 128
            value = None
            for k in range(4):
                term = scale[k] * grads[k, rows_of(layer), start : start + 128].reshape(8, 8, 128)
                value = term if value is None else value + term
            parts_of.append(value)
        even, uneven = parts_of
        if direction == 2:
            return even + uneven, uneven - even
        return even + uneven, even - uneven

    def put_grad(layer, direction, tile, value):
        start = direction * NODES + tile * 128
        gcells[rows_of(layer), start : start + 128] = value.reshape(LAYER, 128).astype(BF16)

    def flat_grads(layer):
        z_sign = (1 - 2 * lax.rem(layer, 2)).astype(F32)
        for pair in (0, 1):
            for tile, value in zip((pair, 3 - pair), combined(layer, 0, pair)):
                put_grad(layer, 0, tile, x_scale * (value - x_others(value)))
            for tile, value in zip((pair, 3 - pair), combined(layer, 1, pair)):
                put_grad(layer, 1, tile, y_scale * (value - y_others(value)))
        for tile, value in zip((1, 2), combined(layer, 2, 1)):
            put_grad(layer, 2, tile, z_sign * value)
        for tile, value in zip((0, 3), combined(layer, 2, 0)):
            store(xstd, layer, tile, z_sign * value)

    over(0, 4, flat_grads)

    def mean_face(layer, tile, other, there):
        value = load(xstd, layer, tile)
        put_grad(layer, 2, tile, value + jnp.where(low_half, there * (other - value), 0.0))

    for layer in range(4):
        mean_face(layer, 3, load(xstd, layer ^ 1, 3), 0.5)
        if layer in (1, 2):
            mean_face(layer, 0, load(xstd, 3 - layer, 0), 0.5)
        else:
            side = 0 if layer == 0 else 1
            other = None
            for k in range(4):
                term = coef8[k] * fghost[k, side].reshape(8, 8, 128)
                other = term if other is None else other + term
            mean_face(layer, 0, other, 0.5 * (has_up if side else has_down))

    target = 1 - lax.rem(grp, 2)
    source = lax.div(grp, 2)
    send_slots = pl.ds(pl.multiple_of(target * HALF, HALF), HALF)
    own_slots = pl.ds(pl.multiple_of((1 - target) * HALF, HALF), HALF)

    def pack(slots, into):
        def body(part, carry):
            cols = pl.ds(pl.multiple_of(part * 512, 512), 512)
            into[:, cols] = jnp.dot(
                gpack[slots, :], gcells[:, cols], preferred_element_type=F32
            ).astype(BF16)
            return carry

        lax.fori_loop(0, 3, body, 0)

    pack(send_slots, packed)

    def chunk_rows(chunk):
        return slice(chunk * CHUNK, chunk * CHUNK + CHUNK)

    group_copies = [
        remote(
            packed.at[chunk_rows(chunk)], recv.at[comp, chunk_rows(chunk)],
            asend.at[chunk], arecv.at[source, chunk], (target, dom),
        )
        for chunk in range(HALF // CHUNK)
    ]
    for copy in group_copies:
        copy.start()

    @pl.when(grp < 2)
    def _():
        pack(own_slots, recv.at[comp])

    wide8 = [value.reshape(1, 8, 128) for value in coef]

    @pl.when(grp < 3)
    def _():
        def solve_layer(layer):
            for tile in every:
                value = wide8[0] * load(v0, layer, tile)
                for k in range(1, 4):
                    value = value + wide8[k] * load(basis[k], layer, tile)
                store(xs, layer - 4, tile, value)

        over(4, 8, solve_layer)
        for tile in every:
            mirror_layers(xs[:, tile * 128 : tile * 128 + 128], tile, xstd, 0, True)
        high, low = split(xstd[...])
        parts[0:CELLS, :] = high
        parts[CELLS : 2 * CELLS, :] = low
        out[...] = jnp.dot(ptr[...], parts[...], preferred_element_type=F32)

    def lambda_rows(block, carry):
        rows = pl.ds(pl.multiple_of(block * 16, 16), 16)
        for part in range(2):
            jac = [
                [
                    recv[c, rows, d * NODES + part * 256 : d * NODES + part * 256 + 256].astype(F32)
                    for d in range(3)
                ]
                for c in range(3)
            ]
            lam[rows, part * 256 : part * 256 + 256] = lambda_two(jac)
        return carry

    def natural_order(chunk):
        rows = chunk_rows(chunk)
        start = pl.multiple_of((1 - target) * HALF, HALF) + chunk * CHUNK
        slots = pl.ds(pl.multiple_of(start, CHUNK), CHUNK)
        odd_x, odd_y, odd_z = [
            classes[slots, k * 128 : k * 128 + 128] > 0.5 for k in range(3)
        ]
        values = [lam[rows, tile * 128 : tile * 128 + 128] for tile in every]
        flipped = reversals(jnp.concatenate(values, 0))
        turned = []
        for tile in every:
            rev_x, rev_y, rev_xy = [part[chunk_rows(tile)] for part in flipped]
            turned.append(
                jnp.where(
                    odd_x,
                    jnp.where(odd_y, rev_xy, rev_x),
                    jnp.where(odd_y, rev_y, values[tile]),
                )
            )
        for tile in every:
            value = jnp.where(odd_z, turned[3 - tile], turned[tile])
            if tile >= 2:
                value = rotated(value, 64, 1)
            lam[rows, tile * 128 : tile * 128 + 128] = value

    here = pl.ds(pl.multiple_of(dom * 8, 8), 8)

    def to_owner(k):
        return remote(
            lam.at[8 * k : 8 * k + 8], lamrecv.at[here], osend.at[k], orecv,
            (3, (1 - target) * (HALF // 8) + k),
        )

    @pl.when(grp < 2)
    def _():
        for chunk in range(HALF // CHUNK):
            for which, other in ((0, 1 - grp), (1, 2)):
                piece = recv.at[other, chunk_rows(chunk)]
                remote(
                    piece, piece, asend.at[chunk], arecv.at[which, chunk], (target, dom)
                ).wait_recv()
            lax.fori_loop(chunk * CHUNK // 16, (chunk + 1) * CHUNK // 16, lambda_rows, 0)
            natural_order(chunk)
            for k in range(chunk * CHUNK // 8, (chunk + 1) * CHUNK // 8):
                to_owner(k).start()
        for k in range(HALF // 8):
            to_owner(k).wait_send()

    for copy in group_copies:
        copy.wait_send()

    @pl.when(grp == 3)
    def _():
        remote(lamrecv, lamrecv, osend.at[0], orecv, (target, dom)).wait_recv()
        out[...] = lamrecv[...]


def lambda_two(jac):
    strain = [[0.5 * (jac[a][b] + jac[b][a]) for b in range(3)] for a in range(3)]
    spin = [[0.5 * (jac[a][b] - jac[b][a]) for b in range(3)] for a in range(3)]
    m = [[None] * 3 for _ in range(3)]
    for a in range(3):
        for b in range(a, 3):
            value = strain[a][0] * strain[0][b] + spin[a][0] * spin[0][b]
            for k in (1, 2):
                value = value + strain[a][k] * strain[k][b] + spin[a][k] * spin[k][b]
            m[a][b] = value
            m[b][a] = value
    for sweep in range(SWEEPS):
        for p, q, r in ((0, 1, 2), (0, 2, 1), (1, 2, 0)):
            last = sweep == SWEEPS - 1
            twice = 2.0 * m[p][q]
            gap = m[p][p] - m[q][q]
            square = twice * twice + gap * gap
            inverse = lax.rsqrt(jnp.maximum(square, 1e-36))
            length = square * inverse
            mean = 0.5 * (m[p][p] + m[q][q])
            m[p][p] = mean + 0.5 * length
            m[q][q] = mean - 0.5 * length
            if last and (p, q) == (1, 2):
                continue
            none = square < 1e-36
            cosine2 = jnp.where(none, 1.0, jnp.abs(gap) * inverse)
            sine2 = jnp.where(none, 0.0, twice * inverse)
            larger = 0.5 + 0.5 * cosine2
            root = lax.rsqrt(larger)
            big = larger * root
            small = 0.5 * sine2 * root
            flip = gap < 0.0
            sine_big = jnp.where(sine2 < 0.0, -big, big)
            cosine = jnp.where(flip, jnp.abs(small), big)
            sine = jnp.where(flip, sine_big, small)
            side_p = m[r][p]
            side_q = m[r][q]
            m[r][p] = m[p][r] = cosine * side_p + sine * side_q
            m[r][q] = m[q][r] = cosine * side_q - sine * side_p
            m[p][q] = m[q][p] = jnp.zeros_like(side_p)
    diagonal = [m[0][0], m[1][1], m[2][2]]
    largest = jnp.maximum(jnp.maximum(diagonal[0], diagonal[1]), diagonal[2])
    smallest = jnp.minimum(jnp.minimum(diagonal[0], diagonal[1]), diagonal[2])
    return diagonal[0] + diagonal[1] + diagonal[2] - largest - smallest


def per_device(forcing, viscosity, mass_coef, element_order, owner):
    mats, flat, lanes = tables()
    vmem = pl.BlockSpec(memory_space=pltpu.VMEM)
    hbm = pl.BlockSpec(memory_space=pltpu.HBM)
    wide = (12 * LAYER, NODES)
    own = (CELLS, NODES)
    dma = pltpu.SemaphoreType.DMA
    result = pl.pallas_call(
        kernel,
        out_shape=pltpu.VMEM(own, F32),
        in_specs=[hbm] * 8,
        out_specs=vmem,
        scratch_shapes=[
            pltpu.VMEM(own, F32),
            pltpu.VMEM((8, NODES), F32),
            pltpu.VMEM((640, 384), BF16),
            pltpu.VMEM((1, CELLS), jnp.int32),
            pltpu.VMEM((1, CELLS), jnp.int32),
            pltpu.VMEM((4, 768, 256), BF16),
            pltpu.VMEM((8, CELLS), F32),
            pltpu.VMEM((2, 8, CELLS), F32),
            pltpu.VMEM((CELLS, 2 * CELLS), BF16),
            pltpu.VMEM((CELLS, 2 * CELLS), BF16),
            pltpu.VMEM((2 * CELLS, NODES), BF16),
            pltpu.VMEM((12 * LAYER, 128), F32),
            pltpu.VMEM((12 * LAYER, 128), F32),
            pltpu.VMEM(wide, F32),
            pltpu.VMEM(wide, F32),
            pltpu.VMEM(wide, F32),
            pltpu.VMEM((12 * LAYER, 3 * NODES), BF16),
            pltpu.VMEM(wide, F32),
            pltpu.VMEM(wide, F32),
            pltpu.VMEM(wide, F32),
            pltpu.VMEM(wide, F32),
            pltpu.VMEM(own, F32),
            pltpu.VMEM(own, F32),
            pltpu.VMEM((4, CELLS, 3 * NODES), F32),
            pltpu.VMEM((CELLS, CELLS), BF16),
            pltpu.VMEM((CELLS, 384), F32),
            pltpu.VMEM((CELLS, 3 * NODES), BF16),
            pltpu.VMEM((2, LAYER, 128), F32),
            pltpu.VMEM((2, LAYER, 128), F32),
            pltpu.VMEM((4, 2, LAYER, 128), F32),
            pltpu.VMEM((8, 128), F32),
            pltpu.VMEM((DOMS, 8, 128), F32),
            pltpu.VMEM((HALF, 3 * NODES), BF16),
            pltpu.VMEM((3, HALF, 3 * NODES), BF16),
            pltpu.VMEM((HALF, NODES), F32),
            pltpu.VMEM(own, F32),
            dma((6,)), dma((12,)), dma, dma((2,)), dma((2,)), dma((4,)), dma((4,)), dma((2,)),
            dma((2,)), dma, dma, dma((HALF // CHUNK,)), dma((2, HALF // CHUNK)), dma((HALF // 8,)), dma,
        ],
        compiler_params=pltpu.CompilerParams(
            collective_id=0, has_side_effects=True, vmem_limit_bytes=60 * 1024 * 1024
        ),
        name="solve_and_analyse",
    )(
        forcing, viscosity[None], mass_coef[None], element_order, owner,
        jnp.asarray(lanes), jnp.asarray(flat), jnp.asarray(mats),
    )
    return result[None]


def solution(mesh):
    in_specs = (P(None, "dom", None), P("dom"), P("dom"), P("dom", None), P("dom", None))
    out_specs = P("grp", "dom", None)
    return jax.shard_map(
        per_device, mesh=mesh, in_specs=in_specs, out_specs=out_specs, check_vma=False
    )
```

```python
import functools

import jax
import jax.numpy as jnp
import ml_dtypes
import numpy as np
from jax import lax
from jax.experimental import pallas as pl
from jax.experimental.pallas import tpu as pltpu
from jax.sharding import PartitionSpec as P

NP = 8
ITERS = 4
SWEEPS = 4
LAYER = 64
CELLS = 256
NODES = 512
DOMS = 32
CHUNK = 32
SHARE = 96
BASIS_LOW = 0.3
BASIS_HIGH = 2.0
THETA = 0.5 * (BASIS_LOW + BASIS_HIGH)
DELTA = 0.5 * (BASIS_HIGH - BASIS_LOW)
MESH = pl.DeviceIdType.MESH
F32 = jnp.float32
BF16 = jnp.bfloat16


def legendre_values(points, node_count):
    legendre = np.zeros((points.shape[0], node_count))
    legendre[:, 0] = 1.0
    legendre[:, 1] = points
    for poly_order in range(2, node_count):
        legendre[:, poly_order] = (
            (2 * poly_order - 1) * points * legendre[:, poly_order - 1]
            - (poly_order - 1) * legendre[:, poly_order - 2]
        ) / poly_order
    return legendre


def lobatto_table(node_count):
    degree = node_count - 1
    points = np.cos(np.pi * np.arange(node_count) / degree)
    for attempt in range(60):
        legendre = legendre_values(points, node_count)
        points = points - (points * legendre[:, degree] - legendre[:, degree - 1]) / (
            node_count * legendre[:, degree]
        )
    points = points[::-1].copy()
    end_values = legendre_values(points, node_count)[:, degree]
    weights = 2.0 / (degree * node_count * end_values * end_values)
    spacing = points[:, None] - points[None, :] + np.eye(node_count)
    diff_matrix = end_values[:, None] / end_values[None, :] / spacing
    diff_matrix = diff_matrix * (1.0 - np.eye(node_count))
    diff_matrix[0, 0] = -degree * node_count / 4.0
    diff_matrix[-1, -1] = degree * node_count / 4.0
    return (weights, diff_matrix)


def split_rows(matrix):
    high = matrix.astype(np.float32).astype(ml_dtypes.bfloat16)
    low = (matrix - high.astype(np.float64)).astype(np.float32).astype(ml_dtypes.bfloat16)
    return high, low


def tables():
    weights, diff = lobatto_table(NP)
    eye = np.eye(NP)
    cube = (
        weights[:, None, None] * weights[None, :, None] * weights[None, None, :]
    ).reshape(-1)
    directional = [
        np.kron(eye, np.kron(eye, diff)),
        np.kron(eye, np.kron(diff, eye)),
        np.kron(diff, np.kron(eye, eye)),
    ]
    stiff = np.zeros((NODES, NODES))
    for matrix in directional:
        stiff = stiff + matrix.T @ (cube[:, None] * matrix)
    flip = np.arange(NODES).reshape(NP, LAYER)[::-1][: NP // 2].reshape(-1)
    mats = []
    for matrix in (stiff, directional[2]):
        near, far = matrix[:256, :256], matrix[:256, flip]
        for block in (0.5 * (near + far), 0.5 * (near - far)):
            mats.append(np.stack(split_rows(block.T)))
    mats = np.stack(mats)
    flat = np.concatenate([directional[0].T[:128, :128], directional[1].T[:128, :128]], 1)
    high, low = split_rows(flat)
    flat = np.concatenate([high, high, low], 0)
    lanes = np.zeros((8, NODES), np.float32)
    lanes[0] = cube
    lanes[1] = np.diag(stiff)
    lanes[2] = np.repeat(diff[0], LAYER)
    order = [0, 1, 2, 3, 5, 4, 7, 6]
    lanes = lanes.reshape(8, NP, LAYER)[:, order].reshape(8, NODES)
    natural = cube.reshape(NP, LAYER).astype(np.float32).reshape(-1)
    lanes[3] = natural
    back = eye[::-1]
    half = np.eye(2)
    mirror = np.concatenate(
        [
            np.kron(half, np.kron(eye, back)),
            np.kron(half, np.kron(back, eye)),
            np.kron(half, np.kron(back, back)),
        ],
        1,
    ).astype(ml_dtypes.bfloat16)
    wide = np.concatenate([flat, np.zeros((384, 128), flat.dtype)], 1)
    return mats, np.concatenate([wide, mirror, mirror], 0), lanes


def rotated(value, shift, axis):
    return pltpu.roll(value, shift % value.shape[axis], axis)


def kernel(
    forcing, visc_in, mass_in, order_in, owner_in, lanes_in, flat_in, mats,
    out,
    fsc, lanes, flat, order_sc, owner_sc, weights, par, parn, pone, ptr, parts, visc, mass, raw, tmp,
    inv, lhs, v0, v1, v2, v3, xs, xstd, grads, gpack, classes, gcells, fsend, frecv, fghost, moments,
    red, packed, recv, lam, lamrecv,
    ssem, wsem, fsem, psend, precv, gsend, grecv, f3send, f3recv, rsend, rrecv, asend, arecv,
    osend, orecv,
):
    grp = lax.axis_index("grp")
    dom = lax.axis_index("dom")
    comp = jnp.minimum(grp, 2)
    up = lax.rem(dom + 1, DOMS)
    down = lax.rem(dom + DOMS - 1, DOMS)
    barrier = pltpu.get_barrier_semaphore()
    basis = (v0, v1, v2, v3)
    every = (0, 1, 2, 3)

    for step in range(1, DOMS):
        pl.semaphore_signal(
            barrier, inc=1, device_id=(grp, lax.rem(dom + step, DOMS)), device_id_type=MESH
        )
    for step in range(1, 4):
        pl.semaphore_signal(
            barrier, inc=1, device_id=(lax.rem(grp + step, 4), dom), device_id_type=MESH
        )

    load_small = [
        pltpu.make_async_copy(source, target, ssem.at[k])
        for k, (source, target) in enumerate(
            (
                (visc_in, par.at[0:1]),
                (mass_in, par.at[1:2]),
                (order_in, order_sc),
                (owner_in, owner_sc),
                (lanes_in, lanes),
                (flat_in, flat),
            )
        )
    ]
    for copy in load_small:
        copy.start()
    load_force = pltpu.make_async_copy(forcing.at[comp], fsc, fsem)
    load_force.start()
    load_mats = []
    for which in range(4):
        for part, source in enumerate((0, 0, 1)):
            copy = pltpu.make_async_copy(
                mats.at[which, source],
                weights.at[which, part * 256 : part * 256 + 256],
                wsem.at[3 * which + part],
            )
            copy.start()
            load_mats.append(copy)

    lane = lax.broadcasted_iota(jnp.int32, (8, 128), 1)
    sub = lax.broadcasted_iota(jnp.int32, (8, 128), 0)
    node_i = lax.rem(lane, 8)
    node_j = lax.rem(lane // 8, 8)
    odd = lax.rem(sub, 2) == 1
    first_i = node_i == 0
    last_i = node_i == 7
    take_up = ((last_i & jnp.logical_not(odd)) | (first_i & odd & (sub < 7)))
    take_down = ((last_i & odd) | (first_i & jnp.logical_not(odd) & (sub > 0)))
    has_up = jnp.where(dom < DOMS - 1, 1.0, 0.0).astype(F32)
    has_down = jnp.where(dom > 0, 1.0, 0.0).astype(F32)

    def wide(mask):
        return jnp.broadcast_to(mask[None], (8, 8, 128))

    x_up = wide(take_up)
    x_down = wide(take_down)
    x_odd = wide(odd)
    y_last = wide(node_j == 7)
    y_first = wide(node_j == 0)
    low_half = wide(lane < LAYER)

    def x_others(a):
        above = rotated(a, -1, 1)
        below = rotated(a, 1, 1)
        return jnp.where(x_up, above, jnp.where(x_down, below, 0.0))

    def y_others(a):
        blank = jnp.zeros((1, 8, 128), F32)
        last = jnp.concatenate([a[k ^ 1 : (k ^ 1) + 1] for k in range(8)], 0)
        first = jnp.concatenate(
            [blank] + [a[k : k + 1] for k in (2, 1, 4, 3, 6, 5)] + [blank], 0
        )
        return jnp.where(y_last, last, jnp.where(y_first, first, 0.0))

    def xy_sum(a):
        a = a + x_others(a)
        return a + y_others(a)

    def rows_of(layer):
        if isinstance(layer, int):
            return slice(layer * LAYER, layer * LAYER + LAYER)
        return pl.ds(pl.multiple_of(layer * LAYER, LAYER), LAYER)

    def load(ref, layer, tile):
        return ref[rows_of(layer), tile * 128 : tile * 128 + 128].reshape(8, 8, 128)

    def store(ref, layer, tile, value):
        ref[rows_of(layer), tile * 128 : tile * 128 + 128] = value.reshape(LAYER, 128)

    def column(ref, layer):
        return ref[rows_of(layer), :].reshape(8, 8, 128)

    def table(row, tile):
        return lanes[row : row + 1, tile * 128 : tile * 128 + 128].reshape(1, 1, 128)

    def split(value):
        high = value.astype(BF16)
        return high, (value - high.astype(F32)).astype(BF16)

    def store_lhs(layer, pair, first, second):
        for start, value in ((0, first + second), (768, first - second)):
            start = start + pair * 128
            high, low = split(value.reshape(LAYER, 128))
            lhs[rows_of(layer), start : start + 128] = high
            lhs[rows_of(layer), start + 256 : start + 384] = low
            lhs[rows_of(layer), start + 512 : start + 640] = high

    def reversals(value):
        total = jnp.dot(
            jnp.concatenate(split(value), 1), flat[384:640, :], preferred_element_type=F32
        )
        return total[:, 0:128], total[:, 128:256], total[:, 256:384]

    def mirror_layers(value, tile, target, base, back):
        flipped = reversals(value)
        for layer in range(4):
            rows = slice(layer * LAYER, layer * LAYER + LAYER)
            plain, rev_x, rev_y, rev_xy = [
                part[rows].reshape(8, 8, 128) for part in (value,) + flipped
            ]
            even_y = jnp.where(x_odd, rev_x, plain)
            odd_y = jnp.where(x_odd, rev_xy, rev_y)
            mixed = jnp.concatenate(
                [(odd_y if k % 2 else even_y)[k : k + 1] for k in range(8)], 0
            )
            place = 3 - tile if layer % 2 else tile
            if (place if back else tile) >= 2:
                mixed = rotated(mixed, 64, 2)
            store(target, base + layer, place, mixed)

    def over(low, high, body):
        lax.fori_loop(low, high, lambda layer, carry: (body(layer), carry)[1], 0)

    cell_sub = lax.broadcasted_iota(jnp.int32, (CELLS, CELLS), 0).astype(F32)
    cell_lane = lax.broadcasted_iota(jnp.int32, (CELLS, CELLS), 1).astype(F32)
    for copy in load_small:
        copy.wait()
    par[2:3, :] = order_sc[...].astype(F32)
    par[3:8, :] = jnp.zeros((5, CELLS), F32)

    def coefficients(ref, base, scale):
        hit = ref[2:3, :] == cell_sub
        for row, target in ((0, visc), (1, mass)):
            col = jnp.sum(jnp.where(hit, ref[row : row + 1, :], 0.0), axis=1, keepdims=True)
            target[base : base + CELLS, :] = jnp.broadcast_to(col * scale, (CELLS, 128))
        return hit

    one_hot = jnp.where(par[2:3, :] == cell_sub, 1.0, 0.0).astype(BF16)
    pone[:, 0:CELLS] = one_hot
    pone[:, CELLS : 2 * CELLS] = one_hot
    load_force.wait()
    high, low = split(fsc[...])
    parts[0:CELLS, :] = high
    parts[CELLS : 2 * CELLS, :] = low
    fsc[...] = jnp.dot(pone[...], parts[...], preferred_element_type=F32) * lanes[3:4, :]
    for tile in every:
        mirror_layers(fsc[:, tile * 128 : tile * 128 + 128], tile, raw, 4, False)

    pl.semaphore_wait(barrier, DOMS - 1 + 3)

    def remote(src, dst, send, recv_sem, device):
        return pltpu.make_async_remote_copy(
            src_ref=src, dst_ref=dst, send_sem=send, recv_sem=recv_sem,
            device_id=device, device_id_type=MESH,
        )

    par_copies = [
        remote(par, parn.at[0], psend.at[0], precv.at[0], (grp, up)),
        remote(par, parn.at[1], psend.at[1], precv.at[1], (grp, down)),
    ]
    ghost_copies = [
        remote(
            raw.at[5 * LAYER : 8 * LAYER], raw.at[1 * LAYER : 4 * LAYER],
            gsend.at[0], grecv.at[0], (grp, up),
        ),
        remote(
            raw.at[4 * LAYER : 7 * LAYER], raw.at[8 * LAYER : 11 * LAYER],
            gsend.at[1], grecv.at[1], (grp, down),
        ),
        remote(
            raw.at[4 * LAYER : 5 * LAYER, 384:512], raw.at[0:LAYER, 384:512],
            gsend.at[2], grecv.at[2], (grp, up),
        ),
        remote(
            raw.at[7 * LAYER : 8 * LAYER, 384:512], raw.at[11 * LAYER : 12 * LAYER, 384:512],
            gsend.at[3], grecv.at[3], (grp, down),
        ),
    ]
    for copy in par_copies + ghost_copies:
        copy.start()

    coefficients(par, CELLS, 1.0)
    order_col = jnp.sum(
        jnp.where(cell_sub == cell_lane, par[2:3, :], 0.0), axis=1, keepdims=True
    )
    one_hot = jnp.where(order_col == cell_lane, 1.0, 0.0).astype(BF16)
    ptr[:, 0:CELLS] = one_hot
    ptr[:, CELLS : 2 * CELLS] = one_hot
    owner_row = owner_sc[...].astype(F32)
    owner_col = jnp.sum(
        jnp.where(cell_sub == cell_lane, owner_row, 0.0), axis=1, keepdims=True
    )
    same = (owner_col == owner_row) & (cell_sub < cell_lane)
    rank_row = jnp.sum(jnp.where(same, 1.0, 0.0), axis=0, keepdims=True)
    owner_int = owner_sc[...]
    place = owner_int >> 3
    piece_row = ((((owner_int >> 1) - place) & 3) << 1) + (owner_int & 1)
    first_row = (piece_row * 4 + place).astype(F32)
    dest_row = jnp.where(owner_row >= 0.0, first_row * 8.0 + rank_row, -1.0)
    slot_of = jnp.where(dest_row == cell_sub, 1.0, 0.0).astype(BF16)
    gpack[...] = jnp.dot(slot_of, one_hot, preferred_element_type=F32).astype(BF16)
    cell_id = lax.broadcasted_iota(jnp.int32, (CELLS, 128), 0)
    for k, width in enumerate((1, 8, 64)):
        parity = lax.rem(cell_id // width, 2).astype(F32).astype(BF16)
        classes[:, k * 128 : k * 128 + 128] = jnp.dot(
            gpack[...], parity, preferred_element_type=F32
        )

    for copy in par_copies:
        copy.wait()
    coefficients(parn.at[0], 0, has_down)
    coefficients(parn.at[1], 2 * CELLS, has_up)

    def partners(layer):
        parity = layer % 2 if isinstance(layer, int) else lax.rem(layer, 2)
        return {0: layer - 1 + 2 * parity, 3: layer + 1 - 2 * parity}

    def face_sum(ref, layer, tile):
        value = load(ref, layer, tile)
        other = load(ref, partners(layer)[tile], tile)
        return value + jnp.where(low_half, other, 0.0)

    def put_inverse(layer, tile, diag):
        store(inv, layer, tile, jnp.where(diag > 0.0, (2.0 / DELTA) / diag, 0.0))

    def diagonal(layer, tiles):
        coef_v = column(visc, layer)
        coef_m = column(mass, layer)
        for tile in tiles:
            diag = xy_sum(coef_v * table(1, tile) + coef_m * table(0, tile))
            if tile in (0, 3):
                store(tmp, layer, tile, diag)
            else:
                put_inverse(layer, tile, diag)

    diagonal(0, (3,))
    over(1, 11, lambda layer: diagonal(layer, every))
    diagonal(11, (3,))

    def diagonal_faces(layer):
        for tile in (0, 3):
            put_inverse(layer, tile, face_sum(tmp, layer, tile))

    over(1, 11, diagonal_faces)

    def put_first(layer, pair, forces):
        values = []
        for tile, force in zip((pair, 3 - pair), forces):
            value = force * load(inv, layer, tile) * (0.5 * DELTA)
            store(v0, layer, tile, value)
            values.append(value)
        store_lhs(layer, pair, *values)

    def assemble(layer, tiles, scale):
        sums = []
        for tile in tiles:
            force = load(raw, layer, tile)
            if scale is not None:
                force = force * scale
            force = xy_sum(force)
            if tile in (0, 3):
                store(tmp, layer, tile, force)
            else:
                sums.append(force)
        if sums:
            put_first(layer, 1, sums)

    over(4, 8, lambda layer: assemble(layer, every, None))
    for copy in load_mats:
        copy.wait()
    for copy in ghost_copies:
        copy.wait()
    assemble(0, (3,), has_down)
    over(1, 4, lambda layer: assemble(layer, every, has_down))
    over(8, 11, lambda layer: assemble(layer, every, has_up))
    assemble(11, (3,), has_up)

    def first_faces(layer):
        put_first(layer, 0, [face_sum(tmp, layer, tile) for tile in (0, 3)])

    over(1, 11, first_faces)

    def multiply(low, high, which, target, first=0):
        for part in range(2):
            target[:, first + part * 256 : first + part * 256 + 256] = jnp.dot(
                lhs[low * LAYER : high * LAYER, part * 768 : part * 768 + 768],
                weights[2 * which + part],
                preferred_element_type=F32,
            )

    def advance(step, layer, pair, totals):
        values = []
        for tile, total in zip((pair, 3 - pair), totals):
            value = total * load(inv, layer, tile)
            current = load(basis[step], layer, tile)
            if step == 0:
                value = 0.5 * value - (THETA / DELTA) * current
            else:
                value = value - (2.0 * THETA / DELTA) * current
                value = value - load(basis[step - 1], layer, tile)
            store(basis[step + 1], layer, tile, value)
            values.append(value)
        store_lhs(layer, pair, *values)

    def apply(step, layer, tiles, sums, going):
        coef_v = column(visc, layer)
        coef_m = column(mass, layer)
        for pair in (1, 0):
            if pair not in tiles and 3 - pair not in tiles:
                continue
            even = load(tmp, layer, pair)
            uneven = load(tmp, layer, 2 + pair)
            images = []
            for tile, product in ((pair, even + uneven), (3 - pair, even - uneven)):
                if tile not in tiles:
                    continue
                value = load(basis[step], layer, tile)
                weighted = coef_m * table(0, tile)
                image = coef_v * product + weighted * value
                if sums is not None:
                    diag = coef_v * table(1, tile) + weighted
                    sums = (
                        sums[0] + jnp.sum(value * image, axis=0),
                        sums[1] + jnp.sum(value * value * diag, axis=0),
                    )
                if going:
                    image = xy_sum(image)
                    if pair == 0:
                        store(tmp, layer, tile, image)
                    else:
                        images.append(image)
            if images:
                advance(step, layer, 1, images)
        return sums

    def faces(step, layer):
        advance(step, layer, 0, [face_sum(tmp, layer, tile) for tile in (0, 3)])

    blank_sums = (jnp.zeros((8, 128), F32), jnp.zeros((8, 128), F32))
    for step in range(ITERS):
        low, high = 1 + step, 11 - step
        going = step + 1 < ITERS
        multiply(low, high, 0, tmp.at[low * LAYER : high * LAYER])
        if going:
            inward = 0 if low % 2 else 3
            apply(step, low, (inward,), None, True)
            over(low + 1, 4, lambda layer: apply(step, layer, every, None, True))
        sums = lax.fori_loop(
            4, 8, lambda layer, carry: apply(step, layer, every, carry, going), blank_sums
        )
        if going:
            over(8, high - 1, lambda layer: apply(step, layer, every, None, True))
            apply(step, high - 1, (inward,), None, True)
        moments[step : step + 1, :] = jnp.sum(sums[0], axis=0, keepdims=True)
        moments[4 + step : 5 + step, :] = jnp.sum(sums[1], axis=0, keepdims=True)
        if going:
            over(low + 1, high - 1, lambda layer: faces(step, layer))

    red[0] = moments[...]
    for step in range(1, DOMS):
        remote(
            moments, red.at[step], rsend, rrecv, (grp, lax.rem(dom + step, DOMS))
        ).start()

    def end_face(ref, layer):
        total = load(ref, layer, 0) * table(2, 0)
        for tile in (1, 2, 3):
            total = total + load(ref, layer, tile) * table(2, tile)
        total = total + rotated(total, 64, 2)
        return -total if layer % 2 else total

    fsend[0] = end_face(v3, 7).reshape(LAYER, 128)
    fsend[1] = end_face(v3, 4).reshape(LAYER, 128)
    face_copies = [
        remote(fsend.at[0], frecv.at[0], f3send.at[0], f3recv.at[0], (grp, up)),
        remote(fsend.at[1], frecv.at[1], f3send.at[1], f3recv.at[1], (grp, down)),
    ]
    for copy in face_copies:
        copy.start()

    own_rows = slice(4 * LAYER, 8 * LAYER)
    for index in (3, 0, 1, 2):
        if index < 3:
            over(
                4,
                8,
                lambda layer: [
                    store_lhs(
                        layer,
                        pair,
                        load(basis[index], layer, pair),
                        load(basis[index], layer, 3 - pair),
                    )
                    for pair in (0, 1)
                ],
            )

        left = jnp.concatenate(
            [
                jnp.concatenate(
                    [
                        lhs[own_rows, start + part * 256 : start + part * 256 + 128]
                        for part in range(3)
                    ],
                    1,
                )
                for start in (0, 128, 768, 896)
            ],
            0,
        )
        both = jnp.dot(left, flat[0:384, 0:256], preferred_element_type=F32)
        for part in range(4):
            rows = slice(part * CELLS, part * CELLS + CELLS)
            grads[index, :, part * 128 : part * 128 + 128] = both[rows, 0:128]
            grads[index, :, NODES + part * 128 : NODES + part * 128 + 128] = both[rows, 128:256]
        multiply(4, 8, 1, grads.at[index], 2 * NODES)
        if index < 3:
            fghost[index, 0] = end_face(basis[index], 3).reshape(LAYER, 128)
            fghost[index, 1] = end_face(basis[index], 8).reshape(LAYER, 128)

    for copy in face_copies:
        copy.wait()
    for side in range(2):
        fghost[3, side] = frecv[side]

    whole = remote(red.at[1:DOMS], red.at[1:DOMS], rsend, rrecv, (grp, up))
    whole.wait_send()
    whole.wait_recv()

    total = jnp.sum(red[...], axis=0)
    total = jnp.broadcast_to(jnp.sum(total, axis=1, keepdims=True), (8, 128))
    moments[...] = total

    def scalar(row):
        return jnp.broadcast_to(moments[row : row + 1, :], (8, 128))

    alpha = [scalar(row) for row in range(4)]
    beta = [scalar(4 + row) for row in range(4)]
    gamma = [(alpha[k] - THETA * beta[k]) * (1.0 / DELTA) for k in range(4)]
    mu = [beta[0], gamma[0]]
    ahead = gamma[0]
    for k in range(1, 4):
        ahead = 2.0 * gamma[k] - ahead
        mu.append(2.0 * beta[k] - mu[0])
        mu.append(2.0 * ahead - mu[1])

    def inner(i, j):
        return 0.5 * (mu[i + j] + mu[abs(i - j)])

    gram = [
        [
            DELTA * 0.5 * (inner(i, j + 1) + inner(i, abs(j - 1))) + THETA * inner(i, j)
            for j in range(4)
        ]
        for i in range(4)
    ]
    right = [mu[k] for k in range(4)]
    pivots = []
    for k in range(4):
        original = DELTA * 0.5 * (inner(k, k + 1) + inner(k, abs(k - 1))) + THETA * inner(k, k)
        pivot = gram[k][k]
        good = pivot > 1e-7 * original
        inverse = jnp.where(good, 1.0 / jnp.where(good, pivot, 1.0), 0.0)
        pivots.append(inverse)
        for i in range(k + 1, 4):
            factor = gram[i][k] * inverse
            for j in range(k + 1, 4):
                gram[i][j] = gram[i][j] - factor * gram[k][j]
            right[i] = right[i] - factor * right[k]
    coef = [None] * 4
    for k in (3, 2, 1, 0):
        value = right[k]
        for j in range(k + 1, 4):
            value = value - gram[k][j] * coef[j]
        coef[k] = value * pivots[k]

    coef8 = [(value * (1.0 / NP)).reshape(1, 8, 128) for value in coef]
    coef16 = [0.5 * value for value in coef8]
    x_sign = jnp.where(odd, -1.0, 1.0).reshape(1, 8, 128)
    x_scale = jnp.where(take_up | take_down, 0.5, 1.0).reshape(1, 8, 128) * x_sign
    y_half = jnp.where((node_j == 7) | (node_j == 0), 0.5, 1.0).reshape(1, 8, 128)
    y_end = jnp.where(node_j == 7, 0.5, 1.0).reshape(1, 8, 128)
    y_scale = jnp.concatenate(
        [y_end, -y_half, y_half, -y_half, y_half, -y_half, y_half, -y_end], 0
    )

    def combined(layer, direction, pair):
        parts_of = []
        scale = coef8 if direction == 2 else coef16
        for start in (0, 256):
            start = start + direction * NODES + pair * 128
            value = None
            for k in range(4):
                term = scale[k] * grads[k, rows_of(layer), start : start + 128].reshape(8, 8, 128)
                value = term if value is None else value + term
            parts_of.append(value)
        even, uneven = parts_of
        if direction == 2:
            return even + uneven, uneven - even
        return even + uneven, even - uneven

    def put_grad(layer, direction, tile, value):
        start = direction * NODES + tile * 128
        gcells[rows_of(layer), start : start + 128] = value.reshape(LAYER, 128).astype(BF16)

    def flat_grads(layer):
        z_sign = (1 - 2 * lax.rem(layer, 2)).astype(F32)
        for pair in (0, 1):
            for tile, value in zip((pair, 3 - pair), combined(layer, 0, pair)):
                put_grad(layer, 0, tile, x_scale * (value - x_others(value)))
            for tile, value in zip((pair, 3 - pair), combined(layer, 1, pair)):
                put_grad(layer, 1, tile, y_scale * (value - y_others(value)))
        for tile, value in zip((1, 2), combined(layer, 2, 1)):
            put_grad(layer, 2, tile, z_sign * value)
        for tile, value in zip((0, 3), combined(layer, 2, 0)):
            store(xstd, layer, tile, z_sign * value)

    over(0, 4, flat_grads)

    def mean_face(layer, tile, other, there):
        value = load(xstd, layer, tile)
        put_grad(layer, 2, tile, value + jnp.where(low_half, there * (other - value), 0.0))

    for layer in range(4):
        mean_face(layer, 3, load(xstd, layer ^ 1, 3), 0.5)
        if layer in (1, 2):
            mean_face(layer, 0, load(xstd, 3 - layer, 0), 0.5)
        else:
            side = 0 if layer == 0 else 1
            other = None
            for k in range(4):
                term = coef8[k] * fghost[k, side].reshape(8, 8, 128)
                other = term if other is None else other + term
            mean_face(layer, 0, other, 0.5 * (has_up if side else has_down))

    target = 1 - lax.rem(grp, 2)
    source = lax.div(grp, 2)
    own_first = jnp.where(grp == 3, 2, lax.rem(grp, 2)) * SHARE
    own_count = jnp.where(grp == 3, 2, 3)

    def pack(first, count, into):
        slots = pl.ds(pl.multiple_of(first, CHUNK), count)

        def body(part, carry):
            cols = pl.ds(pl.multiple_of(part * 512, 512), 512)
            into[:, cols] = jnp.dot(
                gpack[slots, :], gcells[:, cols], preferred_element_type=F32
            ).astype(BF16)
            return carry

        lax.fori_loop(0, 3, body, 0)

    def chunk_rows(chunk):
        return pl.ds(pl.multiple_of(chunk * CHUNK, CHUNK), CHUNK)

    def turn(step, count):
        return lax.rem(dom + step, count)

    def piece_copy(start, chunk, slot, device, which):
        return remote(
            packed.at[chunk_rows(start + chunk)], recv.at[comp, chunk_rows(chunk)],
            asend.at[slot], arecv.at[which, chunk], (device, dom),
        )

    pack(target * SHARE, SHARE, packed.at[0:SHARE])

    first_copies = [piece_copy(0, turn(k, 3), k, target, source) for k in range(3)]
    second_copies = [piece_copy(3, turn(k, 2), 3 + k, 3, grp) for k in range(2)]
    for copy in first_copies:
        copy.start()

    @pl.when(grp < 2)
    def _():
        pack(2 * SHARE, CELLS - 2 * SHARE, packed.at[SHARE : SHARE + CELLS - 2 * SHARE])
        for copy in second_copies:
            copy.start()
        pack(own_first, SHARE, recv.at[comp])

    @pl.when(grp == 3)
    def _():
        pack(own_first, CELLS - 2 * SHARE, recv.at[comp, 0 : CELLS - 2 * SHARE])

    wide8 = [value.reshape(1, 8, 128) for value in coef]

    @pl.when(grp < 3)
    def _():
        def solve_layer(layer):
            for tile in every:
                value = wide8[0] * load(v0, layer, tile)
                for k in range(1, 4):
                    value = value + wide8[k] * load(basis[k], layer, tile)
                store(xs, layer - 4, tile, value)

        over(4, 8, solve_layer)
        for tile in every:
            mirror_layers(xs[:, tile * 128 : tile * 128 + 128], tile, xstd, 0, True)
        high, low = split(xstd[...])
        parts[0:CELLS, :] = high
        parts[CELLS : 2 * CELLS, :] = low
        out[...] = jnp.dot(ptr[...], parts[...], preferred_element_type=F32)

    def lambda_rows(block, carry):
        rows = pl.ds(pl.multiple_of(block * 16, 16), 16)
        for part in range(2):
            jac = [
                [
                    recv[c, rows, d * NODES + part * 256 : d * NODES + part * 256 + 256].astype(F32)
                    for d in range(3)
                ]
                for c in range(3)
            ]
            lam[rows, part * 256 : part * 256 + 256] = lambda_two(jac)
        return carry

    def natural_order(chunk):
        rows = chunk_rows(chunk)
        slots = pl.ds(pl.multiple_of(own_first + chunk * CHUNK, CHUNK), CHUNK)
        odd_x, odd_y, odd_z = [
            classes[slots, k * 128 : k * 128 + 128] > 0.5 for k in range(3)
        ]
        values = [lam[rows, tile * 128 : tile * 128 + 128] for tile in every]
        flipped = reversals(jnp.concatenate(values, 0))
        turned = []
        for tile in every:
            rev_x, rev_y, rev_xy = [
                part[tile * CHUNK : tile * CHUNK + CHUNK] for part in flipped
            ]
            turned.append(
                jnp.where(
                    odd_x,
                    jnp.where(odd_y, rev_xy, rev_x),
                    jnp.where(odd_y, rev_y, values[tile]),
                )
            )
        for tile in every:
            value = jnp.where(odd_z, turned[3 - tile], turned[tile])
            if tile >= 2:
                value = rotated(value, 64, 1)
            lam[rows, tile * 128 : tile * 128 + 128] = value

    here = pl.ds(pl.multiple_of(dom * 8, 8), 8)

    def each_owner(chunk, action, local):
        piece = lax.div(own_first, CHUNK) + chunk
        for place in range(4):
            owner = place * 8 + lax.rem(place + lax.div(piece, 2), 4) * 2 + lax.rem(piece, 2)
            rows = pl.ds(pl.multiple_of(chunk * CHUNK + place * 8, 8), 8)
            own = (grp == 3) & (owner == dom)

            @pl.when(jnp.logical_not(own))
            def _():
                action(
                    remote(
                        lam.at[rows], lamrecv.at[here], osend.at[chunk * 4 + place], orecv,
                        (3, owner),
                    )
                )

            if local:

                @pl.when(own)
                def _():
                    lamrecv[here, :] = lam[rows, :]

    def analyse(chunk):
        others = (jnp.where(grp == 0, 1, 0), jnp.where(grp == 3, 1, 2))
        for which in range(2):
            piece = recv.at[others[which], chunk_rows(chunk)]
            remote(
                piece, piece, asend.at[0], arecv.at[which, chunk], (target, dom)
            ).wait_recv()
        lax.fori_loop(2 * chunk, 2 * chunk + 2, lambda_rows, 0)
        natural_order(chunk)
        each_owner(chunk, lambda copy: copy.start(), True)

    @pl.when(grp != 2)
    def _():
        for step in range(2):
            analyse(turn(step, own_count))

    @pl.when(grp < 2)
    def _():
        analyse(turn(2, own_count))

    @pl.when(grp != 2)
    def _():
        for step in range(2):
            each_owner(turn(step, own_count), lambda copy: copy.wait_send(), False)

    @pl.when(grp < 2)
    def _():
        each_owner(turn(2, own_count), lambda copy: copy.wait_send(), False)
        for copy in second_copies:
            copy.wait_send()

    for copy in first_copies:
        copy.wait_send()

    def wait_rows(count):
        piece = lamrecv.at[0 : 8 * count]
        remote(piece, piece, osend.at[0], orecv, (target, dom)).wait_recv()

    to_itself = lax.rem(lax.div(lax.rem(dom, 8), 2) - lax.div(dom, 8) + 4, 4) == 3

    @pl.when((grp == 3) & to_itself)
    def _():
        wait_rows(31)

    @pl.when((grp == 3) & jnp.logical_not(to_itself))
    def _():
        wait_rows(32)

    @pl.when(grp == 3)
    def _():
        out[...] = lamrecv[...]


def lambda_two(jac):
    strain = [[0.5 * (jac[a][b] + jac[b][a]) for b in range(3)] for a in range(3)]
    spin = [[0.5 * (jac[a][b] - jac[b][a]) for b in range(3)] for a in range(3)]
    m = [[None] * 3 for _ in range(3)]
    for a in range(3):
        for b in range(a, 3):
            value = strain[a][0] * strain[0][b] + spin[a][0] * spin[0][b]
            for k in (1, 2):
                value = value + strain[a][k] * strain[k][b] + spin[a][k] * spin[k][b]
            m[a][b] = value
            m[b][a] = value
    for sweep in range(SWEEPS):
        for p, q, r in ((0, 1, 2), (0, 2, 1), (1, 2, 0)):
            last = sweep == SWEEPS - 1
            twice = 2.0 * m[p][q]
            gap = m[p][p] - m[q][q]
            square = twice * twice + gap * gap
            inverse = lax.rsqrt(jnp.maximum(square, 1e-36))
            length = square * inverse
            mean = 0.5 * (m[p][p] + m[q][q])
            m[p][p] = mean + 0.5 * length
            m[q][q] = mean - 0.5 * length
            if last and (p, q) == (1, 2):
                continue
            none = square < 1e-36
            cosine2 = jnp.where(none, 1.0, jnp.abs(gap) * inverse)
            sine2 = jnp.where(none, 0.0, twice * inverse)
            larger = 0.5 + 0.5 * cosine2
            root = lax.rsqrt(larger)
            big = larger * root
            small = 0.5 * sine2 * root
            flip = gap < 0.0
            sine_big = jnp.where(sine2 < 0.0, -big, big)
            cosine = jnp.where(flip, jnp.abs(small), big)
            sine = jnp.where(flip, sine_big, small)
            side_p = m[r][p]
            side_q = m[r][q]
            m[r][p] = m[p][r] = cosine * side_p + sine * side_q
            m[r][q] = m[q][r] = cosine * side_q - sine * side_p
            m[p][q] = m[q][p] = jnp.zeros_like(side_p)
    diagonal = [m[0][0], m[1][1], m[2][2]]
    largest = jnp.maximum(jnp.maximum(diagonal[0], diagonal[1]), diagonal[2])
    smallest = jnp.minimum(jnp.minimum(diagonal[0], diagonal[1]), diagonal[2])
    return diagonal[0] + diagonal[1] + diagonal[2] - largest - smallest


def per_device(forcing, viscosity, mass_coef, element_order, owner):
    mats, flat, lanes = tables()
    vmem = pl.BlockSpec(memory_space=pltpu.VMEM)
    hbm = pl.BlockSpec(memory_space=pltpu.HBM)
    wide = (12 * LAYER, NODES)
    own = (CELLS, NODES)
    dma = pltpu.SemaphoreType.DMA
    result = pl.pallas_call(
        kernel,
        out_shape=pltpu.VMEM(own, F32),
        in_specs=[hbm] * 8,
        out_specs=vmem,
        scratch_shapes=[
            pltpu.VMEM(own, F32),
            pltpu.VMEM((8, NODES), F32),
            pltpu.VMEM((640, 384), BF16),
            pltpu.VMEM((1, CELLS), jnp.int32),
            pltpu.VMEM((1, CELLS), jnp.int32),
            pltpu.VMEM((4, 768, 256), BF16),
            pltpu.VMEM((8, CELLS), F32),
            pltpu.VMEM((2, 8, CELLS), F32),
            pltpu.VMEM((CELLS, 2 * CELLS), BF16),
            pltpu.VMEM((CELLS, 2 * CELLS), BF16),
            pltpu.VMEM((2 * CELLS, NODES), BF16),
            pltpu.VMEM((12 * LAYER, 128), F32),
            pltpu.VMEM((12 * LAYER, 128), F32),
            pltpu.VMEM(wide, F32),
            pltpu.VMEM(wide, F32),
            pltpu.VMEM(wide, F32),
            pltpu.VMEM((12 * LAYER, 3 * NODES), BF16),
            pltpu.VMEM(wide, F32),
            pltpu.VMEM(wide, F32),
            pltpu.VMEM(wide, F32),
            pltpu.VMEM(wide, F32),
            pltpu.VMEM(own, F32),
            pltpu.VMEM(own, F32),
            pltpu.VMEM((4, CELLS, 3 * NODES), F32),
            pltpu.VMEM((CELLS, CELLS), BF16),
            pltpu.VMEM((CELLS, 384), F32),
            pltpu.VMEM((CELLS, 3 * NODES), BF16),
            pltpu.VMEM((2, LAYER, 128), F32),
            pltpu.VMEM((2, LAYER, 128), F32),
            pltpu.VMEM((4, 2, LAYER, 128), F32),
            pltpu.VMEM((8, 128), F32),
            pltpu.VMEM((DOMS, 8, 128), F32),
            pltpu.VMEM((2 * SHARE, 3 * NODES), BF16),
            pltpu.VMEM((3, SHARE, 3 * NODES), BF16),
            pltpu.VMEM((SHARE, NODES), F32),
            pltpu.VMEM(own, F32),
            dma((6,)), dma((12,)), dma, dma((2,)), dma((2,)), dma((4,)), dma((4,)), dma((2,)),
            dma((2,)), dma, dma, dma((5,)), dma((2, 3)), dma((12,)), dma,
        ],
        compiler_params=pltpu.CompilerParams(
            collective_id=0, has_side_effects=True, vmem_limit_bytes=60 * 1024 * 1024
        ),
        name="solve_and_analyse",
    )(
        forcing, viscosity[None], mass_coef[None], element_order, owner,
        jnp.asarray(lanes), jnp.asarray(flat), jnp.asarray(mats),
    )
    return result[None]


def solution(mesh):
    in_specs = (P(None, "dom", None), P("dom"), P("dom"), P("dom", None), P("dom", None))
    out_specs = P("grp", "dom", None)
    return jax.shard_map(
        per_device, mesh=mesh, in_specs=in_specs, out_specs=out_specs, check_vma=False
    )
```

```python
import functools

import jax
import jax.numpy as jnp
import ml_dtypes
import numpy as np
from jax import lax
from jax.experimental import pallas as pl
from jax.experimental.pallas import tpu as pltpu
from jax.sharding import PartitionSpec as P

NP = 8
ITERS = 4
SWEEPS = 4
LAYER = 64
CELLS = 256
NODES = 512
DOMS = 32
CHUNK = 32
SHARE = 64
BASIS_LOW = 0.3
BASIS_HIGH = 2.0
THETA = 0.5 * (BASIS_LOW + BASIS_HIGH)
DELTA = 0.5 * (BASIS_HIGH - BASIS_LOW)
MESH = pl.DeviceIdType.MESH
F32 = jnp.float32
BF16 = jnp.bfloat16


def legendre_values(points, node_count):
    legendre = np.zeros((points.shape[0], node_count))
    legendre[:, 0] = 1.0
    legendre[:, 1] = points
    for poly_order in range(2, node_count):
        legendre[:, poly_order] = (
            (2 * poly_order - 1) * points * legendre[:, poly_order - 1]
            - (poly_order - 1) * legendre[:, poly_order - 2]
        ) / poly_order
    return legendre


def lobatto_table(node_count):
    degree = node_count - 1
    points = np.cos(np.pi * np.arange(node_count) / degree)
    for attempt in range(60):
        legendre = legendre_values(points, node_count)
        points = points - (points * legendre[:, degree] - legendre[:, degree - 1]) / (
            node_count * legendre[:, degree]
        )
    points = points[::-1].copy()
    end_values = legendre_values(points, node_count)[:, degree]
    weights = 2.0 / (degree * node_count * end_values * end_values)
    spacing = points[:, None] - points[None, :] + np.eye(node_count)
    diff_matrix = end_values[:, None] / end_values[None, :] / spacing
    diff_matrix = diff_matrix * (1.0 - np.eye(node_count))
    diff_matrix[0, 0] = -degree * node_count / 4.0
    diff_matrix[-1, -1] = degree * node_count / 4.0
    return (weights, diff_matrix)


def split_rows(matrix):
    high = matrix.astype(np.float32).astype(ml_dtypes.bfloat16)
    low = (matrix - high.astype(np.float64)).astype(np.float32).astype(ml_dtypes.bfloat16)
    return high, low


def tables():
    weights, diff = lobatto_table(NP)
    eye = np.eye(NP)
    cube = (
        weights[:, None, None] * weights[None, :, None] * weights[None, None, :]
    ).reshape(-1)
    directional = [
        np.kron(eye, np.kron(eye, diff)),
        np.kron(eye, np.kron(diff, eye)),
        np.kron(diff, np.kron(eye, eye)),
    ]
    stiff = np.zeros((NODES, NODES))
    for matrix in directional:
        stiff = stiff + matrix.T @ (cube[:, None] * matrix)
    flip = np.arange(NODES).reshape(NP, LAYER)[::-1][: NP // 2].reshape(-1)
    mats = []
    for matrix in (stiff, directional[2]):
        near, far = matrix[:256, :256], matrix[:256, flip]
        for block in (0.5 * (near + far), 0.5 * (near - far)):
            mats.append(np.stack(split_rows(block.T)))
    mats = np.stack(mats)
    flat = np.concatenate([directional[0].T[:128, :128], directional[1].T[:128, :128]], 1)
    high, low = split_rows(flat)
    flat = np.concatenate([high, high, low], 0)
    lanes = np.zeros((8, NODES), np.float32)
    lanes[0] = cube
    lanes[1] = np.diag(stiff)
    lanes[2] = np.repeat(diff[0], LAYER)
    order = [0, 1, 2, 3, 5, 4, 7, 6]
    lanes = lanes.reshape(8, NP, LAYER)[:, order].reshape(8, NODES)
    natural = cube.reshape(NP, LAYER).astype(np.float32).reshape(-1)
    lanes[3] = natural
    back = eye[::-1]
    half = np.eye(2)
    mirror = np.concatenate(
        [
            np.kron(half, np.kron(eye, back)),
            np.kron(half, np.kron(back, eye)),
            np.kron(half, np.kron(back, back)),
        ],
        1,
    ).astype(ml_dtypes.bfloat16)
    wide = np.concatenate([flat, np.zeros((384, 128), flat.dtype)], 1)
    return mats, np.concatenate([wide, mirror, mirror], 0), lanes


def rotated(value, shift, axis):
    return pltpu.roll(value, shift % value.shape[axis], axis)


def kernel(
    forcing, visc_in, mass_in, order_in, owner_in, lanes_in, flat_in, mats,
    out,
    fsc, lanes, flat, order_sc, owner_sc, weights, par, parn, pone, ptr, parts, visc, mass, raw, tmp,
    inv, lhs, v0, v1, v2, v3, xs, xstd, grads, gpack, classes, gcells, fsend, frecv, fghost, moments,
    red, packed, recv, lam, lamrecv,
    ssem, wsem, fsem, psend, precv, gsend, grecv, f3send, f3recv, rsend, rrecv, asend, arecv,
    osend, orecv,
):
    grp = lax.axis_index("grp")
    dom = lax.axis_index("dom")
    comp = jnp.minimum(grp, 2)
    up = lax.rem(dom + 1, DOMS)
    down = lax.rem(dom + DOMS - 1, DOMS)
    barrier = pltpu.get_barrier_semaphore()
    basis = (v0, v1, v2, v3)
    every = (0, 1, 2, 3)

    for step in range(1, DOMS):
        pl.semaphore_signal(
            barrier, inc=1, device_id=(grp, lax.rem(dom + step, DOMS)), device_id_type=MESH
        )
    for step in range(1, 4):
        pl.semaphore_signal(
            barrier, inc=1, device_id=(lax.rem(grp + step, 4), dom), device_id_type=MESH
        )

    load_small = [
        pltpu.make_async_copy(source, target, ssem.at[k])
        for k, (source, target) in enumerate(
            (
                (visc_in, par.at[0:1]),
                (mass_in, par.at[1:2]),
                (order_in, order_sc),
                (owner_in, owner_sc),
                (lanes_in, lanes),
                (flat_in, flat),
            )
        )
    ]
    for copy in load_small:
        copy.start()
    load_force = pltpu.make_async_copy(forcing.at[comp], fsc, fsem)
    load_force.start()
    load_mats = []
    for which in range(4):
        for part, source in enumerate((0, 0, 1)):
            copy = pltpu.make_async_copy(
                mats.at[which, source],
                weights.at[which, part * 256 : part * 256 + 256],
                wsem.at[3 * which + part],
            )
            copy.start()
            load_mats.append(copy)

    lane = lax.broadcasted_iota(jnp.int32, (8, 128), 1)
    sub = lax.broadcasted_iota(jnp.int32, (8, 128), 0)
    node_i = lax.rem(lane, 8)
    node_j = lax.rem(lane // 8, 8)
    odd = lax.rem(sub, 2) == 1
    first_i = node_i == 0
    last_i = node_i == 7
    take_up = ((last_i & jnp.logical_not(odd)) | (first_i & odd & (sub < 7)))
    take_down = ((last_i & odd) | (first_i & jnp.logical_not(odd) & (sub > 0)))
    has_up = jnp.where(dom < DOMS - 1, 1.0, 0.0).astype(F32)
    has_down = jnp.where(dom > 0, 1.0, 0.0).astype(F32)

    def wide(mask):
        return jnp.broadcast_to(mask[None], (8, 8, 128))

    x_up = wide(take_up)
    x_down = wide(take_down)
    x_odd = wide(odd)
    y_last = wide(node_j == 7)
    y_first = wide(node_j == 0)
    low_half = wide(lane < LAYER)

    def x_others(a):
        above = rotated(a, -1, 1)
        below = rotated(a, 1, 1)
        return jnp.where(x_up, above, jnp.where(x_down, below, 0.0))

    def y_others(a):
        blank = jnp.zeros((1, 8, 128), F32)
        last = jnp.concatenate([a[k ^ 1 : (k ^ 1) + 1] for k in range(8)], 0)
        first = jnp.concatenate(
            [blank] + [a[k : k + 1] for k in (2, 1, 4, 3, 6, 5)] + [blank], 0
        )
        return jnp.where(y_last, last, jnp.where(y_first, first, 0.0))

    def xy_sum(a):
        a = a + x_others(a)
        return a + y_others(a)

    def rows_of(layer):
        if isinstance(layer, int):
            return slice(layer * LAYER, layer * LAYER + LAYER)
        return pl.ds(pl.multiple_of(layer * LAYER, LAYER), LAYER)

    def load(ref, layer, tile):
        return ref[rows_of(layer), tile * 128 : tile * 128 + 128].reshape(8, 8, 128)

    def store(ref, layer, tile, value):
        ref[rows_of(layer), tile * 128 : tile * 128 + 128] = value.reshape(LAYER, 128)

    def column(ref, layer):
        return ref[rows_of(layer), :].reshape(8, 8, 128)

    def table(row, tile):
        return lanes[row : row + 1, tile * 128 : tile * 128 + 128].reshape(1, 1, 128)

    def split(value):
        high = value.astype(BF16)
        return high, (value - high.astype(F32)).astype(BF16)

    def store_lhs(layer, pair, first, second):
        for start, value in ((0, first + second), (768, first - second)):
            start = start + pair * 128
            high, low = split(value.reshape(LAYER, 128))
            lhs[rows_of(layer), start : start + 128] = high
            lhs[rows_of(layer), start + 256 : start + 384] = low
            lhs[rows_of(layer), start + 512 : start + 640] = high

    def reversals(value):
        total = jnp.dot(
            jnp.concatenate(split(value), 1), flat[384:640, :], preferred_element_type=F32
        )
        return total[:, 0:128], total[:, 128:256], total[:, 256:384]

    def mirror_layers(value, tile, target, base, back):
        flipped = reversals(value)
        for layer in range(4):
            rows = slice(layer * LAYER, layer * LAYER + LAYER)
            plain, rev_x, rev_y, rev_xy = [
                part[rows].reshape(8, 8, 128) for part in (value,) + flipped
            ]
            even_y = jnp.where(x_odd, rev_x, plain)
            odd_y = jnp.where(x_odd, rev_xy, rev_y)
            mixed = jnp.concatenate(
                [(odd_y if k % 2 else even_y)[k : k + 1] for k in range(8)], 0
            )
            place = 3 - tile if layer % 2 else tile
            if (place if back else tile) >= 2:
                mixed = rotated(mixed, 64, 2)
            store(target, base + layer, place, mixed)

    def over(low, high, body):
        lax.fori_loop(low, high, lambda layer, carry: (body(layer), carry)[1], 0)

    cell_sub = lax.broadcasted_iota(jnp.int32, (CELLS, CELLS), 0).astype(F32)
    cell_lane = lax.broadcasted_iota(jnp.int32, (CELLS, CELLS), 1).astype(F32)
    for copy in load_small:
        copy.wait()
    par[2:3, :] = order_sc[...].astype(F32)
    par[3:8, :] = jnp.zeros((5, CELLS), F32)

    def coefficients(ref, base, scale):
        hit = ref[2:3, :] == cell_sub
        for row, target in ((0, visc), (1, mass)):
            col = jnp.sum(jnp.where(hit, ref[row : row + 1, :], 0.0), axis=1, keepdims=True)
            target[base : base + CELLS, :] = jnp.broadcast_to(col * scale, (CELLS, 128))
        return hit

    one_hot = jnp.where(par[2:3, :] == cell_sub, 1.0, 0.0).astype(BF16)
    pone[:, 0:CELLS] = one_hot
    pone[:, CELLS : 2 * CELLS] = one_hot
    load_force.wait()
    high, low = split(fsc[...])
    parts[0:CELLS, :] = high
    parts[CELLS : 2 * CELLS, :] = low
    fsc[...] = jnp.dot(pone[...], parts[...], preferred_element_type=F32) * lanes[3:4, :]
    for tile in every:
        mirror_layers(fsc[:, tile * 128 : tile * 128 + 128], tile, raw, 4, False)

    pl.semaphore_wait(barrier, DOMS - 1 + 3)

    def remote(src, dst, send, recv_sem, device):
        return pltpu.make_async_remote_copy(
            src_ref=src, dst_ref=dst, send_sem=send, recv_sem=recv_sem,
            device_id=device, device_id_type=MESH,
        )

    par_copies = [
        remote(par, parn.at[0], psend.at[0], precv.at[0], (grp, up)),
        remote(par, parn.at[1], psend.at[1], precv.at[1], (grp, down)),
    ]
    ghost_copies = [
        remote(
            raw.at[5 * LAYER : 8 * LAYER], raw.at[1 * LAYER : 4 * LAYER],
            gsend.at[0], grecv.at[0], (grp, up),
        ),
        remote(
            raw.at[4 * LAYER : 7 * LAYER], raw.at[8 * LAYER : 11 * LAYER],
            gsend.at[1], grecv.at[1], (grp, down),
        ),
        remote(
            raw.at[4 * LAYER : 5 * LAYER, 384:512], raw.at[0:LAYER, 384:512],
            gsend.at[2], grecv.at[2], (grp, up),
        ),
        remote(
            raw.at[7 * LAYER : 8 * LAYER, 384:512], raw.at[11 * LAYER : 12 * LAYER, 384:512],
            gsend.at[3], grecv.at[3], (grp, down),
        ),
    ]
    for copy in par_copies + ghost_copies:
        copy.start()

    coefficients(par, CELLS, 1.0)
    order_col = jnp.sum(
        jnp.where(cell_sub == cell_lane, par[2:3, :], 0.0), axis=1, keepdims=True
    )
    one_hot = jnp.where(order_col == cell_lane, 1.0, 0.0).astype(BF16)
    ptr[:, 0:CELLS] = one_hot
    ptr[:, CELLS : 2 * CELLS] = one_hot
    owner_row = owner_sc[...].astype(F32)
    owner_col = jnp.sum(
        jnp.where(cell_sub == cell_lane, owner_row, 0.0), axis=1, keepdims=True
    )
    same = (owner_col == owner_row) & (cell_sub < cell_lane)
    rank_row = jnp.sum(jnp.where(same, 1.0, 0.0), axis=0, keepdims=True)
    owner_int = owner_sc[...]
    place = owner_int >> 3
    piece_row = ((((owner_int >> 1) - place) & 3) << 1) + (owner_int & 1)
    first_row = (piece_row * 4 + place).astype(F32)
    dest_row = jnp.where(owner_row >= 0.0, first_row * 8.0 + rank_row, -1.0)
    slot_of = jnp.where(dest_row == cell_sub, 1.0, 0.0).astype(BF16)
    gpack[...] = jnp.dot(slot_of, one_hot, preferred_element_type=F32).astype(BF16)
    cell_id = lax.broadcasted_iota(jnp.int32, (CELLS, 128), 0)
    for k, width in enumerate((1, 8, 64)):
        parity = lax.rem(cell_id // width, 2).astype(F32).astype(BF16)
        classes[:, k * 128 : k * 128 + 128] = jnp.dot(
            gpack[...], parity, preferred_element_type=F32
        )

    for copy in par_copies:
        copy.wait()
    coefficients(parn.at[0], 0, has_down)
    coefficients(parn.at[1], 2 * CELLS, has_up)

    def partners(layer):
        parity = layer % 2 if isinstance(layer, int) else lax.rem(layer, 2)
        return {0: layer - 1 + 2 * parity, 3: layer + 1 - 2 * parity}

    def face_sum(ref, layer, tile):
        value = load(ref, layer, tile)
        other = load(ref, partners(layer)[tile], tile)
        return value + jnp.where(low_half, other, 0.0)

    def put_inverse(layer, tile, diag):
        store(inv, layer, tile, jnp.where(diag > 0.0, (2.0 / DELTA) / diag, 0.0))

    def diagonal(layer, tiles):
        coef_v = column(visc, layer)
        coef_m = column(mass, layer)
        for tile in tiles:
            diag = xy_sum(coef_v * table(1, tile) + coef_m * table(0, tile))
            if tile in (0, 3):
                store(tmp, layer, tile, diag)
            else:
                put_inverse(layer, tile, diag)

    diagonal(0, (3,))
    over(1, 11, lambda layer: diagonal(layer, every))
    diagonal(11, (3,))

    def diagonal_faces(layer):
        for tile in (0, 3):
            put_inverse(layer, tile, face_sum(tmp, layer, tile))

    over(1, 11, diagonal_faces)

    def put_first(layer, pair, forces):
        values = []
        for tile, force in zip((pair, 3 - pair), forces):
            value = force * load(inv, layer, tile) * (0.5 * DELTA)
            store(v0, layer, tile, value)
            values.append(value)
        store_lhs(layer, pair, *values)

    def assemble(layer, tiles, scale):
        sums = []
        for tile in tiles:
            force = load(raw, layer, tile)
            if scale is not None:
                force = force * scale
            force = xy_sum(force)
            if tile in (0, 3):
                store(tmp, layer, tile, force)
            else:
                sums.append(force)
        if sums:
            put_first(layer, 1, sums)

    over(4, 8, lambda layer: assemble(layer, every, None))
    for copy in load_mats:
        copy.wait()
    for copy in ghost_copies:
        copy.wait()
    assemble(0, (3,), has_down)
    over(1, 4, lambda layer: assemble(layer, every, has_down))
    over(8, 11, lambda layer: assemble(layer, every, has_up))
    assemble(11, (3,), has_up)

    def first_faces(layer):
        put_first(layer, 0, [face_sum(tmp, layer, tile) for tile in (0, 3)])

    over(1, 11, first_faces)

    def multiply(low, high, which, target, first=0):
        for part in range(2):
            target[:, first + part * 256 : first + part * 256 + 256] = jnp.dot(
                lhs[low * LAYER : high * LAYER, part * 768 : part * 768 + 768],
                weights[2 * which + part],
                preferred_element_type=F32,
            )

    def advance(step, layer, pair, totals):
        values = []
        for tile, total in zip((pair, 3 - pair), totals):
            value = total * load(inv, layer, tile)
            current = load(basis[step], layer, tile)
            if step == 0:
                value = 0.5 * value - (THETA / DELTA) * current
            else:
                value = value - (2.0 * THETA / DELTA) * current
                value = value - load(basis[step - 1], layer, tile)
            store(basis[step + 1], layer, tile, value)
            values.append(value)
        store_lhs(layer, pair, *values)

    def apply(step, layer, tiles, sums, going):
        coef_v = column(visc, layer)
        coef_m = column(mass, layer)
        for pair in (1, 0):
            if pair not in tiles and 3 - pair not in tiles:
                continue
            even = load(tmp, layer, pair)
            uneven = load(tmp, layer, 2 + pair)
            images = []
            for tile, product in ((pair, even + uneven), (3 - pair, even - uneven)):
                if tile not in tiles:
                    continue
                value = load(basis[step], layer, tile)
                weighted = coef_m * table(0, tile)
                image = coef_v * product + weighted * value
                if sums is not None:
                    diag = coef_v * table(1, tile) + weighted
                    sums = (
                        sums[0] + jnp.sum(value * image, axis=0),
                        sums[1] + jnp.sum(value * value * diag, axis=0),
                    )
                if going:
                    image = xy_sum(image)
                    if pair == 0:
                        store(tmp, layer, tile, image)
                    else:
                        images.append(image)
            if images:
                advance(step, layer, 1, images)
        return sums

    def faces(step, layer):
        advance(step, layer, 0, [face_sum(tmp, layer, tile) for tile in (0, 3)])

    blank_sums = (jnp.zeros((8, 128), F32), jnp.zeros((8, 128), F32))
    for step in range(ITERS):
        low, high = 1 + step, 11 - step
        going = step + 1 < ITERS
        multiply(low, high, 0, tmp.at[low * LAYER : high * LAYER])
        if going:
            inward = 0 if low % 2 else 3
            apply(step, low, (inward,), None, True)
            over(low + 1, 4, lambda layer: apply(step, layer, every, None, True))
        sums = lax.fori_loop(
            4, 8, lambda layer, carry: apply(step, layer, every, carry, going), blank_sums
        )
        if going:
            over(8, high - 1, lambda layer: apply(step, layer, every, None, True))
            apply(step, high - 1, (inward,), None, True)
        moments[step : step + 1, :] = jnp.sum(sums[0], axis=0, keepdims=True)
        moments[4 + step : 5 + step, :] = jnp.sum(sums[1], axis=0, keepdims=True)
        if going:
            over(low + 1, high - 1, lambda layer: faces(step, layer))

    red[0] = moments[...]
    for step in range(1, DOMS):
        remote(
            moments, red.at[step], rsend, rrecv, (grp, lax.rem(dom + step, DOMS))
        ).start()

    def end_face(ref, layer):
        total = load(ref, layer, 0) * table(2, 0)
        for tile in (1, 2, 3):
            total = total + load(ref, layer, tile) * table(2, tile)
        total = total + rotated(total, 64, 2)
        return -total if layer % 2 else total

    fsend[0] = end_face(v3, 7).reshape(LAYER, 128)
    fsend[1] = end_face(v3, 4).reshape(LAYER, 128)
    face_copies = [
        remote(fsend.at[0], frecv.at[0], f3send.at[0], f3recv.at[0], (grp, up)),
        remote(fsend.at[1], frecv.at[1], f3send.at[1], f3recv.at[1], (grp, down)),
    ]
    for copy in face_copies:
        copy.start()

    own_rows = slice(4 * LAYER, 8 * LAYER)
    for index in (3, 0, 1, 2):
        if index < 3:
            over(
                4,
                8,
                lambda layer: [
                    store_lhs(
                        layer,
                        pair,
                        load(basis[index], layer, pair),
                        load(basis[index], layer, 3 - pair),
                    )
                    for pair in (0, 1)
                ],
            )

        left = jnp.concatenate(
            [
                jnp.concatenate(
                    [
                        lhs[own_rows, start + part * 256 : start + part * 256 + 128]
                        for part in range(3)
                    ],
                    1,
                )
                for start in (0, 128, 768, 896)
            ],
            0,
        )
        both = jnp.dot(left, flat[0:384, 0:256], preferred_element_type=F32)
        for part in range(4):
            rows = slice(part * CELLS, part * CELLS + CELLS)
            grads[index, :, part * 128 : part * 128 + 128] = both[rows, 0:128]
            grads[index, :, NODES + part * 128 : NODES + part * 128 + 128] = both[rows, 128:256]
        multiply(4, 8, 1, grads.at[index], 2 * NODES)
        if index < 3:
            fghost[index, 0] = end_face(basis[index], 3).reshape(LAYER, 128)
            fghost[index, 1] = end_face(basis[index], 8).reshape(LAYER, 128)

    for copy in face_copies:
        copy.wait()
    for side in range(2):
        fghost[3, side] = frecv[side]

    whole = remote(red.at[1:DOMS], red.at[1:DOMS], rsend, rrecv, (grp, up))
    whole.wait_send()
    whole.wait_recv()

    total = jnp.sum(red[...], axis=0)
    total = jnp.broadcast_to(jnp.sum(total, axis=1, keepdims=True), (8, 128))
    moments[...] = total

    def scalar(row):
        return jnp.broadcast_to(moments[row : row + 1, :], (8, 128))

    alpha = [scalar(row) for row in range(4)]
    beta = [scalar(4 + row) for row in range(4)]
    gamma = [(alpha[k] - THETA * beta[k]) * (1.0 / DELTA) for k in range(4)]
    mu = [beta[0], gamma[0]]
    ahead = gamma[0]
    for k in range(1, 4):
        ahead = 2.0 * gamma[k] - ahead
        mu.append(2.0 * beta[k] - mu[0])
        mu.append(2.0 * ahead - mu[1])

    def inner(i, j):
        return 0.5 * (mu[i + j] + mu[abs(i - j)])

    gram = [
        [
            DELTA * 0.5 * (inner(i, j + 1) + inner(i, abs(j - 1))) + THETA * inner(i, j)
            for j in range(4)
        ]
        for i in range(4)
    ]
    right = [mu[k] for k in range(4)]
    pivots = []
    for k in range(4):
        original = DELTA * 0.5 * (inner(k, k + 1) + inner(k, abs(k - 1))) + THETA * inner(k, k)
        pivot = gram[k][k]
        good = pivot > 1e-7 * original
        inverse = jnp.where(good, 1.0 / jnp.where(good, pivot, 1.0), 0.0)
        pivots.append(inverse)
        for i in range(k + 1, 4):
            factor = gram[i][k] * inverse
            for j in range(k + 1, 4):
                gram[i][j] = gram[i][j] - factor * gram[k][j]
            right[i] = right[i] - factor * right[k]
    coef = [None] * 4
    for k in (3, 2, 1, 0):
        value = right[k]
        for j in range(k + 1, 4):
            value = value - gram[k][j] * coef[j]
        coef[k] = value * pivots[k]

    coef8 = [(value * (1.0 / NP)).reshape(1, 8, 128) for value in coef]
    coef16 = [0.5 * value for value in coef8]
    x_sign = jnp.where(odd, -1.0, 1.0).reshape(1, 8, 128)
    x_scale = jnp.where(take_up | take_down, 0.5, 1.0).reshape(1, 8, 128) * x_sign
    y_half = jnp.where((node_j == 7) | (node_j == 0), 0.5, 1.0).reshape(1, 8, 128)
    y_end = jnp.where(node_j == 7, 0.5, 1.0).reshape(1, 8, 128)
    y_scale = jnp.concatenate(
        [y_end, -y_half, y_half, -y_half, y_half, -y_half, y_half, -y_end], 0
    )

    def combined(layer, direction, pair):
        parts_of = []
        scale = coef8 if direction == 2 else coef16
        for start in (0, 256):
            start = start + direction * NODES + pair * 128
            value = None
            for k in range(4):
                term = scale[k] * grads[k, rows_of(layer), start : start + 128].reshape(8, 8, 128)
                value = term if value is None else value + term
            parts_of.append(value)
        even, uneven = parts_of
        if direction == 2:
            return even + uneven, uneven - even
        return even + uneven, even - uneven

    def put_grad(layer, direction, tile, value):
        start = direction * NODES + tile * 128
        gcells[rows_of(layer), start : start + 128] = value.reshape(LAYER, 128).astype(BF16)

    def flat_grads(layer):
        z_sign = (1 - 2 * lax.rem(layer, 2)).astype(F32)
        for pair in (0, 1):
            for tile, value in zip((pair, 3 - pair), combined(layer, 0, pair)):
                put_grad(layer, 0, tile, x_scale * (value - x_others(value)))
            for tile, value in zip((pair, 3 - pair), combined(layer, 1, pair)):
                put_grad(layer, 1, tile, y_scale * (value - y_others(value)))
        for tile, value in zip((1, 2), combined(layer, 2, 1)):
            put_grad(layer, 2, tile, z_sign * value)
        for tile, value in zip((0, 3), combined(layer, 2, 0)):
            store(xstd, layer, tile, z_sign * value)

    over(0, 4, flat_grads)

    def mean_face(layer, tile, other, there):
        value = load(xstd, layer, tile)
        put_grad(layer, 2, tile, value + jnp.where(low_half, there * (other - value), 0.0))

    for layer in range(4):
        mean_face(layer, 3, load(xstd, layer ^ 1, 3), 0.5)
        if layer in (1, 2):
            mean_face(layer, 0, load(xstd, 3 - layer, 0), 0.5)
        else:
            side = 0 if layer == 0 else 1
            other = None
            for k in range(4):
                term = coef8[k] * fghost[k, side].reshape(8, 8, 128)
                other = term if other is None else other + term
            mean_face(layer, 0, other, 0.5 * (has_up if side else has_down))

    own_first = grp * SHARE

    def pack(part, carry):
        cols = pl.ds(pl.multiple_of(part * 512, 512), 512)
        packed[:, cols] = jnp.dot(
            gpack[...], gcells[:, cols], preferred_element_type=F32
        ).astype(BF16)
        return carry

    lax.fori_loop(0, 3, pack, 0)

    def chunk_rows(chunk, base=0):
        return pl.ds(pl.multiple_of(base + chunk * CHUNK, CHUNK), CHUNK)

    def turn(step):
        return lax.rem(dom + step, 2)

    def piece_copy(step, target, slot):
        chunk = turn(step)
        return remote(
            packed.at[chunk_rows(chunk, target * SHARE)], recv.at[comp, chunk_rows(chunk)],
            asend.at[slot, step], arecv.at[comp, chunk], (target, dom),
        )

    def each_send(action):
        @pl.when(grp < 2)
        def _():
            for step in range(2):
                for hop in (2, 1, 3):
                    action(piece_copy(step, lax.rem(grp + hop, 4), hop - 1))

        @pl.when(grp >= 2)
        def _():
            for step in range(2):
                action(piece_copy(step, 3 - grp, 0))

    each_send(lambda copy: copy.start())
    recv[comp] = packed[pl.ds(pl.multiple_of(own_first, SHARE), SHARE), :]

    wide8 = [value.reshape(1, 8, 128) for value in coef]

    @pl.when(grp < 3)
    def _():
        def solve_layer(layer):
            for tile in every:
                value = wide8[0] * load(v0, layer, tile)
                for k in range(1, 4):
                    value = value + wide8[k] * load(basis[k], layer, tile)
                store(xs, layer - 4, tile, value)

        over(4, 8, solve_layer)
        for tile in every:
            mirror_layers(xs[:, tile * 128 : tile * 128 + 128], tile, xstd, 0, True)
        high, low = split(xstd[...])
        parts[0:CELLS, :] = high
        parts[CELLS : 2 * CELLS, :] = low
        out[...] = jnp.dot(ptr[...], parts[...], preferred_element_type=F32)

    def lambda_rows(block, carry):
        rows = pl.ds(pl.multiple_of(block * 16, 16), 16)
        for part in range(2):
            jac = [
                [
                    recv[c, rows, d * NODES + part * 256 : d * NODES + part * 256 + 256].astype(F32)
                    for d in range(3)
                ]
                for c in range(3)
            ]
            lam[rows, part * 256 : part * 256 + 256] = lambda_two(jac)
        return carry

    def natural_order(chunk):
        rows = chunk_rows(chunk)
        slots = pl.ds(pl.multiple_of(own_first + chunk * CHUNK, CHUNK), CHUNK)
        odd_x, odd_y, odd_z = [
            classes[slots, k * 128 : k * 128 + 128] > 0.5 for k in range(3)
        ]
        values = [lam[rows, tile * 128 : tile * 128 + 128] for tile in every]
        flipped = reversals(jnp.concatenate(values, 0))
        turned = []
        for tile in every:
            rev_x, rev_y, rev_xy = [
                part[tile * CHUNK : tile * CHUNK + CHUNK] for part in flipped
            ]
            turned.append(
                jnp.where(
                    odd_x,
                    jnp.where(odd_y, rev_xy, rev_x),
                    jnp.where(odd_y, rev_y, values[tile]),
                )
            )
        for tile in every:
            value = jnp.where(odd_z, turned[3 - tile], turned[tile])
            if tile >= 2:
                value = rotated(value, 64, 1)
            lam[rows, tile * 128 : tile * 128 + 128] = value

    here = pl.ds(pl.multiple_of(dom * 8, 8), 8)

    def each_owner(chunk, action, local):
        piece = lax.div(own_first, CHUNK) + chunk
        for place in range(4):
            owner = place * 8 + lax.rem(place + lax.div(piece, 2), 4) * 2 + lax.rem(piece, 2)
            rows = pl.ds(pl.multiple_of(chunk * CHUNK + place * 8, 8), 8)
            own = (grp == 3) & (owner == dom)

            @pl.when(jnp.logical_not(own))
            def _():
                action(
                    remote(
                        lam.at[rows], lamrecv.at[here], osend.at[chunk * 4 + place], orecv,
                        (3, owner),
                    )
                )

            if local:

                @pl.when(own)
                def _():
                    lamrecv[here, :] = lam[rows, :]

    def analyse(chunk):
        for step in (1, 2):
            other = lax.rem(comp + step, 3)
            piece = recv.at[other, chunk_rows(chunk)]
            remote(
                piece, piece, asend.at[0, 0], arecv.at[other, chunk], (lax.rem(grp + 1, 4), dom)
            ).wait_recv()
        lax.fori_loop(2 * chunk, 2 * chunk + 2, lambda_rows, 0)
        natural_order(chunk)
        each_owner(chunk, lambda copy: copy.start(), True)

    for step in range(2):
        analyse(turn(step))
    for step in range(2):
        each_owner(turn(step), lambda copy: copy.wait_send(), False)
    each_send(lambda copy: copy.wait_send())

    def wait_rows(count):
        piece = lamrecv.at[0 : 8 * count]
        remote(piece, piece, osend.at[0], orecv, (lax.rem(grp + 1, 4), dom)).wait_recv()

    to_itself = lax.rem(lax.div(lax.rem(dom, 8), 2) - lax.div(dom, 8) + 4, 4) == 3

    @pl.when((grp == 3) & to_itself)
    def _():
        wait_rows(31)

    @pl.when((grp == 3) & jnp.logical_not(to_itself))
    def _():
        wait_rows(32)

    @pl.when(grp == 3)
    def _():
        out[...] = lamrecv[...]


def lambda_two(jac):
    strain = [[0.5 * (jac[a][b] + jac[b][a]) for b in range(3)] for a in range(3)]
    spin = [[0.5 * (jac[a][b] - jac[b][a]) for b in range(3)] for a in range(3)]
    m = [[None] * 3 for _ in range(3)]
    for a in range(3):
        for b in range(a, 3):
            value = strain[a][0] * strain[0][b] + spin[a][0] * spin[0][b]
            for k in (1, 2):
                value = value + strain[a][k] * strain[k][b] + spin[a][k] * spin[k][b]
            m[a][b] = value
            m[b][a] = value
    for sweep in range(SWEEPS):
        for p, q, r in ((0, 1, 2), (0, 2, 1), (1, 2, 0)):
            last = sweep == SWEEPS - 1
            twice = 2.0 * m[p][q]
            gap = m[p][p] - m[q][q]
            square = twice * twice + gap * gap
            inverse = lax.rsqrt(jnp.maximum(square, 1e-36))
            length = square * inverse
            mean = 0.5 * (m[p][p] + m[q][q])
            m[p][p] = mean + 0.5 * length
            m[q][q] = mean - 0.5 * length
            if last and (p, q) == (1, 2):
                continue
            none = square < 1e-36
            cosine2 = jnp.where(none, 1.0, jnp.abs(gap) * inverse)
            sine2 = jnp.where(none, 0.0, twice * inverse)
            larger = 0.5 + 0.5 * cosine2
            root = lax.rsqrt(larger)
            big = larger * root
            small = 0.5 * sine2 * root
            flip = gap < 0.0
            sine_big = jnp.where(sine2 < 0.0, -big, big)
            cosine = jnp.where(flip, jnp.abs(small), big)
            sine = jnp.where(flip, sine_big, small)
            side_p = m[r][p]
            side_q = m[r][q]
            m[r][p] = m[p][r] = cosine * side_p + sine * side_q
            m[r][q] = m[q][r] = cosine * side_q - sine * side_p
            m[p][q] = m[q][p] = jnp.zeros_like(side_p)
    diagonal = [m[0][0], m[1][1], m[2][2]]
    largest = jnp.maximum(jnp.maximum(diagonal[0], diagonal[1]), diagonal[2])
    smallest = jnp.minimum(jnp.minimum(diagonal[0], diagonal[1]), diagonal[2])
    return diagonal[0] + diagonal[1] + diagonal[2] - largest - smallest


def per_device(forcing, viscosity, mass_coef, element_order, owner):
    mats, flat, lanes = tables()
    vmem = pl.BlockSpec(memory_space=pltpu.VMEM)
    hbm = pl.BlockSpec(memory_space=pltpu.HBM)
    wide = (12 * LAYER, NODES)
    own = (CELLS, NODES)
    dma = pltpu.SemaphoreType.DMA
    result = pl.pallas_call(
        kernel,
        out_shape=pltpu.VMEM(own, F32),
        in_specs=[hbm] * 8,
        out_specs=vmem,
        scratch_shapes=[
            pltpu.VMEM(own, F32),
            pltpu.VMEM((8, NODES), F32),
            pltpu.VMEM((640, 384), BF16),
            pltpu.VMEM((1, CELLS), jnp.int32),
            pltpu.VMEM((1, CELLS), jnp.int32),
            pltpu.VMEM((4, 768, 256), BF16),
            pltpu.VMEM((8, CELLS), F32),
            pltpu.VMEM((2, 8, CELLS), F32),
            pltpu.VMEM((CELLS, 2 * CELLS), BF16),
            pltpu.VMEM((CELLS, 2 * CELLS), BF16),
            pltpu.VMEM((2 * CELLS, NODES), BF16),
            pltpu.VMEM((12 * LAYER, 128), F32),
            pltpu.VMEM((12 * LAYER, 128), F32),
            pltpu.VMEM(wide, F32),
            pltpu.VMEM(wide, F32),
            pltpu.VMEM(wide, F32),
            pltpu.VMEM((12 * LAYER, 3 * NODES), BF16),
            pltpu.VMEM(wide, F32),
            pltpu.VMEM(wide, F32),
            pltpu.VMEM(wide, F32),
            pltpu.VMEM(wide, F32),
            pltpu.VMEM(own, F32),
            pltpu.VMEM(own, F32),
            pltpu.VMEM((4, CELLS, 3 * NODES), F32),
            pltpu.VMEM((CELLS, CELLS), BF16),
            pltpu.VMEM((CELLS, 384), F32),
            pltpu.VMEM((CELLS, 3 * NODES), BF16),
            pltpu.VMEM((2, LAYER, 128), F32),
            pltpu.VMEM((2, LAYER, 128), F32),
            pltpu.VMEM((4, 2, LAYER, 128), F32),
            pltpu.VMEM((8, 128), F32),
            pltpu.VMEM((DOMS, 8, 128), F32),
            pltpu.VMEM((CELLS, 3 * NODES), BF16),
            pltpu.VMEM((3, SHARE, 3 * NODES), BF16),
            pltpu.VMEM((SHARE, NODES), F32),
            pltpu.VMEM(own, F32),
            dma((6,)), dma((12,)), dma, dma((2,)), dma((2,)), dma((4,)), dma((4,)), dma((2,)),
            dma((2,)), dma, dma, dma((3, 2)), dma((3, 2)), dma((8,)), dma,
        ],
        compiler_params=pltpu.CompilerParams(
            collective_id=0, has_side_effects=True, vmem_limit_bytes=60 * 1024 * 1024
        ),
        name="solve_and_analyse",
    )(
        forcing, viscosity[None], mass_coef[None], element_order, owner,
        jnp.asarray(lanes), jnp.asarray(flat), jnp.asarray(mats),
    )
    return result[None]


def solution(mesh):
    in_specs = (P(None, "dom", None), P("dom"), P("dom"), P("dom", None), P("dom", None))
    out_specs = P("grp", "dom", None)
    return jax.shard_map(
        per_device, mesh=mesh, in_specs=in_specs, out_specs=out_specs, check_vma=False
    )
```

```python
import functools

import jax
import jax.numpy as jnp
import ml_dtypes
import numpy as np
from jax import lax
from jax.experimental import pallas as pl
from jax.experimental.pallas import tpu as pltpu
from jax.sharding import PartitionSpec as P

NP = 8
ITERS = 4
SWEEPS = 4
LAYER = 64
CELLS = 256
NODES = 512
DOMS = 32
CHUNK = 16
PIECES = 4
SHARE = 64
BASIS_LOW = 0.3
BASIS_HIGH = 2.0
THETA = 0.5 * (BASIS_LOW + BASIS_HIGH)
DELTA = 0.5 * (BASIS_HIGH - BASIS_LOW)
MESH = pl.DeviceIdType.MESH
F32 = jnp.float32
BF16 = jnp.bfloat16


def legendre_values(points, node_count):
    legendre = np.zeros((points.shape[0], node_count))
    legendre[:, 0] = 1.0
    legendre[:, 1] = points
    for poly_order in range(2, node_count):
        legendre[:, poly_order] = (
            (2 * poly_order - 1) * points * legendre[:, poly_order - 1]
            - (poly_order - 1) * legendre[:, poly_order - 2]
        ) / poly_order
    return legendre


def lobatto_table(node_count):
    degree = node_count - 1
    points = np.cos(np.pi * np.arange(node_count) / degree)
    for attempt in range(60):
        legendre = legendre_values(points, node_count)
        points = points - (points * legendre[:, degree] - legendre[:, degree - 1]) / (
            node_count * legendre[:, degree]
        )
    points = points[::-1].copy()
    end_values = legendre_values(points, node_count)[:, degree]
    weights = 2.0 / (degree * node_count * end_values * end_values)
    spacing = points[:, None] - points[None, :] + np.eye(node_count)
    diff_matrix = end_values[:, None] / end_values[None, :] / spacing
    diff_matrix = diff_matrix * (1.0 - np.eye(node_count))
    diff_matrix[0, 0] = -degree * node_count / 4.0
    diff_matrix[-1, -1] = degree * node_count / 4.0
    return (weights, diff_matrix)


def split_rows(matrix):
    high = matrix.astype(np.float32).astype(ml_dtypes.bfloat16)
    low = (matrix - high.astype(np.float64)).astype(np.float32).astype(ml_dtypes.bfloat16)
    return high, low


def tables():
    weights, diff = lobatto_table(NP)
    eye = np.eye(NP)
    cube = (
        weights[:, None, None] * weights[None, :, None] * weights[None, None, :]
    ).reshape(-1)
    directional = [
        np.kron(eye, np.kron(eye, diff)),
        np.kron(eye, np.kron(diff, eye)),
        np.kron(diff, np.kron(eye, eye)),
    ]
    stiff = np.zeros((NODES, NODES))
    for matrix in directional:
        stiff = stiff + matrix.T @ (cube[:, None] * matrix)
    flip = np.arange(NODES).reshape(NP, LAYER)[::-1][: NP // 2].reshape(-1)
    mats = []
    for matrix in (stiff, directional[2]):
        near, far = matrix[:256, :256], matrix[:256, flip]
        for block in (0.5 * (near + far), 0.5 * (near - far)):
            mats.append(np.stack(split_rows(block.T)))
    mats = np.stack(mats)
    flat = np.concatenate([directional[0].T[:128, :128], directional[1].T[:128, :128]], 1)
    high, low = split_rows(flat)
    flat = np.concatenate([high, high, low], 0)
    lanes = np.zeros((8, NODES), np.float32)
    lanes[0] = cube
    lanes[1] = np.diag(stiff)
    lanes[2] = np.repeat(diff[0], LAYER)
    order = [0, 1, 2, 3, 5, 4, 7, 6]
    lanes = lanes.reshape(8, NP, LAYER)[:, order].reshape(8, NODES)
    natural = cube.reshape(NP, LAYER).astype(np.float32).reshape(-1)
    lanes[3] = natural
    back = eye[::-1]
    half = np.eye(2)
    mirror = np.concatenate(
        [
            np.kron(half, np.kron(eye, back)),
            np.kron(half, np.kron(back, eye)),
            np.kron(half, np.kron(back, back)),
        ],
        1,
    ).astype(ml_dtypes.bfloat16)
    wide = np.concatenate([flat, np.zeros((384, 128), flat.dtype)], 1)
    return mats, np.concatenate([wide, mirror, mirror], 0), lanes


def rotated(value, shift, axis):
    return pltpu.roll(value, shift % value.shape[axis], axis)


def kernel(
    forcing, visc_in, mass_in, order_in, owner_in, lanes_in, flat_in, mats,
    out,
    fsc, lanes, flat, order_sc, owner_sc, weights, par, parn, pone, ptr, parts, visc, mass, raw, tmp,
    inv, lhs, v0, v1, v2, v3, xs, xstd, grads, gpack, classes, gcells, fsend, frecv, fghost, moments,
    red, packed, recv, lam, lamrecv,
    ssem, wsem, fsem, psend, precv, gsend, grecv, f3send, f3recv, rsend, rrecv, asend, arecv,
    osend, orecv,
):
    grp = lax.axis_index("grp")
    dom = lax.axis_index("dom")
    comp = jnp.minimum(grp, 2)
    up = lax.rem(dom + 1, DOMS)
    down = lax.rem(dom + DOMS - 1, DOMS)
    barrier = pltpu.get_barrier_semaphore()
    basis = (v0, v1, v2, v3)
    every = (0, 1, 2, 3)

    for step in range(1, DOMS):
        pl.semaphore_signal(
            barrier, inc=1, device_id=(grp, lax.rem(dom + step, DOMS)), device_id_type=MESH
        )
    for step in range(1, 4):
        pl.semaphore_signal(
            barrier, inc=1, device_id=(lax.rem(grp + step, 4), dom), device_id_type=MESH
        )

    load_small = [
        pltpu.make_async_copy(source, target, ssem.at[k])
        for k, (source, target) in enumerate(
            (
                (visc_in, par.at[0:1]),
                (mass_in, par.at[1:2]),
                (order_in, order_sc),
                (owner_in, owner_sc),
                (lanes_in, lanes),
                (flat_in, flat),
            )
        )
    ]
    for copy in load_small:
        copy.start()
    load_force = pltpu.make_async_copy(forcing.at[comp], fsc, fsem)
    load_force.start()
    load_mats = []
    for which in range(4):
        for part, source in enumerate((0, 0, 1)):
            copy = pltpu.make_async_copy(
                mats.at[which, source],
                weights.at[which, part * 256 : part * 256 + 256],
                wsem.at[3 * which + part],
            )
            copy.start()
            load_mats.append(copy)

    lane = lax.broadcasted_iota(jnp.int32, (8, 128), 1)
    sub = lax.broadcasted_iota(jnp.int32, (8, 128), 0)
    node_i = lax.rem(lane, 8)
    node_j = lax.rem(lane // 8, 8)
    odd = lax.rem(sub, 2) == 1
    first_i = node_i == 0
    last_i = node_i == 7
    take_up = ((last_i & jnp.logical_not(odd)) | (first_i & odd & (sub < 7)))
    take_down = ((last_i & odd) | (first_i & jnp.logical_not(odd) & (sub > 0)))
    has_up = jnp.where(dom < DOMS - 1, 1.0, 0.0).astype(F32)
    has_down = jnp.where(dom > 0, 1.0, 0.0).astype(F32)

    def wide(mask):
        return jnp.broadcast_to(mask[None], (8, 8, 128))

    x_up = wide(take_up)
    x_down = wide(take_down)
    x_odd = wide(odd)
    y_last = wide(node_j == 7)
    y_first = wide(node_j == 0)
    low_half = wide(lane < LAYER)

    def x_others(a):
        above = rotated(a, -1, 1)
        below = rotated(a, 1, 1)
        return jnp.where(x_up, above, jnp.where(x_down, below, 0.0))

    def y_others(a):
        blank = jnp.zeros((1, 8, 128), F32)
        last = jnp.concatenate([a[k ^ 1 : (k ^ 1) + 1] for k in range(8)], 0)
        first = jnp.concatenate(
            [blank] + [a[k : k + 1] for k in (2, 1, 4, 3, 6, 5)] + [blank], 0
        )
        return jnp.where(y_last, last, jnp.where(y_first, first, 0.0))

    def xy_sum(a):
        a = a + x_others(a)
        return a + y_others(a)

    def rows_of(layer):
        if isinstance(layer, int):
            return slice(layer * LAYER, layer * LAYER + LAYER)
        return pl.ds(pl.multiple_of(layer * LAYER, LAYER), LAYER)

    def load(ref, layer, tile):
        return ref[rows_of(layer), tile * 128 : tile * 128 + 128].reshape(8, 8, 128)

    def store(ref, layer, tile, value):
        ref[rows_of(layer), tile * 128 : tile * 128 + 128] = value.reshape(LAYER, 128)

    def column(ref, layer):
        return ref[rows_of(layer), :].reshape(8, 8, 128)

    def table(row, tile):
        return lanes[row : row + 1, tile * 128 : tile * 128 + 128].reshape(1, 1, 128)

    def split(value):
        high = value.astype(BF16)
        return high, (value - high.astype(F32)).astype(BF16)

    def store_lhs(layer, pair, first, second):
        for start, value in ((0, first + second), (768, first - second)):
            start = start + pair * 128
            high, low = split(value.reshape(LAYER, 128))
            lhs[rows_of(layer), start : start + 128] = high
            lhs[rows_of(layer), start + 256 : start + 384] = low
            lhs[rows_of(layer), start + 512 : start + 640] = high

    def reversals(value):
        total = jnp.dot(
            jnp.concatenate(split(value), 1), flat[384:640, :], preferred_element_type=F32
        )
        return total[:, 0:128], total[:, 128:256], total[:, 256:384]

    def mirror_layers(value, tile, target, base, back):
        flipped = reversals(value)
        for layer in range(4):
            rows = slice(layer * LAYER, layer * LAYER + LAYER)
            plain, rev_x, rev_y, rev_xy = [
                part[rows].reshape(8, 8, 128) for part in (value,) + flipped
            ]
            even_y = jnp.where(x_odd, rev_x, plain)
            odd_y = jnp.where(x_odd, rev_xy, rev_y)
            mixed = jnp.concatenate(
                [(odd_y if k % 2 else even_y)[k : k + 1] for k in range(8)], 0
            )
            place = 3 - tile if layer % 2 else tile
            if (place if back else tile) >= 2:
                mixed = rotated(mixed, 64, 2)
            store(target, base + layer, place, mixed)

    def over(low, high, body):
        lax.fori_loop(low, high, lambda layer, carry: (body(layer), carry)[1], 0)

    cell_sub = lax.broadcasted_iota(jnp.int32, (CELLS, CELLS), 0).astype(F32)
    cell_lane = lax.broadcasted_iota(jnp.int32, (CELLS, CELLS), 1).astype(F32)
    for copy in load_small:
        copy.wait()
    par[2:3, :] = order_sc[...].astype(F32)
    par[3:8, :] = jnp.zeros((5, CELLS), F32)

    def coefficients(ref, base, scale):
        hit = ref[2:3, :] == cell_sub
        for row, target in ((0, visc), (1, mass)):
            col = jnp.sum(jnp.where(hit, ref[row : row + 1, :], 0.0), axis=1, keepdims=True)
            target[base : base + CELLS, :] = jnp.broadcast_to(col * scale, (CELLS, 128))
        return hit

    one_hot = jnp.where(par[2:3, :] == cell_sub, 1.0, 0.0).astype(BF16)
    pone[:, 0:CELLS] = one_hot
    pone[:, CELLS : 2 * CELLS] = one_hot
    load_force.wait()
    high, low = split(fsc[...])
    parts[0:CELLS, :] = high
    parts[CELLS : 2 * CELLS, :] = low
    fsc[...] = jnp.dot(pone[...], parts[...], preferred_element_type=F32) * lanes[3:4, :]
    for tile in every:
        mirror_layers(fsc[:, tile * 128 : tile * 128 + 128], tile, raw, 4, False)

    pl.semaphore_wait(barrier, DOMS - 1 + 3)

    def remote(src, dst, send, recv_sem, device):
        return pltpu.make_async_remote_copy(
            src_ref=src, dst_ref=dst, send_sem=send, recv_sem=recv_sem,
            device_id=device, device_id_type=MESH,
        )

    par_copies = [
        remote(par, parn.at[0], psend.at[0], precv.at[0], (grp, up)),
        remote(par, parn.at[1], psend.at[1], precv.at[1], (grp, down)),
    ]
    ghost_copies = [
        remote(
            raw.at[5 * LAYER : 8 * LAYER], raw.at[1 * LAYER : 4 * LAYER],
            gsend.at[0], grecv.at[0], (grp, up),
        ),
        remote(
            raw.at[4 * LAYER : 7 * LAYER], raw.at[8 * LAYER : 11 * LAYER],
            gsend.at[1], grecv.at[1], (grp, down),
        ),
        remote(
            raw.at[4 * LAYER : 5 * LAYER, 384:512], raw.at[0:LAYER, 384:512],
            gsend.at[2], grecv.at[2], (grp, up),
        ),
        remote(
            raw.at[7 * LAYER : 8 * LAYER, 384:512], raw.at[11 * LAYER : 12 * LAYER, 384:512],
            gsend.at[3], grecv.at[3], (grp, down),
        ),
    ]
    for copy in par_copies + ghost_copies:
        copy.start()

    coefficients(par, CELLS, 1.0)
    order_col = jnp.sum(
        jnp.where(cell_sub == cell_lane, par[2:3, :], 0.0), axis=1, keepdims=True
    )
    one_hot = jnp.where(order_col == cell_lane, 1.0, 0.0).astype(BF16)
    ptr[:, 0:CELLS] = one_hot
    ptr[:, CELLS : 2 * CELLS] = one_hot
    owner_row = owner_sc[...].astype(F32)
    owner_col = jnp.sum(
        jnp.where(cell_sub == cell_lane, owner_row, 0.0), axis=1, keepdims=True
    )
    same = (owner_col == owner_row) & (cell_sub < cell_lane)
    rank_row = jnp.sum(jnp.where(same, 1.0, 0.0), axis=0, keepdims=True)
    owner_int = owner_sc[...]
    place = owner_int >> 3
    piece_row = ((((owner_int >> 1) - place) & 3) << 1) + (owner_int & 1)
    first_row = (piece_row * 4 + place).astype(F32)
    dest_row = jnp.where(owner_row >= 0.0, first_row * 8.0 + rank_row, -1.0)
    slot_of = jnp.where(dest_row == cell_sub, 1.0, 0.0).astype(BF16)
    gpack[...] = jnp.dot(slot_of, one_hot, preferred_element_type=F32).astype(BF16)
    cell_id = lax.broadcasted_iota(jnp.int32, (CELLS, 128), 0)
    for k, width in enumerate((1, 8, 64)):
        parity = lax.rem(cell_id // width, 2).astype(F32).astype(BF16)
        classes[:, k * 128 : k * 128 + 128] = jnp.dot(
            gpack[...], parity, preferred_element_type=F32
        )

    for copy in par_copies:
        copy.wait()
    coefficients(parn.at[0], 0, has_down)
    coefficients(parn.at[1], 2 * CELLS, has_up)

    def partners(layer):
        parity = layer % 2 if isinstance(layer, int) else lax.rem(layer, 2)
        return {0: layer - 1 + 2 * parity, 3: layer + 1 - 2 * parity}

    def face_sum(ref, layer, tile):
        value = load(ref, layer, tile)
        other = load(ref, partners(layer)[tile], tile)
        return value + jnp.where(low_half, other, 0.0)

    def put_inverse(layer, tile, diag):
        store(inv, layer, tile, jnp.where(diag > 0.0, (2.0 / DELTA) / diag, 0.0))

    def diagonal(layer, tiles):
        coef_v = column(visc, layer)
        coef_m = column(mass, layer)
        for tile in tiles:
            diag = xy_sum(coef_v * table(1, tile) + coef_m * table(0, tile))
            if tile in (0, 3):
                store(tmp, layer, tile, diag)
            else:
                put_inverse(layer, tile, diag)

    diagonal(0, (3,))
    over(1, 11, lambda layer: diagonal(layer, every))
    diagonal(11, (3,))

    def diagonal_faces(layer):
        for tile in (0, 3):
            put_inverse(layer, tile, face_sum(tmp, layer, tile))

    over(1, 11, diagonal_faces)

    def put_first(layer, pair, forces):
        values = []
        for tile, force in zip((pair, 3 - pair), forces):
            value = force * load(inv, layer, tile) * (0.5 * DELTA)
            store(v0, layer, tile, value)
            values.append(value)
        store_lhs(layer, pair, *values)

    def assemble(layer, tiles, scale):
        sums = []
        for tile in tiles:
            force = load(raw, layer, tile)
            if scale is not None:
                force = force * scale
            force = xy_sum(force)
            if tile in (0, 3):
                store(tmp, layer, tile, force)
            else:
                sums.append(force)
        if sums:
            put_first(layer, 1, sums)

    over(4, 8, lambda layer: assemble(layer, every, None))
    for copy in load_mats:
        copy.wait()
    for copy in ghost_copies:
        copy.wait()
    assemble(0, (3,), has_down)
    over(1, 4, lambda layer: assemble(layer, every, has_down))
    over(8, 11, lambda layer: assemble(layer, every, has_up))
    assemble(11, (3,), has_up)

    def first_faces(layer):
        put_first(layer, 0, [face_sum(tmp, layer, tile) for tile in (0, 3)])

    over(1, 11, first_faces)

    def multiply(low, high, which, target, first=0):
        for part in range(2):
            target[:, first + part * 256 : first + part * 256 + 256] = jnp.dot(
                lhs[low * LAYER : high * LAYER, part * 768 : part * 768 + 768],
                weights[2 * which + part],
                preferred_element_type=F32,
            )

    def advance(step, layer, pair, totals):
        values = []
        for tile, total in zip((pair, 3 - pair), totals):
            value = total * load(inv, layer, tile)
            current = load(basis[step], layer, tile)
            if step == 0:
                value = 0.5 * value - (THETA / DELTA) * current
            else:
                value = value - (2.0 * THETA / DELTA) * current
                value = value - load(basis[step - 1], layer, tile)
            store(basis[step + 1], layer, tile, value)
            values.append(value)
        store_lhs(layer, pair, *values)

    def apply(step, layer, tiles, sums, going):
        coef_v = column(visc, layer)
        coef_m = column(mass, layer)
        for pair in (1, 0):
            if pair not in tiles and 3 - pair not in tiles:
                continue
            even = load(tmp, layer, pair)
            uneven = load(tmp, layer, 2 + pair)
            images = []
            for tile, product in ((pair, even + uneven), (3 - pair, even - uneven)):
                if tile not in tiles:
                    continue
                value = load(basis[step], layer, tile)
                weighted = coef_m * table(0, tile)
                image = coef_v * product + weighted * value
                if sums is not None:
                    diag = coef_v * table(1, tile) + weighted
                    sums = (
                        sums[0] + jnp.sum(value * image, axis=0),
                        sums[1] + jnp.sum(value * value * diag, axis=0),
                    )
                if going:
                    image = xy_sum(image)
                    if pair == 0:
                        store(tmp, layer, tile, image)
                    else:
                        images.append(image)
            if images:
                advance(step, layer, 1, images)
        return sums

    def faces(step, layer):
        advance(step, layer, 0, [face_sum(tmp, layer, tile) for tile in (0, 3)])

    blank_sums = (jnp.zeros((8, 128), F32), jnp.zeros((8, 128), F32))
    for step in range(ITERS):
        low, high = 1 + step, 11 - step
        going = step + 1 < ITERS
        multiply(low, high, 0, tmp.at[low * LAYER : high * LAYER])
        if going:
            inward = 0 if low % 2 else 3
            apply(step, low, (inward,), None, True)
            over(low + 1, 4, lambda layer: apply(step, layer, every, None, True))
        sums = lax.fori_loop(
            4, 8, lambda layer, carry: apply(step, layer, every, carry, going), blank_sums
        )
        if going:
            over(8, high - 1, lambda layer: apply(step, layer, every, None, True))
            apply(step, high - 1, (inward,), None, True)
        moments[step : step + 1, :] = jnp.sum(sums[0], axis=0, keepdims=True)
        moments[4 + step : 5 + step, :] = jnp.sum(sums[1], axis=0, keepdims=True)
        if going:
            over(low + 1, high - 1, lambda layer: faces(step, layer))

    red[0] = moments[...]
    for step in range(1, DOMS):
        remote(
            moments, red.at[step], rsend, rrecv, (grp, lax.rem(dom + step, DOMS))
        ).start()

    def end_face(ref, layer):
        total = load(ref, layer, 0) * table(2, 0)
        for tile in (1, 2, 3):
            total = total + load(ref, layer, tile) * table(2, tile)
        total = total + rotated(total, 64, 2)
        return -total if layer % 2 else total

    fsend[0] = end_face(v3, 7).reshape(LAYER, 128)
    fsend[1] = end_face(v3, 4).reshape(LAYER, 128)
    face_copies = [
        remote(fsend.at[0], frecv.at[0], f3send.at[0], f3recv.at[0], (grp, up)),
        remote(fsend.at[1], frecv.at[1], f3send.at[1], f3recv.at[1], (grp, down)),
    ]
    for copy in face_copies:
        copy.start()

    own_rows = slice(4 * LAYER, 8 * LAYER)
    for index in (3, 0, 1, 2):
        if index < 3:
            over(
                4,
                8,
                lambda layer: [
                    store_lhs(
                        layer,
                        pair,
                        load(basis[index], layer, pair),
                        load(basis[index], layer, 3 - pair),
                    )
                    for pair in (0, 1)
                ],
            )

        left = jnp.concatenate(
            [
                jnp.concatenate(
                    [
                        lhs[own_rows, start + part * 256 : start + part * 256 + 128]
                        for part in range(3)
                    ],
                    1,
                )
                for start in (0, 128, 768, 896)
            ],
            0,
        )
        both = jnp.dot(left, flat[0:384, 0:256], preferred_element_type=F32)
        for part in range(4):
            rows = slice(part * CELLS, part * CELLS + CELLS)
            grads[index, :, part * 128 : part * 128 + 128] = both[rows, 0:128]
            grads[index, :, NODES + part * 128 : NODES + part * 128 + 128] = both[rows, 128:256]
        multiply(4, 8, 1, grads.at[index], 2 * NODES)
        if index < 3:
            fghost[index, 0] = end_face(basis[index], 3).reshape(LAYER, 128)
            fghost[index, 1] = end_face(basis[index], 8).reshape(LAYER, 128)

    for copy in face_copies:
        copy.wait()
    for side in range(2):
        fghost[3, side] = frecv[side]

    whole = remote(red.at[1:DOMS], red.at[1:DOMS], rsend, rrecv, (grp, up))
    whole.wait_send()
    whole.wait_recv()

    total = jnp.sum(red[...], axis=0)
    total = jnp.broadcast_to(jnp.sum(total, axis=1, keepdims=True), (8, 128))
    moments[...] = total

    def scalar(row):
        return jnp.broadcast_to(moments[row : row + 1, :], (8, 128))

    alpha = [scalar(row) for row in range(4)]
    beta = [scalar(4 + row) for row in range(4)]
    gamma = [(alpha[k] - THETA * beta[k]) * (1.0 / DELTA) for k in range(4)]
    mu = [beta[0], gamma[0]]
    ahead = gamma[0]
    for k in range(1, 4):
        ahead = 2.0 * gamma[k] - ahead
        mu.append(2.0 * beta[k] - mu[0])
        mu.append(2.0 * ahead - mu[1])

    def inner(i, j):
        return 0.5 * (mu[i + j] + mu[abs(i - j)])

    gram = [
        [
            DELTA * 0.5 * (inner(i, j + 1) + inner(i, abs(j - 1))) + THETA * inner(i, j)
            for j in range(4)
        ]
        for i in range(4)
    ]
    right = [mu[k] for k in range(4)]
    pivots = []
    for k in range(4):
        original = DELTA * 0.5 * (inner(k, k + 1) + inner(k, abs(k - 1))) + THETA * inner(k, k)
        pivot = gram[k][k]
        good = pivot > 1e-7 * original
        inverse = jnp.where(good, 1.0 / jnp.where(good, pivot, 1.0), 0.0)
        pivots.append(inverse)
        for i in range(k + 1, 4):
            factor = gram[i][k] * inverse
            for j in range(k + 1, 4):
                gram[i][j] = gram[i][j] - factor * gram[k][j]
            right[i] = right[i] - factor * right[k]
    coef = [None] * 4
    for k in (3, 2, 1, 0):
        value = right[k]
        for j in range(k + 1, 4):
            value = value - gram[k][j] * coef[j]
        coef[k] = value * pivots[k]

    coef8 = [(value * (1.0 / NP)).reshape(1, 8, 128) for value in coef]
    coef16 = [0.5 * value for value in coef8]
    x_sign = jnp.where(odd, -1.0, 1.0).reshape(1, 8, 128)
    x_scale = jnp.where(take_up | take_down, 0.5, 1.0).reshape(1, 8, 128) * x_sign
    y_half = jnp.where((node_j == 7) | (node_j == 0), 0.5, 1.0).reshape(1, 8, 128)
    y_end = jnp.where(node_j == 7, 0.5, 1.0).reshape(1, 8, 128)
    y_scale = jnp.concatenate(
        [y_end, -y_half, y_half, -y_half, y_half, -y_half, y_half, -y_end], 0
    )

    def combined(layer, direction, pair):
        parts_of = []
        scale = coef8 if direction == 2 else coef16
        for start in (0, 256):
            start = start + direction * NODES + pair * 128
            value = None
            for k in range(4):
                term = scale[k] * grads[k, rows_of(layer), start : start + 128].reshape(8, 8, 128)
                value = term if value is None else value + term
            parts_of.append(value)
        even, uneven = parts_of
        if direction == 2:
            return even + uneven, uneven - even
        return even + uneven, even - uneven

    def put_grad(layer, direction, tile, value):
        start = direction * NODES + tile * 128
        gcells[rows_of(layer), start : start + 128] = value.reshape(LAYER, 128).astype(BF16)

    def flat_grads(layer):
        z_sign = (1 - 2 * lax.rem(layer, 2)).astype(F32)
        for pair in (0, 1):
            for tile, value in zip((pair, 3 - pair), combined(layer, 0, pair)):
                put_grad(layer, 0, tile, x_scale * (value - x_others(value)))
            for tile, value in zip((pair, 3 - pair), combined(layer, 1, pair)):
                put_grad(layer, 1, tile, y_scale * (value - y_others(value)))
        for tile, value in zip((1, 2), combined(layer, 2, 1)):
            put_grad(layer, 2, tile, z_sign * value)
        for tile, value in zip((0, 3), combined(layer, 2, 0)):
            store(xstd, layer, tile, z_sign * value)

    over(0, 4, flat_grads)

    def mean_face(layer, tile, other, there):
        value = load(xstd, layer, tile)
        put_grad(layer, 2, tile, value + jnp.where(low_half, there * (other - value), 0.0))

    for layer in range(4):
        mean_face(layer, 3, load(xstd, layer ^ 1, 3), 0.5)
        if layer in (1, 2):
            mean_face(layer, 0, load(xstd, 3 - layer, 0), 0.5)
        else:
            side = 0 if layer == 0 else 1
            other = None
            for k in range(4):
                term = coef8[k] * fghost[k, side].reshape(8, 8, 128)
                other = term if other is None else other + term
            mean_face(layer, 0, other, 0.5 * (has_up if side else has_down))

    own_first = grp * SHARE

    def pack(part, carry):
        cols = pl.ds(pl.multiple_of(part * 512, 512), 512)
        packed[:, cols] = jnp.dot(
            gpack[...], gcells[:, cols], preferred_element_type=F32
        ).astype(BF16)
        return carry

    lax.fori_loop(0, 3, pack, 0)

    def chunk_rows(chunk, base=0):
        return pl.ds(pl.multiple_of(base + chunk * CHUNK, CHUNK), CHUNK)

    def turn(step):
        return lax.rem(dom + step, PIECES)

    def piece_copy(step, target, slot):
        chunk = turn(step)
        return remote(
            packed.at[chunk_rows(chunk, target * SHARE)], recv.at[comp, chunk_rows(chunk)],
            asend.at[slot, step], arecv.at[comp, chunk], (target, dom),
        )

    def each_send(action):
        @pl.when(grp < 2)
        def _():
            for step in range(PIECES):
                for hop in (2, 1, 3):
                    action(piece_copy(step, lax.rem(grp + hop, 4), hop - 1))

        @pl.when(grp >= 2)
        def _():
            for step in range(PIECES):
                action(piece_copy(step, 3 - grp, 0))

    each_send(lambda copy: copy.start())
    recv[comp] = packed[pl.ds(pl.multiple_of(own_first, SHARE), SHARE), :]

    wide8 = [value.reshape(1, 8, 128) for value in coef]

    @pl.when(grp < 3)
    def _():
        def solve_layer(layer):
            for tile in every:
                value = wide8[0] * load(v0, layer, tile)
                for k in range(1, 4):
                    value = value + wide8[k] * load(basis[k], layer, tile)
                store(xs, layer - 4, tile, value)

        over(4, 8, solve_layer)
        for tile in every:
            mirror_layers(xs[:, tile * 128 : tile * 128 + 128], tile, xstd, 0, True)
        high, low = split(xstd[...])
        parts[0:CELLS, :] = high
        parts[CELLS : 2 * CELLS, :] = low
        out[...] = jnp.dot(ptr[...], parts[...], preferred_element_type=F32)

    def lambda_rows(block, carry):
        rows = pl.ds(pl.multiple_of(block * 16, 16), 16)
        for part in range(2):
            jac = [
                [
                    recv[c, rows, d * NODES + part * 256 : d * NODES + part * 256 + 256].astype(F32)
                    for d in range(3)
                ]
                for c in range(3)
            ]
            lam[rows, part * 256 : part * 256 + 256] = lambda_two(jac)
        return carry

    def natural_order(chunk):
        rows = chunk_rows(chunk)
        slots = pl.ds(pl.multiple_of(own_first + chunk * CHUNK, CHUNK), CHUNK)
        odd_x, odd_y, odd_z = [
            classes[slots, k * 128 : k * 128 + 128] > 0.5 for k in range(3)
        ]
        values = [lam[rows, tile * 128 : tile * 128 + 128] for tile in every]
        flipped = reversals(jnp.concatenate(values, 0))
        turned = []
        for tile in every:
            rev_x, rev_y, rev_xy = [
                part[tile * CHUNK : tile * CHUNK + CHUNK] for part in flipped
            ]
            turned.append(
                jnp.where(
                    odd_x,
                    jnp.where(odd_y, rev_xy, rev_x),
                    jnp.where(odd_y, rev_y, values[tile]),
                )
            )
        for tile in every:
            value = jnp.where(odd_z, turned[3 - tile], turned[tile])
            if tile >= 2:
                value = rotated(value, 64, 1)
            lam[rows, tile * 128 : tile * 128 + 128] = value

    here = pl.ds(pl.multiple_of(dom * 8, 8), 8)

    def each_owner(chunk, action, local):
        piece = lax.div(own_first, CHUNK) + chunk
        four = lax.div(piece, 2)
        for part in range(2):
            place = lax.rem(piece, 2) * 2 + part
            owner = place * 8 + lax.rem(place + lax.div(four, 2), 4) * 2 + lax.rem(four, 2)
            rows = pl.ds(pl.multiple_of(chunk * CHUNK + part * 8, 8), 8)
            own = (grp == 3) & (owner == dom)

            @pl.when(jnp.logical_not(own))
            def _():
                action(
                    remote(
                        lam.at[rows], lamrecv.at[here], osend.at[chunk * 2 + part], orecv,
                        (3, owner),
                    )
                )

            if local:

                @pl.when(own)
                def _():
                    lamrecv[here, :] = lam[rows, :]

    def analyse(chunk):
        for step in (1, 2):
            other = lax.rem(comp + step, 3)
            piece = recv.at[other, chunk_rows(chunk)]
            remote(
                piece, piece, asend.at[0, 0], arecv.at[other, chunk], (lax.rem(grp + 1, 4), dom)
            ).wait_recv()
        lambda_rows(chunk, 0)
        natural_order(chunk)
        each_owner(chunk, lambda copy: copy.start(), True)

    over(0, PIECES, lambda step: analyse(turn(step)))
    for step in range(PIECES):
        each_owner(turn(step), lambda copy: copy.wait_send(), False)
    each_send(lambda copy: copy.wait_send())

    def wait_rows(count):
        piece = lamrecv.at[0 : 8 * count]
        remote(piece, piece, osend.at[0], orecv, (lax.rem(grp + 1, 4), dom)).wait_recv()

    to_itself = lax.rem(lax.div(lax.rem(dom, 8), 2) - lax.div(dom, 8) + 4, 4) == 3

    @pl.when((grp == 3) & to_itself)
    def _():
        wait_rows(31)

    @pl.when((grp == 3) & jnp.logical_not(to_itself))
    def _():
        wait_rows(32)

    @pl.when(grp == 3)
    def _():
        out[...] = lamrecv[...]


def lambda_two(jac):
    strain = [[0.5 * (jac[a][b] + jac[b][a]) for b in range(3)] for a in range(3)]
    spin = [[0.5 * (jac[a][b] - jac[b][a]) for b in range(3)] for a in range(3)]
    m = [[None] * 3 for _ in range(3)]
    for a in range(3):
        for b in range(a, 3):
            value = strain[a][0] * strain[0][b] + spin[a][0] * spin[0][b]
            for k in (1, 2):
                value = value + strain[a][k] * strain[k][b] + spin[a][k] * spin[k][b]
            m[a][b] = value
            m[b][a] = value
    for sweep in range(SWEEPS):
        for p, q, r in ((0, 1, 2), (0, 2, 1), (1, 2, 0)):
            last = sweep == SWEEPS - 1
            twice = 2.0 * m[p][q]
            gap = m[p][p] - m[q][q]
            square = twice * twice + gap * gap
            inverse = lax.rsqrt(jnp.maximum(square, 1e-36))
            length = square * inverse
            mean = 0.5 * (m[p][p] + m[q][q])
            m[p][p] = mean + 0.5 * length
            m[q][q] = mean - 0.5 * length
            if last and (p, q) == (1, 2):
                continue
            none = square < 1e-36
            cosine2 = jnp.where(none, 1.0, jnp.abs(gap) * inverse)
            sine2 = jnp.where(none, 0.0, twice * inverse)
            larger = 0.5 + 0.5 * cosine2
            root = lax.rsqrt(larger)
            big = larger * root
            small = 0.5 * sine2 * root
            flip = gap < 0.0
            sine_big = jnp.where(sine2 < 0.0, -big, big)
            cosine = jnp.where(flip, jnp.abs(small), big)
            sine = jnp.where(flip, sine_big, small)
            side_p = m[r][p]
            side_q = m[r][q]
            m[r][p] = m[p][r] = cosine * side_p + sine * side_q
            m[r][q] = m[q][r] = cosine * side_q - sine * side_p
            m[p][q] = m[q][p] = jnp.zeros_like(side_p)
    diagonal = [m[0][0], m[1][1], m[2][2]]
    largest = jnp.maximum(jnp.maximum(diagonal[0], diagonal[1]), diagonal[2])
    smallest = jnp.minimum(jnp.minimum(diagonal[0], diagonal[1]), diagonal[2])
    return diagonal[0] + diagonal[1] + diagonal[2] - largest - smallest


def per_device(forcing, viscosity, mass_coef, element_order, owner):
    mats, flat, lanes = tables()
    vmem = pl.BlockSpec(memory_space=pltpu.VMEM)
    hbm = pl.BlockSpec(memory_space=pltpu.HBM)
    wide = (12 * LAYER, NODES)
    own = (CELLS, NODES)
    dma = pltpu.SemaphoreType.DMA
    result = pl.pallas_call(
        kernel,
        out_shape=pltpu.VMEM(own, F32),
        in_specs=[hbm] * 8,
        out_specs=vmem,
        scratch_shapes=[
            pltpu.VMEM(own, F32),
            pltpu.VMEM((8, NODES), F32),
            pltpu.VMEM((640, 384), BF16),
            pltpu.VMEM((1, CELLS), jnp.int32),
            pltpu.VMEM((1, CELLS), jnp.int32),
            pltpu.VMEM((4, 768, 256), BF16),
            pltpu.VMEM((8, CELLS), F32),
            pltpu.VMEM((2, 8, CELLS), F32),
            pltpu.VMEM((CELLS, 2 * CELLS), BF16),
            pltpu.VMEM((CELLS, 2 * CELLS), BF16),
            pltpu.VMEM((2 * CELLS, NODES), BF16),
            pltpu.VMEM((12 * LAYER, 128), F32),
            pltpu.VMEM((12 * LAYER, 128), F32),
            pltpu.VMEM(wide, F32),
            pltpu.VMEM(wide, F32),
            pltpu.VMEM(wide, F32),
            pltpu.VMEM((12 * LAYER, 3 * NODES), BF16),
            pltpu.VMEM(wide, F32),
            pltpu.VMEM(wide, F32),
            pltpu.VMEM(wide, F32),
            pltpu.VMEM(wide, F32),
            pltpu.VMEM(own, F32),
            pltpu.VMEM(own, F32),
            pltpu.VMEM((4, CELLS, 3 * NODES), F32),
            pltpu.VMEM((CELLS, CELLS), BF16),
            pltpu.VMEM((CELLS, 384), F32),
            pltpu.VMEM((CELLS, 3 * NODES), BF16),
            pltpu.VMEM((2, LAYER, 128), F32),
            pltpu.VMEM((2, LAYER, 128), F32),
            pltpu.VMEM((4, 2, LAYER, 128), F32),
            pltpu.VMEM((8, 128), F32),
            pltpu.VMEM((DOMS, 8, 128), F32),
            pltpu.VMEM((CELLS, 3 * NODES), BF16),
            pltpu.VMEM((3, SHARE, 3 * NODES), BF16),
            pltpu.VMEM((SHARE, NODES), F32),
            pltpu.VMEM(own, F32),
            dma((6,)), dma((12,)), dma, dma((2,)), dma((2,)), dma((4,)), dma((4,)), dma((2,)),
            dma((2,)), dma, dma, dma((3, PIECES)), dma((3, PIECES)), dma((8,)), dma,
        ],
        compiler_params=pltpu.CompilerParams(
            collective_id=0, has_side_effects=True, vmem_limit_bytes=60 * 1024 * 1024
        ),
        name="solve_and_analyse",
    )(
        forcing, viscosity[None], mass_coef[None], element_order, owner,
        jnp.asarray(lanes), jnp.asarray(flat), jnp.asarray(mats),
    )
    return result[None]


def solution(mesh):
    in_specs = (P(None, "dom", None), P("dom"), P("dom"), P("dom", None), P("dom", None))
    out_specs = P("grp", "dom", None)
    return jax.shard_map(
        per_device, mesh=mesh, in_specs=in_specs, out_specs=out_specs, check_vma=False
    )
```

```python
import functools

import jax
import jax.numpy as jnp
import ml_dtypes
import numpy as np
from jax import lax
from jax.experimental import pallas as pl
from jax.experimental.pallas import tpu as pltpu
from jax.sharding import PartitionSpec as P

NP = 8
ITERS = 4
SWEEPS = 4
LAYER = 64
CELLS = 256
NODES = 512
DOMS = 32
CHUNK = 16
PIECES = 4
SHARE = 64
BASIS_LOW = 0.3
BASIS_HIGH = 2.0
THETA = 0.5 * (BASIS_LOW + BASIS_HIGH)
DELTA = 0.5 * (BASIS_HIGH - BASIS_LOW)
MESH = pl.DeviceIdType.MESH
F32 = jnp.float32
BF16 = jnp.bfloat16


def legendre_values(points, node_count):
    legendre = np.zeros((points.shape[0], node_count))
    legendre[:, 0] = 1.0
    legendre[:, 1] = points
    for poly_order in range(2, node_count):
        legendre[:, poly_order] = (
            (2 * poly_order - 1) * points * legendre[:, poly_order - 1]
            - (poly_order - 1) * legendre[:, poly_order - 2]
        ) / poly_order
    return legendre


def lobatto_table(node_count):
    degree = node_count - 1
    points = np.cos(np.pi * np.arange(node_count) / degree)
    for attempt in range(60):
        legendre = legendre_values(points, node_count)
        points = points - (points * legendre[:, degree] - legendre[:, degree - 1]) / (
            node_count * legendre[:, degree]
        )
    points = points[::-1].copy()
    end_values = legendre_values(points, node_count)[:, degree]
    weights = 2.0 / (degree * node_count * end_values * end_values)
    spacing = points[:, None] - points[None, :] + np.eye(node_count)
    diff_matrix = end_values[:, None] / end_values[None, :] / spacing
    diff_matrix = diff_matrix * (1.0 - np.eye(node_count))
    diff_matrix[0, 0] = -degree * node_count / 4.0
    diff_matrix[-1, -1] = degree * node_count / 4.0
    return (weights, diff_matrix)


def split_rows(matrix):
    high = matrix.astype(np.float32).astype(ml_dtypes.bfloat16)
    low = (matrix - high.astype(np.float64)).astype(np.float32).astype(ml_dtypes.bfloat16)
    return high, low


def tables():
    weights, diff = lobatto_table(NP)
    eye = np.eye(NP)
    cube = (
        weights[:, None, None] * weights[None, :, None] * weights[None, None, :]
    ).reshape(-1)
    directional = [
        np.kron(eye, np.kron(eye, diff)),
        np.kron(eye, np.kron(diff, eye)),
        np.kron(diff, np.kron(eye, eye)),
    ]
    stiff = np.zeros((NODES, NODES))
    for matrix in directional:
        stiff = stiff + matrix.T @ (cube[:, None] * matrix)
    flip = np.arange(NODES).reshape(NP, LAYER)[::-1][: NP // 2].reshape(-1)
    mats = []
    for matrix in (stiff, directional[2]):
        near, far = matrix[:256, :256], matrix[:256, flip]
        for block in (0.5 * (near + far), 0.5 * (near - far)):
            mats.append(np.stack(split_rows(block.T)))
    mats = np.stack(mats)
    flat = np.concatenate([directional[0].T[:128, :128], directional[1].T[:128, :128]], 1)
    high, low = split_rows(flat)
    flat = np.concatenate([high, high, low], 0)
    lanes = np.zeros((8, NODES), np.float32)
    lanes[0] = cube
    lanes[1] = np.diag(stiff)
    lanes[2] = np.repeat(diff[0], LAYER)
    order = [0, 1, 2, 3, 5, 4, 7, 6]
    lanes = lanes.reshape(8, NP, LAYER)[:, order].reshape(8, NODES)
    natural = cube.reshape(NP, LAYER).astype(np.float32).reshape(-1)
    lanes[3] = natural
    back = eye[::-1]
    half = np.eye(2)
    mirror = np.concatenate(
        [
            np.kron(half, np.kron(eye, back)),
            np.kron(half, np.kron(back, eye)),
            np.kron(half, np.kron(back, back)),
        ],
        1,
    ).astype(ml_dtypes.bfloat16)
    wide = np.concatenate([flat, np.zeros((384, 128), flat.dtype)], 1)
    return mats, np.concatenate([wide, mirror, mirror], 0), lanes


def rotated(value, shift, axis):
    return pltpu.roll(value, shift % value.shape[axis], axis)


def kernel(
    forcing, visc_in, mass_in, order_in, owner_in, lanes_in, flat_in, mats,
    out,
    fsc, lanes, flat, order_sc, owner_sc, weights, par, parn, pone, ptr, parts, visc, mass, raw, tmp,
    inv, lhs0, lhs1, lhs2, lhs3, v0, v1, v2, v3, xs, xstd, grads, gpack, classes, gcells, fsend, frecv, fghost, moments,
    red, packed, recv, lam, lamrecv,
    ssem, wsem, fsem, psend, precv, gsend, grecv, f3send, f3recv, rsend, rrecv, asend, arecv,
    osend, orecv,
):
    grp = lax.axis_index("grp")
    dom = lax.axis_index("dom")
    comp = jnp.minimum(grp, 2)
    up = lax.rem(dom + 1, DOMS)
    down = lax.rem(dom + DOMS - 1, DOMS)
    barrier = pltpu.get_barrier_semaphore()
    basis = (v0, v1, v2, v3)
    lefts = (lhs0, lhs1, lhs2, lhs3)
    every = (0, 1, 2, 3)

    for step in range(1, DOMS):
        pl.semaphore_signal(
            barrier, inc=1, device_id=(grp, lax.rem(dom + step, DOMS)), device_id_type=MESH
        )
    for step in range(1, 4):
        pl.semaphore_signal(
            barrier, inc=1, device_id=(lax.rem(grp + step, 4), dom), device_id_type=MESH
        )

    load_small = [
        pltpu.make_async_copy(source, target, ssem.at[k])
        for k, (source, target) in enumerate(
            (
                (visc_in, par.at[0:1]),
                (mass_in, par.at[1:2]),
                (order_in, order_sc),
                (owner_in, owner_sc),
                (lanes_in, lanes),
                (flat_in, flat),
            )
        )
    ]
    for copy in load_small:
        copy.start()
    load_force = pltpu.make_async_copy(forcing.at[comp], fsc, fsem)
    load_force.start()
    load_mats = []
    for which in range(4):
        for part, source in enumerate((0, 0, 1)):
            copy = pltpu.make_async_copy(
                mats.at[which, source],
                weights.at[which, part * 256 : part * 256 + 256],
                wsem.at[3 * which + part],
            )
            copy.start()
            load_mats.append(copy)

    lane = lax.broadcasted_iota(jnp.int32, (8, 128), 1)
    sub = lax.broadcasted_iota(jnp.int32, (8, 128), 0)
    node_i = lax.rem(lane, 8)
    node_j = lax.rem(lane // 8, 8)
    odd = lax.rem(sub, 2) == 1
    first_i = node_i == 0
    last_i = node_i == 7
    take_up = ((last_i & jnp.logical_not(odd)) | (first_i & odd & (sub < 7)))
    take_down = ((last_i & odd) | (first_i & jnp.logical_not(odd) & (sub > 0)))
    has_up = jnp.where(dom < DOMS - 1, 1.0, 0.0).astype(F32)
    has_down = jnp.where(dom > 0, 1.0, 0.0).astype(F32)

    def wide(mask):
        return jnp.broadcast_to(mask[None], (8, 8, 128))

    x_up = wide(take_up)
    x_down = wide(take_down)
    x_odd = wide(odd)
    y_last = wide(node_j == 7)
    y_first = wide(node_j == 0)
    low_half = wide(lane < LAYER)

    def x_others(a):
        above = rotated(a, -1, 1)
        below = rotated(a, 1, 1)
        return jnp.where(x_up, above, jnp.where(x_down, below, 0.0))

    def y_others(a):
        blank = jnp.zeros((1, 8, 128), F32)
        last = jnp.concatenate([a[k ^ 1 : (k ^ 1) + 1] for k in range(8)], 0)
        first = jnp.concatenate(
            [blank] + [a[k : k + 1] for k in (2, 1, 4, 3, 6, 5)] + [blank], 0
        )
        return jnp.where(y_last, last, jnp.where(y_first, first, 0.0))

    def xy_sum(a):
        a = a + x_others(a)
        return a + y_others(a)

    def rows_of(layer):
        if isinstance(layer, int):
            return slice(layer * LAYER, layer * LAYER + LAYER)
        return pl.ds(pl.multiple_of(layer * LAYER, LAYER), LAYER)

    def load(ref, layer, tile):
        return ref[rows_of(layer), tile * 128 : tile * 128 + 128].reshape(8, 8, 128)

    def store(ref, layer, tile, value):
        ref[rows_of(layer), tile * 128 : tile * 128 + 128] = value.reshape(LAYER, 128)

    def column(ref, layer):
        return ref[rows_of(layer), :].reshape(8, 8, 128)

    def table(row, tile):
        return lanes[row : row + 1, tile * 128 : tile * 128 + 128].reshape(1, 1, 128)

    def split(value):
        high = value.astype(BF16)
        return high, (value - high.astype(F32)).astype(BF16)

    def store_lhs(lhs, layer, pair, first, second):
        for start, value in ((0, first + second), (768, first - second)):
            start = start + pair * 128
            high, low = split(value.reshape(LAYER, 128))
            lhs[rows_of(layer), start : start + 128] = high
            lhs[rows_of(layer), start + 256 : start + 384] = low
            lhs[rows_of(layer), start + 512 : start + 640] = high

    def reversals(value):
        total = jnp.dot(
            jnp.concatenate(split(value), 1), flat[384:640, :], preferred_element_type=F32
        )
        return total[:, 0:128], total[:, 128:256], total[:, 256:384]

    def mirror_layers(value, tile, target, base, back):
        flipped = reversals(value)
        for layer in range(4):
            rows = slice(layer * LAYER, layer * LAYER + LAYER)
            plain, rev_x, rev_y, rev_xy = [
                part[rows].reshape(8, 8, 128) for part in (value,) + flipped
            ]
            even_y = jnp.where(x_odd, rev_x, plain)
            odd_y = jnp.where(x_odd, rev_xy, rev_y)
            mixed = jnp.concatenate(
                [(odd_y if k % 2 else even_y)[k : k + 1] for k in range(8)], 0
            )
            place = 3 - tile if layer % 2 else tile
            if (place if back else tile) >= 2:
                mixed = rotated(mixed, 64, 2)
            store(target, base + layer, place, mixed)

    def over(low, high, body):
        lax.fori_loop(low, high, lambda layer, carry: (body(layer), carry)[1], 0)

    cell_sub = lax.broadcasted_iota(jnp.int32, (CELLS, CELLS), 0).astype(F32)
    cell_lane = lax.broadcasted_iota(jnp.int32, (CELLS, CELLS), 1).astype(F32)
    for copy in load_small:
        copy.wait()
    par[2:3, :] = order_sc[...].astype(F32)
    par[3:8, :] = jnp.zeros((5, CELLS), F32)

    def coefficients(ref, base, scale):
        hit = ref[2:3, :] == cell_sub
        for row, target in ((0, visc), (1, mass)):
            col = jnp.sum(jnp.where(hit, ref[row : row + 1, :], 0.0), axis=1, keepdims=True)
            target[base : base + CELLS, :] = jnp.broadcast_to(col * scale, (CELLS, 128))
        return hit

    one_hot = jnp.where(par[2:3, :] == cell_sub, 1.0, 0.0).astype(BF16)
    pone[:, 0:CELLS] = one_hot
    pone[:, CELLS : 2 * CELLS] = one_hot
    load_force.wait()
    high, low = split(fsc[...])
    parts[0:CELLS, :] = high
    parts[CELLS : 2 * CELLS, :] = low
    fsc[...] = jnp.dot(pone[...], parts[...], preferred_element_type=F32) * lanes[3:4, :]
    for tile in every:
        mirror_layers(fsc[:, tile * 128 : tile * 128 + 128], tile, raw, 4, False)

    pl.semaphore_wait(barrier, DOMS - 1 + 3)

    def remote(src, dst, send, recv_sem, device):
        return pltpu.make_async_remote_copy(
            src_ref=src, dst_ref=dst, send_sem=send, recv_sem=recv_sem,
            device_id=device, device_id_type=MESH,
        )

    par_copies = [
        remote(par, parn.at[0], psend.at[0], precv.at[0], (grp, up)),
        remote(par, parn.at[1], psend.at[1], precv.at[1], (grp, down)),
    ]
    def ghost(source, layers, first, last, target, slot, device):
        return remote(
            raw.at[source * LAYER : (source + layers) * LAYER, first:last],
            raw.at[target * LAYER : (target + layers) * LAYER, first:last],
            gsend.at[slot], grecv.at[slot], (grp, device),
        )

    near_copies = [
        ghost(7, 1, 0, 512, 3, 0, up),
        ghost(4, 1, 0, 512, 8, 1, down),
        ghost(6, 1, 384, 512, 2, 2, up),
        ghost(5, 1, 384, 512, 9, 3, down),
    ]
    far_copies = [
        ghost(6, 1, 0, 384, 2, 4, up),
        ghost(5, 1, 0, 384, 9, 5, down),
        ghost(5, 1, 0, 512, 1, 6, up),
        ghost(6, 1, 0, 512, 10, 7, down),
        ghost(4, 1, 384, 512, 0, 8, up),
        ghost(7, 1, 384, 512, 11, 9, down),
    ]
    for copy in par_copies + near_copies + far_copies:
        copy.start()

    coefficients(par, CELLS, 1.0)
    order_col = jnp.sum(
        jnp.where(cell_sub == cell_lane, par[2:3, :], 0.0), axis=1, keepdims=True
    )
    one_hot = jnp.where(order_col == cell_lane, 1.0, 0.0).astype(BF16)
    ptr[:, 0:CELLS] = one_hot
    ptr[:, CELLS : 2 * CELLS] = one_hot
    owner_row = owner_sc[...].astype(F32)
    owner_col = jnp.sum(
        jnp.where(cell_sub == cell_lane, owner_row, 0.0), axis=1, keepdims=True
    )
    same = (owner_col == owner_row) & (cell_sub < cell_lane)
    rank_row = jnp.sum(jnp.where(same, 1.0, 0.0), axis=0, keepdims=True)
    owner_int = owner_sc[...]
    place = owner_int >> 3
    piece_row = ((((owner_int >> 1) - place) & 3) << 1) + (owner_int & 1)
    first_row = (piece_row * 4 + place).astype(F32)
    dest_row = jnp.where(owner_row >= 0.0, first_row * 8.0 + rank_row, -1.0)
    slot_of = jnp.where(dest_row == cell_sub, 1.0, 0.0).astype(BF16)
    gpack[...] = jnp.dot(slot_of, one_hot, preferred_element_type=F32).astype(BF16)
    cell_id = lax.broadcasted_iota(jnp.int32, (CELLS, 128), 0)
    for k, width in enumerate((1, 8, 64)):
        parity = lax.rem(cell_id // width, 2).astype(F32).astype(BF16)
        classes[:, k * 128 : k * 128 + 128] = jnp.dot(
            gpack[...], parity, preferred_element_type=F32
        )

    for copy in par_copies:
        copy.wait()
    coefficients(parn.at[0], 0, has_down)
    coefficients(parn.at[1], 2 * CELLS, has_up)

    def partners(layer):
        parity = layer % 2 if isinstance(layer, int) else lax.rem(layer, 2)
        return {0: layer - 1 + 2 * parity, 3: layer + 1 - 2 * parity}

    def face_sum(ref, layer, tile):
        value = load(ref, layer, tile)
        other = load(ref, partners(layer)[tile], tile)
        return value + jnp.where(low_half, other, 0.0)

    def put_inverse(layer, tile, diag):
        store(inv, layer, tile, jnp.where(diag > 0.0, (2.0 / DELTA) / diag, 0.0))

    def diagonal(layer, tiles):
        coef_v = column(visc, layer)
        coef_m = column(mass, layer)
        for tile in tiles:
            diag = xy_sum(coef_v * table(1, tile) + coef_m * table(0, tile))
            if tile in (0, 3):
                store(tmp, layer, tile, diag)
            else:
                put_inverse(layer, tile, diag)

    diagonal(0, (3,))
    over(1, 11, lambda layer: diagonal(layer, every))
    diagonal(11, (3,))

    def diagonal_faces(layer):
        for tile in (0, 3):
            put_inverse(layer, tile, face_sum(tmp, layer, tile))

    over(1, 11, diagonal_faces)

    def first_value(layer, tile, force):
        value = force * load(inv, layer, tile) * (0.5 * DELTA)
        store(v0, layer, tile, value)
        return value

    def put_first(layer, pair, forces):
        values = [
            first_value(layer, tile, force) for tile, force in zip((pair, 3 - pair), forces)
        ]
        store_lhs(lhs0, layer, pair, *values)

    def assemble(layer, tiles, scale):
        sums = []
        for tile in tiles:
            force = load(raw, layer, tile)
            if scale is not None:
                force = force * scale
            force = xy_sum(force)
            if tile in (0, 3):
                store(tmp, layer, tile, force)
            else:
                sums.append(force)
        if sums:
            put_first(layer, 1, sums)

    over(4, 8, lambda layer: assemble(layer, every, None))
    for copy in load_mats:
        copy.wait()
    def multiply(lhs, low, high, which, target, first=0):
        for part in range(2):
            target[:, first + part * 256 : first + part * 256 + 256] = jnp.dot(
                lhs[low * LAYER : high * LAYER, part * 768 : part * 768 + 768],
                weights[2 * which + part],
                preferred_element_type=F32,
            )

    def advance(step, layer, pair, totals):
        values = []
        for tile, total in zip((pair, 3 - pair), totals):
            value = total * load(inv, layer, tile)
            current = load(basis[step], layer, tile)
            if step == 0:
                value = 0.5 * value - (THETA / DELTA) * current
            else:
                value = value - (2.0 * THETA / DELTA) * current
                value = value - load(basis[step - 1], layer, tile)
            store(basis[step + 1], layer, tile, value)
            values.append(value)
        store_lhs(lefts[step + 1], layer, pair, *values)

    def apply(step, layer, tiles, sums, going):
        coef_v = column(visc, layer)
        coef_m = column(mass, layer)
        for pair in (1, 0):
            if pair not in tiles and 3 - pair not in tiles:
                continue
            even = load(tmp, layer, pair)
            uneven = load(tmp, layer, 2 + pair)
            images = []
            for tile, product in ((pair, even + uneven), (3 - pair, even - uneven)):
                if tile not in tiles:
                    continue
                value = load(basis[step], layer, tile)
                weighted = coef_m * table(0, tile)
                image = coef_v * product + weighted * value
                if sums is not None:
                    diag = coef_v * table(1, tile) + weighted
                    sums = (
                        sums[0] + jnp.sum(value * image, axis=0),
                        sums[1] + jnp.sum(value * value * diag, axis=0),
                    )
                if going:
                    image = xy_sum(image)
                    if pair == 0:
                        store(tmp, layer, tile, image)
                    else:
                        images.append(image)
            if images:
                advance(step, layer, 1, images)
        return sums

    def faces(step, layer):
        advance(step, layer, 0, [face_sum(tmp, layer, tile) for tile in (0, 3)])

    blank_sums = (jnp.zeros((8, 128), F32), jnp.zeros((8, 128), F32))

    def own_apply(step, going):
        sums = lax.fori_loop(
            4, 8, lambda layer, carry: apply(step, layer, every, carry, going), blank_sums
        )
        moments[step : step + 1, :] = jnp.sum(sums[0], axis=0, keepdims=True)
        moments[4 + step : 5 + step, :] = jnp.sum(sums[1], axis=0, keepdims=True)

    def first_faces(layer):
        put_first(layer, 0, [face_sum(tmp, layer, tile) for tile in (0, 3)])

    for copy in near_copies:
        copy.wait()
    assemble(2, (3,), has_down)
    assemble(3, every, has_down)
    assemble(8, every, has_up)
    assemble(9, (3,), has_up)
    over(3, 9, first_faces)
    for layer in (2, 9):
        first_value(layer, 3, face_sum(tmp, layer, 3))
    multiply(lhs0, 3, 9, 0, tmp.at[3 * LAYER : 9 * LAYER])
    own_apply(0, True)
    for layer in (3, 8):
        apply(0, layer, every, None, True)

    for copy in far_copies:
        copy.wait()
    assemble(0, (3,), has_down)
    assemble(1, every, has_down)
    assemble(2, (0, 1, 2), has_down)
    assemble(9, (0, 1, 2), has_up)
    assemble(10, every, has_up)
    assemble(11, (3,), has_up)
    for layer in (1, 10):
        first_faces(layer)
    for layer in (2, 9):
        value = first_value(layer, 0, face_sum(tmp, layer, 0))
        store_lhs(lhs0, layer, 0, value, load(v0, layer, 3))
    far_rows = (slice(1 * LAYER, 3 * LAYER), slice(9 * LAYER, 11 * LAYER))
    for part in range(2):
        product = jnp.dot(
            jnp.concatenate(
                [lhs0[rows, part * 768 : part * 768 + 768] for rows in far_rows], 0
            ),
            weights[part],
            preferred_element_type=F32,
        )
        for side, rows in enumerate(far_rows):
            tmp[rows, part * 256 : part * 256 + 256] = product[
                side * 2 * LAYER : (side + 1) * 2 * LAYER
            ]
    apply(0, 1, (0,), None, True)
    apply(0, 2, every, None, True)
    apply(0, 9, every, None, True)
    apply(0, 10, (0,), None, True)
    over(2, 10, lambda layer: faces(0, layer))

    for step in range(1, ITERS):
        low, high = 1 + step, 11 - step
        going = step + 1 < ITERS
        multiply(lefts[step], low, high, 0, tmp.at[low * LAYER : high * LAYER])
        own_apply(step, going)
        if going:
            inward = 0 if low % 2 else 3
            apply(step, low, (inward,), None, True)
            over(low + 1, 4, lambda layer: apply(step, layer, every, None, True))
            over(8, high - 1, lambda layer: apply(step, layer, every, None, True))
            apply(step, high - 1, (inward,), None, True)
            over(low + 1, high - 1, lambda layer: faces(step, layer))

    red[0] = moments[...]
    for step in range(1, DOMS):
        remote(
            moments, red.at[step], rsend, rrecv, (grp, lax.rem(dom + step, DOMS))
        ).start()

    def end_face(ref, layer):
        total = load(ref, layer, 0) * table(2, 0)
        for tile in (1, 2, 3):
            total = total + load(ref, layer, tile) * table(2, tile)
        total = total + rotated(total, 64, 2)
        return -total if layer % 2 else total

    fsend[0] = end_face(v3, 7).reshape(LAYER, 128)
    fsend[1] = end_face(v3, 4).reshape(LAYER, 128)
    face_copies = [
        remote(fsend.at[0], frecv.at[0], f3send.at[0], f3recv.at[0], (grp, up)),
        remote(fsend.at[1], frecv.at[1], f3send.at[1], f3recv.at[1], (grp, down)),
    ]
    for copy in face_copies:
        copy.start()

    own_rows = slice(4 * LAYER, 8 * LAYER)
    for index in range(ITERS):
        left = jnp.concatenate(
            [
                jnp.concatenate(
                    [
                        lefts[index][own_rows, start + part * 256 : start + part * 256 + 128]
                        for part in range(3)
                    ],
                    1,
                )
                for start in (0, 128, 768, 896)
            ],
            0,
        )
        both = jnp.dot(left, flat[0:384, 0:256], preferred_element_type=F32)
        for part in range(4):
            rows = slice(part * CELLS, part * CELLS + CELLS)
            grads[index, :, part * 128 : part * 128 + 128] = both[rows, 0:128]
            grads[index, :, NODES + part * 128 : NODES + part * 128 + 128] = both[rows, 128:256]
        multiply(lefts[index], 4, 8, 1, grads.at[index], 2 * NODES)
        if index < 3:
            fghost[index, 0] = end_face(basis[index], 3).reshape(LAYER, 128)
            fghost[index, 1] = end_face(basis[index], 8).reshape(LAYER, 128)

    for copy in face_copies:
        copy.wait()
    for side in range(2):
        fghost[3, side] = frecv[side]

    whole = remote(red.at[1:DOMS], red.at[1:DOMS], rsend, rrecv, (grp, up))
    whole.wait_send()
    whole.wait_recv()

    total = jnp.sum(red[...], axis=0)
    total = jnp.broadcast_to(jnp.sum(total, axis=1, keepdims=True), (8, 128))
    moments[...] = total

    def scalar(row):
        return jnp.broadcast_to(moments[row : row + 1, :], (8, 128))

    alpha = [scalar(row) for row in range(4)]
    beta = [scalar(4 + row) for row in range(4)]
    gamma = [(alpha[k] - THETA * beta[k]) * (1.0 / DELTA) for k in range(4)]
    mu = [beta[0], gamma[0]]
    ahead = gamma[0]
    for k in range(1, 4):
        ahead = 2.0 * gamma[k] - ahead
        mu.append(2.0 * beta[k] - mu[0])
        mu.append(2.0 * ahead - mu[1])

    def inner(i, j):
        return 0.5 * (mu[i + j] + mu[abs(i - j)])

    gram = [
        [
            DELTA * 0.5 * (inner(i, j + 1) + inner(i, abs(j - 1))) + THETA * inner(i, j)
            for j in range(4)
        ]
        for i in range(4)
    ]
    right = [mu[k] for k in range(4)]
    pivots = []
    for k in range(4):
        original = DELTA * 0.5 * (inner(k, k + 1) + inner(k, abs(k - 1))) + THETA * inner(k, k)
        pivot = gram[k][k]
        good = pivot > 1e-7 * original
        inverse = jnp.where(good, 1.0 / jnp.where(good, pivot, 1.0), 0.0)
        pivots.append(inverse)
        for i in range(k + 1, 4):
            factor = gram[i][k] * inverse
            for j in range(k + 1, 4):
                gram[i][j] = gram[i][j] - factor * gram[k][j]
            right[i] = right[i] - factor * right[k]
    coef = [None] * 4
    for k in (3, 2, 1, 0):
        value = right[k]
        for j in range(k + 1, 4):
            value = value - gram[k][j] * coef[j]
        coef[k] = value * pivots[k]

    coef8 = [(value * (1.0 / NP)).reshape(1, 8, 128) for value in coef]
    coef16 = [0.5 * value for value in coef8]
    x_sign = jnp.where(odd, -1.0, 1.0).reshape(1, 8, 128)
    x_scale = jnp.where(take_up | take_down, 0.5, 1.0).reshape(1, 8, 128) * x_sign
    y_half = jnp.where((node_j == 7) | (node_j == 0), 0.5, 1.0).reshape(1, 8, 128)
    y_end = jnp.where(node_j == 7, 0.5, 1.0).reshape(1, 8, 128)
    y_scale = jnp.concatenate(
        [y_end, -y_half, y_half, -y_half, y_half, -y_half, y_half, -y_end], 0
    )

    def combined(layer, direction, pair):
        parts_of = []
        scale = coef8 if direction == 2 else coef16
        for start in (0, 256):
            start = start + direction * NODES + pair * 128
            value = None
            for k in range(4):
                term = scale[k] * grads[k, rows_of(layer), start : start + 128].reshape(8, 8, 128)
                value = term if value is None else value + term
            parts_of.append(value)
        even, uneven = parts_of
        if direction == 2:
            return even + uneven, uneven - even
        return even + uneven, even - uneven

    def put_grad(layer, direction, tile, value):
        start = direction * NODES + tile * 128
        gcells[rows_of(layer), start : start + 128] = value.reshape(LAYER, 128).astype(BF16)

    def flat_grads(layer):
        z_sign = (1 - 2 * lax.rem(layer, 2)).astype(F32)
        for pair in (0, 1):
            for tile, value in zip((pair, 3 - pair), combined(layer, 0, pair)):
                put_grad(layer, 0, tile, x_scale * (value - x_others(value)))
            for tile, value in zip((pair, 3 - pair), combined(layer, 1, pair)):
                put_grad(layer, 1, tile, y_scale * (value - y_others(value)))
        for tile, value in zip((1, 2), combined(layer, 2, 1)):
            put_grad(layer, 2, tile, z_sign * value)
        for tile, value in zip((0, 3), combined(layer, 2, 0)):
            store(xstd, layer, tile, z_sign * value)

    over(0, 4, flat_grads)

    def mean_face(layer, tile, other, there):
        value = load(xstd, layer, tile)
        put_grad(layer, 2, tile, value + jnp.where(low_half, there * (other - value), 0.0))

    for layer in range(4):
        mean_face(layer, 3, load(xstd, layer ^ 1, 3), 0.5)
        if layer in (1, 2):
            mean_face(layer, 0, load(xstd, 3 - layer, 0), 0.5)
        else:
            side = 0 if layer == 0 else 1
            other = None
            for k in range(4):
                term = coef8[k] * fghost[k, side].reshape(8, 8, 128)
                other = term if other is None else other + term
            mean_face(layer, 0, other, 0.5 * (has_up if side else has_down))

    own_first = grp * SHARE

    def pack(part, carry):
        cols = pl.ds(pl.multiple_of(part * 512, 512), 512)
        packed[:, cols] = jnp.dot(
            gpack[...], gcells[:, cols], preferred_element_type=F32
        ).astype(BF16)
        return carry

    lax.fori_loop(0, 3, pack, 0)

    def chunk_rows(chunk, base=0):
        return pl.ds(pl.multiple_of(base + chunk * CHUNK, CHUNK), CHUNK)

    def turn(step):
        return lax.rem(dom + step, PIECES)

    def piece_copy(step, target, slot):
        chunk = turn(step)
        return remote(
            packed.at[chunk_rows(chunk, target * SHARE)], recv.at[comp, chunk_rows(chunk)],
            asend.at[slot, step], arecv.at[comp, chunk], (target, dom),
        )

    def each_send(action):
        @pl.when(grp < 2)
        def _():
            for step in range(PIECES):
                for hop in (2, 1, 3):
                    action(piece_copy(step, lax.rem(grp + hop, 4), hop - 1))

        @pl.when(grp >= 2)
        def _():
            for step in range(PIECES):
                action(piece_copy(step, 3 - grp, 0))

    each_send(lambda copy: copy.start())
    recv[comp] = packed[pl.ds(pl.multiple_of(own_first, SHARE), SHARE), :]

    wide8 = [value.reshape(1, 8, 128) for value in coef]

    @pl.when(grp < 3)
    def _():
        def solve_layer(layer):
            for tile in every:
                value = wide8[0] * load(v0, layer, tile)
                for k in range(1, 4):
                    value = value + wide8[k] * load(basis[k], layer, tile)
                store(xs, layer - 4, tile, value)

        over(4, 8, solve_layer)
        for tile in every:
            mirror_layers(xs[:, tile * 128 : tile * 128 + 128], tile, xstd, 0, True)
        high, low = split(xstd[...])
        parts[0:CELLS, :] = high
        parts[CELLS : 2 * CELLS, :] = low
        out[...] = jnp.dot(ptr[...], parts[...], preferred_element_type=F32)

    def lambda_rows(block, carry):
        rows = pl.ds(pl.multiple_of(block * 16, 16), 16)
        for part in range(2):
            jac = [
                [
                    recv[c, rows, d * NODES + part * 256 : d * NODES + part * 256 + 256].astype(F32)
                    for d in range(3)
                ]
                for c in range(3)
            ]
            lam[rows, part * 256 : part * 256 + 256] = lambda_two(jac)
        return carry

    def natural_order(chunk):
        rows = chunk_rows(chunk)
        slots = pl.ds(pl.multiple_of(own_first + chunk * CHUNK, CHUNK), CHUNK)
        odd_x, odd_y, odd_z = [
            classes[slots, k * 128 : k * 128 + 128] > 0.5 for k in range(3)
        ]
        values = [lam[rows, tile * 128 : tile * 128 + 128] for tile in every]
        flipped = reversals(jnp.concatenate(values, 0))
        turned = []
        for tile in every:
            rev_x, rev_y, rev_xy = [
                part[tile * CHUNK : tile * CHUNK + CHUNK] for part in flipped
            ]
            turned.append(
                jnp.where(
                    odd_x,
                    jnp.where(odd_y, rev_xy, rev_x),
                    jnp.where(odd_y, rev_y, values[tile]),
                )
            )
        for tile in every:
            value = jnp.where(odd_z, turned[3 - tile], turned[tile])
            if tile >= 2:
                value = rotated(value, 64, 1)
            lam[rows, tile * 128 : tile * 128 + 128] = value

    here = pl.ds(pl.multiple_of(dom * 8, 8), 8)

    def each_owner(chunk, action, local):
        piece = lax.div(own_first, CHUNK) + chunk
        four = lax.div(piece, 2)
        for part in range(2):
            place = lax.rem(piece, 2) * 2 + part
            owner = place * 8 + lax.rem(place + lax.div(four, 2), 4) * 2 + lax.rem(four, 2)
            rows = pl.ds(pl.multiple_of(chunk * CHUNK + part * 8, 8), 8)
            own = (grp == 3) & (owner == dom)

            @pl.when(jnp.logical_not(own))
            def _():
                action(
                    remote(
                        lam.at[rows], lamrecv.at[here], osend.at[chunk * 2 + part], orecv,
                        (3, owner),
                    )
                )

            if local:

                @pl.when(own)
                def _():
                    lamrecv[here, :] = lam[rows, :]

    def analyse(chunk):
        for step in (1, 2):
            other = lax.rem(comp + step, 3)
            piece = recv.at[other, chunk_rows(chunk)]
            remote(
                piece, piece, asend.at[0, 0], arecv.at[other, chunk], (lax.rem(grp + 1, 4), dom)
            ).wait_recv()
        lambda_rows(chunk, 0)
        natural_order(chunk)
        each_owner(chunk, lambda copy: copy.start(), True)

    over(0, PIECES, lambda step: analyse(turn(step)))
    for step in range(PIECES):
        each_owner(turn(step), lambda copy: copy.wait_send(), False)
    each_send(lambda copy: copy.wait_send())

    def wait_rows(count):
        piece = lamrecv.at[0 : 8 * count]
        remote(piece, piece, osend.at[0], orecv, (lax.rem(grp + 1, 4), dom)).wait_recv()

    to_itself = lax.rem(lax.div(lax.rem(dom, 8), 2) - lax.div(dom, 8) + 4, 4) == 3

    @pl.when((grp == 3) & to_itself)
    def _():
        wait_rows(31)

    @pl.when((grp == 3) & jnp.logical_not(to_itself))
    def _():
        wait_rows(32)

    @pl.when(grp == 3)
    def _():
        out[...] = lamrecv[...]


def lambda_two(jac):
    strain = [[0.5 * (jac[a][b] + jac[b][a]) for b in range(3)] for a in range(3)]
    spin = [[0.5 * (jac[a][b] - jac[b][a]) for b in range(3)] for a in range(3)]
    m = [[None] * 3 for _ in range(3)]
    for a in range(3):
        for b in range(a, 3):
            value = strain[a][0] * strain[0][b] + spin[a][0] * spin[0][b]
            for k in (1, 2):
                value = value + strain[a][k] * strain[k][b] + spin[a][k] * spin[k][b]
            m[a][b] = value
            m[b][a] = value
    for sweep in range(SWEEPS):
        for p, q, r in ((0, 1, 2), (0, 2, 1), (1, 2, 0)):
            last = sweep == SWEEPS - 1
            twice = 2.0 * m[p][q]
            gap = m[p][p] - m[q][q]
            square = twice * twice + gap * gap
            inverse = lax.rsqrt(jnp.maximum(square, 1e-36))
            length = square * inverse
            mean = 0.5 * (m[p][p] + m[q][q])
            m[p][p] = mean + 0.5 * length
            m[q][q] = mean - 0.5 * length
            if last and (p, q) == (1, 2):
                continue
            none = square < 1e-36
            cosine2 = jnp.where(none, 1.0, jnp.abs(gap) * inverse)
            sine2 = jnp.where(none, 0.0, twice * inverse)
            larger = 0.5 + 0.5 * cosine2
            root = lax.rsqrt(larger)
            big = larger * root
            small = 0.5 * sine2 * root
            flip = gap < 0.0
            sine_big = jnp.where(sine2 < 0.0, -big, big)
            cosine = jnp.where(flip, jnp.abs(small), big)
            sine = jnp.where(flip, sine_big, small)
            side_p = m[r][p]
            side_q = m[r][q]
            m[r][p] = m[p][r] = cosine * side_p + sine * side_q
            m[r][q] = m[q][r] = cosine * side_q - sine * side_p
            m[p][q] = m[q][p] = jnp.zeros_like(side_p)
    diagonal = [m[0][0], m[1][1], m[2][2]]
    largest = jnp.maximum(jnp.maximum(diagonal[0], diagonal[1]), diagonal[2])
    smallest = jnp.minimum(jnp.minimum(diagonal[0], diagonal[1]), diagonal[2])
    return diagonal[0] + diagonal[1] + diagonal[2] - largest - smallest


def per_device(forcing, viscosity, mass_coef, element_order, owner):
    mats, flat, lanes = tables()
    vmem = pl.BlockSpec(memory_space=pltpu.VMEM)
    hbm = pl.BlockSpec(memory_space=pltpu.HBM)
    wide = (12 * LAYER, NODES)
    own = (CELLS, NODES)
    dma = pltpu.SemaphoreType.DMA
    result = pl.pallas_call(
        kernel,
        out_shape=pltpu.VMEM(own, F32),
        in_specs=[hbm] * 8,
        out_specs=vmem,
        scratch_shapes=[
            pltpu.VMEM(own, F32),
            pltpu.VMEM((8, NODES), F32),
            pltpu.VMEM((640, 384), BF16),
            pltpu.VMEM((1, CELLS), jnp.int32),
            pltpu.VMEM((1, CELLS), jnp.int32),
            pltpu.VMEM((4, 768, 256), BF16),
            pltpu.VMEM((8, CELLS), F32),
            pltpu.VMEM((2, 8, CELLS), F32),
            pltpu.VMEM((CELLS, 2 * CELLS), BF16),
            pltpu.VMEM((CELLS, 2 * CELLS), BF16),
            pltpu.VMEM((2 * CELLS, NODES), BF16),
            pltpu.VMEM((12 * LAYER, 128), F32),
            pltpu.VMEM((12 * LAYER, 128), F32),
            pltpu.VMEM(wide, F32),
            pltpu.VMEM(wide, F32),
            pltpu.VMEM(wide, F32),
            pltpu.VMEM((12 * LAYER, 3 * NODES), BF16),
            pltpu.VMEM((12 * LAYER, 3 * NODES), BF16),
            pltpu.VMEM((12 * LAYER, 3 * NODES), BF16),
            pltpu.VMEM((12 * LAYER, 3 * NODES), BF16),
            pltpu.VMEM(wide, F32),
            pltpu.VMEM(wide, F32),
            pltpu.VMEM(wide, F32),
            pltpu.VMEM(wide, F32),
            pltpu.VMEM(own, F32),
            pltpu.VMEM(own, F32),
            pltpu.VMEM((4, CELLS, 3 * NODES), F32),
            pltpu.VMEM((CELLS, CELLS), BF16),
            pltpu.VMEM((CELLS, 384), F32),
            pltpu.VMEM((CELLS, 3 * NODES), BF16),
            pltpu.VMEM((2, LAYER, 128), F32),
            pltpu.VMEM((2, LAYER, 128), F32),
            pltpu.VMEM((4, 2, LAYER, 128), F32),
            pltpu.VMEM((8, 128), F32),
            pltpu.VMEM((DOMS, 8, 128), F32),
            pltpu.VMEM((CELLS, 3 * NODES), BF16),
            pltpu.VMEM((3, SHARE, 3 * NODES), BF16),
            pltpu.VMEM((SHARE, NODES), F32),
            pltpu.VMEM(own, F32),
            dma((6,)), dma((12,)), dma, dma((2,)), dma((2,)), dma((10,)), dma((10,)), dma((2,)),
            dma((2,)), dma, dma, dma((3, PIECES)), dma((3, PIECES)), dma((8,)), dma,
        ],
        compiler_params=pltpu.CompilerParams(
            collective_id=0, has_side_effects=True, vmem_limit_bytes=60 * 1024 * 1024
        ),
        name="solve_and_analyse",
    )(
        forcing, viscosity[None], mass_coef[None], element_order, owner,
        jnp.asarray(lanes), jnp.asarray(flat), jnp.asarray(mats),
    )
    return result[None]


def solution(mesh):
    in_specs = (P(None, "dom", None), P("dom"), P("dom"), P("dom", None), P("dom", None))
    out_specs = P("grp", "dom", None)
    return jax.shard_map(
        per_device, mesh=mesh, in_specs=in_specs, out_specs=out_specs, check_vma=False
    )
```

```python
import functools

import jax
import jax.numpy as jnp
import ml_dtypes
import numpy as np
from jax import lax
from jax.experimental import pallas as pl
from jax.experimental.pallas import tpu as pltpu
from jax.sharding import PartitionSpec as P

NP = 8
ITERS = 4
SWEEPS = 4
LAYER = 64
CELLS = 256
NODES = 512
DOMS = 32
CHUNK = 16
COUNTS = (4, 5, 4, 3)
FIRSTS = (0, 4, 9, 13)
MOST = max(COUNTS)
BASIS_LOW = 0.3
BASIS_HIGH = 2.0
THETA = 0.5 * (BASIS_LOW + BASIS_HIGH)
DELTA = 0.5 * (BASIS_HIGH - BASIS_LOW)
MESH = pl.DeviceIdType.MESH
F32 = jnp.float32
BF16 = jnp.bfloat16


def legendre_values(points, node_count):
    legendre = np.zeros((points.shape[0], node_count))
    legendre[:, 0] = 1.0
    legendre[:, 1] = points
    for poly_order in range(2, node_count):
        legendre[:, poly_order] = (
            (2 * poly_order - 1) * points * legendre[:, poly_order - 1]
            - (poly_order - 1) * legendre[:, poly_order - 2]
        ) / poly_order
    return legendre


def lobatto_table(node_count):
    degree = node_count - 1
    points = np.cos(np.pi * np.arange(node_count) / degree)
    for attempt in range(60):
        legendre = legendre_values(points, node_count)
        points = points - (points * legendre[:, degree] - legendre[:, degree - 1]) / (
            node_count * legendre[:, degree]
        )
    points = points[::-1].copy()
    end_values = legendre_values(points, node_count)[:, degree]
    weights = 2.0 / (degree * node_count * end_values * end_values)
    spacing = points[:, None] - points[None, :] + np.eye(node_count)
    diff_matrix = end_values[:, None] / end_values[None, :] / spacing
    diff_matrix = diff_matrix * (1.0 - np.eye(node_count))
    diff_matrix[0, 0] = -degree * node_count / 4.0
    diff_matrix[-1, -1] = degree * node_count / 4.0
    return (weights, diff_matrix)


def split_rows(matrix):
    high = matrix.astype(np.float32).astype(ml_dtypes.bfloat16)
    low = (matrix - high.astype(np.float64)).astype(np.float32).astype(ml_dtypes.bfloat16)
    return high, low


def tables():
    weights, diff = lobatto_table(NP)
    eye = np.eye(NP)
    cube = (
        weights[:, None, None] * weights[None, :, None] * weights[None, None, :]
    ).reshape(-1)
    directional = [
        np.kron(eye, np.kron(eye, diff)),
        np.kron(eye, np.kron(diff, eye)),
        np.kron(diff, np.kron(eye, eye)),
    ]
    stiff = np.zeros((NODES, NODES))
    for matrix in directional:
        stiff = stiff + matrix.T @ (cube[:, None] * matrix)
    flip = np.arange(NODES).reshape(NP, LAYER)[::-1][: NP // 2].reshape(-1)
    mats = []
    for matrix in (stiff, directional[2]):
        near, far = matrix[:256, :256], matrix[:256, flip]
        for block in (0.5 * (near + far), 0.5 * (near - far)):
            mats.append(np.stack(split_rows(block.T)))
    mats = np.stack(mats)
    flat = np.concatenate([directional[0].T[:128, :128], directional[1].T[:128, :128]], 1)
    high, low = split_rows(flat)
    flat = np.concatenate([high, high, low], 0)
    lanes = np.zeros((8, NODES), np.float32)
    lanes[0] = cube
    lanes[1] = np.diag(stiff)
    lanes[2] = np.repeat(diff[0], LAYER)
    order = [0, 1, 2, 3, 5, 4, 7, 6]
    lanes = lanes.reshape(8, NP, LAYER)[:, order].reshape(8, NODES)
    natural = cube.reshape(NP, LAYER).astype(np.float32).reshape(-1)
    lanes[3] = natural
    back = eye[::-1]
    half = np.eye(2)
    mirror = np.concatenate(
        [
            np.kron(half, np.kron(eye, back)),
            np.kron(half, np.kron(back, eye)),
            np.kron(half, np.kron(back, back)),
        ],
        1,
    ).astype(ml_dtypes.bfloat16)
    wide = np.concatenate([flat, np.zeros((384, 128), flat.dtype)], 1)
    return mats, np.concatenate([wide, mirror, mirror], 0), lanes


def rotated(value, shift, axis):
    return pltpu.roll(value, shift % value.shape[axis], axis)


def kernel(
    forcing, visc_in, mass_in, order_in, owner_in, lanes_in, flat_in, mats,
    out,
    fsc, lanes, flat, order_sc, owner_sc, weights, par, parn, pone, ptr, parts, visc, mass, raw, tmp,
    inv, lhs0, lhs1, lhs2, lhs3, v0, v1, v2, v3, xs, xstd, grads, gpack, classes, gcells, fsend, frecv, fghost, moments,
    red, packed, recv, lam, lamrecv,
    ssem, wsem, fsem, psend, precv, gsend, grecv, f3send, f3recv, rsend, rrecv, asend, arecv,
    osend, orecv,
):
    grp = lax.axis_index("grp")
    dom = lax.axis_index("dom")
    comp = jnp.minimum(grp, 2)
    up = lax.rem(dom + 1, DOMS)
    down = lax.rem(dom + DOMS - 1, DOMS)
    barrier = pltpu.get_barrier_semaphore()
    basis = (v0, v1, v2, v3)
    lefts = (lhs0, lhs1, lhs2, lhs3)
    every = (0, 1, 2, 3)

    for step in range(1, DOMS):
        pl.semaphore_signal(
            barrier, inc=1, device_id=(grp, lax.rem(dom + step, DOMS)), device_id_type=MESH
        )
    for step in range(1, 4):
        pl.semaphore_signal(
            barrier, inc=1, device_id=(lax.rem(grp + step, 4), dom), device_id_type=MESH
        )

    load_small = [
        pltpu.make_async_copy(source, target, ssem.at[k])
        for k, (source, target) in enumerate(
            (
                (visc_in, par.at[0:1]),
                (mass_in, par.at[1:2]),
                (order_in, order_sc),
                (owner_in, owner_sc),
                (lanes_in, lanes),
                (flat_in, flat),
            )
        )
    ]
    for copy in load_small:
        copy.start()
    load_force = pltpu.make_async_copy(forcing.at[comp], fsc, fsem)
    load_force.start()
    load_mats = []
    for which in range(4):
        for part, source in enumerate((0, 0, 1)):
            copy = pltpu.make_async_copy(
                mats.at[which, source],
                weights.at[which, part * 256 : part * 256 + 256],
                wsem.at[3 * which + part],
            )
            copy.start()
            load_mats.append(copy)

    lane = lax.broadcasted_iota(jnp.int32, (8, 128), 1)
    sub = lax.broadcasted_iota(jnp.int32, (8, 128), 0)
    node_i = lax.rem(lane, 8)
    node_j = lax.rem(lane // 8, 8)
    odd = lax.rem(sub, 2) == 1
    first_i = node_i == 0
    last_i = node_i == 7
    take_up = ((last_i & jnp.logical_not(odd)) | (first_i & odd & (sub < 7)))
    take_down = ((last_i & odd) | (first_i & jnp.logical_not(odd) & (sub > 0)))
    has_up = jnp.where(dom < DOMS - 1, 1.0, 0.0).astype(F32)
    has_down = jnp.where(dom > 0, 1.0, 0.0).astype(F32)

    def wide(mask):
        return jnp.broadcast_to(mask[None], (8, 8, 128))

    x_up = wide(take_up)
    x_down = wide(take_down)
    x_odd = wide(odd)
    y_last = wide(node_j == 7)
    y_first = wide(node_j == 0)
    low_half = wide(lane < LAYER)

    def x_others(a):
        above = rotated(a, -1, 1)
        below = rotated(a, 1, 1)
        return jnp.where(x_up, above, jnp.where(x_down, below, 0.0))

    def y_others(a):
        blank = jnp.zeros((1, 8, 128), F32)
        last = jnp.concatenate([a[k ^ 1 : (k ^ 1) + 1] for k in range(8)], 0)
        first = jnp.concatenate(
            [blank] + [a[k : k + 1] for k in (2, 1, 4, 3, 6, 5)] + [blank], 0
        )
        return jnp.where(y_last, last, jnp.where(y_first, first, 0.0))

    def xy_sum(a):
        a = a + x_others(a)
        return a + y_others(a)

    def rows_of(layer):
        if isinstance(layer, int):
            return slice(layer * LAYER, layer * LAYER + LAYER)
        return pl.ds(pl.multiple_of(layer * LAYER, LAYER), LAYER)

    def load(ref, layer, tile):
        return ref[rows_of(layer), tile * 128 : tile * 128 + 128].reshape(8, 8, 128)

    def store(ref, layer, tile, value):
        ref[rows_of(layer), tile * 128 : tile * 128 + 128] = value.reshape(LAYER, 128)

    def column(ref, layer):
        return ref[rows_of(layer), :].reshape(8, 8, 128)

    def table(row, tile):
        return lanes[row : row + 1, tile * 128 : tile * 128 + 128].reshape(1, 1, 128)

    def split(value):
        high = value.astype(BF16)
        return high, (value - high.astype(F32)).astype(BF16)

    def store_lhs(lhs, layer, pair, first, second):
        for start, value in ((0, first + second), (768, first - second)):
            start = start + pair * 128
            high, low = split(value.reshape(LAYER, 128))
            lhs[rows_of(layer), start : start + 128] = high
            lhs[rows_of(layer), start + 256 : start + 384] = low
            lhs[rows_of(layer), start + 512 : start + 640] = high

    def reversals(value):
        total = jnp.dot(
            jnp.concatenate(split(value), 1), flat[384:640, :], preferred_element_type=F32
        )
        return total[:, 0:128], total[:, 128:256], total[:, 256:384]

    def mirror_layers(value, tile, target, base, back):
        flipped = reversals(value)
        for layer in range(4):
            rows = slice(layer * LAYER, layer * LAYER + LAYER)
            plain, rev_x, rev_y, rev_xy = [
                part[rows].reshape(8, 8, 128) for part in (value,) + flipped
            ]
            even_y = jnp.where(x_odd, rev_x, plain)
            odd_y = jnp.where(x_odd, rev_xy, rev_y)
            mixed = jnp.concatenate(
                [(odd_y if k % 2 else even_y)[k : k + 1] for k in range(8)], 0
            )
            place = 3 - tile if layer % 2 else tile
            if (place if back else tile) >= 2:
                mixed = rotated(mixed, 64, 2)
            store(target, base + layer, place, mixed)

    def over(low, high, body):
        lax.fori_loop(low, high, lambda layer, carry: (body(layer), carry)[1], 0)

    cell_sub = lax.broadcasted_iota(jnp.int32, (CELLS, CELLS), 0).astype(F32)
    cell_lane = lax.broadcasted_iota(jnp.int32, (CELLS, CELLS), 1).astype(F32)
    for copy in load_small:
        copy.wait()
    par[2:3, :] = order_sc[...].astype(F32)
    par[3:8, :] = jnp.zeros((5, CELLS), F32)

    def coefficients(ref, base, scale):
        hit = ref[2:3, :] == cell_sub
        for row, target in ((0, visc), (1, mass)):
            col = jnp.sum(jnp.where(hit, ref[row : row + 1, :], 0.0), axis=1, keepdims=True)
            target[base : base + CELLS, :] = jnp.broadcast_to(col * scale, (CELLS, 128))
        return hit

    one_hot = jnp.where(par[2:3, :] == cell_sub, 1.0, 0.0).astype(BF16)
    pone[:, 0:CELLS] = one_hot
    pone[:, CELLS : 2 * CELLS] = one_hot
    load_force.wait()
    high, low = split(fsc[...])
    parts[0:CELLS, :] = high
    parts[CELLS : 2 * CELLS, :] = low
    fsc[...] = jnp.dot(pone[...], parts[...], preferred_element_type=F32) * lanes[3:4, :]
    for tile in every:
        mirror_layers(fsc[:, tile * 128 : tile * 128 + 128], tile, raw, 4, False)

    pl.semaphore_wait(barrier, DOMS - 1 + 3)

    def remote(src, dst, send, recv_sem, device):
        return pltpu.make_async_remote_copy(
            src_ref=src, dst_ref=dst, send_sem=send, recv_sem=recv_sem,
            device_id=device, device_id_type=MESH,
        )

    par_copies = [
        remote(par, parn.at[0], psend.at[0], precv.at[0], (grp, up)),
        remote(par, parn.at[1], psend.at[1], precv.at[1], (grp, down)),
    ]
    def ghost(source, layers, first, last, target, slot, device):
        return remote(
            raw.at[source * LAYER : (source + layers) * LAYER, first:last],
            raw.at[target * LAYER : (target + layers) * LAYER, first:last],
            gsend.at[slot], grecv.at[slot], (grp, device),
        )

    near_copies = [
        ghost(7, 1, 0, 512, 3, 0, up),
        ghost(4, 1, 0, 512, 8, 1, down),
        ghost(6, 1, 384, 512, 2, 2, up),
        ghost(5, 1, 384, 512, 9, 3, down),
    ]
    far_copies = [
        ghost(6, 1, 0, 384, 2, 4, up),
        ghost(5, 1, 0, 384, 9, 5, down),
        ghost(5, 1, 0, 512, 1, 6, up),
        ghost(6, 1, 0, 512, 10, 7, down),
        ghost(4, 1, 384, 512, 0, 8, up),
        ghost(7, 1, 384, 512, 11, 9, down),
    ]
    for copy in par_copies + near_copies + far_copies:
        copy.start()

    coefficients(par, CELLS, 1.0)
    order_col = jnp.sum(
        jnp.where(cell_sub == cell_lane, par[2:3, :], 0.0), axis=1, keepdims=True
    )
    one_hot = jnp.where(order_col == cell_lane, 1.0, 0.0).astype(BF16)
    ptr[:, 0:CELLS] = one_hot
    ptr[:, CELLS : 2 * CELLS] = one_hot
    owner_row = owner_sc[...].astype(F32)
    owner_col = jnp.sum(
        jnp.where(cell_sub == cell_lane, owner_row, 0.0), axis=1, keepdims=True
    )
    same = (owner_col == owner_row) & (cell_sub < cell_lane)
    rank_row = jnp.sum(jnp.where(same, 1.0, 0.0), axis=0, keepdims=True)
    owner_int = owner_sc[...]
    place = owner_int >> 3
    piece_row = ((((owner_int >> 1) - place) & 3) << 1) + (owner_int & 1)
    first_row = (piece_row * 4 + place).astype(F32)
    dest_row = jnp.where(owner_row >= 0.0, first_row * 8.0 + rank_row, -1.0)
    slot_of = jnp.where(dest_row == cell_sub, 1.0, 0.0).astype(BF16)
    gpack[...] = jnp.dot(slot_of, one_hot, preferred_element_type=F32).astype(BF16)
    cell_id = lax.broadcasted_iota(jnp.int32, (CELLS, 128), 0)
    for k, width in enumerate((1, 8, 64)):
        parity = lax.rem(cell_id // width, 2).astype(F32).astype(BF16)
        classes[:, k * 128 : k * 128 + 128] = jnp.dot(
            gpack[...], parity, preferred_element_type=F32
        )

    for copy in par_copies:
        copy.wait()
    coefficients(parn.at[0], 0, has_down)
    coefficients(parn.at[1], 2 * CELLS, has_up)

    def partners(layer):
        parity = layer % 2 if isinstance(layer, int) else lax.rem(layer, 2)
        return {0: layer - 1 + 2 * parity, 3: layer + 1 - 2 * parity}

    def face_sum(ref, layer, tile):
        value = load(ref, layer, tile)
        other = load(ref, partners(layer)[tile], tile)
        return value + jnp.where(low_half, other, 0.0)

    def put_inverse(layer, tile, diag):
        store(inv, layer, tile, jnp.where(diag > 0.0, (2.0 / DELTA) / diag, 0.0))

    def diagonal(layer, tiles):
        coef_v = column(visc, layer)
        coef_m = column(mass, layer)
        for tile in tiles:
            diag = xy_sum(coef_v * table(1, tile) + coef_m * table(0, tile))
            if tile in (0, 3):
                store(tmp, layer, tile, diag)
            else:
                put_inverse(layer, tile, diag)

    diagonal(0, (3,))
    over(1, 11, lambda layer: diagonal(layer, every))
    diagonal(11, (3,))

    def diagonal_faces(layer):
        for tile in (0, 3):
            put_inverse(layer, tile, face_sum(tmp, layer, tile))

    over(1, 11, diagonal_faces)

    def first_value(layer, tile, force):
        value = force * load(inv, layer, tile) * (0.5 * DELTA)
        store(v0, layer, tile, value)
        return value

    def put_first(layer, pair, forces):
        values = [
            first_value(layer, tile, force) for tile, force in zip((pair, 3 - pair), forces)
        ]
        store_lhs(lhs0, layer, pair, *values)

    def assemble(layer, tiles, scale):
        sums = []
        for tile in tiles:
            force = load(raw, layer, tile)
            if scale is not None:
                force = force * scale
            force = xy_sum(force)
            if tile in (0, 3):
                store(tmp, layer, tile, force)
            else:
                sums.append(force)
        if sums:
            put_first(layer, 1, sums)

    over(4, 8, lambda layer: assemble(layer, every, None))
    for copy in load_mats:
        copy.wait()
    def multiply(lhs, low, high, which, target, first=0):
        for part in range(2):
            target[:, first + part * 256 : first + part * 256 + 256] = jnp.dot(
                lhs[low * LAYER : high * LAYER, part * 768 : part * 768 + 768],
                weights[2 * which + part],
                preferred_element_type=F32,
            )

    def advance(step, layer, pair, totals):
        values = []
        for tile, total in zip((pair, 3 - pair), totals):
            value = total * load(inv, layer, tile)
            current = load(basis[step], layer, tile)
            if step == 0:
                value = 0.5 * value - (THETA / DELTA) * current
            else:
                value = value - (2.0 * THETA / DELTA) * current
                value = value - load(basis[step - 1], layer, tile)
            store(basis[step + 1], layer, tile, value)
            values.append(value)
        store_lhs(lefts[step + 1], layer, pair, *values)

    def apply(step, layer, tiles, sums, going):
        coef_v = column(visc, layer)
        coef_m = column(mass, layer)
        for pair in (1, 0):
            if pair not in tiles and 3 - pair not in tiles:
                continue
            even = load(tmp, layer, pair)
            uneven = load(tmp, layer, 2 + pair)
            images = []
            for tile, product in ((pair, even + uneven), (3 - pair, even - uneven)):
                if tile not in tiles:
                    continue
                value = load(basis[step], layer, tile)
                weighted = coef_m * table(0, tile)
                image = coef_v * product + weighted * value
                if sums is not None:
                    diag = coef_v * table(1, tile) + weighted
                    sums = (
                        sums[0] + jnp.sum(value * image, axis=0),
                        sums[1] + jnp.sum(value * value * diag, axis=0),
                    )
                if going:
                    image = xy_sum(image)
                    if pair == 0:
                        store(tmp, layer, tile, image)
                    else:
                        images.append(image)
            if images:
                advance(step, layer, 1, images)
        return sums

    def faces(step, layer):
        advance(step, layer, 0, [face_sum(tmp, layer, tile) for tile in (0, 3)])

    blank_sums = (jnp.zeros((8, 128), F32), jnp.zeros((8, 128), F32))

    def own_apply(step, going):
        sums = lax.fori_loop(
            4, 8, lambda layer, carry: apply(step, layer, every, carry, going), blank_sums
        )
        moments[step : step + 1, :] = jnp.sum(sums[0], axis=0, keepdims=True)
        moments[4 + step : 5 + step, :] = jnp.sum(sums[1], axis=0, keepdims=True)

    def first_faces(layer):
        put_first(layer, 0, [face_sum(tmp, layer, tile) for tile in (0, 3)])

    for copy in near_copies:
        copy.wait()
    assemble(2, (3,), has_down)
    assemble(3, every, has_down)
    assemble(8, every, has_up)
    assemble(9, (3,), has_up)
    over(3, 9, first_faces)
    for layer in (2, 9):
        first_value(layer, 3, face_sum(tmp, layer, 3))
    multiply(lhs0, 3, 9, 0, tmp.at[3 * LAYER : 9 * LAYER])
    own_apply(0, True)
    for layer in (3, 8):
        apply(0, layer, every, None, True)

    for copy in far_copies:
        copy.wait()
    assemble(0, (3,), has_down)
    assemble(1, every, has_down)
    assemble(2, (0, 1, 2), has_down)
    assemble(9, (0, 1, 2), has_up)
    assemble(10, every, has_up)
    assemble(11, (3,), has_up)
    for layer in (1, 10):
        first_faces(layer)
    for layer in (2, 9):
        value = first_value(layer, 0, face_sum(tmp, layer, 0))
        store_lhs(lhs0, layer, 0, value, load(v0, layer, 3))
    far_rows = (slice(1 * LAYER, 3 * LAYER), slice(9 * LAYER, 11 * LAYER))
    for part in range(2):
        product = jnp.dot(
            jnp.concatenate(
                [lhs0[rows, part * 768 : part * 768 + 768] for rows in far_rows], 0
            ),
            weights[part],
            preferred_element_type=F32,
        )
        for side, rows in enumerate(far_rows):
            tmp[rows, part * 256 : part * 256 + 256] = product[
                side * 2 * LAYER : (side + 1) * 2 * LAYER
            ]
    apply(0, 1, (0,), None, True)
    apply(0, 2, every, None, True)
    apply(0, 9, every, None, True)
    apply(0, 10, (0,), None, True)
    over(2, 10, lambda layer: faces(0, layer))

    for step in range(1, ITERS):
        low, high = 1 + step, 11 - step
        going = step + 1 < ITERS
        multiply(lefts[step], low, high, 0, tmp.at[low * LAYER : high * LAYER])
        own_apply(step, going)
        if going:
            inward = 0 if low % 2 else 3
            apply(step, low, (inward,), None, True)
            over(low + 1, 4, lambda layer: apply(step, layer, every, None, True))
            over(8, high - 1, lambda layer: apply(step, layer, every, None, True))
            apply(step, high - 1, (inward,), None, True)
            over(low + 1, high - 1, lambda layer: faces(step, layer))

    red[0] = moments[...]
    for step in range(1, DOMS):
        remote(
            moments, red.at[step], rsend, rrecv, (grp, lax.rem(dom + step, DOMS))
        ).start()

    def end_face(ref, layer):
        total = load(ref, layer, 0) * table(2, 0)
        for tile in (1, 2, 3):
            total = total + load(ref, layer, tile) * table(2, tile)
        total = total + rotated(total, 64, 2)
        return -total if layer % 2 else total

    fsend[0] = end_face(v3, 7).reshape(LAYER, 128)
    fsend[1] = end_face(v3, 4).reshape(LAYER, 128)
    face_copies = [
        remote(fsend.at[0], frecv.at[0], f3send.at[0], f3recv.at[0], (grp, up)),
        remote(fsend.at[1], frecv.at[1], f3send.at[1], f3recv.at[1], (grp, down)),
    ]
    for copy in face_copies:
        copy.start()

    own_rows = slice(4 * LAYER, 8 * LAYER)
    for index in range(ITERS):
        left = jnp.concatenate(
            [
                jnp.concatenate(
                    [
                        lefts[index][own_rows, start + part * 256 : start + part * 256 + 128]
                        for part in range(3)
                    ],
                    1,
                )
                for start in (0, 128, 768, 896)
            ],
            0,
        )
        both = jnp.dot(left, flat[0:384, 0:256], preferred_element_type=F32)
        for part in range(4):
            rows = slice(part * CELLS, part * CELLS + CELLS)
            grads[index, :, part * 128 : part * 128 + 128] = both[rows, 0:128]
            grads[index, :, NODES + part * 128 : NODES + part * 128 + 128] = both[rows, 128:256]
        multiply(lefts[index], 4, 8, 1, grads.at[index], 2 * NODES)
        if index < 3:
            fghost[index, 0] = end_face(basis[index], 3).reshape(LAYER, 128)
            fghost[index, 1] = end_face(basis[index], 8).reshape(LAYER, 128)

    for copy in face_copies:
        copy.wait()
    for side in range(2):
        fghost[3, side] = frecv[side]

    whole = remote(red.at[1:DOMS], red.at[1:DOMS], rsend, rrecv, (grp, up))
    whole.wait_send()
    whole.wait_recv()

    total = jnp.sum(red[...], axis=0)
    total = jnp.broadcast_to(jnp.sum(total, axis=1, keepdims=True), (8, 128))
    moments[...] = total

    def scalar(row):
        return jnp.broadcast_to(moments[row : row + 1, :], (8, 128))

    alpha = [scalar(row) for row in range(4)]
    beta = [scalar(4 + row) for row in range(4)]
    gamma = [(alpha[k] - THETA * beta[k]) * (1.0 / DELTA) for k in range(4)]
    mu = [beta[0], gamma[0]]
    ahead = gamma[0]
    for k in range(1, 4):
        ahead = 2.0 * gamma[k] - ahead
        mu.append(2.0 * beta[k] - mu[0])
        mu.append(2.0 * ahead - mu[1])

    def inner(i, j):
        return 0.5 * (mu[i + j] + mu[abs(i - j)])

    gram = [
        [
            DELTA * 0.5 * (inner(i, j + 1) + inner(i, abs(j - 1))) + THETA * inner(i, j)
            for j in range(4)
        ]
        for i in range(4)
    ]
    right = [mu[k] for k in range(4)]
    pivots = []
    for k in range(4):
        original = DELTA * 0.5 * (inner(k, k + 1) + inner(k, abs(k - 1))) + THETA * inner(k, k)
        pivot = gram[k][k]
        good = pivot > 1e-7 * original
        inverse = jnp.where(good, 1.0 / jnp.where(good, pivot, 1.0), 0.0)
        pivots.append(inverse)
        for i in range(k + 1, 4):
            factor = gram[i][k] * inverse
            for j in range(k + 1, 4):
                gram[i][j] = gram[i][j] - factor * gram[k][j]
            right[i] = right[i] - factor * right[k]
    coef = [None] * 4
    for k in (3, 2, 1, 0):
        value = right[k]
        for j in range(k + 1, 4):
            value = value - gram[k][j] * coef[j]
        coef[k] = value * pivots[k]

    coef8 = [(value * (1.0 / NP)).reshape(1, 8, 128) for value in coef]
    coef16 = [0.5 * value for value in coef8]
    x_sign = jnp.where(odd, -1.0, 1.0).reshape(1, 8, 128)
    x_scale = jnp.where(take_up | take_down, 0.5, 1.0).reshape(1, 8, 128) * x_sign
    y_half = jnp.where((node_j == 7) | (node_j == 0), 0.5, 1.0).reshape(1, 8, 128)
    y_end = jnp.where(node_j == 7, 0.5, 1.0).reshape(1, 8, 128)
    y_scale = jnp.concatenate(
        [y_end, -y_half, y_half, -y_half, y_half, -y_half, y_half, -y_end], 0
    )

    def combined(layer, direction, pair):
        parts_of = []
        scale = coef8 if direction == 2 else coef16
        for start in (0, 256):
            start = start + direction * NODES + pair * 128
            value = None
            for k in range(4):
                term = scale[k] * grads[k, rows_of(layer), start : start + 128].reshape(8, 8, 128)
                value = term if value is None else value + term
            parts_of.append(value)
        even, uneven = parts_of
        if direction == 2:
            return even + uneven, uneven - even
        return even + uneven, even - uneven

    def put_grad(layer, direction, tile, value):
        start = direction * NODES + tile * 128
        gcells[rows_of(layer), start : start + 128] = value.reshape(LAYER, 128).astype(BF16)

    def flat_grads(layer):
        z_sign = (1 - 2 * lax.rem(layer, 2)).astype(F32)
        for pair in (0, 1):
            for tile, value in zip((pair, 3 - pair), combined(layer, 0, pair)):
                put_grad(layer, 0, tile, x_scale * (value - x_others(value)))
            for tile, value in zip((pair, 3 - pair), combined(layer, 1, pair)):
                put_grad(layer, 1, tile, y_scale * (value - y_others(value)))
        for tile, value in zip((1, 2), combined(layer, 2, 1)):
            put_grad(layer, 2, tile, z_sign * value)
        for tile, value in zip((0, 3), combined(layer, 2, 0)):
            store(xstd, layer, tile, z_sign * value)

    over(0, 4, flat_grads)

    def mean_face(layer, tile, other, there):
        value = load(xstd, layer, tile)
        put_grad(layer, 2, tile, value + jnp.where(low_half, there * (other - value), 0.0))

    for layer in range(4):
        mean_face(layer, 3, load(xstd, layer ^ 1, 3), 0.5)
        if layer in (1, 2):
            mean_face(layer, 0, load(xstd, 3 - layer, 0), 0.5)
        else:
            side = 0 if layer == 0 else 1
            other = None
            for k in range(4):
                term = coef8[k] * fghost[k, side].reshape(8, 8, 128)
                other = term if other is None else other + term
            mean_face(layer, 0, other, 0.5 * (has_up if side else has_down))

    def by_row(values):
        picked = values[3]
        for row in (2, 1, 0):
            picked = jnp.where(grp == row, values[row], picked)
        return picked

    own_first = by_row([first * CHUNK for first in FIRSTS])
    own_count = by_row(COUNTS)

    def pack(part, carry):
        cols = pl.ds(pl.multiple_of(part * 512, 512), 512)
        packed[:, cols] = jnp.dot(
            gpack[...], gcells[:, cols], preferred_element_type=F32
        ).astype(BF16)
        return carry

    lax.fori_loop(0, 3, pack, 0)

    def chunk_rows(chunk, base=0):
        return pl.ds(pl.multiple_of(base + chunk * CHUNK, CHUNK), CHUNK)

    def turn(step, count):
        return lax.rem(dom + step, count)

    def piece_copy(step, target, slot):
        chunk = turn(step, COUNTS[target])
        return remote(
            packed.at[chunk_rows(chunk, FIRSTS[target] * CHUNK)],
            recv.at[comp, chunk_rows(chunk)],
            asend.at[slot, step], arecv.at[comp, chunk], (target, dom),
        )

    def each_send(action):
        for row, targets in enumerate(((2, 1, 3), (3, 2, 0), (1,), (0,))):

            @pl.when(grp == row)
            def _():
                for step in range(MOST):
                    for slot, target in enumerate(targets):
                        if step < COUNTS[target]:
                            action(piece_copy(step, target, slot))

    each_send(lambda copy: copy.start())
    for row in range(4):

        @pl.when(grp == row)
        def _():
            slots = COUNTS[row] * CHUNK
            first = FIRSTS[row] * CHUNK
            recv[min(row, 2), 0:slots] = packed[first : first + slots, :]

    wide8 = [value.reshape(1, 8, 128) for value in coef]

    @pl.when(grp < 3)
    def _():
        def solve_layer(layer):
            for tile in every:
                value = wide8[0] * load(v0, layer, tile)
                for k in range(1, 4):
                    value = value + wide8[k] * load(basis[k], layer, tile)
                store(xs, layer - 4, tile, value)

        over(4, 8, solve_layer)
        for tile in every:
            mirror_layers(xs[:, tile * 128 : tile * 128 + 128], tile, xstd, 0, True)
        high, low = split(xstd[...])
        parts[0:CELLS, :] = high
        parts[CELLS : 2 * CELLS, :] = low
        out[...] = jnp.dot(ptr[...], parts[...], preferred_element_type=F32)

    def lambda_rows(block, carry):
        rows = pl.ds(pl.multiple_of(block * 16, 16), 16)
        for part in range(2):
            jac = [
                [
                    recv[c, rows, d * NODES + part * 256 : d * NODES + part * 256 + 256].astype(F32)
                    for d in range(3)
                ]
                for c in range(3)
            ]
            lam[rows, part * 256 : part * 256 + 256] = lambda_two(jac)
        return carry

    def natural_order(chunk):
        rows = chunk_rows(chunk)
        slots = pl.ds(pl.multiple_of(own_first + chunk * CHUNK, CHUNK), CHUNK)
        odd_x, odd_y, odd_z = [
            classes[slots, k * 128 : k * 128 + 128] > 0.5 for k in range(3)
        ]
        values = [lam[rows, tile * 128 : tile * 128 + 128] for tile in every]
        flipped = reversals(jnp.concatenate(values, 0))
        turned = []
        for tile in every:
            rev_x, rev_y, rev_xy = [
                part[tile * CHUNK : tile * CHUNK + CHUNK] for part in flipped
            ]
            turned.append(
                jnp.where(
                    odd_x,
                    jnp.where(odd_y, rev_xy, rev_x),
                    jnp.where(odd_y, rev_y, values[tile]),
                )
            )
        for tile in every:
            value = jnp.where(odd_z, turned[3 - tile], turned[tile])
            if tile >= 2:
                value = rotated(value, 64, 1)
            lam[rows, tile * 128 : tile * 128 + 128] = value

    here = pl.ds(pl.multiple_of(dom * 8, 8), 8)

    def each_owner(chunk, action, local):
        piece = lax.div(own_first, CHUNK) + chunk
        four = lax.div(piece, 2)
        for part in range(2):
            place = lax.rem(piece, 2) * 2 + part
            owner = place * 8 + lax.rem(place + lax.div(four, 2), 4) * 2 + lax.rem(four, 2)
            rows = pl.ds(pl.multiple_of(chunk * CHUNK + part * 8, 8), 8)
            own = (grp == 3) & (owner == dom)

            @pl.when(jnp.logical_not(own))
            def _():
                action(
                    remote(
                        lam.at[rows], lamrecv.at[here], osend.at[chunk * 2 + part], orecv,
                        (3, owner),
                    )
                )

            if local:

                @pl.when(own)
                def _():
                    lamrecv[here, :] = lam[rows, :]

    def analyse(chunk):
        for step in (1, 2):
            other = lax.rem(comp + step, 3)
            piece = recv.at[other, chunk_rows(chunk)]
            remote(
                piece, piece, asend.at[0, 0], arecv.at[other, chunk], (lax.rem(grp + 1, 4), dom)
            ).wait_recv()
        lambda_rows(chunk, 0)
        natural_order(chunk)
        each_owner(chunk, lambda copy: copy.start(), True)

    over(0, own_count, lambda step: analyse(turn(step, own_count)))
    over(
        0,
        own_count,
        lambda step: each_owner(turn(step, own_count), lambda copy: copy.wait_send(), False),
    )
    each_send(lambda copy: copy.wait_send())

    def wait_rows(count):
        piece = lamrecv.at[0 : 8 * count]
        remote(piece, piece, osend.at[0], orecv, (lax.rem(grp + 1, 4), dom)).wait_recv()

    four = lax.rem(lax.div(lax.rem(dom, 8), 2) - lax.div(dom, 8) + 4, 4) * 2 + lax.rem(dom, 2)
    to_itself = four * 2 + lax.div(dom, 16) >= FIRSTS[3]

    @pl.when((grp == 3) & to_itself)
    def _():
        wait_rows(31)

    @pl.when((grp == 3) & jnp.logical_not(to_itself))
    def _():
        wait_rows(32)

    @pl.when(grp == 3)
    def _():
        out[...] = lamrecv[...]


def lambda_two(jac):
    strain = [[0.5 * (jac[a][b] + jac[b][a]) for b in range(3)] for a in range(3)]
    spin = [[0.5 * (jac[a][b] - jac[b][a]) for b in range(3)] for a in range(3)]
    m = [[None] * 3 for _ in range(3)]
    for a in range(3):
        for b in range(a, 3):
            value = strain[a][0] * strain[0][b] + spin[a][0] * spin[0][b]
            for k in (1, 2):
                value = value + strain[a][k] * strain[k][b] + spin[a][k] * spin[k][b]
            m[a][b] = value
            m[b][a] = value
    for sweep in range(SWEEPS):
        for p, q, r in ((0, 1, 2), (0, 2, 1), (1, 2, 0)):
            last = sweep == SWEEPS - 1
            twice = 2.0 * m[p][q]
            gap = m[p][p] - m[q][q]
            square = twice * twice + gap * gap
            inverse = lax.rsqrt(jnp.maximum(square, 1e-36))
            length = square * inverse
            mean = 0.5 * (m[p][p] + m[q][q])
            m[p][p] = mean + 0.5 * length
            m[q][q] = mean - 0.5 * length
            if last and (p, q) == (1, 2):
                continue
            none = square < 1e-36
            cosine2 = jnp.where(none, 1.0, jnp.abs(gap) * inverse)
            sine2 = jnp.where(none, 0.0, twice * inverse)
            larger = 0.5 + 0.5 * cosine2
            root = lax.rsqrt(larger)
            big = larger * root
            small = 0.5 * sine2 * root
            flip = gap < 0.0
            sine_big = jnp.where(sine2 < 0.0, -big, big)
            cosine = jnp.where(flip, jnp.abs(small), big)
            sine = jnp.where(flip, sine_big, small)
            side_p = m[r][p]
            side_q = m[r][q]
            m[r][p] = m[p][r] = cosine * side_p + sine * side_q
            m[r][q] = m[q][r] = cosine * side_q - sine * side_p
            m[p][q] = m[q][p] = jnp.zeros_like(side_p)
    diagonal = [m[0][0], m[1][1], m[2][2]]
    largest = jnp.maximum(jnp.maximum(diagonal[0], diagonal[1]), diagonal[2])
    smallest = jnp.minimum(jnp.minimum(diagonal[0], diagonal[1]), diagonal[2])
    return diagonal[0] + diagonal[1] + diagonal[2] - largest - smallest


def per_device(forcing, viscosity, mass_coef, element_order, owner):
    mats, flat, lanes = tables()
    vmem = pl.BlockSpec(memory_space=pltpu.VMEM)
    hbm = pl.BlockSpec(memory_space=pltpu.HBM)
    wide = (12 * LAYER, NODES)
    own = (CELLS, NODES)
    dma = pltpu.SemaphoreType.DMA
    result = pl.pallas_call(
        kernel,
        out_shape=pltpu.VMEM(own, F32),
        in_specs=[hbm] * 8,
        out_specs=vmem,
        scratch_shapes=[
            pltpu.VMEM(own, F32),
            pltpu.VMEM((8, NODES), F32),
            pltpu.VMEM((640, 384), BF16),
            pltpu.VMEM((1, CELLS), jnp.int32),
            pltpu.VMEM((1, CELLS), jnp.int32),
            pltpu.VMEM((4, 768, 256), BF16),
            pltpu.VMEM((8, CELLS), F32),
            pltpu.VMEM((2, 8, CELLS), F32),
            pltpu.VMEM((CELLS, 2 * CELLS), BF16),
            pltpu.VMEM((CELLS, 2 * CELLS), BF16),
            pltpu.VMEM((2 * CELLS, NODES), BF16),
            pltpu.VMEM((12 * LAYER, 128), F32),
            pltpu.VMEM((12 * LAYER, 128), F32),
            pltpu.VMEM(wide, F32),
            pltpu.VMEM(wide, F32),
            pltpu.VMEM(wide, F32),
            pltpu.VMEM((12 * LAYER, 3 * NODES), BF16),
            pltpu.VMEM((12 * LAYER, 3 * NODES), BF16),
            pltpu.VMEM((12 * LAYER, 3 * NODES), BF16),
            pltpu.VMEM((12 * LAYER, 3 * NODES), BF16),
            pltpu.VMEM(wide, F32),
            pltpu.VMEM(wide, F32),
            pltpu.VMEM(wide, F32),
            pltpu.VMEM(wide, F32),
            pltpu.VMEM(own, F32),
            pltpu.VMEM(own, F32),
            pltpu.VMEM((4, CELLS, 3 * NODES), F32),
            pltpu.VMEM((CELLS, CELLS), BF16),
            pltpu.VMEM((CELLS, 384), F32),
            pltpu.VMEM((CELLS, 3 * NODES), BF16),
            pltpu.VMEM((2, LAYER, 128), F32),
            pltpu.VMEM((2, LAYER, 128), F32),
            pltpu.VMEM((4, 2, LAYER, 128), F32),
            pltpu.VMEM((8, 128), F32),
            pltpu.VMEM((DOMS, 8, 128), F32),
            pltpu.VMEM((CELLS, 3 * NODES), BF16),
            pltpu.VMEM((3, MOST * CHUNK, 3 * NODES), BF16),
            pltpu.VMEM((MOST * CHUNK, NODES), F32),
            pltpu.VMEM(own, F32),
            dma((6,)), dma((12,)), dma, dma((2,)), dma((2,)), dma((10,)), dma((10,)), dma((2,)),
            dma((2,)), dma, dma, dma((3, MOST)), dma((3, MOST)), dma((2 * MOST,)), dma,
        ],
        compiler_params=pltpu.CompilerParams(
            collective_id=0, has_side_effects=True, vmem_limit_bytes=60 * 1024 * 1024
        ),
        name="solve_and_analyse",
    )(
        forcing, viscosity[None], mass_coef[None], element_order, owner,
        jnp.asarray(lanes), jnp.asarray(flat), jnp.asarray(mats),
    )
    return result[None]


def solution(mesh):
    in_specs = (P(None, "dom", None), P("dom"), P("dom"), P("dom", None), P("dom", None))
    out_specs = P("grp", "dom", None)
    return jax.shard_map(
        per_device, mesh=mesh, in_specs=in_specs, out_specs=out_specs, check_vma=False
    )
```

```python
import functools

import jax
import jax.numpy as jnp
import ml_dtypes
import numpy as np
from jax import lax
from jax.experimental import pallas as pl
from jax.experimental.pallas import tpu as pltpu
from jax.sharding import PartitionSpec as P

NP = 8
ITERS = 4
SWEEPS = 4
LAYER = 64
CELLS = 256
NODES = 512
DOMS = 32
CHUNK = 16
COUNTS = (4, 5, 4, 3)
FIRSTS = (0, 4, 9, 13)
MOST = max(COUNTS)
BASIS_LOW = 0.3
BASIS_HIGH = 2.0
THETA = 0.5 * (BASIS_LOW + BASIS_HIGH)
DELTA = 0.5 * (BASIS_HIGH - BASIS_LOW)
MESH = pl.DeviceIdType.MESH
F32 = jnp.float32
BF16 = jnp.bfloat16


def legendre_values(points, node_count):
    legendre = np.zeros((points.shape[0], node_count))
    legendre[:, 0] = 1.0
    legendre[:, 1] = points
    for poly_order in range(2, node_count):
        legendre[:, poly_order] = (
            (2 * poly_order - 1) * points * legendre[:, poly_order - 1]
            - (poly_order - 1) * legendre[:, poly_order - 2]
        ) / poly_order
    return legendre


def lobatto_table(node_count):
    degree = node_count - 1
    points = np.cos(np.pi * np.arange(node_count) / degree)
    for attempt in range(60):
        legendre = legendre_values(points, node_count)
        points = points - (points * legendre[:, degree] - legendre[:, degree - 1]) / (
            node_count * legendre[:, degree]
        )
    points = points[::-1].copy()
    end_values = legendre_values(points, node_count)[:, degree]
    weights = 2.0 / (degree * node_count * end_values * end_values)
    spacing = points[:, None] - points[None, :] + np.eye(node_count)
    diff_matrix = end_values[:, None] / end_values[None, :] / spacing
    diff_matrix = diff_matrix * (1.0 - np.eye(node_count))
    diff_matrix[0, 0] = -degree * node_count / 4.0
    diff_matrix[-1, -1] = degree * node_count / 4.0
    return (weights, diff_matrix)


def split_rows(matrix):
    high = matrix.astype(np.float32).astype(ml_dtypes.bfloat16)
    low = (matrix - high.astype(np.float64)).astype(np.float32).astype(ml_dtypes.bfloat16)
    return high, low


def tables():
    weights, diff = lobatto_table(NP)
    eye = np.eye(NP)
    cube = (
        weights[:, None, None] * weights[None, :, None] * weights[None, None, :]
    ).reshape(-1)
    directional = [
        np.kron(eye, np.kron(eye, diff)),
        np.kron(eye, np.kron(diff, eye)),
        np.kron(diff, np.kron(eye, eye)),
    ]
    stiff = np.zeros((NODES, NODES))
    for matrix in directional:
        stiff = stiff + matrix.T @ (cube[:, None] * matrix)
    flip = np.arange(NODES).reshape(NP, LAYER)[::-1][: NP // 2].reshape(-1)
    mats = []
    for matrix in (stiff, directional[2]):
        near, far = matrix[:256, :256], matrix[:256, flip]
        for block in (0.5 * (near + far), 0.5 * (near - far)):
            mats.append(np.stack(split_rows(block.T)))
    mats = np.stack(mats)
    flat = np.concatenate([directional[0].T[:128, :128], directional[1].T[:128, :128]], 1)
    high, low = split_rows(flat)
    flat = np.concatenate([high, high, low], 0)
    lanes = np.zeros((8, NODES), np.float32)
    lanes[0] = cube
    lanes[1] = np.diag(stiff)
    lanes[2] = np.repeat(diff[0], LAYER)
    order = [0, 1, 2, 3, 5, 4, 7, 6]
    lanes = lanes.reshape(8, NP, LAYER)[:, order].reshape(8, NODES)
    natural = cube.reshape(NP, LAYER).astype(np.float32).reshape(-1)
    lanes[3] = natural
    back = eye[::-1]
    half = np.eye(2)
    mirror = np.concatenate(
        [
            np.kron(half, np.kron(eye, back)),
            np.kron(half, np.kron(back, eye)),
            np.kron(half, np.kron(back, back)),
        ],
        1,
    ).astype(ml_dtypes.bfloat16)
    wide = np.concatenate([flat, np.zeros((384, 128), flat.dtype)], 1)
    return mats, np.concatenate([wide, mirror, mirror], 0), lanes


def rotated(value, shift, axis):
    return pltpu.roll(value, shift % value.shape[axis], axis)


def kernel(
    forcing, visc_in, mass_in, order_in, owner_in, lanes_in, flat_in, mats,
    out,
    fsc, lanes, flat, order_sc, owner_sc, weights, par, parn, pone, ptr, parts, visc, mass, raw, tmp,
    inv, lhs0, lhs1, lhs2, lhs3, v0, v1, v2, v3, xs, xstd, grads, gpack, classes, gcells, fsend, frecv, fghost, moments,
    red, packed, recv, lam, lamrecv,
    ssem, wsem, fsem, psend, precv, gsend, grecv, f3send, f3recv, rsend, rrecv, asend, arecv,
    osend, orecv,
):
    grp = lax.axis_index("grp")
    dom = lax.axis_index("dom")
    comp = jnp.minimum(grp, 2)
    up = lax.rem(dom + 1, DOMS)
    down = lax.rem(dom + DOMS - 1, DOMS)
    barrier = pltpu.get_barrier_semaphore()
    basis = (v0, v1, v2, v3)
    lefts = (lhs0, lhs1, lhs2, lhs3)
    every = (0, 1, 2, 3)

    at_y = [lax.rem(lax.div(dom, 8) + k, 4) * 8 for k in range(4)]
    at_z = [lax.rem(lax.div(dom, 2) + k, 4) * 2 for k in range(4)]
    at_core = [lax.rem(dom + k, 2) for k in range(2)]

    def hops(offset):
        return sum(min(k, 4 - k) for k in (offset // 8, offset // 2 % 4))

    peers = [
        (offset, at_y[offset // 8] + at_z[offset // 2 % 4] + at_core[offset % 2])
        for offset in sorted(range(1, DOMS), key=lambda offset: -hops(offset))
    ]

    for offset, peer in peers:
        pl.semaphore_signal(barrier, inc=1, device_id=(grp, peer), device_id_type=MESH)
    for step in range(1, 4):
        pl.semaphore_signal(
            barrier, inc=1, device_id=(lax.rem(grp + step, 4), dom), device_id_type=MESH
        )

    load_small = [
        pltpu.make_async_copy(source, target, ssem.at[k])
        for k, (source, target) in enumerate(
            (
                (visc_in, par.at[0:1]),
                (mass_in, par.at[1:2]),
                (order_in, order_sc),
                (owner_in, owner_sc),
                (lanes_in, lanes),
                (flat_in, flat),
            )
        )
    ]
    for copy in load_small:
        copy.start()
    load_force = pltpu.make_async_copy(forcing.at[comp], fsc, fsem)
    load_force.start()
    load_mats = []
    for which in range(4):
        for part, source in enumerate((0, 0, 1)):
            copy = pltpu.make_async_copy(
                mats.at[which, source],
                weights.at[which, part * 256 : part * 256 + 256],
                wsem.at[3 * which + part],
            )
            copy.start()
            load_mats.append(copy)

    lane = lax.broadcasted_iota(jnp.int32, (8, 128), 1)
    sub = lax.broadcasted_iota(jnp.int32, (8, 128), 0)
    node_i = lax.rem(lane, 8)
    node_j = lax.rem(lane // 8, 8)
    odd = lax.rem(sub, 2) == 1
    first_i = node_i == 0
    last_i = node_i == 7
    take_up = ((last_i & jnp.logical_not(odd)) | (first_i & odd & (sub < 7)))
    take_down = ((last_i & odd) | (first_i & jnp.logical_not(odd) & (sub > 0)))
    has_up = jnp.where(dom < DOMS - 1, 1.0, 0.0).astype(F32)
    has_down = jnp.where(dom > 0, 1.0, 0.0).astype(F32)

    def wide(mask):
        return jnp.broadcast_to(mask[None], (8, 8, 128))

    x_up = wide(take_up)
    x_down = wide(take_down)
    x_odd = wide(odd)
    y_last = wide(node_j == 7)
    y_first = wide(node_j == 0)
    low_half = wide(lane < LAYER)

    def x_others(a):
        above = rotated(a, -1, 1)
        below = rotated(a, 1, 1)
        return jnp.where(x_up, above, jnp.where(x_down, below, 0.0))

    def y_others(a):
        blank = jnp.zeros((1, 8, 128), F32)
        last = jnp.concatenate([a[k ^ 1 : (k ^ 1) + 1] for k in range(8)], 0)
        first = jnp.concatenate(
            [blank] + [a[k : k + 1] for k in (2, 1, 4, 3, 6, 5)] + [blank], 0
        )
        return jnp.where(y_last, last, jnp.where(y_first, first, 0.0))

    def xy_sum(a):
        a = a + x_others(a)
        return a + y_others(a)

    def rows_of(layer):
        if isinstance(layer, int):
            return slice(layer * LAYER, layer * LAYER + LAYER)
        return pl.ds(pl.multiple_of(layer * LAYER, LAYER), LAYER)

    def load(ref, layer, tile):
        return ref[rows_of(layer), tile * 128 : tile * 128 + 128].reshape(8, 8, 128)

    def store(ref, layer, tile, value):
        ref[rows_of(layer), tile * 128 : tile * 128 + 128] = value.reshape(LAYER, 128)

    def column(ref, layer):
        return ref[rows_of(layer), :].reshape(8, 8, 128)

    def table(row, tile):
        return lanes[row : row + 1, tile * 128 : tile * 128 + 128].reshape(1, 1, 128)

    def split(value):
        high = value.astype(BF16)
        return high, (value - high.astype(F32)).astype(BF16)

    def store_lhs(lhs, layer, pair, first, second):
        for start, value in ((0, first + second), (768, first - second)):
            start = start + pair * 128
            high, low = split(value.reshape(LAYER, 128))
            lhs[rows_of(layer), start : start + 128] = high
            lhs[rows_of(layer), start + 256 : start + 384] = low
            lhs[rows_of(layer), start + 512 : start + 640] = high

    def reversals(value):
        total = jnp.dot(
            jnp.concatenate(split(value), 1), flat[384:640, :], preferred_element_type=F32
        )
        return total[:, 0:128], total[:, 128:256], total[:, 256:384]

    def mirror_layers(value, tile, target, base, back):
        flipped = reversals(value)
        for layer in range(4):
            rows = slice(layer * LAYER, layer * LAYER + LAYER)
            plain, rev_x, rev_y, rev_xy = [
                part[rows].reshape(8, 8, 128) for part in (value,) + flipped
            ]
            even_y = jnp.where(x_odd, rev_x, plain)
            odd_y = jnp.where(x_odd, rev_xy, rev_y)
            mixed = jnp.concatenate(
                [(odd_y if k % 2 else even_y)[k : k + 1] for k in range(8)], 0
            )
            place = 3 - tile if layer % 2 else tile
            if (place if back else tile) >= 2:
                mixed = rotated(mixed, 64, 2)
            store(target, base + layer, place, mixed)

    def over(low, high, body):
        lax.fori_loop(low, high, lambda layer, carry: (body(layer), carry)[1], 0)

    cell_sub = lax.broadcasted_iota(jnp.int32, (CELLS, CELLS), 0).astype(F32)
    cell_lane = lax.broadcasted_iota(jnp.int32, (CELLS, CELLS), 1).astype(F32)
    for copy in load_small:
        copy.wait()
    par[2:3, :] = order_sc[...].astype(F32)
    par[3:8, :] = jnp.zeros((5, CELLS), F32)

    def coefficients(ref, base, scale):
        hit = ref[2:3, :] == cell_sub
        for row, target in ((0, visc), (1, mass)):
            col = jnp.sum(jnp.where(hit, ref[row : row + 1, :], 0.0), axis=1, keepdims=True)
            target[base : base + CELLS, :] = jnp.broadcast_to(col * scale, (CELLS, 128))
        return hit

    one_hot = jnp.where(par[2:3, :] == cell_sub, 1.0, 0.0).astype(BF16)
    pone[:, 0:CELLS] = one_hot
    pone[:, CELLS : 2 * CELLS] = one_hot
    load_force.wait()
    high, low = split(fsc[...])
    parts[0:CELLS, :] = high
    parts[CELLS : 2 * CELLS, :] = low
    fsc[...] = jnp.dot(pone[...], parts[...], preferred_element_type=F32) * lanes[3:4, :]
    for tile in every:
        mirror_layers(fsc[:, tile * 128 : tile * 128 + 128], tile, raw, 4, False)

    pl.semaphore_wait(barrier, DOMS - 1 + 3)

    def remote(src, dst, send, recv_sem, device):
        return pltpu.make_async_remote_copy(
            src_ref=src, dst_ref=dst, send_sem=send, recv_sem=recv_sem,
            device_id=device, device_id_type=MESH,
        )

    par_copies = [
        remote(par, parn.at[0], psend.at[0], precv.at[0], (grp, up)),
        remote(par, parn.at[1], psend.at[1], precv.at[1], (grp, down)),
    ]
    def ghost(source, layers, first, last, target, slot, device):
        return remote(
            raw.at[source * LAYER : (source + layers) * LAYER, first:last],
            raw.at[target * LAYER : (target + layers) * LAYER, first:last],
            gsend.at[slot], grecv.at[slot], (grp, device),
        )

    near_copies = [
        ghost(7, 1, 0, 512, 3, 0, up),
        ghost(4, 1, 0, 512, 8, 1, down),
        ghost(6, 1, 384, 512, 2, 2, up),
        ghost(5, 1, 384, 512, 9, 3, down),
    ]
    far_copies = [
        ghost(6, 1, 0, 384, 2, 4, up),
        ghost(5, 1, 0, 384, 9, 5, down),
        ghost(5, 1, 0, 512, 1, 6, up),
        ghost(6, 1, 0, 512, 10, 7, down),
        ghost(4, 1, 384, 512, 0, 8, up),
        ghost(7, 1, 384, 512, 11, 9, down),
    ]
    for copy in par_copies + near_copies + far_copies:
        copy.start()

    coefficients(par, CELLS, 1.0)
    order_col = jnp.sum(
        jnp.where(cell_sub == cell_lane, par[2:3, :], 0.0), axis=1, keepdims=True
    )
    one_hot = jnp.where(order_col == cell_lane, 1.0, 0.0).astype(BF16)
    ptr[:, 0:CELLS] = one_hot
    ptr[:, CELLS : 2 * CELLS] = one_hot
    owner_row = owner_sc[...].astype(F32)
    owner_col = jnp.sum(
        jnp.where(cell_sub == cell_lane, owner_row, 0.0), axis=1, keepdims=True
    )
    same = (owner_col == owner_row) & (cell_sub < cell_lane)
    rank_row = jnp.sum(jnp.where(same, 1.0, 0.0), axis=0, keepdims=True)
    owner_int = owner_sc[...]
    place = owner_int >> 3
    piece_row = ((((owner_int >> 1) - place) & 3) << 1) + (owner_int & 1)
    first_row = (piece_row * 4 + place).astype(F32)
    dest_row = jnp.where(owner_row >= 0.0, first_row * 8.0 + rank_row, -1.0)
    slot_of = jnp.where(dest_row == cell_sub, 1.0, 0.0).astype(BF16)
    gpack[...] = jnp.dot(slot_of, one_hot, preferred_element_type=F32).astype(BF16)
    cell_id = lax.broadcasted_iota(jnp.int32, (CELLS, 128), 0)
    for k, width in enumerate((1, 8, 64)):
        parity = lax.rem(cell_id // width, 2).astype(F32).astype(BF16)
        classes[:, k * 128 : k * 128 + 128] = jnp.dot(
            gpack[...], parity, preferred_element_type=F32
        )

    for copy in par_copies:
        copy.wait()
    coefficients(parn.at[0], 0, has_down)
    coefficients(parn.at[1], 2 * CELLS, has_up)

    def partners(layer):
        parity = layer % 2 if isinstance(layer, int) else lax.rem(layer, 2)
        return {0: layer - 1 + 2 * parity, 3: layer + 1 - 2 * parity}

    def face_sum(ref, layer, tile):
        value = load(ref, layer, tile)
        other = load(ref, partners(layer)[tile], tile)
        return value + jnp.where(low_half, other, 0.0)

    def put_inverse(layer, tile, diag):
        store(inv, layer, tile, jnp.where(diag > 0.0, (2.0 / DELTA) / diag, 0.0))

    def diagonal(layer, tiles):
        coef_v = column(visc, layer)
        coef_m = column(mass, layer)
        for tile in tiles:
            diag = xy_sum(coef_v * table(1, tile) + coef_m * table(0, tile))
            if tile in (0, 3):
                store(tmp, layer, tile, diag)
            else:
                put_inverse(layer, tile, diag)

    diagonal(0, (3,))
    over(1, 11, lambda layer: diagonal(layer, every))
    diagonal(11, (3,))

    def diagonal_faces(layer):
        for tile in (0, 3):
            put_inverse(layer, tile, face_sum(tmp, layer, tile))

    over(1, 11, diagonal_faces)

    def first_value(layer, tile, force):
        value = force * load(inv, layer, tile) * (0.5 * DELTA)
        store(v0, layer, tile, value)
        return value

    def put_first(layer, pair, forces):
        values = [
            first_value(layer, tile, force) for tile, force in zip((pair, 3 - pair), forces)
        ]
        store_lhs(lhs0, layer, pair, *values)

    def assemble(layer, tiles, scale):
        sums = []
        for tile in tiles:
            force = load(raw, layer, tile)
            if scale is not None:
                force = force * scale
            force = xy_sum(force)
            if tile in (0, 3):
                store(tmp, layer, tile, force)
            else:
                sums.append(force)
        if sums:
            put_first(layer, 1, sums)

    over(4, 8, lambda layer: assemble(layer, every, None))
    for copy in load_mats:
        copy.wait()
    def multiply(lhs, low, high, which, target, first=0):
        for part in range(2):
            target[:, first + part * 256 : first + part * 256 + 256] = jnp.dot(
                lhs[low * LAYER : high * LAYER, part * 768 : part * 768 + 768],
                weights[2 * which + part],
                preferred_element_type=F32,
            )

    def advance(step, layer, pair, totals):
        values = []
        for tile, total in zip((pair, 3 - pair), totals):
            value = total * load(inv, layer, tile)
            current = load(basis[step], layer, tile)
            if step == 0:
                value = 0.5 * value - (THETA / DELTA) * current
            else:
                value = value - (2.0 * THETA / DELTA) * current
                value = value - load(basis[step - 1], layer, tile)
            store(basis[step + 1], layer, tile, value)
            values.append(value)
        store_lhs(lefts[step + 1], layer, pair, *values)

    def apply(step, layer, tiles, sums, going):
        coef_v = column(visc, layer)
        coef_m = column(mass, layer)
        for pair in (1, 0):
            if pair not in tiles and 3 - pair not in tiles:
                continue
            even = load(tmp, layer, pair)
            uneven = load(tmp, layer, 2 + pair)
            images = []
            for tile, product in ((pair, even + uneven), (3 - pair, even - uneven)):
                if tile not in tiles:
                    continue
                value = load(basis[step], layer, tile)
                weighted = coef_m * table(0, tile)
                image = coef_v * product + weighted * value
                if sums is not None:
                    diag = coef_v * table(1, tile) + weighted
                    sums = (
                        sums[0] + jnp.sum(value * image, axis=0),
                        sums[1] + jnp.sum(value * value * diag, axis=0),
                    )
                if going:
                    image = xy_sum(image)
                    if pair == 0:
                        store(tmp, layer, tile, image)
                    else:
                        images.append(image)
            if images:
                advance(step, layer, 1, images)
        return sums

    def faces(step, layer):
        advance(step, layer, 0, [face_sum(tmp, layer, tile) for tile in (0, 3)])

    blank_sums = (jnp.zeros((8, 128), F32), jnp.zeros((8, 128), F32))

    def own_apply(step, going):
        sums = lax.fori_loop(
            4, 8, lambda layer, carry: apply(step, layer, every, carry, going), blank_sums
        )
        moments[step : step + 1, :] = jnp.sum(sums[0], axis=0, keepdims=True)
        moments[4 + step : 5 + step, :] = jnp.sum(sums[1], axis=0, keepdims=True)

    def first_faces(layer):
        put_first(layer, 0, [face_sum(tmp, layer, tile) for tile in (0, 3)])

    for copy in near_copies:
        copy.wait()
    assemble(2, (3,), has_down)
    assemble(3, every, has_down)
    assemble(8, every, has_up)
    assemble(9, (3,), has_up)
    over(3, 9, first_faces)
    for layer in (2, 9):
        first_value(layer, 3, face_sum(tmp, layer, 3))
    multiply(lhs0, 3, 9, 0, tmp.at[3 * LAYER : 9 * LAYER])
    own_apply(0, True)
    for layer in (3, 8):
        apply(0, layer, every, None, True)

    for copy in far_copies:
        copy.wait()
    assemble(0, (3,), has_down)
    assemble(1, every, has_down)
    assemble(2, (0, 1, 2), has_down)
    assemble(9, (0, 1, 2), has_up)
    assemble(10, every, has_up)
    assemble(11, (3,), has_up)
    for layer in (1, 10):
        first_faces(layer)
    for layer in (2, 9):
        value = first_value(layer, 0, face_sum(tmp, layer, 0))
        store_lhs(lhs0, layer, 0, value, load(v0, layer, 3))
    far_rows = (slice(1 * LAYER, 3 * LAYER), slice(9 * LAYER, 11 * LAYER))
    for part in range(2):
        product = jnp.dot(
            jnp.concatenate(
                [lhs0[rows, part * 768 : part * 768 + 768] for rows in far_rows], 0
            ),
            weights[part],
            preferred_element_type=F32,
        )
        for side, rows in enumerate(far_rows):
            tmp[rows, part * 256 : part * 256 + 256] = product[
                side * 2 * LAYER : (side + 1) * 2 * LAYER
            ]
    apply(0, 1, (0,), None, True)
    apply(0, 2, every, None, True)
    apply(0, 9, every, None, True)
    apply(0, 10, (0,), None, True)
    over(2, 10, lambda layer: faces(0, layer))

    for step in range(1, ITERS):
        low, high = 1 + step, 11 - step
        going = step + 1 < ITERS
        multiply(lefts[step], low, high, 0, tmp.at[low * LAYER : high * LAYER])
        own_apply(step, going)
        if going:
            inward = 0 if low % 2 else 3
            apply(step, low, (inward,), None, True)
            over(low + 1, 4, lambda layer: apply(step, layer, every, None, True))
            over(8, high - 1, lambda layer: apply(step, layer, every, None, True))
            apply(step, high - 1, (inward,), None, True)
            over(low + 1, high - 1, lambda layer: faces(step, layer))

    red[0] = moments[...]
    for offset, peer in peers:
        remote(moments, red.at[offset], rsend, rrecv, (grp, peer)).start()

    def end_face(ref, layer):
        total = load(ref, layer, 0) * table(2, 0)
        for tile in (1, 2, 3):
            total = total + load(ref, layer, tile) * table(2, tile)
        total = total + rotated(total, 64, 2)
        return -total if layer % 2 else total

    fsend[0] = end_face(v3, 7).reshape(LAYER, 128)
    fsend[1] = end_face(v3, 4).reshape(LAYER, 128)
    face_copies = [
        remote(fsend.at[0], frecv.at[0], f3send.at[0], f3recv.at[0], (grp, up)),
        remote(fsend.at[1], frecv.at[1], f3send.at[1], f3recv.at[1], (grp, down)),
    ]
    for copy in face_copies:
        copy.start()

    own_rows = slice(4 * LAYER, 8 * LAYER)
    for index in range(ITERS):
        left = jnp.concatenate(
            [
                jnp.concatenate(
                    [
                        lefts[index][own_rows, start + part * 256 : start + part * 256 + 128]
                        for part in range(3)
                    ],
                    1,
                )
                for start in (0, 128, 768, 896)
            ],
            0,
        )
        both = jnp.dot(left, flat[0:384, 0:256], preferred_element_type=F32)
        for part in range(4):
            rows = slice(part * CELLS, part * CELLS + CELLS)
            grads[index, :, part * 128 : part * 128 + 128] = both[rows, 0:128]
            grads[index, :, NODES + part * 128 : NODES + part * 128 + 128] = both[rows, 128:256]
        multiply(lefts[index], 4, 8, 1, grads.at[index], 2 * NODES)
        if index < 3:
            fghost[index, 0] = end_face(basis[index], 3).reshape(LAYER, 128)
            fghost[index, 1] = end_face(basis[index], 8).reshape(LAYER, 128)

    for copy in face_copies:
        copy.wait()
    for side in range(2):
        fghost[3, side] = frecv[side]

    whole = remote(red.at[1:DOMS], red.at[1:DOMS], rsend, rrecv, (grp, up))
    whole.wait_send()
    whole.wait_recv()

    total = jnp.sum(red[...], axis=0)
    total = jnp.broadcast_to(jnp.sum(total, axis=1, keepdims=True), (8, 128))
    moments[...] = total

    def scalar(row):
        return jnp.broadcast_to(moments[row : row + 1, :], (8, 128))

    alpha = [scalar(row) for row in range(4)]
    beta = [scalar(4 + row) for row in range(4)]
    gamma = [(alpha[k] - THETA * beta[k]) * (1.0 / DELTA) for k in range(4)]
    mu = [beta[0], gamma[0]]
    ahead = gamma[0]
    for k in range(1, 4):
        ahead = 2.0 * gamma[k] - ahead
        mu.append(2.0 * beta[k] - mu[0])
        mu.append(2.0 * ahead - mu[1])

    def inner(i, j):
        return 0.5 * (mu[i + j] + mu[abs(i - j)])

    gram = [
        [
            DELTA * 0.5 * (inner(i, j + 1) + inner(i, abs(j - 1))) + THETA * inner(i, j)
            for j in range(4)
        ]
        for i in range(4)
    ]
    right = [mu[k] for k in range(4)]
    pivots = []
    for k in range(4):
        original = DELTA * 0.5 * (inner(k, k + 1) + inner(k, abs(k - 1))) + THETA * inner(k, k)
        pivot = gram[k][k]
        good = pivot > 1e-7 * original
        inverse = jnp.where(good, 1.0 / jnp.where(good, pivot, 1.0), 0.0)
        pivots.append(inverse)
        for i in range(k + 1, 4):
            factor = gram[i][k] * inverse
            for j in range(k + 1, 4):
                gram[i][j] = gram[i][j] - factor * gram[k][j]
            right[i] = right[i] - factor * right[k]
    coef = [None] * 4
    for k in (3, 2, 1, 0):
        value = right[k]
        for j in range(k + 1, 4):
            value = value - gram[k][j] * coef[j]
        coef[k] = value * pivots[k]

    coef8 = [(value * (1.0 / NP)).reshape(1, 8, 128) for value in coef]
    coef16 = [0.5 * value for value in coef8]
    x_sign = jnp.where(odd, -1.0, 1.0).reshape(1, 8, 128)
    x_scale = jnp.where(take_up | take_down, 0.5, 1.0).reshape(1, 8, 128) * x_sign
    y_half = jnp.where((node_j == 7) | (node_j == 0), 0.5, 1.0).reshape(1, 8, 128)
    y_end = jnp.where(node_j == 7, 0.5, 1.0).reshape(1, 8, 128)
    y_scale = jnp.concatenate(
        [y_end, -y_half, y_half, -y_half, y_half, -y_half, y_half, -y_end], 0
    )

    def combined(layer, direction, pair):
        parts_of = []
        scale = coef8 if direction == 2 else coef16
        for start in (0, 256):
            start = start + direction * NODES + pair * 128
            value = None
            for k in range(4):
                term = scale[k] * grads[k, rows_of(layer), start : start + 128].reshape(8, 8, 128)
                value = term if value is None else value + term
            parts_of.append(value)
        even, uneven = parts_of
        if direction == 2:
            return even + uneven, uneven - even
        return even + uneven, even - uneven

    def put_grad(layer, direction, tile, value):
        start = direction * NODES + tile * 128
        gcells[rows_of(layer), start : start + 128] = value.reshape(LAYER, 128).astype(BF16)

    def flat_grads(layer):
        z_sign = (1 - 2 * lax.rem(layer, 2)).astype(F32)
        for pair in (0, 1):
            for tile, value in zip((pair, 3 - pair), combined(layer, 0, pair)):
                put_grad(layer, 0, tile, x_scale * (value - x_others(value)))
            for tile, value in zip((pair, 3 - pair), combined(layer, 1, pair)):
                put_grad(layer, 1, tile, y_scale * (value - y_others(value)))
        for tile, value in zip((1, 2), combined(layer, 2, 1)):
            put_grad(layer, 2, tile, z_sign * value)
        for tile, value in zip((0, 3), combined(layer, 2, 0)):
            store(xstd, layer, tile, z_sign * value)

    over(0, 4, flat_grads)

    def mean_face(layer, tile, other, there):
        value = load(xstd, layer, tile)
        put_grad(layer, 2, tile, value + jnp.where(low_half, there * (other - value), 0.0))

    for layer in range(4):
        mean_face(layer, 3, load(xstd, layer ^ 1, 3), 0.5)
        if layer in (1, 2):
            mean_face(layer, 0, load(xstd, 3 - layer, 0), 0.5)
        else:
            side = 0 if layer == 0 else 1
            other = None
            for k in range(4):
                term = coef8[k] * fghost[k, side].reshape(8, 8, 128)
                other = term if other is None else other + term
            mean_face(layer, 0, other, 0.5 * (has_up if side else has_down))

    def by_row(values):
        picked = values[3]
        for row in (2, 1, 0):
            picked = jnp.where(grp == row, values[row], picked)
        return picked

    own_first = by_row([first * CHUNK for first in FIRSTS])
    own_count = by_row(COUNTS)

    def pack(part, carry):
        cols = pl.ds(pl.multiple_of(part * 512, 512), 512)
        packed[:, cols] = jnp.dot(
            gpack[...], gcells[:, cols], preferred_element_type=F32
        ).astype(BF16)
        return carry

    lax.fori_loop(0, 3, pack, 0)

    def chunk_rows(chunk, base=0):
        return pl.ds(pl.multiple_of(base + chunk * CHUNK, CHUNK), CHUNK)

    def turn(step, count):
        return lax.rem(dom + step, count)

    def piece_copy(step, target, slot):
        chunk = turn(step, COUNTS[target])
        return remote(
            packed.at[chunk_rows(chunk, FIRSTS[target] * CHUNK)],
            recv.at[comp, chunk_rows(chunk)],
            asend.at[slot, step], arecv.at[comp, chunk], (target, dom),
        )

    def each_send(action):
        for row, targets in enumerate(((2, 1, 3), (3, 2, 0), (1,), (0,))):

            @pl.when(grp == row)
            def _():
                for step in range(MOST):
                    for slot, target in enumerate(targets):
                        if step < COUNTS[target]:
                            action(piece_copy(step, target, slot))

    each_send(lambda copy: copy.start())
    for row in range(4):

        @pl.when(grp == row)
        def _():
            slots = COUNTS[row] * CHUNK
            first = FIRSTS[row] * CHUNK
            recv[min(row, 2), 0:slots] = packed[first : first + slots, :]

    wide8 = [value.reshape(1, 8, 128) for value in coef]

    @pl.when(grp < 3)
    def _():
        def solve_layer(layer):
            for tile in every:
                value = wide8[0] * load(v0, layer, tile)
                for k in range(1, 4):
                    value = value + wide8[k] * load(basis[k], layer, tile)
                store(xs, layer - 4, tile, value)

        over(4, 8, solve_layer)
        for tile in every:
            mirror_layers(xs[:, tile * 128 : tile * 128 + 128], tile, xstd, 0, True)
        high, low = split(xstd[...])
        parts[0:CELLS, :] = high
        parts[CELLS : 2 * CELLS, :] = low
        out[...] = jnp.dot(ptr[...], parts[...], preferred_element_type=F32)

    def lambda_rows(block, carry):
        rows = pl.ds(pl.multiple_of(block * 16, 16), 16)
        for part in range(2):
            jac = [
                [
                    recv[c, rows, d * NODES + part * 256 : d * NODES + part * 256 + 256].astype(F32)
                    for d in range(3)
                ]
                for c in range(3)
            ]
            lam[rows, part * 256 : part * 256 + 256] = lambda_two(jac)
        return carry

    def natural_order(chunk):
        rows = chunk_rows(chunk)
        slots = pl.ds(pl.multiple_of(own_first + chunk * CHUNK, CHUNK), CHUNK)
        odd_x, odd_y, odd_z = [
            classes[slots, k * 128 : k * 128 + 128] > 0.5 for k in range(3)
        ]
        values = [lam[rows, tile * 128 : tile * 128 + 128] for tile in every]
        flipped = reversals(jnp.concatenate(values, 0))
        turned = []
        for tile in every:
            rev_x, rev_y, rev_xy = [
                part[tile * CHUNK : tile * CHUNK + CHUNK] for part in flipped
            ]
            turned.append(
                jnp.where(
                    odd_x,
                    jnp.where(odd_y, rev_xy, rev_x),
                    jnp.where(odd_y, rev_y, values[tile]),
                )
            )
        for tile in every:
            value = jnp.where(odd_z, turned[3 - tile], turned[tile])
            if tile >= 2:
                value = rotated(value, 64, 1)
            lam[rows, tile * 128 : tile * 128 + 128] = value

    here = pl.ds(pl.multiple_of(dom * 8, 8), 8)

    def each_owner(chunk, action, local):
        piece = lax.div(own_first, CHUNK) + chunk
        four = lax.div(piece, 2)
        for part in range(2):
            place = lax.rem(piece, 2) * 2 + part
            owner = place * 8 + lax.rem(place + lax.div(four, 2), 4) * 2 + lax.rem(four, 2)
            rows = pl.ds(pl.multiple_of(chunk * CHUNK + part * 8, 8), 8)
            own = (grp == 3) & (owner == dom)

            @pl.when(jnp.logical_not(own))
            def _():
                action(
                    remote(
                        lam.at[rows], lamrecv.at[here], osend.at[chunk * 2 + part], orecv,
                        (3, owner),
                    )
                )

            if local:

                @pl.when(own)
                def _():
                    lamrecv[here, :] = lam[rows, :]

    def analyse(chunk):
        for step in (1, 2):
            other = lax.rem(comp + step, 3)
            piece = recv.at[other, chunk_rows(chunk)]
            remote(
                piece, piece, asend.at[0, 0], arecv.at[other, chunk], (lax.rem(grp + 1, 4), dom)
            ).wait_recv()
        lambda_rows(chunk, 0)
        natural_order(chunk)
        each_owner(chunk, lambda copy: copy.start(), True)

    over(0, own_count, lambda step: analyse(turn(step, own_count)))
    over(
        0,
        own_count,
        lambda step: each_owner(turn(step, own_count), lambda copy: copy.wait_send(), False),
    )
    each_send(lambda copy: copy.wait_send())

    def wait_rows(count):
        piece = lamrecv.at[0 : 8 * count]
        remote(piece, piece, osend.at[0], orecv, (lax.rem(grp + 1, 4), dom)).wait_recv()

    four = lax.rem(lax.div(lax.rem(dom, 8), 2) - lax.div(dom, 8) + 4, 4) * 2 + lax.rem(dom, 2)
    to_itself = four * 2 + lax.div(dom, 16) >= FIRSTS[3]

    @pl.when((grp == 3) & to_itself)
    def _():
        wait_rows(31)

    @pl.when((grp == 3) & jnp.logical_not(to_itself))
    def _():
        wait_rows(32)

    @pl.when(grp == 3)
    def _():
        out[...] = lamrecv[...]


def lambda_two(jac):
    strain = [[0.5 * (jac[a][b] + jac[b][a]) for b in range(3)] for a in range(3)]
    spin = [[0.5 * (jac[a][b] - jac[b][a]) for b in range(3)] for a in range(3)]
    m = [[None] * 3 for _ in range(3)]
    for a in range(3):
        for b in range(a, 3):
            value = strain[a][0] * strain[0][b] + spin[a][0] * spin[0][b]
            for k in (1, 2):
                value = value + strain[a][k] * strain[k][b] + spin[a][k] * spin[k][b]
            m[a][b] = value
            m[b][a] = value
    for sweep in range(SWEEPS):
        for p, q, r in ((0, 1, 2), (0, 2, 1), (1, 2, 0)):
            last = sweep == SWEEPS - 1
            twice = 2.0 * m[p][q]
            gap = m[p][p] - m[q][q]
            square = twice * twice + gap * gap
            inverse = lax.rsqrt(jnp.maximum(square, 1e-36))
            length = square * inverse
            mean = 0.5 * (m[p][p] + m[q][q])
            m[p][p] = mean + 0.5 * length
            m[q][q] = mean - 0.5 * length
            if last and (p, q) == (1, 2):
                continue
            none = square < 1e-36
            cosine2 = jnp.where(none, 1.0, jnp.abs(gap) * inverse)
            sine2 = jnp.where(none, 0.0, twice * inverse)
            larger = 0.5 + 0.5 * cosine2
            root = lax.rsqrt(larger)
            big = larger * root
            small = 0.5 * sine2 * root
            flip = gap < 0.0
            sine_big = jnp.where(sine2 < 0.0, -big, big)
            cosine = jnp.where(flip, jnp.abs(small), big)
            sine = jnp.where(flip, sine_big, small)
            side_p = m[r][p]
            side_q = m[r][q]
            m[r][p] = m[p][r] = cosine * side_p + sine * side_q
            m[r][q] = m[q][r] = cosine * side_q - sine * side_p
            m[p][q] = m[q][p] = jnp.zeros_like(side_p)
    diagonal = [m[0][0], m[1][1], m[2][2]]
    largest = jnp.maximum(jnp.maximum(diagonal[0], diagonal[1]), diagonal[2])
    smallest = jnp.minimum(jnp.minimum(diagonal[0], diagonal[1]), diagonal[2])
    return diagonal[0] + diagonal[1] + diagonal[2] - largest - smallest


def per_device(forcing, viscosity, mass_coef, element_order, owner):
    mats, flat, lanes = tables()
    vmem = pl.BlockSpec(memory_space=pltpu.VMEM)
    hbm = pl.BlockSpec(memory_space=pltpu.HBM)
    wide = (12 * LAYER, NODES)
    own = (CELLS, NODES)
    dma = pltpu.SemaphoreType.DMA
    result = pl.pallas_call(
        kernel,
        out_shape=pltpu.VMEM(own, F32),
        in_specs=[hbm] * 8,
        out_specs=vmem,
        scratch_shapes=[
            pltpu.VMEM(own, F32),
            pltpu.VMEM((8, NODES), F32),
            pltpu.VMEM((640, 384), BF16),
            pltpu.VMEM((1, CELLS), jnp.int32),
            pltpu.VMEM((1, CELLS), jnp.int32),
            pltpu.VMEM((4, 768, 256), BF16),
            pltpu.VMEM((8, CELLS), F32),
            pltpu.VMEM((2, 8, CELLS), F32),
            pltpu.VMEM((CELLS, 2 * CELLS), BF16),
            pltpu.VMEM((CELLS, 2 * CELLS), BF16),
            pltpu.VMEM((2 * CELLS, NODES), BF16),
            pltpu.VMEM((12 * LAYER, 128), F32),
            pltpu.VMEM((12 * LAYER, 128), F32),
            pltpu.VMEM(wide, F32),
            pltpu.VMEM(wide, F32),
            pltpu.VMEM(wide, F32),
            pltpu.VMEM((12 * LAYER, 3 * NODES), BF16),
            pltpu.VMEM((12 * LAYER, 3 * NODES), BF16),
            pltpu.VMEM((12 * LAYER, 3 * NODES), BF16),
            pltpu.VMEM((12 * LAYER, 3 * NODES), BF16),
            pltpu.VMEM(wide, F32),
            pltpu.VMEM(wide, F32),
            pltpu.VMEM(wide, F32),
            pltpu.VMEM(wide, F32),
            pltpu.VMEM(own, F32),
            pltpu.VMEM(own, F32),
            pltpu.VMEM((4, CELLS, 3 * NODES), F32),
            pltpu.VMEM((CELLS, CELLS), BF16),
            pltpu.VMEM((CELLS, 384), F32),
            pltpu.VMEM((CELLS, 3 * NODES), BF16),
            pltpu.VMEM((2, LAYER, 128), F32),
            pltpu.VMEM((2, LAYER, 128), F32),
            pltpu.VMEM((4, 2, LAYER, 128), F32),
            pltpu.VMEM((8, 128), F32),
            pltpu.VMEM((DOMS, 8, 128), F32),
            pltpu.VMEM((CELLS, 3 * NODES), BF16),
            pltpu.VMEM((3, MOST * CHUNK, 3 * NODES), BF16),
            pltpu.VMEM((MOST * CHUNK, NODES), F32),
            pltpu.VMEM(own, F32),
            dma((6,)), dma((12,)), dma, dma((2,)), dma((2,)), dma((10,)), dma((10,)), dma((2,)),
            dma((2,)), dma, dma, dma((3, MOST)), dma((3, MOST)), dma((2 * MOST,)), dma,
        ],
        compiler_params=pltpu.CompilerParams(
            collective_id=0, has_side_effects=True, vmem_limit_bytes=60 * 1024 * 1024
        ),
        name="solve_and_analyse",
    )(
        forcing, viscosity[None], mass_coef[None], element_order, owner,
        jnp.asarray(lanes), jnp.asarray(flat), jnp.asarray(mats),
    )
    return result[None]


def solution(mesh):
    in_specs = (P(None, "dom", None), P("dom"), P("dom"), P("dom", None), P("dom", None))
    out_specs = P("grp", "dom", None)
    return jax.shard_map(
        per_device, mesh=mesh, in_specs=in_specs, out_specs=out_specs, check_vma=False
    )
```

```python
import functools

import jax
import jax.numpy as jnp
import ml_dtypes
import numpy as np
from jax import lax
from jax.experimental import pallas as pl
from jax.experimental.pallas import tpu as pltpu
from jax.sharding import PartitionSpec as P

NP = 8
ITERS = 4
SWEEPS = 4
LAYER = 64
CELLS = 256
NODES = 512
DOMS = 32
CHUNK = 16
COUNTS = (5, 5, 4, 2)
FIRSTS = (0, 5, 10, 14)
MOST = max(COUNTS)
BASIS_LOW = 0.3
BASIS_HIGH = 2.0
THETA = 0.5 * (BASIS_LOW + BASIS_HIGH)
DELTA = 0.5 * (BASIS_HIGH - BASIS_LOW)
MESH = pl.DeviceIdType.MESH
F32 = jnp.float32
BF16 = jnp.bfloat16


def legendre_values(points, node_count):
    legendre = np.zeros((points.shape[0], node_count))
    legendre[:, 0] = 1.0
    legendre[:, 1] = points
    for poly_order in range(2, node_count):
        legendre[:, poly_order] = (
            (2 * poly_order - 1) * points * legendre[:, poly_order - 1]
            - (poly_order - 1) * legendre[:, poly_order - 2]
        ) / poly_order
    return legendre


def lobatto_table(node_count):
    degree = node_count - 1
    points = np.cos(np.pi * np.arange(node_count) / degree)
    for attempt in range(60):
        legendre = legendre_values(points, node_count)
        points = points - (points * legendre[:, degree] - legendre[:, degree - 1]) / (
            node_count * legendre[:, degree]
        )
    points = points[::-1].copy()
    end_values = legendre_values(points, node_count)[:, degree]
    weights = 2.0 / (degree * node_count * end_values * end_values)
    spacing = points[:, None] - points[None, :] + np.eye(node_count)
    diff_matrix = end_values[:, None] / end_values[None, :] / spacing
    diff_matrix = diff_matrix * (1.0 - np.eye(node_count))
    diff_matrix[0, 0] = -degree * node_count / 4.0
    diff_matrix[-1, -1] = degree * node_count / 4.0
    return (weights, diff_matrix)


def split_rows(matrix):
    high = matrix.astype(np.float32).astype(ml_dtypes.bfloat16)
    low = (matrix - high.astype(np.float64)).astype(np.float32).astype(ml_dtypes.bfloat16)
    return high, low


def tables():
    weights, diff = lobatto_table(NP)
    eye = np.eye(NP)
    cube = (
        weights[:, None, None] * weights[None, :, None] * weights[None, None, :]
    ).reshape(-1)
    directional = [
        np.kron(eye, np.kron(eye, diff)),
        np.kron(eye, np.kron(diff, eye)),
        np.kron(diff, np.kron(eye, eye)),
    ]
    stiff = np.zeros((NODES, NODES))
    for matrix in directional:
        stiff = stiff + matrix.T @ (cube[:, None] * matrix)
    flip = np.arange(NODES).reshape(NP, LAYER)[::-1][: NP // 2].reshape(-1)
    mats = []
    for matrix in (stiff, directional[2]):
        near, far = matrix[:256, :256], matrix[:256, flip]
        for block in (0.5 * (near + far), 0.5 * (near - far)):
            mats.append(np.stack(split_rows(block.T)))
    mats = np.stack(mats)
    flat = np.concatenate([directional[0].T[:128, :128], directional[1].T[:128, :128]], 1)
    high, low = split_rows(flat)
    flat = np.concatenate([high, high, low], 0)
    lanes = np.zeros((8, NODES), np.float32)
    lanes[0] = cube
    lanes[1] = np.diag(stiff)
    lanes[2] = np.repeat(diff[0], LAYER)
    order = [0, 1, 2, 3, 5, 4, 7, 6]
    lanes = lanes.reshape(8, NP, LAYER)[:, order].reshape(8, NODES)
    natural = cube.reshape(NP, LAYER).astype(np.float32).reshape(-1)
    lanes[3] = natural
    back = eye[::-1]
    half = np.eye(2)
    mirror = np.concatenate(
        [
            np.kron(half, np.kron(eye, back)),
            np.kron(half, np.kron(back, eye)),
            np.kron(half, np.kron(back, back)),
        ],
        1,
    ).astype(ml_dtypes.bfloat16)
    wide = np.concatenate([flat, np.zeros((384, 128), flat.dtype)], 1)
    return mats, np.concatenate([wide, mirror, mirror], 0), lanes


def rotated(value, shift, axis):
    return pltpu.roll(value, shift % value.shape[axis], axis)


def kernel(
    forcing, visc_in, mass_in, order_in, owner_in, lanes_in, flat_in, mats,
    out,
    fsc, lanes, flat, order_sc, owner_sc, weights, par, parn, pone, ptr, parts, visc, mass, raw, tmp,
    inv, lhs0, lhs1, lhs2, lhs3, v0, v1, v2, v3, xs, xstd, grads, gpack, classes, gcells, fsend, frecv, fghost, moments,
    red, packed, recv, lam, lamrecv,
    ssem, wsem, fsem, psend, precv, gsend, grecv, f3send, f3recv, rsend, rrecv, asend, arecv,
    osend, orecv,
):
    grp = lax.axis_index("grp")
    dom = lax.axis_index("dom")
    comp = jnp.minimum(grp, 2)
    up = lax.rem(dom + 1, DOMS)
    down = lax.rem(dom + DOMS - 1, DOMS)
    barrier = pltpu.get_barrier_semaphore()
    basis = (v0, v1, v2, v3)
    lefts = (lhs0, lhs1, lhs2, lhs3)
    every = (0, 1, 2, 3)

    at_y = [lax.rem(lax.div(dom, 8) + k, 4) * 8 for k in range(4)]
    at_z = [lax.rem(lax.div(dom, 2) + k, 4) * 2 for k in range(4)]
    at_core = [lax.rem(dom + k, 2) for k in range(2)]

    def hops(offset):
        return sum(min(k, 4 - k) for k in (offset // 8, offset // 2 % 4))

    peers = [
        (offset, at_y[offset // 8] + at_z[offset // 2 % 4] + at_core[offset % 2])
        for offset in sorted(range(1, DOMS), key=lambda offset: -hops(offset))
    ]

    for offset, peer in peers:
        pl.semaphore_signal(barrier, inc=1, device_id=(grp, peer), device_id_type=MESH)
    for step in range(1, 4):
        pl.semaphore_signal(
            barrier, inc=1, device_id=(lax.rem(grp + step, 4), dom), device_id_type=MESH
        )

    load_small = [
        pltpu.make_async_copy(source, target, ssem.at[k])
        for k, (source, target) in enumerate(
            (
                (visc_in, par.at[0:1]),
                (mass_in, par.at[1:2]),
                (order_in, order_sc),
                (owner_in, owner_sc),
                (lanes_in, lanes),
                (flat_in, flat),
            )
        )
    ]
    for copy in load_small:
        copy.start()
    load_force = pltpu.make_async_copy(forcing.at[comp], fsc, fsem)
    load_force.start()
    load_mats = []
    for which in range(4):
        for part, source in enumerate((0, 0, 1)):
            copy = pltpu.make_async_copy(
                mats.at[which, source],
                weights.at[which, part * 256 : part * 256 + 256],
                wsem.at[3 * which + part],
            )
            copy.start()
            load_mats.append(copy)

    lane = lax.broadcasted_iota(jnp.int32, (8, 128), 1)
    sub = lax.broadcasted_iota(jnp.int32, (8, 128), 0)
    node_i = lax.rem(lane, 8)
    node_j = lax.rem(lane // 8, 8)
    odd = lax.rem(sub, 2) == 1
    first_i = node_i == 0
    last_i = node_i == 7
    take_up = ((last_i & jnp.logical_not(odd)) | (first_i & odd & (sub < 7)))
    take_down = ((last_i & odd) | (first_i & jnp.logical_not(odd) & (sub > 0)))
    has_up = jnp.where(dom < DOMS - 1, 1.0, 0.0).astype(F32)
    has_down = jnp.where(dom > 0, 1.0, 0.0).astype(F32)

    def wide(mask):
        return jnp.broadcast_to(mask[None], (8, 8, 128))

    x_up = wide(take_up)
    x_down = wide(take_down)
    x_odd = wide(odd)
    y_last = wide(node_j == 7)
    y_first = wide(node_j == 0)
    low_half = wide(lane < LAYER)

    def x_others(a):
        above = rotated(a, -1, 1)
        below = rotated(a, 1, 1)
        return jnp.where(x_up, above, jnp.where(x_down, below, 0.0))

    def y_others(a):
        blank = jnp.zeros((1, 8, 128), F32)
        last = jnp.concatenate([a[k ^ 1 : (k ^ 1) + 1] for k in range(8)], 0)
        first = jnp.concatenate(
            [blank] + [a[k : k + 1] for k in (2, 1, 4, 3, 6, 5)] + [blank], 0
        )
        return jnp.where(y_last, last, jnp.where(y_first, first, 0.0))

    def xy_sum(a):
        a = a + x_others(a)
        return a + y_others(a)

    def rows_of(layer):
        if isinstance(layer, int):
            return slice(layer * LAYER, layer * LAYER + LAYER)
        return pl.ds(pl.multiple_of(layer * LAYER, LAYER), LAYER)

    def load(ref, layer, tile):
        return ref[rows_of(layer), tile * 128 : tile * 128 + 128].reshape(8, 8, 128)

    def store(ref, layer, tile, value):
        ref[rows_of(layer), tile * 128 : tile * 128 + 128] = value.reshape(LAYER, 128)

    def column(ref, layer):
        return ref[rows_of(layer), :].reshape(8, 8, 128)

    def table(row, tile):
        return lanes[row : row + 1, tile * 128 : tile * 128 + 128].reshape(1, 1, 128)

    def split(value):
        high = value.astype(BF16)
        return high, (value - high.astype(F32)).astype(BF16)

    def store_lhs(lhs, layer, pair, first, second):
        for start, value in ((0, first + second), (768, first - second)):
            start = start + pair * 128
            high, low = split(value.reshape(LAYER, 128))
            lhs[rows_of(layer), start : start + 128] = high
            lhs[rows_of(layer), start + 256 : start + 384] = low
            lhs[rows_of(layer), start + 512 : start + 640] = high

    def reversals(value):
        total = jnp.dot(
            jnp.concatenate(split(value), 1), flat[384:640, :], preferred_element_type=F32
        )
        return total[:, 0:128], total[:, 128:256], total[:, 256:384]

    def mirror_layers(value, tile, target, base, back):
        flipped = reversals(value)
        for layer in range(4):
            rows = slice(layer * LAYER, layer * LAYER + LAYER)
            plain, rev_x, rev_y, rev_xy = [
                part[rows].reshape(8, 8, 128) for part in (value,) + flipped
            ]
            even_y = jnp.where(x_odd, rev_x, plain)
            odd_y = jnp.where(x_odd, rev_xy, rev_y)
            mixed = jnp.concatenate(
                [(odd_y if k % 2 else even_y)[k : k + 1] for k in range(8)], 0
            )
            place = 3 - tile if layer % 2 else tile
            if (place if back else tile) >= 2:
                mixed = rotated(mixed, 64, 2)
            store(target, base + layer, place, mixed)

    def over(low, high, body):
        lax.fori_loop(low, high, lambda layer, carry: (body(layer), carry)[1], 0)

    cell_sub = lax.broadcasted_iota(jnp.int32, (CELLS, CELLS), 0).astype(F32)
    cell_lane = lax.broadcasted_iota(jnp.int32, (CELLS, CELLS), 1).astype(F32)
    for copy in load_small:
        copy.wait()
    par[2:3, :] = order_sc[...].astype(F32)
    par[3:8, :] = jnp.zeros((5, CELLS), F32)

    def coefficients(ref, base, scale):
        hit = ref[2:3, :] == cell_sub
        for row, target in ((0, visc), (1, mass)):
            col = jnp.sum(jnp.where(hit, ref[row : row + 1, :], 0.0), axis=1, keepdims=True)
            target[base : base + CELLS, :] = jnp.broadcast_to(col * scale, (CELLS, 128))
        return hit

    one_hot = jnp.where(par[2:3, :] == cell_sub, 1.0, 0.0).astype(BF16)
    pone[:, 0:CELLS] = one_hot
    pone[:, CELLS : 2 * CELLS] = one_hot
    load_force.wait()
    high, low = split(fsc[...])
    parts[0:CELLS, :] = high
    parts[CELLS : 2 * CELLS, :] = low
    fsc[...] = jnp.dot(pone[...], parts[...], preferred_element_type=F32) * lanes[3:4, :]
    for tile in every:
        mirror_layers(fsc[:, tile * 128 : tile * 128 + 128], tile, raw, 4, False)

    pl.semaphore_wait(barrier, DOMS - 1 + 3)

    def remote(src, dst, send, recv_sem, device):
        return pltpu.make_async_remote_copy(
            src_ref=src, dst_ref=dst, send_sem=send, recv_sem=recv_sem,
            device_id=device, device_id_type=MESH,
        )

    par_copies = [
        remote(par, parn.at[0], psend.at[0], precv.at[0], (grp, up)),
        remote(par, parn.at[1], psend.at[1], precv.at[1], (grp, down)),
    ]
    def ghost(source, layers, first, last, target, slot, device):
        return remote(
            raw.at[source * LAYER : (source + layers) * LAYER, first:last],
            raw.at[target * LAYER : (target + layers) * LAYER, first:last],
            gsend.at[slot], grecv.at[slot], (grp, device),
        )

    near_copies = [
        ghost(7, 1, 0, 512, 3, 0, up),
        ghost(4, 1, 0, 512, 8, 1, down),
        ghost(6, 1, 384, 512, 2, 2, up),
        ghost(5, 1, 384, 512, 9, 3, down),
    ]
    far_copies = [
        ghost(6, 1, 0, 384, 2, 4, up),
        ghost(5, 1, 0, 384, 9, 5, down),
        ghost(5, 1, 0, 512, 1, 6, up),
        ghost(6, 1, 0, 512, 10, 7, down),
        ghost(4, 1, 384, 512, 0, 8, up),
        ghost(7, 1, 384, 512, 11, 9, down),
    ]
    for copy in par_copies + near_copies + far_copies:
        copy.start()

    coefficients(par, CELLS, 1.0)
    order_col = jnp.sum(
        jnp.where(cell_sub == cell_lane, par[2:3, :], 0.0), axis=1, keepdims=True
    )
    one_hot = jnp.where(order_col == cell_lane, 1.0, 0.0).astype(BF16)
    ptr[:, 0:CELLS] = one_hot
    ptr[:, CELLS : 2 * CELLS] = one_hot
    owner_row = owner_sc[...].astype(F32)
    owner_col = jnp.sum(
        jnp.where(cell_sub == cell_lane, owner_row, 0.0), axis=1, keepdims=True
    )
    same = (owner_col == owner_row) & (cell_sub < cell_lane)
    rank_row = jnp.sum(jnp.where(same, 1.0, 0.0), axis=0, keepdims=True)
    owner_int = owner_sc[...]
    place = owner_int >> 3
    piece_row = ((((owner_int >> 1) - place) & 3) << 1) + (owner_int & 1)
    first_row = (piece_row * 4 + place).astype(F32)
    dest_row = jnp.where(owner_row >= 0.0, first_row * 8.0 + rank_row, -1.0)
    slot_of = jnp.where(dest_row == cell_sub, 1.0, 0.0).astype(BF16)
    gpack[...] = jnp.dot(slot_of, one_hot, preferred_element_type=F32).astype(BF16)
    cell_id = lax.broadcasted_iota(jnp.int32, (CELLS, 128), 0)
    for k, width in enumerate((1, 8, 64)):
        parity = lax.rem(cell_id // width, 2).astype(F32).astype(BF16)
        classes[:, k * 128 : k * 128 + 128] = jnp.dot(
            gpack[...], parity, preferred_element_type=F32
        )

    for copy in par_copies:
        copy.wait()
    coefficients(parn.at[0], 0, has_down)
    coefficients(parn.at[1], 2 * CELLS, has_up)

    def partners(layer):
        parity = layer % 2 if isinstance(layer, int) else lax.rem(layer, 2)
        return {0: layer - 1 + 2 * parity, 3: layer + 1 - 2 * parity}

    def face_sum(ref, layer, tile):
        value = load(ref, layer, tile)
        other = load(ref, partners(layer)[tile], tile)
        return value + jnp.where(low_half, other, 0.0)

    def put_inverse(layer, tile, diag):
        store(inv, layer, tile, jnp.where(diag > 0.0, (2.0 / DELTA) / diag, 0.0))

    def diagonal(layer, tiles):
        coef_v = column(visc, layer)
        coef_m = column(mass, layer)
        for tile in tiles:
            diag = xy_sum(coef_v * table(1, tile) + coef_m * table(0, tile))
            if tile in (0, 3):
                store(tmp, layer, tile, diag)
            else:
                put_inverse(layer, tile, diag)

    diagonal(0, (3,))
    over(1, 11, lambda layer: diagonal(layer, every))
    diagonal(11, (3,))

    def diagonal_faces(layer):
        for tile in (0, 3):
            put_inverse(layer, tile, face_sum(tmp, layer, tile))

    over(1, 11, diagonal_faces)

    def first_value(layer, tile, force):
        value = force * load(inv, layer, tile) * (0.5 * DELTA)
        store(v0, layer, tile, value)
        return value

    def put_first(layer, pair, forces):
        values = [
            first_value(layer, tile, force) for tile, force in zip((pair, 3 - pair), forces)
        ]
        store_lhs(lhs0, layer, pair, *values)

    def assemble(layer, tiles, scale):
        sums = []
        for tile in tiles:
            force = load(raw, layer, tile)
            if scale is not None:
                force = force * scale
            force = xy_sum(force)
            if tile in (0, 3):
                store(tmp, layer, tile, force)
            else:
                sums.append(force)
        if sums:
            put_first(layer, 1, sums)

    over(4, 8, lambda layer: assemble(layer, every, None))
    for copy in load_mats:
        copy.wait()
    def multiply(lhs, low, high, which, target, first=0):
        for part in range(2):
            target[:, first + part * 256 : first + part * 256 + 256] = jnp.dot(
                lhs[low * LAYER : high * LAYER, part * 768 : part * 768 + 768],
                weights[2 * which + part],
                preferred_element_type=F32,
            )

    def advance(step, layer, pair, totals):
        values = []
        for tile, total in zip((pair, 3 - pair), totals):
            value = total * load(inv, layer, tile)
            current = load(basis[step], layer, tile)
            if step == 0:
                value = 0.5 * value - (THETA / DELTA) * current
            else:
                value = value - (2.0 * THETA / DELTA) * current
                value = value - load(basis[step - 1], layer, tile)
            store(basis[step + 1], layer, tile, value)
            values.append(value)
        store_lhs(lefts[step + 1], layer, pair, *values)

    def apply(step, layer, tiles, sums, going):
        coef_v = column(visc, layer)
        coef_m = column(mass, layer)
        for pair in (1, 0):
            if pair not in tiles and 3 - pair not in tiles:
                continue
            even = load(tmp, layer, pair)
            uneven = load(tmp, layer, 2 + pair)
            images = []
            for tile, product in ((pair, even + uneven), (3 - pair, even - uneven)):
                if tile not in tiles:
                    continue
                value = load(basis[step], layer, tile)
                weighted = coef_m * table(0, tile)
                image = coef_v * product + weighted * value
                if sums is not None:
                    diag = coef_v * table(1, tile) + weighted
                    sums = (
                        sums[0] + jnp.sum(value * image, axis=0),
                        sums[1] + jnp.sum(value * value * diag, axis=0),
                    )
                if going:
                    image = xy_sum(image)
                    if pair == 0:
                        store(tmp, layer, tile, image)
                    else:
                        images.append(image)
            if images:
                advance(step, layer, 1, images)
        return sums

    def faces(step, layer):
        advance(step, layer, 0, [face_sum(tmp, layer, tile) for tile in (0, 3)])

    blank_sums = (jnp.zeros((8, 128), F32), jnp.zeros((8, 128), F32))

    def own_apply(step, going):
        sums = lax.fori_loop(
            4, 8, lambda layer, carry: apply(step, layer, every, carry, going), blank_sums
        )
        moments[step : step + 1, :] = jnp.sum(sums[0], axis=0, keepdims=True)
        moments[4 + step : 5 + step, :] = jnp.sum(sums[1], axis=0, keepdims=True)

    def first_faces(layer):
        put_first(layer, 0, [face_sum(tmp, layer, tile) for tile in (0, 3)])

    for copy in near_copies:
        copy.wait()
    assemble(2, (3,), has_down)
    assemble(3, every, has_down)
    assemble(8, every, has_up)
    assemble(9, (3,), has_up)
    over(3, 9, first_faces)
    for layer in (2, 9):
        first_value(layer, 3, face_sum(tmp, layer, 3))
    multiply(lhs0, 3, 9, 0, tmp.at[3 * LAYER : 9 * LAYER])
    own_apply(0, True)
    for layer in (3, 8):
        apply(0, layer, every, None, True)

    for copy in far_copies:
        copy.wait()
    assemble(0, (3,), has_down)
    assemble(1, every, has_down)
    assemble(2, (0, 1, 2), has_down)
    assemble(9, (0, 1, 2), has_up)
    assemble(10, every, has_up)
    assemble(11, (3,), has_up)
    for layer in (1, 10):
        first_faces(layer)
    for layer in (2, 9):
        value = first_value(layer, 0, face_sum(tmp, layer, 0))
        store_lhs(lhs0, layer, 0, value, load(v0, layer, 3))
    far_rows = (slice(1 * LAYER, 3 * LAYER), slice(9 * LAYER, 11 * LAYER))
    for part in range(2):
        product = jnp.dot(
            jnp.concatenate(
                [lhs0[rows, part * 768 : part * 768 + 768] for rows in far_rows], 0
            ),
            weights[part],
            preferred_element_type=F32,
        )
        for side, rows in enumerate(far_rows):
            tmp[rows, part * 256 : part * 256 + 256] = product[
                side * 2 * LAYER : (side + 1) * 2 * LAYER
            ]
    apply(0, 1, (0,), None, True)
    apply(0, 2, every, None, True)
    apply(0, 9, every, None, True)
    apply(0, 10, (0,), None, True)
    over(2, 10, lambda layer: faces(0, layer))

    for step in range(1, ITERS):
        low, high = 1 + step, 11 - step
        going = step + 1 < ITERS
        multiply(lefts[step], low, high, 0, tmp.at[low * LAYER : high * LAYER])
        own_apply(step, going)
        if going:
            inward = 0 if low % 2 else 3
            apply(step, low, (inward,), None, True)
            over(low + 1, 4, lambda layer: apply(step, layer, every, None, True))
            over(8, high - 1, lambda layer: apply(step, layer, every, None, True))
            apply(step, high - 1, (inward,), None, True)
            over(low + 1, high - 1, lambda layer: faces(step, layer))

    red[0] = moments[...]
    for offset, peer in peers:
        remote(moments, red.at[offset], rsend, rrecv, (grp, peer)).start()

    def end_face(ref, layer):
        total = load(ref, layer, 0) * table(2, 0)
        for tile in (1, 2, 3):
            total = total + load(ref, layer, tile) * table(2, tile)
        total = total + rotated(total, 64, 2)
        return -total if layer % 2 else total

    fsend[0] = end_face(v3, 7).reshape(LAYER, 128)
    fsend[1] = end_face(v3, 4).reshape(LAYER, 128)
    face_copies = [
        remote(fsend.at[0], frecv.at[0], f3send.at[0], f3recv.at[0], (grp, up)),
        remote(fsend.at[1], frecv.at[1], f3send.at[1], f3recv.at[1], (grp, down)),
    ]
    for copy in face_copies:
        copy.start()

    own_rows = slice(4 * LAYER, 8 * LAYER)
    for index in range(ITERS):
        left = jnp.concatenate(
            [
                jnp.concatenate(
                    [
                        lefts[index][own_rows, start + part * 256 : start + part * 256 + 128]
                        for part in range(3)
                    ],
                    1,
                )
                for start in (0, 128, 768, 896)
            ],
            0,
        )
        both = jnp.dot(left, flat[0:384, 0:256], preferred_element_type=F32)
        for part in range(4):
            rows = slice(part * CELLS, part * CELLS + CELLS)
            grads[index, :, part * 128 : part * 128 + 128] = both[rows, 0:128]
            grads[index, :, NODES + part * 128 : NODES + part * 128 + 128] = both[rows, 128:256]
        multiply(lefts[index], 4, 8, 1, grads.at[index], 2 * NODES)
        if index < 3:
            fghost[index, 0] = end_face(basis[index], 3).reshape(LAYER, 128)
            fghost[index, 1] = end_face(basis[index], 8).reshape(LAYER, 128)

    for copy in face_copies:
        copy.wait()
    for side in range(2):
        fghost[3, side] = frecv[side]

    whole = remote(red.at[1:DOMS], red.at[1:DOMS], rsend, rrecv, (grp, up))
    whole.wait_send()
    whole.wait_recv()

    total = jnp.sum(red[...], axis=0)
    total = jnp.broadcast_to(jnp.sum(total, axis=1, keepdims=True), (8, 128))
    moments[...] = total

    def scalar(row):
        return jnp.broadcast_to(moments[row : row + 1, :], (8, 128))

    alpha = [scalar(row) for row in range(4)]
    beta = [scalar(4 + row) for row in range(4)]
    gamma = [(alpha[k] - THETA * beta[k]) * (1.0 / DELTA) for k in range(4)]
    mu = [beta[0], gamma[0]]
    ahead = gamma[0]
    for k in range(1, 4):
        ahead = 2.0 * gamma[k] - ahead
        mu.append(2.0 * beta[k] - mu[0])
        mu.append(2.0 * ahead - mu[1])

    def inner(i, j):
        return 0.5 * (mu[i + j] + mu[abs(i - j)])

    gram = [
        [
            DELTA * 0.5 * (inner(i, j + 1) + inner(i, abs(j - 1))) + THETA * inner(i, j)
            for j in range(4)
        ]
        for i in range(4)
    ]
    right = [mu[k] for k in range(4)]
    pivots = []
    for k in range(4):
        original = DELTA * 0.5 * (inner(k, k + 1) + inner(k, abs(k - 1))) + THETA * inner(k, k)
        pivot = gram[k][k]
        good = pivot > 1e-7 * original
        inverse = jnp.where(good, 1.0 / jnp.where(good, pivot, 1.0), 0.0)
        pivots.append(inverse)
        for i in range(k + 1, 4):
            factor = gram[i][k] * inverse
            for j in range(k + 1, 4):
                gram[i][j] = gram[i][j] - factor * gram[k][j]
            right[i] = right[i] - factor * right[k]
    coef = [None] * 4
    for k in (3, 2, 1, 0):
        value = right[k]
        for j in range(k + 1, 4):
            value = value - gram[k][j] * coef[j]
        coef[k] = value * pivots[k]

    coef8 = [(value * (1.0 / NP)).reshape(1, 8, 128) for value in coef]
    coef16 = [0.5 * value for value in coef8]
    x_sign = jnp.where(odd, -1.0, 1.0).reshape(1, 8, 128)
    x_scale = jnp.where(take_up | take_down, 0.5, 1.0).reshape(1, 8, 128) * x_sign
    y_half = jnp.where((node_j == 7) | (node_j == 0), 0.5, 1.0).reshape(1, 8, 128)
    y_end = jnp.where(node_j == 7, 0.5, 1.0).reshape(1, 8, 128)
    y_scale = jnp.concatenate(
        [y_end, -y_half, y_half, -y_half, y_half, -y_half, y_half, -y_end], 0
    )

    def combined(layer, direction, pair):
        parts_of = []
        scale = coef8 if direction == 2 else coef16
        for start in (0, 256):
            start = start + direction * NODES + pair * 128
            value = None
            for k in range(4):
                term = scale[k] * grads[k, rows_of(layer), start : start + 128].reshape(8, 8, 128)
                value = term if value is None else value + term
            parts_of.append(value)
        even, uneven = parts_of
        if direction == 2:
            return even + uneven, uneven - even
        return even + uneven, even - uneven

    def put_grad(layer, direction, tile, value):
        start = direction * NODES + tile * 128
        gcells[rows_of(layer), start : start + 128] = value.reshape(LAYER, 128).astype(BF16)

    def flat_grads(layer):
        z_sign = (1 - 2 * lax.rem(layer, 2)).astype(F32)
        for pair in (0, 1):
            for tile, value in zip((pair, 3 - pair), combined(layer, 0, pair)):
                put_grad(layer, 0, tile, x_scale * (value - x_others(value)))
            for tile, value in zip((pair, 3 - pair), combined(layer, 1, pair)):
                put_grad(layer, 1, tile, y_scale * (value - y_others(value)))
        for tile, value in zip((1, 2), combined(layer, 2, 1)):
            put_grad(layer, 2, tile, z_sign * value)
        for tile, value in zip((0, 3), combined(layer, 2, 0)):
            store(xstd, layer, tile, z_sign * value)

    over(0, 4, flat_grads)

    def mean_face(layer, tile, other, there):
        value = load(xstd, layer, tile)
        put_grad(layer, 2, tile, value + jnp.where(low_half, there * (other - value), 0.0))

    for layer in range(4):
        mean_face(layer, 3, load(xstd, layer ^ 1, 3), 0.5)
        if layer in (1, 2):
            mean_face(layer, 0, load(xstd, 3 - layer, 0), 0.5)
        else:
            side = 0 if layer == 0 else 1
            other = None
            for k in range(4):
                term = coef8[k] * fghost[k, side].reshape(8, 8, 128)
                other = term if other is None else other + term
            mean_face(layer, 0, other, 0.5 * (has_up if side else has_down))

    def by_row(values):
        picked = values[3]
        for row in (2, 1, 0):
            picked = jnp.where(grp == row, values[row], picked)
        return picked

    own_first = by_row([first * CHUNK for first in FIRSTS])
    own_count = by_row(COUNTS)

    def pack(part, carry):
        cols = pl.ds(pl.multiple_of(part * 512, 512), 512)
        packed[:, cols] = jnp.dot(
            gpack[...], gcells[:, cols], preferred_element_type=F32
        ).astype(BF16)
        return carry

    lax.fori_loop(0, 3, pack, 0)

    def chunk_rows(chunk, base=0):
        return pl.ds(pl.multiple_of(base + chunk * CHUNK, CHUNK), CHUNK)

    def turn(step, count):
        return lax.rem(dom + step, count)

    def piece_copy(step, target, slot):
        chunk = turn(step, COUNTS[target])
        return remote(
            packed.at[chunk_rows(chunk, FIRSTS[target] * CHUNK)],
            recv.at[comp, chunk_rows(chunk)],
            asend.at[slot, step], arecv.at[comp, chunk], (target, dom),
        )

    def each_send(action):
        for row, targets in enumerate(((2, 1, 3), (3, 2, 0), (1,), (0,))):

            @pl.when(grp == row)
            def _():
                for step in range(MOST):
                    for slot, target in enumerate(targets):
                        if step < COUNTS[target]:
                            action(piece_copy(step, target, slot))

    each_send(lambda copy: copy.start())
    for row in range(4):

        @pl.when(grp == row)
        def _():
            slots = COUNTS[row] * CHUNK
            first = FIRSTS[row] * CHUNK
            recv[min(row, 2), 0:slots] = packed[first : first + slots, :]

    wide8 = [value.reshape(1, 8, 128) for value in coef]

    @pl.when(grp < 3)
    def _():
        def solve_layer(layer):
            for tile in every:
                value = wide8[0] * load(v0, layer, tile)
                for k in range(1, 4):
                    value = value + wide8[k] * load(basis[k], layer, tile)
                store(xs, layer - 4, tile, value)

        over(4, 8, solve_layer)
        for tile in every:
            mirror_layers(xs[:, tile * 128 : tile * 128 + 128], tile, xstd, 0, True)
        high, low = split(xstd[...])
        parts[0:CELLS, :] = high
        parts[CELLS : 2 * CELLS, :] = low
        out[...] = jnp.dot(ptr[...], parts[...], preferred_element_type=F32)

    def lambda_rows(block, carry):
        rows = pl.ds(pl.multiple_of(block * 16, 16), 16)
        jac = [
            [recv[c, rows, d * NODES : d * NODES + NODES].astype(F32) for d in range(3)]
            for c in range(3)
        ]
        lam[rows, :] = lambda_two(jac)
        return carry

    def natural_order(chunk):
        rows = chunk_rows(chunk)
        slots = pl.ds(pl.multiple_of(own_first + chunk * CHUNK, CHUNK), CHUNK)
        odd_x, odd_y, odd_z = [
            classes[slots, k * 128 : k * 128 + 128] > 0.5 for k in range(3)
        ]
        values = [lam[rows, tile * 128 : tile * 128 + 128] for tile in every]
        flipped = reversals(jnp.concatenate(values, 0))
        turned = []
        for tile in every:
            rev_x, rev_y, rev_xy = [
                part[tile * CHUNK : tile * CHUNK + CHUNK] for part in flipped
            ]
            turned.append(
                jnp.where(
                    odd_x,
                    jnp.where(odd_y, rev_xy, rev_x),
                    jnp.where(odd_y, rev_y, values[tile]),
                )
            )
        for tile in every:
            value = jnp.where(odd_z, turned[3 - tile], turned[tile])
            if tile >= 2:
                value = rotated(value, 64, 1)
            lam[rows, tile * 128 : tile * 128 + 128] = value

    here = pl.ds(pl.multiple_of(dom * 8, 8), 8)

    def each_owner(chunk, action, local):
        piece = lax.div(own_first, CHUNK) + chunk
        four = lax.div(piece, 2)
        for part in range(2):
            place = lax.rem(piece, 2) * 2 + part
            owner = place * 8 + lax.rem(place + lax.div(four, 2), 4) * 2 + lax.rem(four, 2)
            rows = pl.ds(pl.multiple_of(chunk * CHUNK + part * 8, 8), 8)
            own = (grp == 3) & (owner == dom)

            @pl.when(jnp.logical_not(own))
            def _():
                action(
                    remote(
                        lam.at[rows], lamrecv.at[here], osend.at[chunk * 2 + part], orecv,
                        (3, owner),
                    )
                )

            if local:

                @pl.when(own)
                def _():
                    lamrecv[here, :] = lam[rows, :]

    def analyse(chunk):
        for step in (1, 2):
            other = lax.rem(comp + step, 3)
            piece = recv.at[other, chunk_rows(chunk)]
            remote(
                piece, piece, asend.at[0, 0], arecv.at[other, chunk], (lax.rem(grp + 1, 4), dom)
            ).wait_recv()
        lambda_rows(chunk, 0)
        natural_order(chunk)
        each_owner(chunk, lambda copy: copy.start(), True)

    over(0, own_count, lambda step: analyse(turn(step, own_count)))
    over(
        0,
        own_count,
        lambda step: each_owner(turn(step, own_count), lambda copy: copy.wait_send(), False),
    )
    each_send(lambda copy: copy.wait_send())

    def wait_rows(count):
        piece = lamrecv.at[0 : 8 * count]
        remote(piece, piece, osend.at[0], orecv, (lax.rem(grp + 1, 4), dom)).wait_recv()

    four = lax.rem(lax.div(lax.rem(dom, 8), 2) - lax.div(dom, 8) + 4, 4) * 2 + lax.rem(dom, 2)
    to_itself = four * 2 + lax.div(dom, 16) >= FIRSTS[3]

    @pl.when((grp == 3) & to_itself)
    def _():
        wait_rows(31)

    @pl.when((grp == 3) & jnp.logical_not(to_itself))
    def _():
        wait_rows(32)

    @pl.when(grp == 3)
    def _():
        out[...] = lamrecv[...]


def lambda_two(jac):
    strain = [[0.5 * (jac[a][b] + jac[b][a]) for b in range(3)] for a in range(3)]
    spin = [[0.5 * (jac[a][b] - jac[b][a]) for b in range(3)] for a in range(3)]
    m = [[None] * 3 for _ in range(3)]
    for a in range(3):
        for b in range(a, 3):
            value = strain[a][0] * strain[0][b] + spin[a][0] * spin[0][b]
            for k in (1, 2):
                value = value + strain[a][k] * strain[k][b] + spin[a][k] * spin[k][b]
            m[a][b] = value
            m[b][a] = value
    for sweep in range(SWEEPS):
        for p, q, r in ((0, 1, 2), (0, 2, 1), (1, 2, 0)):
            last = sweep == SWEEPS - 1
            twice = 2.0 * m[p][q]
            gap = m[p][p] - m[q][q]
            square = twice * twice + gap * gap
            inverse = lax.rsqrt(jnp.maximum(square, 1e-36))
            length = square * inverse
            mean = 0.5 * (m[p][p] + m[q][q])
            m[p][p] = mean + 0.5 * length
            m[q][q] = mean - 0.5 * length
            if last and (p, q) == (1, 2):
                continue
            none = square < 1e-36
            cosine2 = jnp.where(none, 1.0, jnp.abs(gap) * inverse)
            sine2 = jnp.where(none, 0.0, twice * inverse)
            larger = 0.5 + 0.5 * cosine2
            root = lax.rsqrt(larger)
            big = larger * root
            small = 0.5 * sine2 * root
            flip = gap < 0.0
            sine_big = jnp.where(sine2 < 0.0, -big, big)
            cosine = jnp.where(flip, jnp.abs(small), big)
            sine = jnp.where(flip, sine_big, small)
            side_p = m[r][p]
            side_q = m[r][q]
            m[r][p] = m[p][r] = cosine * side_p + sine * side_q
            m[r][q] = m[q][r] = cosine * side_q - sine * side_p
            m[p][q] = m[q][p] = jnp.zeros_like(side_p)
    diagonal = [m[0][0], m[1][1], m[2][2]]
    largest = jnp.maximum(jnp.maximum(diagonal[0], diagonal[1]), diagonal[2])
    smallest = jnp.minimum(jnp.minimum(diagonal[0], diagonal[1]), diagonal[2])
    return diagonal[0] + diagonal[1] + diagonal[2] - largest - smallest


def per_device(forcing, viscosity, mass_coef, element_order, owner):
    mats, flat, lanes = tables()
    vmem = pl.BlockSpec(memory_space=pltpu.VMEM)
    hbm = pl.BlockSpec(memory_space=pltpu.HBM)
    wide = (12 * LAYER, NODES)
    own = (CELLS, NODES)
    dma = pltpu.SemaphoreType.DMA
    result = pl.pallas_call(
        kernel,
        out_shape=pltpu.VMEM(own, F32),
        in_specs=[hbm] * 8,
        out_specs=vmem,
        scratch_shapes=[
            pltpu.VMEM(own, F32),
            pltpu.VMEM((8, NODES), F32),
            pltpu.VMEM((640, 384), BF16),
            pltpu.VMEM((1, CELLS), jnp.int32),
            pltpu.VMEM((1, CELLS), jnp.int32),
            pltpu.VMEM((4, 768, 256), BF16),
            pltpu.VMEM((8, CELLS), F32),
            pltpu.VMEM((2, 8, CELLS), F32),
            pltpu.VMEM((CELLS, 2 * CELLS), BF16),
            pltpu.VMEM((CELLS, 2 * CELLS), BF16),
            pltpu.VMEM((2 * CELLS, NODES), BF16),
            pltpu.VMEM((12 * LAYER, 128), F32),
            pltpu.VMEM((12 * LAYER, 128), F32),
            pltpu.VMEM(wide, F32),
            pltpu.VMEM(wide, F32),
            pltpu.VMEM(wide, F32),
            pltpu.VMEM((12 * LAYER, 3 * NODES), BF16),
            pltpu.VMEM((12 * LAYER, 3 * NODES), BF16),
            pltpu.VMEM((12 * LAYER, 3 * NODES), BF16),
            pltpu.VMEM((12 * LAYER, 3 * NODES), BF16),
            pltpu.VMEM(wide, F32),
            pltpu.VMEM(wide, F32),
            pltpu.VMEM(wide, F32),
            pltpu.VMEM(wide, F32),
            pltpu.VMEM(own, F32),
            pltpu.VMEM(own, F32),
            pltpu.VMEM((4, CELLS, 3 * NODES), F32),
            pltpu.VMEM((CELLS, CELLS), BF16),
            pltpu.VMEM((CELLS, 384), F32),
            pltpu.VMEM((CELLS, 3 * NODES), BF16),
            pltpu.VMEM((2, LAYER, 128), F32),
            pltpu.VMEM((2, LAYER, 128), F32),
            pltpu.VMEM((4, 2, LAYER, 128), F32),
            pltpu.VMEM((8, 128), F32),
            pltpu.VMEM((DOMS, 8, 128), F32),
            pltpu.VMEM((CELLS, 3 * NODES), BF16),
            pltpu.VMEM((3, MOST * CHUNK, 3 * NODES), BF16),
            pltpu.VMEM((MOST * CHUNK, NODES), F32),
            pltpu.VMEM(own, F32),
            dma((6,)), dma((12,)), dma, dma((2,)), dma((2,)), dma((10,)), dma((10,)), dma((2,)),
            dma((2,)), dma, dma, dma((3, MOST)), dma((3, MOST)), dma((2 * MOST,)), dma,
        ],
        compiler_params=pltpu.CompilerParams(
            collective_id=0, has_side_effects=True, vmem_limit_bytes=60 * 1024 * 1024
        ),
        name="solve_and_analyse",
    )(
        forcing, viscosity[None], mass_coef[None], element_order, owner,
        jnp.asarray(lanes), jnp.asarray(flat), jnp.asarray(mats),
    )
    return result[None]


def solution(mesh):
    in_specs = (P(None, "dom", None), P("dom"), P("dom"), P("dom", None), P("dom", None))
    out_specs = P("grp", "dom", None)
    return jax.shard_map(
        per_device, mesh=mesh, in_specs=in_specs, out_specs=out_specs, check_vma=False
    )
```

```python
import functools

import jax
import jax.numpy as jnp
import ml_dtypes
import numpy as np
from jax import lax
from jax.experimental import pallas as pl
from jax.experimental.pallas import tpu as pltpu
from jax.sharding import PartitionSpec as P

NP = 8
ITERS = 4
SWEEPS = 4
LAYER = 64
CELLS = 256
NODES = 512
DOMS = 32
CHUNK = 16
COUNTS = (5, 5, 4, 2)
FIRSTS = (0, 5, 10, 14)
MOST = max(COUNTS)
BASIS_LOW = 0.3
BASIS_HIGH = 2.0
THETA = 0.5 * (BASIS_LOW + BASIS_HIGH)
DELTA = 0.5 * (BASIS_HIGH - BASIS_LOW)
MESH = pl.DeviceIdType.MESH
F32 = jnp.float32
BF16 = jnp.bfloat16


def legendre_values(points, node_count):
    legendre = np.zeros((points.shape[0], node_count))
    legendre[:, 0] = 1.0
    legendre[:, 1] = points
    for poly_order in range(2, node_count):
        legendre[:, poly_order] = (
            (2 * poly_order - 1) * points * legendre[:, poly_order - 1]
            - (poly_order - 1) * legendre[:, poly_order - 2]
        ) / poly_order
    return legendre


def lobatto_table(node_count):
    degree = node_count - 1
    points = np.cos(np.pi * np.arange(node_count) / degree)
    for attempt in range(60):
        legendre = legendre_values(points, node_count)
        points = points - (points * legendre[:, degree] - legendre[:, degree - 1]) / (
            node_count * legendre[:, degree]
        )
    points = points[::-1].copy()
    end_values = legendre_values(points, node_count)[:, degree]
    weights = 2.0 / (degree * node_count * end_values * end_values)
    spacing = points[:, None] - points[None, :] + np.eye(node_count)
    diff_matrix = end_values[:, None] / end_values[None, :] / spacing
    diff_matrix = diff_matrix * (1.0 - np.eye(node_count))
    diff_matrix[0, 0] = -degree * node_count / 4.0
    diff_matrix[-1, -1] = degree * node_count / 4.0
    return (weights, diff_matrix)


def split_rows(matrix):
    high = matrix.astype(np.float32).astype(ml_dtypes.bfloat16)
    low = (matrix - high.astype(np.float64)).astype(np.float32).astype(ml_dtypes.bfloat16)
    return high, low


def tables():
    weights, diff = lobatto_table(NP)
    eye = np.eye(NP)
    cube = (
        weights[:, None, None] * weights[None, :, None] * weights[None, None, :]
    ).reshape(-1)
    directional = [
        np.kron(eye, np.kron(eye, diff)),
        np.kron(eye, np.kron(diff, eye)),
        np.kron(diff, np.kron(eye, eye)),
    ]
    stiff = np.zeros((NODES, NODES))
    for matrix in directional:
        stiff = stiff + matrix.T @ (cube[:, None] * matrix)
    flip = np.arange(NODES).reshape(NP, LAYER)[::-1][: NP // 2].reshape(-1)
    mats = []
    for matrix in (stiff, directional[2]):
        near, far = matrix[:256, :256], matrix[:256, flip]
        for block in (0.5 * (near + far), 0.5 * (near - far)):
            mats.append(np.stack(split_rows(block.T)))
    mats = np.stack(mats)
    flat = np.concatenate([directional[0].T[:128, :128], directional[1].T[:128, :128]], 1)
    high, low = split_rows(flat)
    flat = np.concatenate([high, high, low], 0)
    lanes = np.zeros((8, NODES), np.float32)
    lanes[0] = cube
    lanes[1] = np.diag(stiff)
    lanes[2] = np.repeat(diff[0], LAYER)
    order = [0, 1, 2, 3, 5, 4, 7, 6]
    lanes = lanes.reshape(8, NP, LAYER)[:, order].reshape(8, NODES)
    natural = cube.reshape(NP, LAYER).astype(np.float32).reshape(-1)
    lanes[3] = natural
    back = eye[::-1]
    half = np.eye(2)
    mirror = np.concatenate(
        [
            np.kron(half, np.kron(eye, back)),
            np.kron(half, np.kron(back, eye)),
            np.kron(half, np.kron(back, back)),
        ],
        1,
    ).astype(ml_dtypes.bfloat16)
    wide = np.concatenate([flat, np.zeros((384, 128), flat.dtype)], 1)
    return mats, np.concatenate([wide, mirror, mirror], 0), lanes


def rotated(value, shift, axis):
    return pltpu.roll(value, shift % value.shape[axis], axis)


def kernel(
    forcing, visc_in, mass_in, order_in, owner_in, lanes_in, flat_in, mats,
    out,
    fsc, lanes, flat, order_sc, owner_sc, weights, par, parn, pone, ptr, parts, visc, mass, raw, tmp,
    inv, lhs0, lhs1, lhs2, lhs3, v0, v1, v2, v3, xs, xstd, grads, gpack, classes, gcells, fsend, frecv, fghost, moments,
    red, packed, recv, lam, lamrecv,
    ssem, wsem, fsem, psend, precv, gsend, grecv, f3send, f3recv, rsend, rrecv, asend, arecv,
    osend, orecv,
):
    grp = lax.axis_index("grp")
    dom = lax.axis_index("dom")
    comp = jnp.minimum(grp, 2)
    up = lax.rem(dom + 1, DOMS)
    down = lax.rem(dom + DOMS - 1, DOMS)
    barrier = pltpu.get_barrier_semaphore()
    basis = (v0, v1, v2, v3)
    lefts = (lhs0, lhs1, lhs2, lhs3)
    every = (0, 1, 2, 3)

    at_y = [lax.rem(lax.div(dom, 8) + k, 4) * 8 for k in range(4)]
    at_z = [lax.rem(lax.div(dom, 2) + k, 4) * 2 for k in range(4)]
    at_core = [lax.rem(dom + k, 2) for k in range(2)]

    def hops(offset):
        return sum(min(k, 4 - k) for k in (offset // 8, offset // 2 % 4))

    peers = [
        (offset, at_y[offset // 8] + at_z[offset // 2 % 4] + at_core[offset % 2])
        for offset in sorted(range(1, DOMS), key=lambda offset: -hops(offset))
    ]

    for offset, peer in peers:
        pl.semaphore_signal(barrier, inc=1, device_id=(grp, peer), device_id_type=MESH)
    for step in range(1, 4):
        pl.semaphore_signal(
            barrier, inc=1, device_id=(lax.rem(grp + step, 4), dom), device_id_type=MESH
        )

    load_small = [
        pltpu.make_async_copy(source, target, ssem.at[k])
        for k, (source, target) in enumerate(
            (
                (visc_in, par.at[0:1]),
                (mass_in, par.at[1:2]),
                (order_in, order_sc),
                (owner_in, owner_sc),
                (lanes_in, lanes),
                (flat_in, flat),
            )
        )
    ]
    for copy in load_small:
        copy.start()
    load_force = pltpu.make_async_copy(forcing.at[comp], fsc, fsem)
    load_force.start()
    load_mats = []
    for which in range(4):
        for part, source in enumerate((0, 0, 1)):
            copy = pltpu.make_async_copy(
                mats.at[which, source],
                weights.at[which, part * 256 : part * 256 + 256],
                wsem.at[3 * which + part],
            )
            copy.start()
            load_mats.append(copy)

    lane = lax.broadcasted_iota(jnp.int32, (8, 128), 1)
    sub = lax.broadcasted_iota(jnp.int32, (8, 128), 0)
    node_i = lax.rem(lane, 8)
    node_j = lax.rem(lane // 8, 8)
    odd = lax.rem(sub, 2) == 1
    first_i = node_i == 0
    last_i = node_i == 7
    take_up = ((last_i & jnp.logical_not(odd)) | (first_i & odd & (sub < 7)))
    take_down = ((last_i & odd) | (first_i & jnp.logical_not(odd) & (sub > 0)))
    has_up = jnp.where(dom < DOMS - 1, 1.0, 0.0).astype(F32)
    has_down = jnp.where(dom > 0, 1.0, 0.0).astype(F32)

    def wide(mask):
        return jnp.broadcast_to(mask[None], (8, 8, 128))

    x_up = wide(take_up)
    x_down = wide(take_down)
    x_odd = wide(odd)
    y_last = wide(node_j == 7)
    y_first = wide(node_j == 0)
    low_half = wide(lane < LAYER)

    def x_others(a):
        above = rotated(a, -1, 1)
        below = rotated(a, 1, 1)
        return jnp.where(x_up, above, jnp.where(x_down, below, 0.0))

    def y_others(a):
        blank = jnp.zeros((1, 8, 128), F32)
        last = jnp.concatenate([a[k ^ 1 : (k ^ 1) + 1] for k in range(8)], 0)
        first = jnp.concatenate(
            [blank] + [a[k : k + 1] for k in (2, 1, 4, 3, 6, 5)] + [blank], 0
        )
        return jnp.where(y_last, last, jnp.where(y_first, first, 0.0))

    def xy_sum(a):
        a = a + x_others(a)
        return a + y_others(a)

    def rows_of(layer):
        if isinstance(layer, int):
            return slice(layer * LAYER, layer * LAYER + LAYER)
        return pl.ds(pl.multiple_of(layer * LAYER, LAYER), LAYER)

    def load(ref, layer, tile):
        return ref[rows_of(layer), tile * 128 : tile * 128 + 128].reshape(8, 8, 128)

    def store(ref, layer, tile, value):
        ref[rows_of(layer), tile * 128 : tile * 128 + 128] = value.reshape(LAYER, 128)

    def column(ref, layer):
        return ref[rows_of(layer), :].reshape(8, 8, 128)

    def table(row, tile):
        return lanes[row : row + 1, tile * 128 : tile * 128 + 128].reshape(1, 1, 128)

    def split(value):
        high = value.astype(BF16)
        return high, (value - high.astype(F32)).astype(BF16)

    def store_lhs(lhs, layer, pair, first, second):
        for start, value in ((0, first + second), (768, first - second)):
            start = start + pair * 128
            high, low = split(value.reshape(LAYER, 128))
            lhs[rows_of(layer), start : start + 128] = high
            lhs[rows_of(layer), start + 256 : start + 384] = low
            lhs[rows_of(layer), start + 512 : start + 640] = high

    def reversals(value):
        total = jnp.dot(
            jnp.concatenate(split(value), 1), flat[384:640, :], preferred_element_type=F32
        )
        return total[:, 0:128], total[:, 128:256], total[:, 256:384]

    def mirror_layers(value, tile, target, base, back):
        flipped = reversals(value)
        for layer in range(4):
            rows = slice(layer * LAYER, layer * LAYER + LAYER)
            plain, rev_x, rev_y, rev_xy = [
                part[rows].reshape(8, 8, 128) for part in (value,) + flipped
            ]
            even_y = jnp.where(x_odd, rev_x, plain)
            odd_y = jnp.where(x_odd, rev_xy, rev_y)
            mixed = jnp.concatenate(
                [(odd_y if k % 2 else even_y)[k : k + 1] for k in range(8)], 0
            )
            place = 3 - tile if layer % 2 else tile
            if (place if back else tile) >= 2:
                mixed = rotated(mixed, 64, 2)
            store(target, base + layer, place, mixed)

    def over(low, high, body):
        if isinstance(high, int):
            for layer in range(low, high):
                body(layer)
        else:
            lax.fori_loop(low, high, lambda layer, carry: (body(layer), carry)[1], 0)

    cell_sub = lax.broadcasted_iota(jnp.int32, (CELLS, CELLS), 0).astype(F32)
    cell_lane = lax.broadcasted_iota(jnp.int32, (CELLS, CELLS), 1).astype(F32)
    for copy in load_small:
        copy.wait()
    par[2:3, :] = order_sc[...].astype(F32)
    par[3:8, :] = jnp.zeros((5, CELLS), F32)

    def coefficients(ref, base, scale):
        hit = ref[2:3, :] == cell_sub
        for row, target in ((0, visc), (1, mass)):
            col = jnp.sum(jnp.where(hit, ref[row : row + 1, :], 0.0), axis=1, keepdims=True)
            target[base : base + CELLS, :] = jnp.broadcast_to(col * scale, (CELLS, 128))
        return hit

    one_hot = jnp.where(par[2:3, :] == cell_sub, 1.0, 0.0).astype(BF16)
    pone[:, 0:CELLS] = one_hot
    pone[:, CELLS : 2 * CELLS] = one_hot
    load_force.wait()
    high, low = split(fsc[...])
    parts[0:CELLS, :] = high
    parts[CELLS : 2 * CELLS, :] = low
    fsc[...] = jnp.dot(pone[...], parts[...], preferred_element_type=F32) * lanes[3:4, :]
    for tile in every:
        mirror_layers(fsc[:, tile * 128 : tile * 128 + 128], tile, raw, 4, False)

    pl.semaphore_wait(barrier, DOMS - 1 + 3)

    def remote(src, dst, send, recv_sem, device):
        return pltpu.make_async_remote_copy(
            src_ref=src, dst_ref=dst, send_sem=send, recv_sem=recv_sem,
            device_id=device, device_id_type=MESH,
        )

    par_copies = [
        remote(par, parn.at[0], psend.at[0], precv.at[0], (grp, up)),
        remote(par, parn.at[1], psend.at[1], precv.at[1], (grp, down)),
    ]
    def ghost(source, layers, first, last, target, slot, device):
        return remote(
            raw.at[source * LAYER : (source + layers) * LAYER, first:last],
            raw.at[target * LAYER : (target + layers) * LAYER, first:last],
            gsend.at[slot], grecv.at[slot], (grp, device),
        )

    near_copies = [
        ghost(7, 1, 0, 512, 3, 0, up),
        ghost(4, 1, 0, 512, 8, 1, down),
        ghost(6, 1, 384, 512, 2, 2, up),
        ghost(5, 1, 384, 512, 9, 3, down),
    ]
    far_copies = [
        ghost(6, 1, 0, 384, 2, 4, up),
        ghost(5, 1, 0, 384, 9, 5, down),
        ghost(5, 1, 0, 512, 1, 6, up),
        ghost(6, 1, 0, 512, 10, 7, down),
        ghost(4, 1, 384, 512, 0, 8, up),
        ghost(7, 1, 384, 512, 11, 9, down),
    ]
    for copy in par_copies + near_copies + far_copies:
        copy.start()

    coefficients(par, CELLS, 1.0)
    order_col = jnp.sum(
        jnp.where(cell_sub == cell_lane, par[2:3, :], 0.0), axis=1, keepdims=True
    )
    one_hot = jnp.where(order_col == cell_lane, 1.0, 0.0).astype(BF16)
    ptr[:, 0:CELLS] = one_hot
    ptr[:, CELLS : 2 * CELLS] = one_hot
    owner_row = owner_sc[...].astype(F32)
    owner_col = jnp.sum(
        jnp.where(cell_sub == cell_lane, owner_row, 0.0), axis=1, keepdims=True
    )
    same = (owner_col == owner_row) & (cell_sub < cell_lane)
    rank_row = jnp.sum(jnp.where(same, 1.0, 0.0), axis=0, keepdims=True)
    owner_int = owner_sc[...]
    place = owner_int >> 3
    piece_row = ((((owner_int >> 1) - place) & 3) << 1) + (owner_int & 1)
    first_row = (piece_row * 4 + place).astype(F32)
    dest_row = jnp.where(owner_row >= 0.0, first_row * 8.0 + rank_row, -1.0)
    slot_of = jnp.where(dest_row == cell_sub, 1.0, 0.0).astype(BF16)
    gpack[...] = jnp.dot(slot_of, one_hot, preferred_element_type=F32).astype(BF16)
    cell_id = lax.broadcasted_iota(jnp.int32, (CELLS, 128), 0)
    for k, width in enumerate((1, 8, 64)):
        parity = lax.rem(cell_id // width, 2).astype(F32).astype(BF16)
        classes[:, k * 128 : k * 128 + 128] = jnp.dot(
            gpack[...], parity, preferred_element_type=F32
        )

    for copy in par_copies:
        copy.wait()
    coefficients(parn.at[0], 0, has_down)
    coefficients(parn.at[1], 2 * CELLS, has_up)

    def partners(layer):
        parity = layer % 2 if isinstance(layer, int) else lax.rem(layer, 2)
        return {0: layer - 1 + 2 * parity, 3: layer + 1 - 2 * parity}

    def face_sum(ref, layer, tile):
        value = load(ref, layer, tile)
        other = load(ref, partners(layer)[tile], tile)
        return value + jnp.where(low_half, other, 0.0)

    def put_inverse(layer, tile, diag):
        store(inv, layer, tile, jnp.where(diag > 0.0, (2.0 / DELTA) / diag, 0.0))

    def diagonal(layer, tiles):
        coef_v = column(visc, layer)
        coef_m = column(mass, layer)
        for tile in tiles:
            diag = xy_sum(coef_v * table(1, tile) + coef_m * table(0, tile))
            if tile in (0, 3):
                store(tmp, layer, tile, diag)
            else:
                put_inverse(layer, tile, diag)

    diagonal(0, (3,))
    over(1, 11, lambda layer: diagonal(layer, every))
    diagonal(11, (3,))

    def diagonal_faces(layer):
        for tile in (0, 3):
            put_inverse(layer, tile, face_sum(tmp, layer, tile))

    over(1, 11, diagonal_faces)

    def first_value(layer, tile, force):
        value = force * load(inv, layer, tile) * (0.5 * DELTA)
        store(v0, layer, tile, value)
        return value

    def put_first(layer, pair, forces):
        values = [
            first_value(layer, tile, force) for tile, force in zip((pair, 3 - pair), forces)
        ]
        store_lhs(lhs0, layer, pair, *values)

    def assemble(layer, tiles, scale):
        sums = []
        for tile in tiles:
            force = load(raw, layer, tile)
            if scale is not None:
                force = force * scale
            force = xy_sum(force)
            if tile in (0, 3):
                store(tmp, layer, tile, force)
            else:
                sums.append(force)
        if sums:
            put_first(layer, 1, sums)

    over(4, 8, lambda layer: assemble(layer, every, None))
    for copy in load_mats:
        copy.wait()
    def multiply(lhs, low, high, which, target, first=0):
        for part in range(2):
            target[:, first + part * 256 : first + part * 256 + 256] = jnp.dot(
                lhs[low * LAYER : high * LAYER, part * 768 : part * 768 + 768],
                weights[2 * which + part],
                preferred_element_type=F32,
            )

    def advance(step, layer, pair, totals):
        values = []
        for tile, total in zip((pair, 3 - pair), totals):
            value = total * load(inv, layer, tile)
            current = load(basis[step], layer, tile)
            if step == 0:
                value = 0.5 * value - (THETA / DELTA) * current
            else:
                value = value - (2.0 * THETA / DELTA) * current
                value = value - load(basis[step - 1], layer, tile)
            store(basis[step + 1], layer, tile, value)
            values.append(value)
        store_lhs(lefts[step + 1], layer, pair, *values)

    def apply(step, layer, tiles, sums, going):
        coef_v = column(visc, layer)
        coef_m = column(mass, layer)
        for pair in (1, 0):
            if pair not in tiles and 3 - pair not in tiles:
                continue
            even = load(tmp, layer, pair)
            uneven = load(tmp, layer, 2 + pair)
            images = []
            for tile, product in ((pair, even + uneven), (3 - pair, even - uneven)):
                if tile not in tiles:
                    continue
                value = load(basis[step], layer, tile)
                weighted = coef_m * table(0, tile)
                image = coef_v * product + weighted * value
                if sums is not None:
                    diag = coef_v * table(1, tile) + weighted
                    sums = (
                        sums[0] + jnp.sum(value * image, axis=0),
                        sums[1] + jnp.sum(value * value * diag, axis=0),
                    )
                if going:
                    image = xy_sum(image)
                    if pair == 0:
                        store(tmp, layer, tile, image)
                    else:
                        images.append(image)
            if images:
                advance(step, layer, 1, images)
        return sums

    def faces(step, layer):
        advance(step, layer, 0, [face_sum(tmp, layer, tile) for tile in (0, 3)])

    blank_sums = (jnp.zeros((8, 128), F32), jnp.zeros((8, 128), F32))

    def own_apply(step, going):
        sums = blank_sums
        for layer in range(4, 8):
            sums = apply(step, layer, every, sums, going)
        moments[step : step + 1, :] = jnp.sum(sums[0], axis=0, keepdims=True)
        moments[4 + step : 5 + step, :] = jnp.sum(sums[1], axis=0, keepdims=True)

    def first_faces(layer):
        put_first(layer, 0, [face_sum(tmp, layer, tile) for tile in (0, 3)])

    for copy in near_copies:
        copy.wait()
    assemble(2, (3,), has_down)
    assemble(3, every, has_down)
    assemble(8, every, has_up)
    assemble(9, (3,), has_up)
    over(3, 9, first_faces)
    for layer in (2, 9):
        first_value(layer, 3, face_sum(tmp, layer, 3))
    multiply(lhs0, 3, 9, 0, tmp.at[3 * LAYER : 9 * LAYER])
    own_apply(0, True)
    for layer in (3, 8):
        apply(0, layer, every, None, True)

    for copy in far_copies:
        copy.wait()
    assemble(0, (3,), has_down)
    assemble(1, every, has_down)
    assemble(2, (0, 1, 2), has_down)
    assemble(9, (0, 1, 2), has_up)
    assemble(10, every, has_up)
    assemble(11, (3,), has_up)
    for layer in (1, 10):
        first_faces(layer)
    for layer in (2, 9):
        value = first_value(layer, 0, face_sum(tmp, layer, 0))
        store_lhs(lhs0, layer, 0, value, load(v0, layer, 3))
    far_rows = (slice(1 * LAYER, 3 * LAYER), slice(9 * LAYER, 11 * LAYER))
    for part in range(2):
        product = jnp.dot(
            jnp.concatenate(
                [lhs0[rows, part * 768 : part * 768 + 768] for rows in far_rows], 0
            ),
            weights[part],
            preferred_element_type=F32,
        )
        for side, rows in enumerate(far_rows):
            tmp[rows, part * 256 : part * 256 + 256] = product[
                side * 2 * LAYER : (side + 1) * 2 * LAYER
            ]
    apply(0, 1, (0,), None, True)
    apply(0, 2, every, None, True)
    apply(0, 9, every, None, True)
    apply(0, 10, (0,), None, True)
    over(2, 10, lambda layer: faces(0, layer))

    for step in range(1, ITERS):
        low, high = 1 + step, 11 - step
        going = step + 1 < ITERS
        multiply(lefts[step], low, high, 0, tmp.at[low * LAYER : high * LAYER])
        own_apply(step, going)
        if going:
            inward = 0 if low % 2 else 3
            apply(step, low, (inward,), None, True)
            over(low + 1, 4, lambda layer: apply(step, layer, every, None, True))
            over(8, high - 1, lambda layer: apply(step, layer, every, None, True))
            apply(step, high - 1, (inward,), None, True)
            over(low + 1, high - 1, lambda layer: faces(step, layer))

    red[0] = moments[...]
    for offset, peer in peers:
        remote(moments, red.at[offset], rsend, rrecv, (grp, peer)).start()

    def end_face(ref, layer):
        total = load(ref, layer, 0) * table(2, 0)
        for tile in (1, 2, 3):
            total = total + load(ref, layer, tile) * table(2, tile)
        total = total + rotated(total, 64, 2)
        return -total if layer % 2 else total

    fsend[0] = end_face(v3, 7).reshape(LAYER, 128)
    fsend[1] = end_face(v3, 4).reshape(LAYER, 128)
    face_copies = [
        remote(fsend.at[0], frecv.at[0], f3send.at[0], f3recv.at[0], (grp, up)),
        remote(fsend.at[1], frecv.at[1], f3send.at[1], f3recv.at[1], (grp, down)),
    ]
    for copy in face_copies:
        copy.start()

    own_rows = slice(4 * LAYER, 8 * LAYER)
    for index in range(ITERS):
        left = jnp.concatenate(
            [
                jnp.concatenate(
                    [
                        lefts[index][own_rows, start + part * 256 : start + part * 256 + 128]
                        for part in range(3)
                    ],
                    1,
                )
                for start in (0, 128, 768, 896)
            ],
            0,
        )
        both = jnp.dot(left, flat[0:384, 0:256], preferred_element_type=F32)
        for part in range(4):
            rows = slice(part * CELLS, part * CELLS + CELLS)
            grads[index, :, part * 128 : part * 128 + 128] = both[rows, 0:128]
            grads[index, :, NODES + part * 128 : NODES + part * 128 + 128] = both[rows, 128:256]
        multiply(lefts[index], 4, 8, 1, grads.at[index], 2 * NODES)
        if index < 3:
            fghost[index, 0] = end_face(basis[index], 3).reshape(LAYER, 128)
            fghost[index, 1] = end_face(basis[index], 8).reshape(LAYER, 128)

    for copy in face_copies:
        copy.wait()
    for side in range(2):
        fghost[3, side] = frecv[side]

    whole = remote(red.at[1:DOMS], red.at[1:DOMS], rsend, rrecv, (grp, up))
    whole.wait_send()
    whole.wait_recv()

    total = jnp.sum(red[...], axis=0)
    total = jnp.broadcast_to(jnp.sum(total, axis=1, keepdims=True), (8, 128))
    moments[...] = total

    def scalar(row):
        return jnp.broadcast_to(moments[row : row + 1, :], (8, 128))

    alpha = [scalar(row) for row in range(4)]
    beta = [scalar(4 + row) for row in range(4)]
    gamma = [(alpha[k] - THETA * beta[k]) * (1.0 / DELTA) for k in range(4)]
    mu = [beta[0], gamma[0]]
    ahead = gamma[0]
    for k in range(1, 4):
        ahead = 2.0 * gamma[k] - ahead
        mu.append(2.0 * beta[k] - mu[0])
        mu.append(2.0 * ahead - mu[1])

    def inner(i, j):
        return 0.5 * (mu[i + j] + mu[abs(i - j)])

    gram = [
        [
            DELTA * 0.5 * (inner(i, j + 1) + inner(i, abs(j - 1))) + THETA * inner(i, j)
            for j in range(4)
        ]
        for i in range(4)
    ]
    right = [mu[k] for k in range(4)]
    pivots = []
    for k in range(4):
        original = DELTA * 0.5 * (inner(k, k + 1) + inner(k, abs(k - 1))) + THETA * inner(k, k)
        pivot = gram[k][k]
        good = pivot > 1e-7 * original
        inverse = jnp.where(good, 1.0 / jnp.where(good, pivot, 1.0), 0.0)
        pivots.append(inverse)
        for i in range(k + 1, 4):
            factor = gram[i][k] * inverse
            for j in range(k + 1, 4):
                gram[i][j] = gram[i][j] - factor * gram[k][j]
            right[i] = right[i] - factor * right[k]
    coef = [None] * 4
    for k in (3, 2, 1, 0):
        value = right[k]
        for j in range(k + 1, 4):
            value = value - gram[k][j] * coef[j]
        coef[k] = value * pivots[k]

    coef8 = [(value * (1.0 / NP)).reshape(1, 8, 128) for value in coef]
    coef16 = [0.5 * value for value in coef8]
    x_sign = jnp.where(odd, -1.0, 1.0).reshape(1, 8, 128)
    x_scale = jnp.where(take_up | take_down, 0.5, 1.0).reshape(1, 8, 128) * x_sign
    y_half = jnp.where((node_j == 7) | (node_j == 0), 0.5, 1.0).reshape(1, 8, 128)
    y_end = jnp.where(node_j == 7, 0.5, 1.0).reshape(1, 8, 128)
    y_scale = jnp.concatenate(
        [y_end, -y_half, y_half, -y_half, y_half, -y_half, y_half, -y_end], 0
    )

    def combined(layer, direction, pair):
        parts_of = []
        scale = coef8 if direction == 2 else coef16
        for start in (0, 256):
            start = start + direction * NODES + pair * 128
            value = None
            for k in range(4):
                term = scale[k] * grads[k, rows_of(layer), start : start + 128].reshape(8, 8, 128)
                value = term if value is None else value + term
            parts_of.append(value)
        even, uneven = parts_of
        if direction == 2:
            return even + uneven, uneven - even
        return even + uneven, even - uneven

    def put_grad(layer, direction, tile, value):
        start = direction * NODES + tile * 128
        gcells[rows_of(layer), start : start + 128] = value.reshape(LAYER, 128).astype(BF16)

    def flat_grads(layer):
        z_sign = -1.0 if layer % 2 else 1.0
        for pair in (0, 1):
            for tile, value in zip((pair, 3 - pair), combined(layer, 0, pair)):
                put_grad(layer, 0, tile, x_scale * (value - x_others(value)))
            for tile, value in zip((pair, 3 - pair), combined(layer, 1, pair)):
                put_grad(layer, 1, tile, y_scale * (value - y_others(value)))
        for tile, value in zip((1, 2), combined(layer, 2, 1)):
            put_grad(layer, 2, tile, z_sign * value)
        for tile, value in zip((0, 3), combined(layer, 2, 0)):
            store(xstd, layer, tile, z_sign * value)

    over(0, 4, flat_grads)

    def mean_face(layer, tile, other, there):
        value = load(xstd, layer, tile)
        put_grad(layer, 2, tile, value + jnp.where(low_half, there * (other - value), 0.0))

    for layer in range(4):
        mean_face(layer, 3, load(xstd, layer ^ 1, 3), 0.5)
        if layer in (1, 2):
            mean_face(layer, 0, load(xstd, 3 - layer, 0), 0.5)
        else:
            side = 0 if layer == 0 else 1
            other = None
            for k in range(4):
                term = coef8[k] * fghost[k, side].reshape(8, 8, 128)
                other = term if other is None else other + term
            mean_face(layer, 0, other, 0.5 * (has_up if side else has_down))

    def by_row(values):
        picked = values[3]
        for row in (2, 1, 0):
            picked = jnp.where(grp == row, values[row], picked)
        return picked

    own_first = by_row([first * CHUNK for first in FIRSTS])
    own_count = by_row(COUNTS)

    def pack(part, carry):
        cols = pl.ds(pl.multiple_of(part * 512, 512), 512)
        packed[:, cols] = jnp.dot(
            gpack[...], gcells[:, cols], preferred_element_type=F32
        ).astype(BF16)
        return carry

    lax.fori_loop(0, 3, pack, 0)

    def chunk_rows(chunk, base=0):
        return pl.ds(pl.multiple_of(base + chunk * CHUNK, CHUNK), CHUNK)

    def turn(step, count):
        return lax.rem(dom + step, count)

    def piece_copy(step, target, slot):
        chunk = turn(step, COUNTS[target])
        return remote(
            packed.at[chunk_rows(chunk, FIRSTS[target] * CHUNK)],
            recv.at[comp, chunk_rows(chunk)],
            asend.at[slot, step], arecv.at[comp, chunk], (target, dom),
        )

    def each_send(action):
        for row, targets in enumerate(((2, 1, 3), (3, 2, 0), (1,), (0,))):

            @pl.when(grp == row)
            def _():
                for step in range(MOST):
                    for slot, target in enumerate(targets):
                        if step < COUNTS[target]:
                            action(piece_copy(step, target, slot))

    each_send(lambda copy: copy.start())
    for row in range(4):

        @pl.when(grp == row)
        def _():
            slots = COUNTS[row] * CHUNK
            first = FIRSTS[row] * CHUNK
            recv[min(row, 2), 0:slots] = packed[first : first + slots, :]

    wide8 = [value.reshape(1, 8, 128) for value in coef]

    @pl.when(grp < 3)
    def _():
        def solve_layer(layer):
            for tile in every:
                value = wide8[0] * load(v0, layer, tile)
                for k in range(1, 4):
                    value = value + wide8[k] * load(basis[k], layer, tile)
                store(xs, layer - 4, tile, value)

        over(4, 8, solve_layer)
        for tile in every:
            mirror_layers(xs[:, tile * 128 : tile * 128 + 128], tile, xstd, 0, True)
        high, low = split(xstd[...])
        parts[0:CELLS, :] = high
        parts[CELLS : 2 * CELLS, :] = low
        out[...] = jnp.dot(ptr[...], parts[...], preferred_element_type=F32)

    def lambda_rows(block, carry):
        rows = pl.ds(pl.multiple_of(block * 16, 16), 16)
        jac = [
            [recv[c, rows, d * NODES : d * NODES + NODES].astype(F32) for d in range(3)]
            for c in range(3)
        ]
        lam[rows, :] = lambda_two(jac)
        return carry

    def natural_order(chunk):
        rows = chunk_rows(chunk)
        slots = pl.ds(pl.multiple_of(own_first + chunk * CHUNK, CHUNK), CHUNK)
        odd_x, odd_y, odd_z = [
            classes[slots, k * 128 : k * 128 + 128] > 0.5 for k in range(3)
        ]
        values = [lam[rows, tile * 128 : tile * 128 + 128] for tile in every]
        flipped = reversals(jnp.concatenate(values, 0))
        turned = []
        for tile in every:
            rev_x, rev_y, rev_xy = [
                part[tile * CHUNK : tile * CHUNK + CHUNK] for part in flipped
            ]
            turned.append(
                jnp.where(
                    odd_x,
                    jnp.where(odd_y, rev_xy, rev_x),
                    jnp.where(odd_y, rev_y, values[tile]),
                )
            )
        for tile in every:
            value = jnp.where(odd_z, turned[3 - tile], turned[tile])
            if tile >= 2:
                value = rotated(value, 64, 1)
            lam[rows, tile * 128 : tile * 128 + 128] = value

    here = pl.ds(pl.multiple_of(dom * 8, 8), 8)

    def each_owner(chunk, action, local):
        piece = lax.div(own_first, CHUNK) + chunk
        four = lax.div(piece, 2)
        for part in range(2):
            place = lax.rem(piece, 2) * 2 + part
            owner = place * 8 + lax.rem(place + lax.div(four, 2), 4) * 2 + lax.rem(four, 2)
            rows = pl.ds(pl.multiple_of(chunk * CHUNK + part * 8, 8), 8)
            own = (grp == 3) & (owner == dom)

            @pl.when(jnp.logical_not(own))
            def _():
                action(
                    remote(
                        lam.at[rows], lamrecv.at[here], osend.at[chunk * 2 + part], orecv,
                        (3, owner),
                    )
                )

            if local:

                @pl.when(own)
                def _():
                    lamrecv[here, :] = lam[rows, :]

    def analyse(chunk):
        for step in (1, 2):
            other = lax.rem(comp + step, 3)
            piece = recv.at[other, chunk_rows(chunk)]
            remote(
                piece, piece, asend.at[0, 0], arecv.at[other, chunk], (lax.rem(grp + 1, 4), dom)
            ).wait_recv()
        lambda_rows(chunk, 0)
        natural_order(chunk)
        each_owner(chunk, lambda copy: copy.start(), True)

    over(0, own_count, lambda step: analyse(turn(step, own_count)))
    over(
        0,
        own_count,
        lambda step: each_owner(turn(step, own_count), lambda copy: copy.wait_send(), False),
    )
    each_send(lambda copy: copy.wait_send())

    def wait_rows(count):
        piece = lamrecv.at[0 : 8 * count]
        remote(piece, piece, osend.at[0], orecv, (lax.rem(grp + 1, 4), dom)).wait_recv()

    four = lax.rem(lax.div(lax.rem(dom, 8), 2) - lax.div(dom, 8) + 4, 4) * 2 + lax.rem(dom, 2)
    to_itself = four * 2 + lax.div(dom, 16) >= FIRSTS[3]

    @pl.when((grp == 3) & to_itself)
    def _():
        wait_rows(31)

    @pl.when((grp == 3) & jnp.logical_not(to_itself))
    def _():
        wait_rows(32)

    @pl.when(grp == 3)
    def _():
        out[...] = lamrecv[...]


def lambda_two(jac):
    strain = [[0.5 * (jac[a][b] + jac[b][a]) for b in range(3)] for a in range(3)]
    spin = [[0.5 * (jac[a][b] - jac[b][a]) for b in range(3)] for a in range(3)]
    m = [[None] * 3 for _ in range(3)]
    for a in range(3):
        for b in range(a, 3):
            value = strain[a][0] * strain[0][b] + spin[a][0] * spin[0][b]
            for k in (1, 2):
                value = value + strain[a][k] * strain[k][b] + spin[a][k] * spin[k][b]
            m[a][b] = value
            m[b][a] = value
    for sweep in range(SWEEPS):
        for p, q, r in ((0, 1, 2), (0, 2, 1), (1, 2, 0)):
            last = sweep == SWEEPS - 1
            twice = 2.0 * m[p][q]
            gap = m[p][p] - m[q][q]
            square = twice * twice + gap * gap
            inverse = lax.rsqrt(jnp.maximum(square, 1e-36))
            length = square * inverse
            mean = 0.5 * (m[p][p] + m[q][q])
            m[p][p] = mean + 0.5 * length
            m[q][q] = mean - 0.5 * length
            if last and (p, q) == (1, 2):
                continue
            none = square < 1e-36
            cosine2 = jnp.where(none, 1.0, jnp.abs(gap) * inverse)
            sine2 = jnp.where(none, 0.0, twice * inverse)
            larger = 0.5 + 0.5 * cosine2
            root = lax.rsqrt(larger)
            big = larger * root
            small = 0.5 * sine2 * root
            flip = gap < 0.0
            sine_big = jnp.where(sine2 < 0.0, -big, big)
            cosine = jnp.where(flip, jnp.abs(small), big)
            sine = jnp.where(flip, sine_big, small)
            side_p = m[r][p]
            side_q = m[r][q]
            m[r][p] = m[p][r] = cosine * side_p + sine * side_q
            m[r][q] = m[q][r] = cosine * side_q - sine * side_p
            m[p][q] = m[q][p] = jnp.zeros_like(side_p)
    diagonal = [m[0][0], m[1][1], m[2][2]]
    largest = jnp.maximum(jnp.maximum(diagonal[0], diagonal[1]), diagonal[2])
    smallest = jnp.minimum(jnp.minimum(diagonal[0], diagonal[1]), diagonal[2])
    return diagonal[0] + diagonal[1] + diagonal[2] - largest - smallest


def per_device(forcing, viscosity, mass_coef, element_order, owner):
    mats, flat, lanes = tables()
    vmem = pl.BlockSpec(memory_space=pltpu.VMEM)
    hbm = pl.BlockSpec(memory_space=pltpu.HBM)
    wide = (12 * LAYER, NODES)
    own = (CELLS, NODES)
    dma = pltpu.SemaphoreType.DMA
    result = pl.pallas_call(
        kernel,
        out_shape=pltpu.VMEM(own, F32),
        in_specs=[hbm] * 8,
        out_specs=vmem,
        scratch_shapes=[
            pltpu.VMEM(own, F32),
            pltpu.VMEM((8, NODES), F32),
            pltpu.VMEM((640, 384), BF16),
            pltpu.VMEM((1, CELLS), jnp.int32),
            pltpu.VMEM((1, CELLS), jnp.int32),
            pltpu.VMEM((4, 768, 256), BF16),
            pltpu.VMEM((8, CELLS), F32),
            pltpu.VMEM((2, 8, CELLS), F32),
            pltpu.VMEM((CELLS, 2 * CELLS), BF16),
            pltpu.VMEM((CELLS, 2 * CELLS), BF16),
            pltpu.VMEM((2 * CELLS, NODES), BF16),
            pltpu.VMEM((12 * LAYER, 128), F32),
            pltpu.VMEM((12 * LAYER, 128), F32),
            pltpu.VMEM(wide, F32),
            pltpu.VMEM(wide, F32),
            pltpu.VMEM(wide, F32),
            pltpu.VMEM((12 * LAYER, 3 * NODES), BF16),
            pltpu.VMEM((12 * LAYER, 3 * NODES), BF16),
            pltpu.VMEM((12 * LAYER, 3 * NODES), BF16),
            pltpu.VMEM((12 * LAYER, 3 * NODES), BF16),
            pltpu.VMEM(wide, F32),
            pltpu.VMEM(wide, F32),
            pltpu.VMEM(wide, F32),
            pltpu.VMEM(wide, F32),
            pltpu.VMEM(own, F32),
            pltpu.VMEM(own, F32),
            pltpu.VMEM((4, CELLS, 3 * NODES), F32),
            pltpu.VMEM((CELLS, CELLS), BF16),
            pltpu.VMEM((CELLS, 384), F32),
            pltpu.VMEM((CELLS, 3 * NODES), BF16),
            pltpu.VMEM((2, LAYER, 128), F32),
            pltpu.VMEM((2, LAYER, 128), F32),
            pltpu.VMEM((4, 2, LAYER, 128), F32),
            pltpu.VMEM((8, 128), F32),
            pltpu.VMEM((DOMS, 8, 128), F32),
            pltpu.VMEM((CELLS, 3 * NODES), BF16),
            pltpu.VMEM((3, MOST * CHUNK, 3 * NODES), BF16),
            pltpu.VMEM((MOST * CHUNK, NODES), F32),
            pltpu.VMEM(own, F32),
            dma((6,)), dma((12,)), dma, dma((2,)), dma((2,)), dma((10,)), dma((10,)), dma((2,)),
            dma((2,)), dma, dma, dma((3, MOST)), dma((3, MOST)), dma((2 * MOST,)), dma,
        ],
        compiler_params=pltpu.CompilerParams(
            collective_id=0, has_side_effects=True, vmem_limit_bytes=60 * 1024 * 1024
        ),
        name="solve_and_analyse",
    )(
        forcing, viscosity[None], mass_coef[None], element_order, owner,
        jnp.asarray(lanes), jnp.asarray(flat), jnp.asarray(mats),
    )
    return result[None]


def solution(mesh):
    in_specs = (P(None, "dom", None), P("dom"), P("dom"), P("dom", None), P("dom", None))
    out_specs = P("grp", "dom", None)
    return jax.shard_map(
        per_device, mesh=mesh, in_specs=in_specs, out_specs=out_specs, check_vma=False
    )
```

```python
import functools

import jax
import jax.numpy as jnp
import ml_dtypes
import numpy as np
from jax import lax
from jax.experimental import pallas as pl
from jax.experimental.pallas import tpu as pltpu
from jax.sharding import PartitionSpec as P

NP = 8
ITERS = 4
SWEEPS = 4
LAYER = 64
CELLS = 256
NODES = 512
DOMS = 32
CHUNK = 16
COUNTS = (5, 5, 4, 2)
FIRSTS = (0, 5, 10, 14)
MOST = max(COUNTS)
BASIS_LOW = 0.3
BASIS_HIGH = 2.0
THETA = 0.5 * (BASIS_LOW + BASIS_HIGH)
DELTA = 0.5 * (BASIS_HIGH - BASIS_LOW)
MESH = pl.DeviceIdType.MESH
F32 = jnp.float32
BF16 = jnp.bfloat16


def legendre_values(points, node_count):
    legendre = np.zeros((points.shape[0], node_count))
    legendre[:, 0] = 1.0
    legendre[:, 1] = points
    for poly_order in range(2, node_count):
        legendre[:, poly_order] = (
            (2 * poly_order - 1) * points * legendre[:, poly_order - 1]
            - (poly_order - 1) * legendre[:, poly_order - 2]
        ) / poly_order
    return legendre


def lobatto_table(node_count):
    degree = node_count - 1
    points = np.cos(np.pi * np.arange(node_count) / degree)
    for attempt in range(60):
        legendre = legendre_values(points, node_count)
        points = points - (points * legendre[:, degree] - legendre[:, degree - 1]) / (
            node_count * legendre[:, degree]
        )
    points = points[::-1].copy()
    end_values = legendre_values(points, node_count)[:, degree]
    weights = 2.0 / (degree * node_count * end_values * end_values)
    spacing = points[:, None] - points[None, :] + np.eye(node_count)
    diff_matrix = end_values[:, None] / end_values[None, :] / spacing
    diff_matrix = diff_matrix * (1.0 - np.eye(node_count))
    diff_matrix[0, 0] = -degree * node_count / 4.0
    diff_matrix[-1, -1] = degree * node_count / 4.0
    return (weights, diff_matrix)


def split_rows(matrix):
    high = matrix.astype(np.float32).astype(ml_dtypes.bfloat16)
    low = (matrix - high.astype(np.float64)).astype(np.float32).astype(ml_dtypes.bfloat16)
    return high, low


def tables():
    weights, diff = lobatto_table(NP)
    eye = np.eye(NP)
    cube = (
        weights[:, None, None] * weights[None, :, None] * weights[None, None, :]
    ).reshape(-1)
    directional = [
        np.kron(eye, np.kron(eye, diff)),
        np.kron(eye, np.kron(diff, eye)),
        np.kron(diff, np.kron(eye, eye)),
    ]
    stiff = np.zeros((NODES, NODES))
    for matrix in directional:
        stiff = stiff + matrix.T @ (cube[:, None] * matrix)
    flip = np.arange(NODES).reshape(NP, LAYER)[::-1][: NP // 2].reshape(-1)
    mats = []
    for matrix in (stiff, directional[2]):
        near, far = matrix[:256, :256], matrix[:256, flip]
        for block in (0.5 * (near + far), 0.5 * (near - far)):
            mats.append(np.stack(split_rows(block.T)))
    mats = np.stack(mats)
    flat = np.concatenate([directional[0].T[:128, :128], directional[1].T[:128, :128]], 1)
    high, low = split_rows(flat)
    flat = np.concatenate([high, high, low], 0)
    lanes = np.zeros((8, NODES), np.float32)
    lanes[0] = cube
    lanes[1] = np.diag(stiff)
    lanes[2] = np.repeat(diff[0], LAYER)
    order = [0, 1, 2, 3, 5, 4, 7, 6]
    lanes = lanes.reshape(8, NP, LAYER)[:, order].reshape(8, NODES)
    natural = cube.reshape(NP, LAYER).astype(np.float32).reshape(-1)
    lanes[3] = natural
    back = eye[::-1]
    half = np.eye(2)
    mirror = np.concatenate(
        [
            np.kron(half, np.kron(eye, back)),
            np.kron(half, np.kron(back, eye)),
            np.kron(half, np.kron(back, back)),
        ],
        1,
    ).astype(ml_dtypes.bfloat16)
    wide = np.concatenate([flat, np.zeros((384, 128), flat.dtype)], 1)
    return mats, np.concatenate([wide, mirror, mirror], 0), lanes


def rotated(value, shift, axis):
    return pltpu.roll(value, shift % value.shape[axis], axis)


def kernel(
    forcing, visc_in, mass_in, order_in, owner_in, lanes_in, flat_in, mats,
    out,
    fsc, lanes, flat, order_sc, owner_sc, weights, par, parn, pone, ptr, parts, visc, mass, raw, tmp,
    inv, lhs0, lhs1, lhs2, lhs3, v0, v1, v2, v3, xs, xstd, grads, gpack, classes, gcells, fsend, frecv, fghost, moments,
    red, packed, recv, lam, lamrecv,
    ssem, wsem, fsem, psend, precv, gsend, grecv, f3send, f3recv, rsend, rrecv, asend, arecv,
    osend, orecv,
):
    grp = lax.axis_index("grp")
    dom = lax.axis_index("dom")
    comp = jnp.minimum(grp, 2)
    up = lax.rem(dom + 1, DOMS)
    down = lax.rem(dom + DOMS - 1, DOMS)
    barrier = pltpu.get_barrier_semaphore()
    basis = (v0, v1, v2, v3)
    lefts = (lhs0, lhs1, lhs2, lhs3)
    every = (0, 1, 2, 3)

    at_y = [lax.rem(lax.div(dom, 8) + k, 4) * 8 for k in range(4)]
    at_z = [lax.rem(lax.div(dom, 2) + k, 4) * 2 for k in range(4)]
    at_core = [lax.rem(dom + k, 2) for k in range(2)]

    def hops(offset):
        return sum(min(k, 4 - k) for k in (offset // 8, offset // 2 % 4))

    peers = [
        (offset, at_y[offset // 8] + at_z[offset // 2 % 4] + at_core[offset % 2])
        for offset in sorted(range(1, DOMS), key=lambda offset: -hops(offset))
    ]

    for offset, peer in peers:
        pl.semaphore_signal(barrier, inc=1, device_id=(grp, peer), device_id_type=MESH)
    for step in range(1, 4):
        pl.semaphore_signal(
            barrier, inc=1, device_id=(lax.rem(grp + step, 4), dom), device_id_type=MESH
        )

    load_small = [
        pltpu.make_async_copy(source, target, ssem.at[k])
        for k, (source, target) in enumerate(
            (
                (visc_in, par.at[0:1]),
                (mass_in, par.at[1:2]),
                (order_in, order_sc),
                (owner_in, owner_sc),
                (lanes_in, lanes),
                (flat_in, flat),
            )
        )
    ]
    for copy in load_small:
        copy.start()
    load_force = pltpu.make_async_copy(forcing.at[comp], fsc, fsem)
    load_force.start()
    load_mats = []
    for which in range(4):
        for part, source in enumerate((0, 0, 1)):
            copy = pltpu.make_async_copy(
                mats.at[which, source],
                weights.at[which, part * 256 : part * 256 + 256],
                wsem.at[3 * which + part],
            )
            copy.start()
            load_mats.append(copy)

    lane = lax.broadcasted_iota(jnp.int32, (8, 128), 1)
    sub = lax.broadcasted_iota(jnp.int32, (8, 128), 0)
    node_i = lax.rem(lane, 8)
    node_j = lax.rem(lane // 8, 8)
    odd = lax.rem(sub, 2) == 1
    first_i = node_i == 0
    last_i = node_i == 7
    take_up = ((last_i & jnp.logical_not(odd)) | (first_i & odd & (sub < 7)))
    take_down = ((last_i & odd) | (first_i & jnp.logical_not(odd) & (sub > 0)))
    has_up = jnp.where(dom < DOMS - 1, 1.0, 0.0).astype(F32)
    has_down = jnp.where(dom > 0, 1.0, 0.0).astype(F32)

    def wide(mask):
        return jnp.broadcast_to(mask[None], (8, 8, 128))

    x_up = wide(take_up)
    x_down = wide(take_down)
    x_odd = wide(odd)
    y_last = wide(node_j == 7)
    y_first = wide(node_j == 0)
    low_half = wide(lane < LAYER)

    def x_others(a):
        above = rotated(a, -1, 1)
        below = rotated(a, 1, 1)
        return jnp.where(x_up, above, jnp.where(x_down, below, 0.0))

    def y_others(a):
        blank = jnp.zeros((1, 8, 128), F32)
        last = jnp.concatenate([a[k ^ 1 : (k ^ 1) + 1] for k in range(8)], 0)
        first = jnp.concatenate(
            [blank] + [a[k : k + 1] for k in (2, 1, 4, 3, 6, 5)] + [blank], 0
        )
        return jnp.where(y_last, last, jnp.where(y_first, first, 0.0))

    def xy_sum(a):
        a = a + x_others(a)
        return a + y_others(a)

    def rows_of(layer):
        if isinstance(layer, int):
            return slice(layer * LAYER, layer * LAYER + LAYER)
        return pl.ds(pl.multiple_of(layer * LAYER, LAYER), LAYER)

    def load(ref, layer, tile):
        return ref[rows_of(layer), tile * 128 : tile * 128 + 128].reshape(8, 8, 128)

    def store(ref, layer, tile, value):
        ref[rows_of(layer), tile * 128 : tile * 128 + 128] = value.reshape(LAYER, 128)

    def column(ref, layer):
        return ref[rows_of(layer), :].reshape(8, 8, 128)

    def table(row, tile):
        return lanes[row : row + 1, tile * 128 : tile * 128 + 128].reshape(1, 1, 128)

    def split(value):
        high = value.astype(BF16)
        return high, (value - high.astype(F32)).astype(BF16)

    def store_lhs(lhs, layer, pair, first, second):
        for start, value in ((0, first + second), (768, first - second)):
            start = start + pair * 128
            high, low = split(value.reshape(LAYER, 128))
            lhs[rows_of(layer), start : start + 128] = high
            lhs[rows_of(layer), start + 256 : start + 384] = low
            lhs[rows_of(layer), start + 512 : start + 640] = high

    def reversals(value):
        total = jnp.dot(
            jnp.concatenate(split(value), 1), flat[384:640, :], preferred_element_type=F32
        )
        return total[:, 0:128], total[:, 128:256], total[:, 256:384]

    def mirror_layers(value, tile, target, base, back):
        flipped = reversals(value)
        for layer in range(4):
            rows = slice(layer * LAYER, layer * LAYER + LAYER)
            plain, rev_x, rev_y, rev_xy = [
                part[rows].reshape(8, 8, 128) for part in (value,) + flipped
            ]
            even_y = jnp.where(x_odd, rev_x, plain)
            odd_y = jnp.where(x_odd, rev_xy, rev_y)
            mixed = jnp.concatenate(
                [(odd_y if k % 2 else even_y)[k : k + 1] for k in range(8)], 0
            )
            place = 3 - tile if layer % 2 else tile
            if (place if back else tile) >= 2:
                mixed = rotated(mixed, 64, 2)
            store(target, base + layer, place, mixed)

    def over(low, high, body):
        if isinstance(high, int):
            for layer in range(low, high):
                body(layer)
        else:
            lax.fori_loop(low, high, lambda layer, carry: (body(layer), carry)[1], 0)

    cell_sub = lax.broadcasted_iota(jnp.int32, (CELLS, CELLS), 0).astype(F32)
    cell_lane = lax.broadcasted_iota(jnp.int32, (CELLS, CELLS), 1).astype(F32)
    for copy in load_small:
        copy.wait()
    par[2:3, :] = order_sc[...].astype(F32)
    par[3:8, :] = jnp.zeros((5, CELLS), F32)

    def coefficients(ref, base, scale):
        hit = ref[2:3, :] == cell_sub
        for row, target in ((0, visc), (1, mass)):
            col = jnp.sum(jnp.where(hit, ref[row : row + 1, :], 0.0), axis=1, keepdims=True)
            target[base : base + CELLS, :] = jnp.broadcast_to(col * scale, (CELLS, 128))
        return hit

    one_hot = jnp.where(par[2:3, :] == cell_sub, 1.0, 0.0).astype(BF16)
    pone[:, 0:CELLS] = one_hot
    pone[:, CELLS : 2 * CELLS] = one_hot
    load_force.wait()
    high, low = split(fsc[...])
    parts[0:CELLS, :] = high
    parts[CELLS : 2 * CELLS, :] = low
    fsc[...] = jnp.dot(pone[...], parts[...], preferred_element_type=F32) * lanes[3:4, :]
    for tile in every:
        mirror_layers(fsc[:, tile * 128 : tile * 128 + 128], tile, raw, 4, False)

    pl.semaphore_wait(barrier, DOMS - 1 + 3)

    def remote(src, dst, send, recv_sem, device):
        return pltpu.make_async_remote_copy(
            src_ref=src, dst_ref=dst, send_sem=send, recv_sem=recv_sem,
            device_id=device, device_id_type=MESH,
        )

    par_copies = [
        remote(par, parn.at[0], psend.at[0], precv.at[0], (grp, up)),
        remote(par, parn.at[1], psend.at[1], precv.at[1], (grp, down)),
    ]
    def ghost(source, layers, first, last, target, slot, device):
        return remote(
            raw.at[source * LAYER : (source + layers) * LAYER, first:last],
            raw.at[target * LAYER : (target + layers) * LAYER, first:last],
            gsend.at[slot], grecv.at[slot], (grp, device),
        )

    near_copies = [
        ghost(7, 1, 0, 512, 3, 0, up),
        ghost(4, 1, 0, 512, 8, 1, down),
        ghost(6, 1, 384, 512, 2, 2, up),
        ghost(5, 1, 384, 512, 9, 3, down),
    ]
    far_copies = [
        ghost(6, 1, 0, 384, 2, 4, up),
        ghost(5, 1, 0, 384, 9, 5, down),
        ghost(5, 1, 0, 512, 1, 6, up),
        ghost(6, 1, 0, 512, 10, 7, down),
        ghost(4, 1, 384, 512, 0, 8, up),
        ghost(7, 1, 384, 512, 11, 9, down),
    ]
    for copy in par_copies + near_copies + far_copies:
        copy.start()

    coefficients(par, CELLS, 1.0)
    order_col = jnp.sum(
        jnp.where(cell_sub == cell_lane, par[2:3, :], 0.0), axis=1, keepdims=True
    )
    one_hot = jnp.where(order_col == cell_lane, 1.0, 0.0).astype(BF16)
    ptr[:, 0:CELLS] = one_hot
    ptr[:, CELLS : 2 * CELLS] = one_hot
    owner_row = owner_sc[...].astype(F32)
    owner_col = jnp.sum(
        jnp.where(cell_sub == cell_lane, owner_row, 0.0), axis=1, keepdims=True
    )
    same = (owner_col == owner_row) & (cell_sub < cell_lane)
    rank_row = jnp.sum(jnp.where(same, 1.0, 0.0), axis=0, keepdims=True)
    owner_int = owner_sc[...]
    place = owner_int >> 3
    piece_row = ((((owner_int >> 1) - place) & 3) << 1) + (owner_int & 1)
    first_row = (piece_row * 4 + place).astype(F32)
    dest_row = jnp.where(owner_row >= 0.0, first_row * 8.0 + rank_row, -1.0)
    slot_of = jnp.where(dest_row == cell_sub, 1.0, 0.0).astype(BF16)
    gpack[...] = jnp.dot(slot_of, one_hot, preferred_element_type=F32).astype(BF16)
    cell_id = lax.broadcasted_iota(jnp.int32, (CELLS, 128), 0)
    for k, width in enumerate((1, 8, 64)):
        parity = lax.rem(cell_id // width, 2).astype(F32).astype(BF16)
        classes[:, k * 128 : k * 128 + 128] = jnp.dot(
            gpack[...], parity, preferred_element_type=F32
        )

    for copy in par_copies:
        copy.wait()
    coefficients(parn.at[0], 0, has_down)
    coefficients(parn.at[1], 2 * CELLS, has_up)

    def partners(layer):
        parity = layer % 2 if isinstance(layer, int) else lax.rem(layer, 2)
        return {0: layer - 1 + 2 * parity, 3: layer + 1 - 2 * parity}

    def face_sum(ref, layer, tile):
        value = load(ref, layer, tile)
        other = load(ref, partners(layer)[tile], tile)
        return value + jnp.where(low_half, other, 0.0)

    def put_inverse(layer, tile, diag):
        store(inv, layer, tile, jnp.where(diag > 0.0, (2.0 / DELTA) / diag, 0.0))

    def diagonal(layer, tiles):
        coef_v = column(visc, layer)
        coef_m = column(mass, layer)
        for tile in tiles:
            diag = xy_sum(coef_v * table(1, tile) + coef_m * table(0, tile))
            if tile in (0, 3):
                store(tmp, layer, tile, diag)
            else:
                put_inverse(layer, tile, diag)

    diagonal(0, (3,))
    over(1, 11, lambda layer: diagonal(layer, every))
    diagonal(11, (3,))

    def diagonal_faces(layer):
        for tile in (0, 3):
            put_inverse(layer, tile, face_sum(tmp, layer, tile))

    over(1, 11, diagonal_faces)

    def first_value(layer, tile, force):
        value = force * load(inv, layer, tile) * (0.5 * DELTA)
        store(v0, layer, tile, value)
        return value

    def put_first(layer, pair, forces):
        values = [
            first_value(layer, tile, force) for tile, force in zip((pair, 3 - pair), forces)
        ]
        store_lhs(lhs0, layer, pair, *values)

    def assemble(layer, tiles, scale):
        sums = []
        for tile in tiles:
            force = load(raw, layer, tile)
            if scale is not None:
                force = force * scale
            force = xy_sum(force)
            if tile in (0, 3):
                store(tmp, layer, tile, force)
            else:
                sums.append(force)
        if sums:
            put_first(layer, 1, sums)

    over(4, 8, lambda layer: assemble(layer, every, None))
    for copy in load_mats:
        copy.wait()
    def multiply(lhs, low, high, which, target, first=0):
        for part in range(2):
            target[:, first + part * 256 : first + part * 256 + 256] = jnp.dot(
                lhs[low * LAYER : high * LAYER, part * 768 : part * 768 + 768],
                weights[2 * which + part],
                preferred_element_type=F32,
            )

    def advance(step, layer, pair, totals):
        values = []
        for tile, total in zip((pair, 3 - pair), totals):
            value = total * load(inv, layer, tile)
            current = load(basis[step], layer, tile)
            if step == 0:
                value = 0.5 * value - (THETA / DELTA) * current
            else:
                value = value - (2.0 * THETA / DELTA) * current
                value = value - load(basis[step - 1], layer, tile)
            store(basis[step + 1], layer, tile, value)
            values.append(value)
        store_lhs(lefts[step + 1], layer, pair, *values)

    def apply(step, layer, tiles, sums, going):
        coef_v = column(visc, layer)
        coef_m = column(mass, layer)
        for pair in (1, 0):
            if pair not in tiles and 3 - pair not in tiles:
                continue
            even = load(tmp, layer, pair)
            uneven = load(tmp, layer, 2 + pair)
            images = []
            for tile, product in ((pair, even + uneven), (3 - pair, even - uneven)):
                if tile not in tiles:
                    continue
                value = load(basis[step], layer, tile)
                weighted = coef_m * table(0, tile)
                image = coef_v * product + weighted * value
                if sums is not None:
                    diag = coef_v * table(1, tile) + weighted
                    sums = (
                        sums[0] + jnp.sum(value * image, axis=0),
                        sums[1] + jnp.sum(value * value * diag, axis=0),
                    )
                if going:
                    image = xy_sum(image)
                    if pair == 0:
                        store(tmp, layer, tile, image)
                    else:
                        images.append(image)
            if images:
                advance(step, layer, 1, images)
        return sums

    def faces(step, layer):
        advance(step, layer, 0, [face_sum(tmp, layer, tile) for tile in (0, 3)])

    blank_sums = (jnp.zeros((8, 128), F32), jnp.zeros((8, 128), F32))

    def own_apply(step, going):
        sums = blank_sums
        for layer in range(4, 8):
            sums = apply(step, layer, every, sums, going)
        moments[step : step + 1, :] = jnp.sum(sums[0], axis=0, keepdims=True)
        moments[4 + step : 5 + step, :] = jnp.sum(sums[1], axis=0, keepdims=True)

    def first_faces(layer):
        put_first(layer, 0, [face_sum(tmp, layer, tile) for tile in (0, 3)])

    for copy in near_copies:
        copy.wait()
    assemble(2, (3,), has_down)
    assemble(3, every, has_down)
    assemble(8, every, has_up)
    assemble(9, (3,), has_up)
    over(3, 9, first_faces)
    for layer in (2, 9):
        first_value(layer, 3, face_sum(tmp, layer, 3))
    multiply(lhs0, 3, 9, 0, tmp.at[3 * LAYER : 9 * LAYER])
    own_apply(0, True)
    for layer in (3, 8):
        apply(0, layer, every, None, True)

    for copy in far_copies:
        copy.wait()
    assemble(0, (3,), has_down)
    assemble(1, every, has_down)
    assemble(2, (0, 1, 2), has_down)
    assemble(9, (0, 1, 2), has_up)
    assemble(10, every, has_up)
    assemble(11, (3,), has_up)
    for layer in (1, 10):
        first_faces(layer)
    for layer in (2, 9):
        value = first_value(layer, 0, face_sum(tmp, layer, 0))
        store_lhs(lhs0, layer, 0, value, load(v0, layer, 3))
    far_rows = (slice(1 * LAYER, 3 * LAYER), slice(9 * LAYER, 11 * LAYER))
    for part in range(2):
        product = jnp.dot(
            jnp.concatenate(
                [lhs0[rows, part * 768 : part * 768 + 768] for rows in far_rows], 0
            ),
            weights[part],
            preferred_element_type=F32,
        )
        for side, rows in enumerate(far_rows):
            tmp[rows, part * 256 : part * 256 + 256] = product[
                side * 2 * LAYER : (side + 1) * 2 * LAYER
            ]
    apply(0, 1, (0,), None, True)
    apply(0, 2, every, None, True)
    apply(0, 9, every, None, True)
    apply(0, 10, (0,), None, True)
    over(2, 10, lambda layer: faces(0, layer))

    for step in range(1, ITERS):
        low, high = 1 + step, 11 - step
        going = step + 1 < ITERS
        multiply(lefts[step], low, high, 0, tmp.at[low * LAYER : high * LAYER])
        own_apply(step, going)
        if going:
            inward = 0 if low % 2 else 3
            apply(step, low, (inward,), None, True)
            over(low + 1, 4, lambda layer: apply(step, layer, every, None, True))
            over(8, high - 1, lambda layer: apply(step, layer, every, None, True))
            apply(step, high - 1, (inward,), None, True)
            over(low + 1, high - 1, lambda layer: faces(step, layer))

    red[0] = moments[...]
    for offset, peer in peers:
        remote(moments, red.at[offset], rsend, rrecv, (grp, peer)).start()

    def end_face(ref, layer):
        total = load(ref, layer, 0) * table(2, 0)
        for tile in (1, 2, 3):
            total = total + load(ref, layer, tile) * table(2, tile)
        total = total + rotated(total, 64, 2)
        return -total if layer % 2 else total

    fsend[0] = end_face(v3, 7).reshape(LAYER, 128)
    fsend[1] = end_face(v3, 4).reshape(LAYER, 128)
    face_copies = [
        remote(fsend.at[0], frecv.at[0], f3send.at[0], f3recv.at[0], (grp, up)),
        remote(fsend.at[1], frecv.at[1], f3send.at[1], f3recv.at[1], (grp, down)),
    ]
    for copy in face_copies:
        copy.start()

    own_rows = slice(4 * LAYER, 8 * LAYER)
    for index in range(ITERS):
        left = jnp.concatenate(
            [
                jnp.concatenate(
                    [
                        lefts[index][own_rows, start + part * 256 : start + part * 256 + 128]
                        for part in range(3)
                    ],
                    1,
                )
                for start in (0, 128, 768, 896)
            ],
            0,
        )
        both = jnp.dot(left, flat[0:384, 0:256], preferred_element_type=F32)
        for part in range(4):
            rows = slice(part * CELLS, part * CELLS + CELLS)
            grads[index, :, part * 128 : part * 128 + 128] = both[rows, 0:128]
            grads[index, :, NODES + part * 128 : NODES + part * 128 + 128] = both[rows, 128:256]
        multiply(lefts[index], 4, 8, 1, grads.at[index], 2 * NODES)
        if index < 3:
            fghost[index, 0] = end_face(basis[index], 3).reshape(LAYER, 128)
            fghost[index, 1] = end_face(basis[index], 8).reshape(LAYER, 128)

    for copy in face_copies:
        copy.wait()
    for side in range(2):
        fghost[3, side] = frecv[side]

    whole = remote(red.at[1:DOMS], red.at[1:DOMS], rsend, rrecv, (grp, up))
    whole.wait_send()
    whole.wait_recv()

    total = jnp.sum(red[...], axis=0)
    total = jnp.broadcast_to(jnp.sum(total, axis=1, keepdims=True), (8, 128))
    moments[...] = total

    def scalar(row):
        return jnp.broadcast_to(moments[row : row + 1, :], (8, 128))

    alpha = [scalar(row) for row in range(4)]
    beta = [scalar(4 + row) for row in range(4)]
    gamma = [(alpha[k] - THETA * beta[k]) * (1.0 / DELTA) for k in range(4)]
    mu = [beta[0], gamma[0]]
    ahead = gamma[0]
    for k in range(1, 4):
        ahead = 2.0 * gamma[k] - ahead
        mu.append(2.0 * beta[k] - mu[0])
        mu.append(2.0 * ahead - mu[1])

    def inner(i, j):
        return 0.5 * (mu[i + j] + mu[abs(i - j)])

    gram = [
        [
            DELTA * 0.5 * (inner(i, j + 1) + inner(i, abs(j - 1))) + THETA * inner(i, j)
            for j in range(4)
        ]
        for i in range(4)
    ]
    right = [mu[k] for k in range(4)]
    pivots = []
    for k in range(4):
        original = DELTA * 0.5 * (inner(k, k + 1) + inner(k, abs(k - 1))) + THETA * inner(k, k)
        pivot = gram[k][k]
        good = pivot > 1e-7 * original
        inverse = jnp.where(good, 1.0 / jnp.where(good, pivot, 1.0), 0.0)
        pivots.append(inverse)
        for i in range(k + 1, 4):
            factor = gram[i][k] * inverse
            for j in range(k + 1, 4):
                gram[i][j] = gram[i][j] - factor * gram[k][j]
            right[i] = right[i] - factor * right[k]
    coef = [None] * 4
    for k in (3, 2, 1, 0):
        value = right[k]
        for j in range(k + 1, 4):
            value = value - gram[k][j] * coef[j]
        coef[k] = value * pivots[k]

    coef8 = [(value * (1.0 / NP)).reshape(1, 8, 128) for value in coef]
    coef16 = [0.5 * value for value in coef8]
    x_sign = jnp.where(odd, -1.0, 1.0).reshape(1, 8, 128)
    x_scale = jnp.where(take_up | take_down, 0.5, 1.0).reshape(1, 8, 128) * x_sign
    y_half = jnp.where((node_j == 7) | (node_j == 0), 0.5, 1.0).reshape(1, 8, 128)
    y_end = jnp.where(node_j == 7, 0.5, 1.0).reshape(1, 8, 128)
    y_scale = jnp.concatenate(
        [y_end, -y_half, y_half, -y_half, y_half, -y_half, y_half, -y_end], 0
    )

    def combined(layer, direction, pair):
        parts_of = []
        scale = coef8 if direction == 2 else coef16
        for start in (0, 256):
            start = start + direction * NODES + pair * 128
            value = None
            for k in range(4):
                term = scale[k] * grads[k, rows_of(layer), start : start + 128].reshape(8, 8, 128)
                value = term if value is None else value + term
            parts_of.append(value)
        even, uneven = parts_of
        if direction == 2:
            return even + uneven, uneven - even
        return even + uneven, even - uneven

    def put_grad(layer, direction, tile, value):
        start = direction * NODES + tile * 128
        gcells[rows_of(layer), start : start + 128] = value.reshape(LAYER, 128).astype(BF16)

    def pack(direction):
        cols = slice(direction * NODES, direction * NODES + NODES)
        packed[:, cols] = jnp.dot(
            gpack[...], gcells[:, cols], preferred_element_type=F32
        ).astype(BF16)

    for direction, scale, others in ((0, x_scale, x_others), (1, y_scale, y_others)):
        for layer in range(4):
            for pair in (0, 1):
                for tile, value in zip((pair, 3 - pair), combined(layer, direction, pair)):
                    put_grad(layer, direction, tile, scale * (value - others(value)))
        pack(direction)

    for layer in range(4):
        z_sign = -1.0 if layer % 2 else 1.0
        for tile, value in zip((1, 2), combined(layer, 2, 1)):
            put_grad(layer, 2, tile, z_sign * value)
        for tile, value in zip((0, 3), combined(layer, 2, 0)):
            store(xstd, layer, tile, z_sign * value)

    def mean_face(layer, tile, other, there):
        value = load(xstd, layer, tile)
        put_grad(layer, 2, tile, value + jnp.where(low_half, there * (other - value), 0.0))

    for layer in range(4):
        mean_face(layer, 3, load(xstd, layer ^ 1, 3), 0.5)
        if layer in (1, 2):
            mean_face(layer, 0, load(xstd, 3 - layer, 0), 0.5)
        else:
            side = 0 if layer == 0 else 1
            other = None
            for k in range(4):
                term = coef8[k] * fghost[k, side].reshape(8, 8, 128)
                other = term if other is None else other + term
            mean_face(layer, 0, other, 0.5 * (has_up if side else has_down))

    def by_row(values):
        picked = values[3]
        for row in (2, 1, 0):
            picked = jnp.where(grp == row, values[row], picked)
        return picked

    own_first = by_row([first * CHUNK for first in FIRSTS])
    own_count = by_row(COUNTS)

    pack(2)

    def chunk_rows(chunk, base=0):
        return pl.ds(pl.multiple_of(base + chunk * CHUNK, CHUNK), CHUNK)

    def turn(step, count):
        return lax.rem(dom + step, count)

    def piece_copy(step, target, slot):
        chunk = turn(step, COUNTS[target])
        return remote(
            packed.at[chunk_rows(chunk, FIRSTS[target] * CHUNK)],
            recv.at[comp, chunk_rows(chunk)],
            asend.at[slot, step], arecv.at[comp, chunk], (target, dom),
        )

    def each_send(action):
        for row, targets in enumerate(((2, 1, 3), (3, 2, 0), (1,), (0,))):

            @pl.when(grp == row)
            def _():
                for step in range(MOST):
                    for slot, target in enumerate(targets):
                        if step < COUNTS[target]:
                            action(piece_copy(step, target, slot))

    each_send(lambda copy: copy.start())
    for row in range(4):

        @pl.when(grp == row)
        def _():
            slots = COUNTS[row] * CHUNK
            first = FIRSTS[row] * CHUNK
            recv[min(row, 2), 0:slots] = packed[first : first + slots, :]

    wide8 = [value.reshape(1, 8, 128) for value in coef]

    @pl.when(grp < 3)
    def _():
        def solve_layer(layer):
            for tile in every:
                value = wide8[0] * load(v0, layer, tile)
                for k in range(1, 4):
                    value = value + wide8[k] * load(basis[k], layer, tile)
                store(xs, layer - 4, tile, value)

        over(4, 8, solve_layer)
        for tile in every:
            mirror_layers(xs[:, tile * 128 : tile * 128 + 128], tile, xstd, 0, True)
        high, low = split(xstd[...])
        parts[0:CELLS, :] = high
        parts[CELLS : 2 * CELLS, :] = low
        out[...] = jnp.dot(ptr[...], parts[...], preferred_element_type=F32)

    def lambda_rows(block, carry):
        rows = pl.ds(pl.multiple_of(block * 16, 16), 16)
        jac = [
            [recv[c, rows, d * NODES : d * NODES + NODES].astype(F32) for d in range(3)]
            for c in range(3)
        ]
        lam[rows, :] = lambda_two(jac)
        return carry

    def natural_order(chunk):
        rows = chunk_rows(chunk)
        slots = pl.ds(pl.multiple_of(own_first + chunk * CHUNK, CHUNK), CHUNK)
        odd_x, odd_y, odd_z = [
            classes[slots, k * 128 : k * 128 + 128] > 0.5 for k in range(3)
        ]
        values = [lam[rows, tile * 128 : tile * 128 + 128] for tile in every]
        flipped = reversals(jnp.concatenate(values, 0))
        turned = []
        for tile in every:
            rev_x, rev_y, rev_xy = [
                part[tile * CHUNK : tile * CHUNK + CHUNK] for part in flipped
            ]
            turned.append(
                jnp.where(
                    odd_x,
                    jnp.where(odd_y, rev_xy, rev_x),
                    jnp.where(odd_y, rev_y, values[tile]),
                )
            )
        for tile in every:
            value = jnp.where(odd_z, turned[3 - tile], turned[tile])
            if tile >= 2:
                value = rotated(value, 64, 1)
            lam[rows, tile * 128 : tile * 128 + 128] = value

    here = pl.ds(pl.multiple_of(dom * 8, 8), 8)

    def each_owner(chunk, action, local):
        piece = lax.div(own_first, CHUNK) + chunk
        four = lax.div(piece, 2)
        for part in range(2):
            place = lax.rem(piece, 2) * 2 + part
            owner = place * 8 + lax.rem(place + lax.div(four, 2), 4) * 2 + lax.rem(four, 2)
            rows = pl.ds(pl.multiple_of(chunk * CHUNK + part * 8, 8), 8)
            own = (grp == 3) & (owner == dom)

            @pl.when(jnp.logical_not(own))
            def _():
                action(
                    remote(
                        lam.at[rows], lamrecv.at[here], osend.at[chunk * 2 + part], orecv,
                        (3, owner),
                    )
                )

            if local:

                @pl.when(own)
                def _():
                    lamrecv[here, :] = lam[rows, :]

    def analyse(chunk):
        for step in (1, 2):
            other = lax.rem(comp + step, 3)
            piece = recv.at[other, chunk_rows(chunk)]
            remote(
                piece, piece, asend.at[0, 0], arecv.at[other, chunk], (lax.rem(grp + 1, 4), dom)
            ).wait_recv()
        lambda_rows(chunk, 0)
        natural_order(chunk)
        each_owner(chunk, lambda copy: copy.start(), True)

    over(0, own_count, lambda step: analyse(turn(step, own_count)))
    over(
        0,
        own_count,
        lambda step: each_owner(turn(step, own_count), lambda copy: copy.wait_send(), False),
    )
    each_send(lambda copy: copy.wait_send())

    def wait_rows(count):
        piece = lamrecv.at[0 : 8 * count]
        remote(piece, piece, osend.at[0], orecv, (lax.rem(grp + 1, 4), dom)).wait_recv()

    four = lax.rem(lax.div(lax.rem(dom, 8), 2) - lax.div(dom, 8) + 4, 4) * 2 + lax.rem(dom, 2)
    to_itself = four * 2 + lax.div(dom, 16) >= FIRSTS[3]

    @pl.when((grp == 3) & to_itself)
    def _():
        wait_rows(31)

    @pl.when((grp == 3) & jnp.logical_not(to_itself))
    def _():
        wait_rows(32)

    @pl.when(grp == 3)
    def _():
        out[...] = lamrecv[...]


def lambda_two(jac):
    strain = [[0.5 * (jac[a][b] + jac[b][a]) for b in range(3)] for a in range(3)]
    spin = [[0.5 * (jac[a][b] - jac[b][a]) for b in range(3)] for a in range(3)]
    m = [[None] * 3 for _ in range(3)]
    for a in range(3):
        for b in range(a, 3):
            value = strain[a][0] * strain[0][b] + spin[a][0] * spin[0][b]
            for k in (1, 2):
                value = value + strain[a][k] * strain[k][b] + spin[a][k] * spin[k][b]
            m[a][b] = value
            m[b][a] = value
    for sweep in range(SWEEPS):
        for p, q, r in ((0, 1, 2), (0, 2, 1), (1, 2, 0)):
            last = sweep == SWEEPS - 1
            twice = 2.0 * m[p][q]
            gap = m[p][p] - m[q][q]
            square = twice * twice + gap * gap
            inverse = lax.rsqrt(jnp.maximum(square, 1e-36))
            length = square * inverse
            mean = 0.5 * (m[p][p] + m[q][q])
            m[p][p] = mean + 0.5 * length
            m[q][q] = mean - 0.5 * length
            if last and (p, q) == (1, 2):
                continue
            none = square < 1e-36
            cosine2 = jnp.where(none, 1.0, jnp.abs(gap) * inverse)
            sine2 = jnp.where(none, 0.0, twice * inverse)
            larger = 0.5 + 0.5 * cosine2
            root = lax.rsqrt(larger)
            big = larger * root
            small = 0.5 * sine2 * root
            flip = gap < 0.0
            sine_big = jnp.where(sine2 < 0.0, -big, big)
            cosine = jnp.where(flip, jnp.abs(small), big)
            sine = jnp.where(flip, sine_big, small)
            side_p = m[r][p]
            side_q = m[r][q]
            m[r][p] = m[p][r] = cosine * side_p + sine * side_q
            m[r][q] = m[q][r] = cosine * side_q - sine * side_p
            m[p][q] = m[q][p] = jnp.zeros_like(side_p)
    diagonal = [m[0][0], m[1][1], m[2][2]]
    largest = jnp.maximum(jnp.maximum(diagonal[0], diagonal[1]), diagonal[2])
    smallest = jnp.minimum(jnp.minimum(diagonal[0], diagonal[1]), diagonal[2])
    return diagonal[0] + diagonal[1] + diagonal[2] - largest - smallest


def per_device(forcing, viscosity, mass_coef, element_order, owner):
    mats, flat, lanes = tables()
    vmem = pl.BlockSpec(memory_space=pltpu.VMEM)
    hbm = pl.BlockSpec(memory_space=pltpu.HBM)
    wide = (12 * LAYER, NODES)
    own = (CELLS, NODES)
    dma = pltpu.SemaphoreType.DMA
    result = pl.pallas_call(
        kernel,
        out_shape=pltpu.VMEM(own, F32),
        in_specs=[hbm] * 8,
        out_specs=vmem,
        scratch_shapes=[
            pltpu.VMEM(own, F32),
            pltpu.VMEM((8, NODES), F32),
            pltpu.VMEM((640, 384), BF16),
            pltpu.VMEM((1, CELLS), jnp.int32),
            pltpu.VMEM((1, CELLS), jnp.int32),
            pltpu.VMEM((4, 768, 256), BF16),
            pltpu.VMEM((8, CELLS), F32),
            pltpu.VMEM((2, 8, CELLS), F32),
            pltpu.VMEM((CELLS, 2 * CELLS), BF16),
            pltpu.VMEM((CELLS, 2 * CELLS), BF16),
            pltpu.VMEM((2 * CELLS, NODES), BF16),
            pltpu.VMEM((12 * LAYER, 128), F32),
            pltpu.VMEM((12 * LAYER, 128), F32),
            pltpu.VMEM(wide, F32),
            pltpu.VMEM(wide, F32),
            pltpu.VMEM(wide, F32),
            pltpu.VMEM((12 * LAYER, 3 * NODES), BF16),
            pltpu.VMEM((12 * LAYER, 3 * NODES), BF16),
            pltpu.VMEM((12 * LAYER, 3 * NODES), BF16),
            pltpu.VMEM((12 * LAYER, 3 * NODES), BF16),
            pltpu.VMEM(wide, F32),
            pltpu.VMEM(wide, F32),
            pltpu.VMEM(wide, F32),
            pltpu.VMEM(wide, F32),
            pltpu.VMEM(own, F32),
            pltpu.VMEM(own, F32),
            pltpu.VMEM((4, CELLS, 3 * NODES), F32),
            pltpu.VMEM((CELLS, CELLS), BF16),
            pltpu.VMEM((CELLS, 384), F32),
            pltpu.VMEM((CELLS, 3 * NODES), BF16),
            pltpu.VMEM((2, LAYER, 128), F32),
            pltpu.VMEM((2, LAYER, 128), F32),
            pltpu.VMEM((4, 2, LAYER, 128), F32),
            pltpu.VMEM((8, 128), F32),
            pltpu.VMEM((DOMS, 8, 128), F32),
            pltpu.VMEM((CELLS, 3 * NODES), BF16),
            pltpu.VMEM((3, MOST * CHUNK, 3 * NODES), BF16),
            pltpu.VMEM((MOST * CHUNK, NODES), F32),
            pltpu.VMEM(own, F32),
            dma((6,)), dma((12,)), dma, dma((2,)), dma((2,)), dma((10,)), dma((10,)), dma((2,)),
            dma((2,)), dma, dma, dma((3, MOST)), dma((3, MOST)), dma((2 * MOST,)), dma,
        ],
        compiler_params=pltpu.CompilerParams(
            collective_id=0, has_side_effects=True, vmem_limit_bytes=60 * 1024 * 1024
        ),
        name="solve_and_analyse",
    )(
        forcing, viscosity[None], mass_coef[None], element_order, owner,
        jnp.asarray(lanes), jnp.asarray(flat), jnp.asarray(mats),
    )
    return result[None]


def solution(mesh):
    in_specs = (P(None, "dom", None), P("dom"), P("dom"), P("dom", None), P("dom", None))
    out_specs = P("grp", "dom", None)
    return jax.shard_map(
        per_device, mesh=mesh, in_specs=in_specs, out_specs=out_specs, check_vma=False
    )
```

```python
import functools

import jax
import jax.numpy as jnp
import ml_dtypes
import numpy as np
from jax import lax
from jax.experimental import pallas as pl
from jax.experimental.pallas import tpu as pltpu
from jax.sharding import PartitionSpec as P

NP = 8
ITERS = 4
SWEEPS = 4
LAYER = 64
CELLS = 256
NODES = 512
DOMS = 32
CHUNK = 16
COUNTS = (5, 5, 4, 2)
FIRSTS = (0, 5, 10, 14)
MOST = max(COUNTS)
BASIS_LOW = 0.3
BASIS_HIGH = 2.0
THETA = 0.5 * (BASIS_LOW + BASIS_HIGH)
DELTA = 0.5 * (BASIS_HIGH - BASIS_LOW)
MESH = pl.DeviceIdType.MESH
F32 = jnp.float32
BF16 = jnp.bfloat16


def legendre_values(points, node_count):
    legendre = np.zeros((points.shape[0], node_count))
    legendre[:, 0] = 1.0
    legendre[:, 1] = points
    for poly_order in range(2, node_count):
        legendre[:, poly_order] = (
            (2 * poly_order - 1) * points * legendre[:, poly_order - 1]
            - (poly_order - 1) * legendre[:, poly_order - 2]
        ) / poly_order
    return legendre


def lobatto_table(node_count):
    degree = node_count - 1
    points = np.cos(np.pi * np.arange(node_count) / degree)
    for attempt in range(60):
        legendre = legendre_values(points, node_count)
        points = points - (points * legendre[:, degree] - legendre[:, degree - 1]) / (
            node_count * legendre[:, degree]
        )
    points = points[::-1].copy()
    end_values = legendre_values(points, node_count)[:, degree]
    weights = 2.0 / (degree * node_count * end_values * end_values)
    spacing = points[:, None] - points[None, :] + np.eye(node_count)
    diff_matrix = end_values[:, None] / end_values[None, :] / spacing
    diff_matrix = diff_matrix * (1.0 - np.eye(node_count))
    diff_matrix[0, 0] = -degree * node_count / 4.0
    diff_matrix[-1, -1] = degree * node_count / 4.0
    return (weights, diff_matrix)


def split_rows(matrix):
    high = matrix.astype(np.float32).astype(ml_dtypes.bfloat16)
    low = (matrix - high.astype(np.float64)).astype(np.float32).astype(ml_dtypes.bfloat16)
    return high, low


def tables():
    weights, diff = lobatto_table(NP)
    eye = np.eye(NP)
    cube = (
        weights[:, None, None] * weights[None, :, None] * weights[None, None, :]
    ).reshape(-1)
    directional = [
        np.kron(eye, np.kron(eye, diff)),
        np.kron(eye, np.kron(diff, eye)),
        np.kron(diff, np.kron(eye, eye)),
    ]
    stiff = np.zeros((NODES, NODES))
    for matrix in directional:
        stiff = stiff + matrix.T @ (cube[:, None] * matrix)
    flip = np.arange(NODES).reshape(NP, LAYER)[::-1][: NP // 2].reshape(-1)
    mats = []
    for matrix in (stiff, directional[2]):
        near, far = matrix[:256, :256], matrix[:256, flip]
        for block in (0.5 * (near + far), 0.5 * (near - far)):
            mats.append(np.stack(split_rows(block.T)))
    mats = np.stack(mats)
    flat = np.concatenate([directional[0].T[:128, :128], directional[1].T[:128, :128]], 1)
    high, low = split_rows(flat)
    flat = np.concatenate([high, high, low], 0)
    lanes = np.zeros((8, NODES), np.float32)
    lanes[0] = cube
    lanes[1] = np.diag(stiff)
    lanes[2] = np.repeat(diff[0], LAYER)
    order = [0, 1, 2, 3, 5, 4, 7, 6]
    lanes = lanes.reshape(8, NP, LAYER)[:, order].reshape(8, NODES)
    natural = cube.reshape(NP, LAYER).astype(np.float32).reshape(-1)
    lanes[3] = natural
    back = eye[::-1]
    half = np.eye(2)
    mirror = np.concatenate(
        [
            np.kron(half, np.kron(eye, back)),
            np.kron(half, np.kron(back, eye)),
            np.kron(half, np.kron(back, back)),
        ],
        1,
    ).astype(ml_dtypes.bfloat16)
    wide = np.concatenate([flat, np.zeros((384, 128), flat.dtype)], 1)
    return mats, np.concatenate([wide, mirror, mirror], 0), lanes


def rotated(value, shift, axis):
    return pltpu.roll(value, shift % value.shape[axis], axis)


def kernel(
    forcing, visc_in, mass_in, order_in, owner_in, lanes_in, flat_in, mats,
    out,
    fsc, lanes, flat, order_sc, owner_sc, weights, par, parn, pone, ptr, parts, visc, mass, raw, tmp,
    inv, lhs0, lhs1, lhs2, lhs3, v0, v1, v2, v3, xs, xstd, grads, gpack, classes, gcells, fsend, frecv, fghost, moments,
    red, packed, recv, lam, lamrecv,
    ssem, wsem, fsem, psend, precv, gsend, grecv, f3send, f3recv, rsend, rrecv, asend, arecv,
    osend, orecv,
):
    grp = lax.axis_index("grp")
    dom = lax.axis_index("dom")
    comp = jnp.minimum(grp, 2)
    up = lax.rem(dom + 1, DOMS)
    down = lax.rem(dom + DOMS - 1, DOMS)
    barrier = pltpu.get_barrier_semaphore()
    basis = (v0, v1, v2, v3)
    lefts = (lhs0, lhs1, lhs2, lhs3)
    every = (0, 1, 2, 3)

    at_y = [lax.rem(lax.div(dom, 8) + k, 4) * 8 for k in range(4)]
    at_z = [lax.rem(lax.div(dom, 2) + k, 4) * 2 for k in range(4)]
    at_core = [lax.rem(dom + k, 2) for k in range(2)]

    def hops(offset):
        return sum(min(k, 4 - k) for k in (offset // 8, offset // 2 % 4))

    peers = [
        (offset, at_y[offset // 8] + at_z[offset // 2 % 4] + at_core[offset % 2])
        for offset in sorted(range(1, DOMS), key=lambda offset: -hops(offset))
    ]

    for offset, peer in peers:
        pl.semaphore_signal(barrier, inc=1, device_id=(grp, peer), device_id_type=MESH)
    for step in range(1, 4):
        pl.semaphore_signal(
            barrier, inc=1, device_id=(lax.rem(grp + step, 4), dom), device_id_type=MESH
        )

    load_small = [
        pltpu.make_async_copy(source, target, ssem.at[k])
        for k, (source, target) in enumerate(
            (
                (visc_in, par.at[0:1]),
                (mass_in, par.at[1:2]),
                (order_in, order_sc),
                (owner_in, owner_sc),
                (lanes_in, lanes),
                (flat_in, flat),
            )
        )
    ]
    for copy in load_small:
        copy.start()
    load_force = pltpu.make_async_copy(forcing.at[comp], fsc, fsem)
    load_force.start()
    load_mats = []
    for which in range(4):
        for part, source in enumerate((0, 0, 1)):
            copy = pltpu.make_async_copy(
                mats.at[which, source],
                weights.at[which, part * 256 : part * 256 + 256],
                wsem.at[3 * which + part],
            )
            copy.start()
            load_mats.append(copy)

    lane = lax.broadcasted_iota(jnp.int32, (8, 128), 1)
    sub = lax.broadcasted_iota(jnp.int32, (8, 128), 0)
    node_i = lax.rem(lane, 8)
    node_j = lax.rem(lane // 8, 8)
    odd = lax.rem(sub, 2) == 1
    first_i = node_i == 0
    last_i = node_i == 7
    take_up = ((last_i & jnp.logical_not(odd)) | (first_i & odd & (sub < 7)))
    take_down = ((last_i & odd) | (first_i & jnp.logical_not(odd) & (sub > 0)))
    has_up = jnp.where(dom < DOMS - 1, 1.0, 0.0).astype(F32)
    has_down = jnp.where(dom > 0, 1.0, 0.0).astype(F32)

    def wide(mask):
        return jnp.broadcast_to(mask[None], (8, 8, 128))

    x_up = wide(take_up)
    x_down = wide(take_down)
    x_odd = wide(odd)
    y_last = wide(node_j == 7)
    y_first = wide(node_j == 0)
    low_half = wide(lane < LAYER)

    def x_others(a):
        above = rotated(a, -1, 1)
        below = rotated(a, 1, 1)
        return jnp.where(x_up, above, jnp.where(x_down, below, 0.0))

    def y_others(a):
        blank = jnp.zeros((1, 8, 128), F32)
        last = jnp.concatenate([a[k ^ 1 : (k ^ 1) + 1] for k in range(8)], 0)
        first = jnp.concatenate(
            [blank] + [a[k : k + 1] for k in (2, 1, 4, 3, 6, 5)] + [blank], 0
        )
        return jnp.where(y_last, last, jnp.where(y_first, first, 0.0))

    def xy_sum(a):
        a = a + x_others(a)
        return a + y_others(a)

    def rows_of(layer):
        if isinstance(layer, int):
            return slice(layer * LAYER, layer * LAYER + LAYER)
        return pl.ds(pl.multiple_of(layer * LAYER, LAYER), LAYER)

    def load(ref, layer, tile):
        return ref[rows_of(layer), tile * 128 : tile * 128 + 128].reshape(8, 8, 128)

    def store(ref, layer, tile, value):
        ref[rows_of(layer), tile * 128 : tile * 128 + 128] = value.reshape(LAYER, 128)

    def column(ref, layer):
        return ref[rows_of(layer), :].reshape(8, 8, 128)

    def table(row, tile):
        return lanes[row : row + 1, tile * 128 : tile * 128 + 128].reshape(1, 1, 128)

    def split(value):
        high = value.astype(BF16)
        return high, (value - high.astype(F32)).astype(BF16)

    def store_lhs(lhs, layer, pair, first, second):
        for start, value in ((0, first + second), (768, first - second)):
            start = start + pair * 128
            high, low = split(value.reshape(LAYER, 128))
            lhs[rows_of(layer), start : start + 128] = high
            lhs[rows_of(layer), start + 256 : start + 384] = low
            lhs[rows_of(layer), start + 512 : start + 640] = high

    def reversals(value):
        total = jnp.dot(
            jnp.concatenate(split(value), 1), flat[384:640, :], preferred_element_type=F32
        )
        return total[:, 0:128], total[:, 128:256], total[:, 256:384]

    def mirror_layers(value, tile, target, base, back):
        flipped = reversals(value)
        for layer in range(4):
            rows = slice(layer * LAYER, layer * LAYER + LAYER)
            plain, rev_x, rev_y, rev_xy = [
                part[rows].reshape(8, 8, 128) for part in (value,) + flipped
            ]
            even_y = jnp.where(x_odd, rev_x, plain)
            odd_y = jnp.where(x_odd, rev_xy, rev_y)
            mixed = jnp.concatenate(
                [(odd_y if k % 2 else even_y)[k : k + 1] for k in range(8)], 0
            )
            place = 3 - tile if layer % 2 else tile
            if (place if back else tile) >= 2:
                mixed = rotated(mixed, 64, 2)
            store(target, base + layer, place, mixed)

    def over(low, high, body):
        if isinstance(high, int):
            for layer in range(low, high):
                body(layer)
        else:
            lax.fori_loop(low, high, lambda layer, carry: (body(layer), carry)[1], 0)

    cell_sub = lax.broadcasted_iota(jnp.int32, (CELLS, CELLS), 0).astype(F32)
    cell_lane = lax.broadcasted_iota(jnp.int32, (CELLS, CELLS), 1).astype(F32)
    for copy in load_small:
        copy.wait()
    par[2:3, :] = order_sc[...].astype(F32)
    par[3:8, :] = jnp.zeros((5, CELLS), F32)

    def coefficients(ref, base, scale):
        hit = ref[2:3, :] == cell_sub
        for row, target in ((0, visc), (1, mass)):
            col = jnp.sum(jnp.where(hit, ref[row : row + 1, :], 0.0), axis=1, keepdims=True)
            target[base : base + CELLS, :] = jnp.broadcast_to(col * scale, (CELLS, 128))
        return hit

    one_hot = jnp.where(par[2:3, :] == cell_sub, 1.0, 0.0).astype(BF16)
    pone[:, 0:CELLS] = one_hot
    pone[:, CELLS : 2 * CELLS] = one_hot
    load_force.wait()
    high, low = split(fsc[...])
    parts[0:CELLS, :] = high
    parts[CELLS : 2 * CELLS, :] = low
    fsc[...] = jnp.dot(pone[...], parts[...], preferred_element_type=F32) * lanes[3:4, :]
    for tile in every:
        mirror_layers(fsc[:, tile * 128 : tile * 128 + 128], tile, raw, 4, False)

    pl.semaphore_wait(barrier, DOMS - 1 + 3)

    def remote(src, dst, send, recv_sem, device):
        return pltpu.make_async_remote_copy(
            src_ref=src, dst_ref=dst, send_sem=send, recv_sem=recv_sem,
            device_id=device, device_id_type=MESH,
        )

    par_copies = [
        remote(par, parn.at[0], psend.at[0], precv.at[0], (grp, up)),
        remote(par, parn.at[1], psend.at[1], precv.at[1], (grp, down)),
    ]
    def ghost(source, layers, first, last, target, slot, device):
        return remote(
            raw.at[source * LAYER : (source + layers) * LAYER, first:last],
            raw.at[target * LAYER : (target + layers) * LAYER, first:last],
            gsend.at[slot], grecv.at[slot], (grp, device),
        )

    near_copies = [
        ghost(7, 1, 0, 512, 3, 0, up),
        ghost(4, 1, 0, 512, 8, 1, down),
        ghost(6, 1, 384, 512, 2, 2, up),
        ghost(5, 1, 384, 512, 9, 3, down),
    ]
    far_copies = [
        ghost(6, 1, 0, 384, 2, 4, up),
        ghost(5, 1, 0, 384, 9, 5, down),
        ghost(5, 1, 0, 512, 1, 6, up),
        ghost(6, 1, 0, 512, 10, 7, down),
        ghost(4, 1, 384, 512, 0, 8, up),
        ghost(7, 1, 384, 512, 11, 9, down),
    ]
    for copy in par_copies + near_copies + far_copies:
        copy.start()

    coefficients(par, CELLS, 1.0)
    order_col = jnp.sum(
        jnp.where(cell_sub == cell_lane, par[2:3, :], 0.0), axis=1, keepdims=True
    )
    one_hot = jnp.where(order_col == cell_lane, 1.0, 0.0).astype(BF16)
    ptr[:, 0:CELLS] = one_hot
    ptr[:, CELLS : 2 * CELLS] = one_hot
    owner_row = owner_sc[...].astype(F32)
    owner_col = jnp.sum(
        jnp.where(cell_sub == cell_lane, owner_row, 0.0), axis=1, keepdims=True
    )
    same = (owner_col == owner_row) & (cell_sub < cell_lane)
    rank_row = jnp.sum(jnp.where(same, 1.0, 0.0), axis=0, keepdims=True)
    owner_int = owner_sc[...]
    place = owner_int >> 3
    piece_row = ((((owner_int >> 1) - place) & 3) << 1) + (owner_int & 1)
    first_row = (piece_row * 4 + place).astype(F32)
    dest_row = jnp.where(owner_row >= 0.0, first_row * 8.0 + rank_row, -1.0)
    slot_of = jnp.where(dest_row == cell_sub, 1.0, 0.0).astype(BF16)
    gpack[...] = jnp.dot(slot_of, one_hot, preferred_element_type=F32).astype(BF16)
    cell_id = lax.broadcasted_iota(jnp.int32, (CELLS, 128), 0)
    for k, width in enumerate((1, 8, 64)):
        parity = lax.rem(cell_id // width, 2).astype(F32).astype(BF16)
        classes[:, k * 128 : k * 128 + 128] = jnp.dot(
            gpack[...], parity, preferred_element_type=F32
        )

    for copy in par_copies:
        copy.wait()
    coefficients(parn.at[0], 0, has_down)
    coefficients(parn.at[1], 2 * CELLS, has_up)

    def partners(layer):
        parity = layer % 2 if isinstance(layer, int) else lax.rem(layer, 2)
        return {0: layer - 1 + 2 * parity, 3: layer + 1 - 2 * parity}

    def face_sum(ref, layer, tile):
        value = load(ref, layer, tile)
        other = load(ref, partners(layer)[tile], tile)
        return value + jnp.where(low_half, other, 0.0)

    def put_inverse(layer, tile, diag):
        store(inv, layer, tile, jnp.where(diag > 0.0, (2.0 / DELTA) / diag, 0.0))

    def diagonal(layer, tiles):
        coef_v = column(visc, layer)
        coef_m = column(mass, layer)
        for tile in tiles:
            diag = xy_sum(coef_v * table(1, tile) + coef_m * table(0, tile))
            if tile in (0, 3):
                store(tmp, layer, tile, diag)
            else:
                put_inverse(layer, tile, diag)

    diagonal(0, (3,))
    over(1, 11, lambda layer: diagonal(layer, every))
    diagonal(11, (3,))

    def diagonal_faces(layer):
        for tile in (0, 3):
            put_inverse(layer, tile, face_sum(tmp, layer, tile))

    over(1, 11, diagonal_faces)

    def first_value(layer, tile, force):
        value = force * load(inv, layer, tile) * (0.5 * DELTA)
        store(v0, layer, tile, value)
        return value

    def put_first(layer, pair, forces):
        values = [
            first_value(layer, tile, force) for tile, force in zip((pair, 3 - pair), forces)
        ]
        store_lhs(lhs0, layer, pair, *values)

    def assemble(layer, tiles, scale):
        sums = []
        for tile in tiles:
            force = load(raw, layer, tile)
            if scale is not None:
                force = force * scale
            force = xy_sum(force)
            if tile in (0, 3):
                store(tmp, layer, tile, force)
            else:
                sums.append(force)
        if sums:
            put_first(layer, 1, sums)

    over(4, 8, lambda layer: assemble(layer, every, None))
    for copy in load_mats:
        copy.wait()
    def multiply(lhs, low, high, which, target, first=0):
        for part in range(2):
            target[:, first + part * 256 : first + part * 256 + 256] = jnp.dot(
                lhs[low * LAYER : high * LAYER, part * 768 : part * 768 + 768],
                weights[2 * which + part],
                preferred_element_type=F32,
            )

    def advance(step, layer, pair, totals):
        values = []
        for tile, total in zip((pair, 3 - pair), totals):
            value = total * load(inv, layer, tile)
            current = load(basis[step], layer, tile)
            if step == 0:
                value = 0.5 * value - (THETA / DELTA) * current
            else:
                value = value - (2.0 * THETA / DELTA) * current
                value = value - load(basis[step - 1], layer, tile)
            store(basis[step + 1], layer, tile, value)
            values.append(value)
        store_lhs(lefts[step + 1], layer, pair, *values)

    def apply(step, layer, tiles, sums, going):
        coef_v = column(visc, layer)
        coef_m = column(mass, layer)
        for pair in (1, 0):
            if pair not in tiles and 3 - pair not in tiles:
                continue
            even = load(tmp, layer, pair)
            uneven = load(tmp, layer, 2 + pair)
            images = []
            for tile, product in ((pair, even + uneven), (3 - pair, even - uneven)):
                if tile not in tiles:
                    continue
                value = load(basis[step], layer, tile)
                weighted = coef_m * table(0, tile)
                image = coef_v * product + weighted * value
                if sums is not None:
                    diag = coef_v * table(1, tile) + weighted
                    sums = (
                        sums[0] + jnp.sum(value * image, axis=0),
                        sums[1] + jnp.sum(value * value * diag, axis=0),
                    )
                if going:
                    image = xy_sum(image)
                    if pair == 0:
                        store(tmp, layer, tile, image)
                    else:
                        images.append(image)
            if images:
                advance(step, layer, 1, images)
        return sums

    def faces(step, layer):
        advance(step, layer, 0, [face_sum(tmp, layer, tile) for tile in (0, 3)])

    blank_sums = (jnp.zeros((8, 128), F32), jnp.zeros((8, 128), F32))

    def own_apply(step, going):
        sums = blank_sums
        for layer in range(4, 8):
            sums = apply(step, layer, every, sums, going)
        moments[step : step + 1, :] = jnp.sum(sums[0], axis=0, keepdims=True)
        moments[4 + step : 5 + step, :] = jnp.sum(sums[1], axis=0, keepdims=True)

    def first_faces(layer):
        put_first(layer, 0, [face_sum(tmp, layer, tile) for tile in (0, 3)])

    for copy in near_copies:
        copy.wait()
    assemble(2, (3,), has_down)
    assemble(3, every, has_down)
    assemble(8, every, has_up)
    assemble(9, (3,), has_up)
    over(3, 9, first_faces)
    for layer in (2, 9):
        first_value(layer, 3, face_sum(tmp, layer, 3))
    multiply(lhs0, 3, 9, 0, tmp.at[3 * LAYER : 9 * LAYER])
    own_apply(0, True)
    for layer in (3, 8):
        apply(0, layer, every, None, True)

    for copy in far_copies:
        copy.wait()
    assemble(0, (3,), has_down)
    assemble(1, every, has_down)
    assemble(2, (0, 1, 2), has_down)
    assemble(9, (0, 1, 2), has_up)
    assemble(10, every, has_up)
    assemble(11, (3,), has_up)
    for layer in (1, 10):
        first_faces(layer)
    for layer in (2, 9):
        value = first_value(layer, 0, face_sum(tmp, layer, 0))
        store_lhs(lhs0, layer, 0, value, load(v0, layer, 3))
    far_rows = (slice(1 * LAYER, 3 * LAYER), slice(9 * LAYER, 11 * LAYER))
    for part in range(2):
        product = jnp.dot(
            jnp.concatenate(
                [lhs0[rows, part * 768 : part * 768 + 768] for rows in far_rows], 0
            ),
            weights[part],
            preferred_element_type=F32,
        )
        for side, rows in enumerate(far_rows):
            tmp[rows, part * 256 : part * 256 + 256] = product[
                side * 2 * LAYER : (side + 1) * 2 * LAYER
            ]
    apply(0, 1, (0,), None, True)
    apply(0, 2, every, None, True)
    apply(0, 9, every, None, True)
    apply(0, 10, (0,), None, True)
    over(2, 10, lambda layer: faces(0, layer))

    for step in range(1, ITERS):
        low, high = 1 + step, 11 - step
        going = step + 1 < ITERS
        multiply(lefts[step], low, 6, 0, tmp.at[low * LAYER : 6 * LAYER])
        multiply(lefts[step], 6, high, 0, tmp.at[6 * LAYER : high * LAYER])
        own_apply(step, going)
        if going:
            inward = 0 if low % 2 else 3
            apply(step, low, (inward,), None, True)
            over(low + 1, 4, lambda layer: apply(step, layer, every, None, True))
            over(8, high - 1, lambda layer: apply(step, layer, every, None, True))
            apply(step, high - 1, (inward,), None, True)
            over(low + 1, high - 1, lambda layer: faces(step, layer))

    red[0] = moments[...]
    for offset, peer in peers:
        remote(moments, red.at[offset], rsend, rrecv, (grp, peer)).start()

    def end_face(ref, layer):
        total = load(ref, layer, 0) * table(2, 0)
        for tile in (1, 2, 3):
            total = total + load(ref, layer, tile) * table(2, tile)
        total = total + rotated(total, 64, 2)
        return -total if layer % 2 else total

    fsend[0] = end_face(v3, 7).reshape(LAYER, 128)
    fsend[1] = end_face(v3, 4).reshape(LAYER, 128)
    face_copies = [
        remote(fsend.at[0], frecv.at[0], f3send.at[0], f3recv.at[0], (grp, up)),
        remote(fsend.at[1], frecv.at[1], f3send.at[1], f3recv.at[1], (grp, down)),
    ]
    for copy in face_copies:
        copy.start()

    own_rows = slice(4 * LAYER, 8 * LAYER)
    for index in range(ITERS):
        left = jnp.concatenate(
            [
                jnp.concatenate(
                    [
                        lefts[index][own_rows, start + part * 256 : start + part * 256 + 128]
                        for part in range(3)
                    ],
                    1,
                )
                for start in (0, 128, 768, 896)
            ],
            0,
        )
        both = jnp.dot(left, flat[0:384, 0:256], preferred_element_type=F32)
        for part in range(4):
            rows = slice(part * CELLS, part * CELLS + CELLS)
            grads[index, :, part * 128 : part * 128 + 128] = both[rows, 0:128]
            grads[index, :, NODES + part * 128 : NODES + part * 128 + 128] = both[rows, 128:256]
        multiply(lefts[index], 4, 8, 1, grads.at[index], 2 * NODES)
        if index < 3:
            fghost[index, 0] = end_face(basis[index], 3).reshape(LAYER, 128)
            fghost[index, 1] = end_face(basis[index], 8).reshape(LAYER, 128)

    for copy in face_copies:
        copy.wait()
    for side in range(2):
        fghost[3, side] = frecv[side]

    whole = remote(red.at[1:DOMS], red.at[1:DOMS], rsend, rrecv, (grp, up))
    whole.wait_send()
    whole.wait_recv()

    total = jnp.sum(red[...], axis=0)
    total = jnp.broadcast_to(jnp.sum(total, axis=1, keepdims=True), (8, 128))
    moments[...] = total

    def scalar(row):
        return jnp.broadcast_to(moments[row : row + 1, :], (8, 128))

    alpha = [scalar(row) for row in range(4)]
    beta = [scalar(4 + row) for row in range(4)]
    gamma = [(alpha[k] - THETA * beta[k]) * (1.0 / DELTA) for k in range(4)]
    mu = [beta[0], gamma[0]]
    ahead = gamma[0]
    for k in range(1, 4):
        ahead = 2.0 * gamma[k] - ahead
        mu.append(2.0 * beta[k] - mu[0])
        mu.append(2.0 * ahead - mu[1])

    def inner(i, j):
        return 0.5 * (mu[i + j] + mu[abs(i - j)])

    gram = [
        [
            DELTA * 0.5 * (inner(i, j + 1) + inner(i, abs(j - 1))) + THETA * inner(i, j)
            for j in range(4)
        ]
        for i in range(4)
    ]
    right = [mu[k] for k in range(4)]
    pivots = []
    for k in range(4):
        original = DELTA * 0.5 * (inner(k, k + 1) + inner(k, abs(k - 1))) + THETA * inner(k, k)
        pivot = gram[k][k]
        good = pivot > 1e-7 * original
        inverse = jnp.where(good, 1.0 / jnp.where(good, pivot, 1.0), 0.0)
        pivots.append(inverse)
        for i in range(k + 1, 4):
            factor = gram[i][k] * inverse
            for j in range(k + 1, 4):
                gram[i][j] = gram[i][j] - factor * gram[k][j]
            right[i] = right[i] - factor * right[k]
    coef = [None] * 4
    for k in (3, 2, 1, 0):
        value = right[k]
        for j in range(k + 1, 4):
            value = value - gram[k][j] * coef[j]
        coef[k] = value * pivots[k]

    coef8 = [(value * (1.0 / NP)).reshape(1, 8, 128) for value in coef]
    coef16 = [0.5 * value for value in coef8]
    x_sign = jnp.where(odd, -1.0, 1.0).reshape(1, 8, 128)
    x_scale = jnp.where(take_up | take_down, 0.5, 1.0).reshape(1, 8, 128) * x_sign
    y_half = jnp.where((node_j == 7) | (node_j == 0), 0.5, 1.0).reshape(1, 8, 128)
    y_end = jnp.where(node_j == 7, 0.5, 1.0).reshape(1, 8, 128)
    y_scale = jnp.concatenate(
        [y_end, -y_half, y_half, -y_half, y_half, -y_half, y_half, -y_end], 0
    )

    def combined(layer, direction, pair):
        parts_of = []
        scale = coef8 if direction == 2 else coef16
        for start in (0, 256):
            start = start + direction * NODES + pair * 128
            value = None
            for k in range(4):
                term = scale[k] * grads[k, rows_of(layer), start : start + 128].reshape(8, 8, 128)
                value = term if value is None else value + term
            parts_of.append(value)
        even, uneven = parts_of
        if direction == 2:
            return even + uneven, uneven - even
        return even + uneven, even - uneven

    def put_grad(layer, direction, tile, value):
        start = direction * NODES + tile * 128
        gcells[rows_of(layer), start : start + 128] = value.reshape(LAYER, 128).astype(BF16)

    def pack(direction):
        cols = slice(direction * NODES, direction * NODES + NODES)
        packed[:, cols] = jnp.dot(
            gpack[...], gcells[:, cols], preferred_element_type=F32
        ).astype(BF16)

    for direction, scale, others in ((0, x_scale, x_others), (1, y_scale, y_others)):
        for layer in range(4):
            for pair in (0, 1):
                for tile, value in zip((pair, 3 - pair), combined(layer, direction, pair)):
                    put_grad(layer, direction, tile, scale * (value - others(value)))
        pack(direction)

    for layer in range(4):
        z_sign = -1.0 if layer % 2 else 1.0
        for tile, value in zip((1, 2), combined(layer, 2, 1)):
            put_grad(layer, 2, tile, z_sign * value)
        for tile, value in zip((0, 3), combined(layer, 2, 0)):
            store(xstd, layer, tile, z_sign * value)

    def mean_face(layer, tile, other, there):
        value = load(xstd, layer, tile)
        put_grad(layer, 2, tile, value + jnp.where(low_half, there * (other - value), 0.0))

    for layer in range(4):
        mean_face(layer, 3, load(xstd, layer ^ 1, 3), 0.5)
        if layer in (1, 2):
            mean_face(layer, 0, load(xstd, 3 - layer, 0), 0.5)
        else:
            side = 0 if layer == 0 else 1
            other = None
            for k in range(4):
                term = coef8[k] * fghost[k, side].reshape(8, 8, 128)
                other = term if other is None else other + term
            mean_face(layer, 0, other, 0.5 * (has_up if side else has_down))

    def by_row(values):
        picked = values[3]
        for row in (2, 1, 0):
            picked = jnp.where(grp == row, values[row], picked)
        return picked

    own_first = by_row([first * CHUNK for first in FIRSTS])
    own_count = by_row(COUNTS)

    pack(2)

    def chunk_rows(chunk, base=0):
        return pl.ds(pl.multiple_of(base + chunk * CHUNK, CHUNK), CHUNK)

    def turn(step, count):
        return lax.rem(dom + step, count)

    def piece_copy(step, target, slot):
        chunk = turn(step, COUNTS[target])
        return remote(
            packed.at[chunk_rows(chunk, FIRSTS[target] * CHUNK)],
            recv.at[comp, chunk_rows(chunk)],
            asend.at[slot, step], arecv.at[comp, chunk], (target, dom),
        )

    def each_send(action):
        for row, targets in enumerate(((2, 1, 3), (3, 2, 0), (1,), (0,))):

            @pl.when(grp == row)
            def _():
                for step in range(MOST):
                    for slot, target in enumerate(targets):
                        if step < COUNTS[target]:
                            action(piece_copy(step, target, slot))

    each_send(lambda copy: copy.start())
    for row in range(4):

        @pl.when(grp == row)
        def _():
            slots = COUNTS[row] * CHUNK
            first = FIRSTS[row] * CHUNK
            recv[min(row, 2), 0:slots] = packed[first : first + slots, :]

    wide8 = [value.reshape(1, 8, 128) for value in coef]

    @pl.when(grp < 3)
    def _():
        def solve_layer(layer):
            for tile in every:
                value = wide8[0] * load(v0, layer, tile)
                for k in range(1, 4):
                    value = value + wide8[k] * load(basis[k], layer, tile)
                store(xs, layer - 4, tile, value)

        over(4, 8, solve_layer)
        for tile in every:
            mirror_layers(xs[:, tile * 128 : tile * 128 + 128], tile, xstd, 0, True)
        high, low = split(xstd[...])
        parts[0:CELLS, :] = high
        parts[CELLS : 2 * CELLS, :] = low
        out[...] = jnp.dot(ptr[...], parts[...], preferred_element_type=F32)

    def lambda_rows(block, carry):
        rows = pl.ds(pl.multiple_of(block * 16, 16), 16)
        jac = [
            [recv[c, rows, d * NODES : d * NODES + NODES].astype(F32) for d in range(3)]
            for c in range(3)
        ]
        lam[rows, :] = lambda_two(jac)
        return carry

    def natural_order(chunk):
        rows = chunk_rows(chunk)
        slots = pl.ds(pl.multiple_of(own_first + chunk * CHUNK, CHUNK), CHUNK)
        odd_x, odd_y, odd_z = [
            classes[slots, k * 128 : k * 128 + 128] > 0.5 for k in range(3)
        ]
        values = [lam[rows, tile * 128 : tile * 128 + 128] for tile in every]
        flipped = reversals(jnp.concatenate(values, 0))
        turned = []
        for tile in every:
            rev_x, rev_y, rev_xy = [
                part[tile * CHUNK : tile * CHUNK + CHUNK] for part in flipped
            ]
            turned.append(
                jnp.where(
                    odd_x,
                    jnp.where(odd_y, rev_xy, rev_x),
                    jnp.where(odd_y, rev_y, values[tile]),
                )
            )
        for tile in every:
            value = jnp.where(odd_z, turned[3 - tile], turned[tile])
            if tile >= 2:
                value = rotated(value, 64, 1)
            lam[rows, tile * 128 : tile * 128 + 128] = value

    here = pl.ds(pl.multiple_of(dom * 8, 8), 8)

    def each_owner(chunk, action, local):
        piece = lax.div(own_first, CHUNK) + chunk
        four = lax.div(piece, 2)
        for part in range(2):
            place = lax.rem(piece, 2) * 2 + part
            owner = place * 8 + lax.rem(place + lax.div(four, 2), 4) * 2 + lax.rem(four, 2)
            rows = pl.ds(pl.multiple_of(chunk * CHUNK + part * 8, 8), 8)
            own = (grp == 3) & (owner == dom)

            @pl.when(jnp.logical_not(own))
            def _():
                action(
                    remote(
                        lam.at[rows], lamrecv.at[here], osend.at[chunk * 2 + part], orecv,
                        (3, owner),
                    )
                )

            if local:

                @pl.when(own)
                def _():
                    lamrecv[here, :] = lam[rows, :]

    def analyse(chunk):
        for step in (1, 2):
            other = lax.rem(comp + step, 3)
            piece = recv.at[other, chunk_rows(chunk)]
            remote(
                piece, piece, asend.at[0, 0], arecv.at[other, chunk], (lax.rem(grp + 1, 4), dom)
            ).wait_recv()
        lambda_rows(chunk, 0)
        natural_order(chunk)
        each_owner(chunk, lambda copy: copy.start(), True)

    over(0, own_count, lambda step: analyse(turn(step, own_count)))
    over(
        0,
        own_count,
        lambda step: each_owner(turn(step, own_count), lambda copy: copy.wait_send(), False),
    )
    each_send(lambda copy: copy.wait_send())

    def wait_rows(count):
        piece = lamrecv.at[0 : 8 * count]
        remote(piece, piece, osend.at[0], orecv, (lax.rem(grp + 1, 4), dom)).wait_recv()

    four = lax.rem(lax.div(lax.rem(dom, 8), 2) - lax.div(dom, 8) + 4, 4) * 2 + lax.rem(dom, 2)
    to_itself = four * 2 + lax.div(dom, 16) >= FIRSTS[3]

    @pl.when((grp == 3) & to_itself)
    def _():
        wait_rows(31)

    @pl.when((grp == 3) & jnp.logical_not(to_itself))
    def _():
        wait_rows(32)

    @pl.when(grp == 3)
    def _():
        out[...] = lamrecv[...]


def lambda_two(jac):
    strain = [[0.5 * (jac[a][b] + jac[b][a]) for b in range(3)] for a in range(3)]
    spin = [[0.5 * (jac[a][b] - jac[b][a]) for b in range(3)] for a in range(3)]
    m = [[None] * 3 for _ in range(3)]
    for a in range(3):
        for b in range(a, 3):
            value = strain[a][0] * strain[0][b] + spin[a][0] * spin[0][b]
            for k in (1, 2):
                value = value + strain[a][k] * strain[k][b] + spin[a][k] * spin[k][b]
            m[a][b] = value
            m[b][a] = value
    for sweep in range(SWEEPS):
        for p, q, r in ((0, 1, 2), (0, 2, 1), (1, 2, 0)):
            last = sweep == SWEEPS - 1
            twice = 2.0 * m[p][q]
            gap = m[p][p] - m[q][q]
            square = twice * twice + gap * gap
            inverse = lax.rsqrt(jnp.maximum(square, 1e-36))
            length = square * inverse
            mean = 0.5 * (m[p][p] + m[q][q])
            m[p][p] = mean + 0.5 * length
            m[q][q] = mean - 0.5 * length
            if last and (p, q) == (1, 2):
                continue
            none = square < 1e-36
            cosine2 = jnp.where(none, 1.0, jnp.abs(gap) * inverse)
            sine2 = jnp.where(none, 0.0, twice * inverse)
            larger = 0.5 + 0.5 * cosine2
            root = lax.rsqrt(larger)
            big = larger * root
            small = 0.5 * sine2 * root
            flip = gap < 0.0
            sine_big = jnp.where(sine2 < 0.0, -big, big)
            cosine = jnp.where(flip, jnp.abs(small), big)
            sine = jnp.where(flip, sine_big, small)
            side_p = m[r][p]
            side_q = m[r][q]
            m[r][p] = m[p][r] = cosine * side_p + sine * side_q
            m[r][q] = m[q][r] = cosine * side_q - sine * side_p
            m[p][q] = m[q][p] = jnp.zeros_like(side_p)
    diagonal = [m[0][0], m[1][1], m[2][2]]
    largest = jnp.maximum(jnp.maximum(diagonal[0], diagonal[1]), diagonal[2])
    smallest = jnp.minimum(jnp.minimum(diagonal[0], diagonal[1]), diagonal[2])
    return diagonal[0] + diagonal[1] + diagonal[2] - largest - smallest


def per_device(forcing, viscosity, mass_coef, element_order, owner):
    mats, flat, lanes = tables()
    vmem = pl.BlockSpec(memory_space=pltpu.VMEM)
    hbm = pl.BlockSpec(memory_space=pltpu.HBM)
    wide = (12 * LAYER, NODES)
    own = (CELLS, NODES)
    dma = pltpu.SemaphoreType.DMA
    result = pl.pallas_call(
        kernel,
        out_shape=pltpu.VMEM(own, F32),
        in_specs=[hbm] * 8,
        out_specs=vmem,
        scratch_shapes=[
            pltpu.VMEM(own, F32),
            pltpu.VMEM((8, NODES), F32),
            pltpu.VMEM((640, 384), BF16),
            pltpu.VMEM((1, CELLS), jnp.int32),
            pltpu.VMEM((1, CELLS), jnp.int32),
            pltpu.VMEM((4, 768, 256), BF16),
            pltpu.VMEM((8, CELLS), F32),
            pltpu.VMEM((2, 8, CELLS), F32),
            pltpu.VMEM((CELLS, 2 * CELLS), BF16),
            pltpu.VMEM((CELLS, 2 * CELLS), BF16),
            pltpu.VMEM((2 * CELLS, NODES), BF16),
            pltpu.VMEM((12 * LAYER, 128), F32),
            pltpu.VMEM((12 * LAYER, 128), F32),
            pltpu.VMEM(wide, F32),
            pltpu.VMEM(wide, F32),
            pltpu.VMEM(wide, F32),
            pltpu.VMEM((12 * LAYER, 3 * NODES), BF16),
            pltpu.VMEM((12 * LAYER, 3 * NODES), BF16),
            pltpu.VMEM((12 * LAYER, 3 * NODES), BF16),
            pltpu.VMEM((12 * LAYER, 3 * NODES), BF16),
            pltpu.VMEM(wide, F32),
            pltpu.VMEM(wide, F32),
            pltpu.VMEM(wide, F32),
            pltpu.VMEM(wide, F32),
            pltpu.VMEM(own, F32),
            pltpu.VMEM(own, F32),
            pltpu.VMEM((4, CELLS, 3 * NODES), F32),
            pltpu.VMEM((CELLS, CELLS), BF16),
            pltpu.VMEM((CELLS, 384), F32),
            pltpu.VMEM((CELLS, 3 * NODES), BF16),
            pltpu.VMEM((2, LAYER, 128), F32),
            pltpu.VMEM((2, LAYER, 128), F32),
            pltpu.VMEM((4, 2, LAYER, 128), F32),
            pltpu.VMEM((8, 128), F32),
            pltpu.VMEM((DOMS, 8, 128), F32),
            pltpu.VMEM((CELLS, 3 * NODES), BF16),
            pltpu.VMEM((3, MOST * CHUNK, 3 * NODES), BF16),
            pltpu.VMEM((MOST * CHUNK, NODES), F32),
            pltpu.VMEM(own, F32),
            dma((6,)), dma((12,)), dma, dma((2,)), dma((2,)), dma((10,)), dma((10,)), dma((2,)),
            dma((2,)), dma, dma, dma((3, MOST)), dma((3, MOST)), dma((2 * MOST,)), dma,
        ],
        compiler_params=pltpu.CompilerParams(
            collective_id=0, has_side_effects=True, vmem_limit_bytes=60 * 1024 * 1024
        ),
        name="solve_and_analyse",
    )(
        forcing, viscosity[None], mass_coef[None], element_order, owner,
        jnp.asarray(lanes), jnp.asarray(flat), jnp.asarray(mats),
    )
    return result[None]


def solution(mesh):
    in_specs = (P(None, "dom", None), P("dom"), P("dom"), P("dom", None), P("dom", None))
    out_specs = P("grp", "dom", None)
    return jax.shard_map(
        per_device, mesh=mesh, in_specs=in_specs, out_specs=out_specs, check_vma=False
    )
```

```python
import functools

import jax
import jax.numpy as jnp
import ml_dtypes
import numpy as np
from jax import lax
from jax.experimental import pallas as pl
from jax.experimental.pallas import tpu as pltpu
from jax.sharding import PartitionSpec as P

NP = 8
ITERS = 4
SWEEPS = 4
LAYER = 64
CELLS = 256
NODES = 512
DOMS = 32
CHUNK = 16
COUNTS = (5, 5, 4, 2)
FIRSTS = (0, 5, 10, 14)
MOST = max(COUNTS)
BASIS_LOW = 0.3
BASIS_HIGH = 2.0
THETA = 0.5 * (BASIS_LOW + BASIS_HIGH)
DELTA = 0.5 * (BASIS_HIGH - BASIS_LOW)
MESH = pl.DeviceIdType.MESH
F32 = jnp.float32
BF16 = jnp.bfloat16


def legendre_values(points, node_count):
    legendre = np.zeros((points.shape[0], node_count))
    legendre[:, 0] = 1.0
    legendre[:, 1] = points
    for poly_order in range(2, node_count):
        legendre[:, poly_order] = (
            (2 * poly_order - 1) * points * legendre[:, poly_order - 1]
            - (poly_order - 1) * legendre[:, poly_order - 2]
        ) / poly_order
    return legendre


def lobatto_table(node_count):
    degree = node_count - 1
    points = np.cos(np.pi * np.arange(node_count) / degree)
    for attempt in range(60):
        legendre = legendre_values(points, node_count)
        points = points - (points * legendre[:, degree] - legendre[:, degree - 1]) / (
            node_count * legendre[:, degree]
        )
    points = points[::-1].copy()
    end_values = legendre_values(points, node_count)[:, degree]
    weights = 2.0 / (degree * node_count * end_values * end_values)
    spacing = points[:, None] - points[None, :] + np.eye(node_count)
    diff_matrix = end_values[:, None] / end_values[None, :] / spacing
    diff_matrix = diff_matrix * (1.0 - np.eye(node_count))
    diff_matrix[0, 0] = -degree * node_count / 4.0
    diff_matrix[-1, -1] = degree * node_count / 4.0
    return (weights, diff_matrix)


def split_rows(matrix):
    high = matrix.astype(np.float32).astype(ml_dtypes.bfloat16)
    low = (matrix - high.astype(np.float64)).astype(np.float32).astype(ml_dtypes.bfloat16)
    return high, low


def tables():
    weights, diff = lobatto_table(NP)
    eye = np.eye(NP)
    cube = (
        weights[:, None, None] * weights[None, :, None] * weights[None, None, :]
    ).reshape(-1)
    directional = [
        np.kron(eye, np.kron(eye, diff)),
        np.kron(eye, np.kron(diff, eye)),
        np.kron(diff, np.kron(eye, eye)),
    ]
    stiff = np.zeros((NODES, NODES))
    for matrix in directional:
        stiff = stiff + matrix.T @ (cube[:, None] * matrix)
    flip = np.arange(NODES).reshape(NP, LAYER)[::-1][: NP // 2].reshape(-1)
    mats = []
    for matrix in (stiff, directional[2]):
        near, far = matrix[:256, :256], matrix[:256, flip]
        for block in (0.5 * (near + far), 0.5 * (near - far)):
            mats.append(np.stack(split_rows(block.T)))
    mats = np.stack(mats)
    flat = np.concatenate([directional[0].T[:128, :128], directional[1].T[:128, :128]], 1)
    high, low = split_rows(flat)
    flat = np.concatenate([high, high, low], 0)
    lanes = np.zeros((8, NODES), np.float32)
    lanes[0] = cube
    lanes[1] = np.diag(stiff)
    lanes[2] = np.repeat(diff[0], LAYER)
    order = [0, 1, 2, 3, 5, 4, 7, 6]
    lanes = lanes.reshape(8, NP, LAYER)[:, order].reshape(8, NODES)
    natural = cube.reshape(NP, LAYER).astype(np.float32).reshape(-1)
    lanes[3] = natural
    back = eye[::-1]
    half = np.eye(2)
    mirror = np.concatenate(
        [
            np.kron(half, np.kron(eye, back)),
            np.kron(half, np.kron(back, eye)),
            np.kron(half, np.kron(back, back)),
        ],
        1,
    ).astype(ml_dtypes.bfloat16)
    wide = np.concatenate([flat, np.zeros((384, 128), flat.dtype)], 1)
    return mats, np.concatenate([wide, mirror, mirror], 0), lanes


def rotated(value, shift, axis):
    return pltpu.roll(value, shift % value.shape[axis], axis)


def kernel(
    forcing, visc_in, mass_in, order_in, owner_in, lanes_in, flat_in, mats,
    out,
    fsc, lanes, flat, order_sc, owner_sc, weights, par, parn, pone, ptr, parts, visc, mass, raw, tmp,
    inv, lhs0, lhs1, lhs2, lhs3, v0, v1, v2, v3, xs, xstd, grads, gpack, classes, gcells, fsend, frecv, fghost, moments,
    red, packed, recv, lam, lamrecv,
    ssem, wsem, fsem, psend, precv, gsend, grecv, f3send, f3recv, rsend, rrecv, asend, arecv,
    osend, orecv,
):
    grp = lax.axis_index("grp")
    dom = lax.axis_index("dom")
    comp = jnp.minimum(grp, 2)
    up = lax.rem(dom + 1, DOMS)
    down = lax.rem(dom + DOMS - 1, DOMS)
    barrier = pltpu.get_barrier_semaphore()
    basis = (v0, v1, v2, v3)
    lefts = (lhs0, lhs1, lhs2, lhs3)
    every = (0, 1, 2, 3)

    at_y = [lax.rem(lax.div(dom, 8) + k, 4) * 8 for k in range(4)]
    at_z = [lax.rem(lax.div(dom, 2) + k, 4) * 2 for k in range(4)]
    at_core = [lax.rem(dom + k, 2) for k in range(2)]

    def hops(offset):
        return sum(min(k, 4 - k) for k in (offset // 8, offset // 2 % 4))

    peers = [
        (offset, at_y[offset // 8] + at_z[offset // 2 % 4] + at_core[offset % 2])
        for offset in sorted(range(1, DOMS), key=lambda offset: -hops(offset))
    ]

    for offset, peer in peers:
        pl.semaphore_signal(barrier, inc=1, device_id=(grp, peer), device_id_type=MESH)
    for step in range(1, 4):
        pl.semaphore_signal(
            barrier, inc=1, device_id=(lax.rem(grp + step, 4), dom), device_id_type=MESH
        )

    load_small = [
        pltpu.make_async_copy(source, target, ssem.at[k])
        for k, (source, target) in enumerate(
            (
                (visc_in, par.at[0:1]),
                (mass_in, par.at[1:2]),
                (order_in, order_sc),
                (owner_in, owner_sc),
                (lanes_in, lanes),
                (flat_in, flat),
            )
        )
    ]
    for copy in load_small:
        copy.start()
    load_force = pltpu.make_async_copy(forcing.at[comp], fsc, fsem)
    load_force.start()
    load_mats = []
    for which in range(4):
        for part, source in enumerate((0, 0, 1)):
            copy = pltpu.make_async_copy(
                mats.at[which, source],
                weights.at[which, part * 256 : part * 256 + 256],
                wsem.at[3 * which + part],
            )
            copy.start()
            load_mats.append(copy)

    lane = lax.broadcasted_iota(jnp.int32, (8, 128), 1)
    sub = lax.broadcasted_iota(jnp.int32, (8, 128), 0)
    node_i = lax.rem(lane, 8)
    node_j = lax.rem(lane // 8, 8)
    odd = lax.rem(sub, 2) == 1
    first_i = node_i == 0
    last_i = node_i == 7
    take_up = ((last_i & jnp.logical_not(odd)) | (first_i & odd & (sub < 7)))
    take_down = ((last_i & odd) | (first_i & jnp.logical_not(odd) & (sub > 0)))
    has_up = jnp.where(dom < DOMS - 1, 1.0, 0.0).astype(F32)
    has_down = jnp.where(dom > 0, 1.0, 0.0).astype(F32)

    def wide(mask):
        return jnp.broadcast_to(mask[None], (8, 8, 128))

    x_up = wide(take_up)
    x_down = wide(take_down)
    x_odd = wide(odd)
    y_last = wide(node_j == 7)
    y_first = wide(node_j == 0)
    low_half = wide(lane < LAYER)

    def x_others(a):
        above = rotated(a, -1, 1)
        below = rotated(a, 1, 1)
        return jnp.where(x_up, above, jnp.where(x_down, below, 0.0))

    def y_others(a):
        blank = jnp.zeros((1, 8, 128), F32)
        last = jnp.concatenate([a[k ^ 1 : (k ^ 1) + 1] for k in range(8)], 0)
        first = jnp.concatenate(
            [blank] + [a[k : k + 1] for k in (2, 1, 4, 3, 6, 5)] + [blank], 0
        )
        return jnp.where(y_last, last, jnp.where(y_first, first, 0.0))

    def xy_sum(a):
        a = a + x_others(a)
        return a + y_others(a)

    def rows_of(layer):
        if isinstance(layer, int):
            return slice(layer * LAYER, layer * LAYER + LAYER)
        return pl.ds(pl.multiple_of(layer * LAYER, LAYER), LAYER)

    def load(ref, layer, tile):
        return ref[rows_of(layer), tile * 128 : tile * 128 + 128].reshape(8, 8, 128)

    def store(ref, layer, tile, value):
        ref[rows_of(layer), tile * 128 : tile * 128 + 128] = value.reshape(LAYER, 128)

    def column(ref, layer):
        return ref[rows_of(layer), :].reshape(8, 8, 128)

    def table(row, tile):
        return lanes[row : row + 1, tile * 128 : tile * 128 + 128].reshape(1, 1, 128)

    def split(value):
        high = value.astype(BF16)
        return high, (value - high.astype(F32)).astype(BF16)

    def store_lhs(lhs, layer, pair, first, second):
        for start, value in ((0, first + second), (768, first - second)):
            start = start + pair * 128
            high, low = split(value.reshape(LAYER, 128))
            lhs[rows_of(layer), start : start + 128] = high
            lhs[rows_of(layer), start + 256 : start + 384] = low
            lhs[rows_of(layer), start + 512 : start + 640] = high

    def reversals(value):
        total = jnp.dot(
            jnp.concatenate(split(value), 1), flat[384:640, :], preferred_element_type=F32
        )
        return total[:, 0:128], total[:, 128:256], total[:, 256:384]

    def mirror_layers(value, tile, target, base, back):
        flipped = reversals(value)
        for layer in range(4):
            rows = slice(layer * LAYER, layer * LAYER + LAYER)
            plain, rev_x, rev_y, rev_xy = [
                part[rows].reshape(8, 8, 128) for part in (value,) + flipped
            ]
            even_y = jnp.where(x_odd, rev_x, plain)
            odd_y = jnp.where(x_odd, rev_xy, rev_y)
            mixed = jnp.concatenate(
                [(odd_y if k % 2 else even_y)[k : k + 1] for k in range(8)], 0
            )
            place = 3 - tile if layer % 2 else tile
            if (place if back else tile) >= 2:
                mixed = rotated(mixed, 64, 2)
            store(target, base + layer, place, mixed)

    def over(low, high, body):
        if isinstance(high, int):
            for layer in range(low, high):
                body(layer)
        else:
            lax.fori_loop(low, high, lambda layer, carry: (body(layer), carry)[1], 0)

    cell_sub = lax.broadcasted_iota(jnp.int32, (CELLS, CELLS), 0).astype(F32)
    cell_lane = lax.broadcasted_iota(jnp.int32, (CELLS, CELLS), 1).astype(F32)
    for copy in load_small:
        copy.wait()
    par[2:3, :] = order_sc[...].astype(F32)
    par[3:8, :] = jnp.zeros((5, CELLS), F32)

    def coefficients(ref, base, scale):
        hit = ref[2:3, :] == cell_sub
        for row, target in ((0, visc), (1, mass)):
            col = jnp.sum(jnp.where(hit, ref[row : row + 1, :], 0.0), axis=1, keepdims=True)
            target[base : base + CELLS, :] = jnp.broadcast_to(col * scale, (CELLS, 128))
        return hit

    one_hot = jnp.where(par[2:3, :] == cell_sub, 1.0, 0.0).astype(BF16)
    pone[:, 0:CELLS] = one_hot
    pone[:, CELLS : 2 * CELLS] = one_hot
    load_force.wait()
    high, low = split(fsc[...])
    parts[0:CELLS, :] = high
    parts[CELLS : 2 * CELLS, :] = low
    fsc[...] = jnp.dot(pone[...], parts[...], preferred_element_type=F32) * lanes[3:4, :]
    for tile in every:
        mirror_layers(fsc[:, tile * 128 : tile * 128 + 128], tile, raw, 4, False)

    pl.semaphore_wait(barrier, DOMS - 1 + 3)

    def remote(src, dst, send, recv_sem, device):
        return pltpu.make_async_remote_copy(
            src_ref=src, dst_ref=dst, send_sem=send, recv_sem=recv_sem,
            device_id=device, device_id_type=MESH,
        )

    par_copies = [
        remote(par, parn.at[0], psend.at[0], precv.at[0], (grp, up)),
        remote(par, parn.at[1], psend.at[1], precv.at[1], (grp, down)),
    ]
    def ghost(source, layers, first, last, target, slot, device):
        return remote(
            raw.at[source * LAYER : (source + layers) * LAYER, first:last],
            raw.at[target * LAYER : (target + layers) * LAYER, first:last],
            gsend.at[slot], grecv.at[slot], (grp, device),
        )

    near_copies = [
        ghost(7, 1, 0, 512, 3, 0, up),
        ghost(4, 1, 0, 512, 8, 1, down),
        ghost(6, 1, 384, 512, 2, 2, up),
        ghost(5, 1, 384, 512, 9, 3, down),
    ]
    far_copies = [
        ghost(6, 1, 0, 384, 2, 4, up),
        ghost(5, 1, 0, 384, 9, 5, down),
        ghost(5, 1, 0, 512, 1, 6, up),
        ghost(6, 1, 0, 512, 10, 7, down),
        ghost(4, 1, 384, 512, 0, 8, up),
        ghost(7, 1, 384, 512, 11, 9, down),
    ]
    for copy in par_copies + near_copies + far_copies:
        copy.start()

    coefficients(par, CELLS, 1.0)
    order_col = jnp.sum(
        jnp.where(cell_sub == cell_lane, par[2:3, :], 0.0), axis=1, keepdims=True
    )
    one_hot = jnp.where(order_col == cell_lane, 1.0, 0.0).astype(BF16)
    ptr[:, 0:CELLS] = one_hot
    ptr[:, CELLS : 2 * CELLS] = one_hot
    owner_row = owner_sc[...].astype(F32)
    owner_col = jnp.sum(
        jnp.where(cell_sub == cell_lane, owner_row, 0.0), axis=1, keepdims=True
    )
    same = (owner_col == owner_row) & (cell_sub < cell_lane)
    rank_row = jnp.sum(jnp.where(same, 1.0, 0.0), axis=0, keepdims=True)
    owner_int = owner_sc[...]
    place = owner_int >> 3
    piece_row = ((((owner_int >> 1) - place) & 3) << 1) + (owner_int & 1)
    first_row = (piece_row * 4 + place).astype(F32)
    dest_row = jnp.where(owner_row >= 0.0, first_row * 8.0 + rank_row, -1.0)
    slot_of = jnp.where(dest_row == cell_sub, 1.0, 0.0).astype(BF16)
    gpack[...] = jnp.dot(slot_of, one_hot, preferred_element_type=F32).astype(BF16)
    cell_id = lax.broadcasted_iota(jnp.int32, (CELLS, 128), 0)
    for k, width in enumerate((1, 8, 64)):
        parity = lax.rem(cell_id // width, 2).astype(F32).astype(BF16)
        classes[:, k * 128 : k * 128 + 128] = jnp.dot(
            gpack[...], parity, preferred_element_type=F32
        )

    for copy in par_copies:
        copy.wait()
    coefficients(parn.at[0], 0, has_down)
    coefficients(parn.at[1], 2 * CELLS, has_up)

    def partners(layer):
        parity = layer % 2 if isinstance(layer, int) else lax.rem(layer, 2)
        return {0: layer - 1 + 2 * parity, 3: layer + 1 - 2 * parity}

    def face_sum(ref, layer, tile):
        value = load(ref, layer, tile)
        other = load(ref, partners(layer)[tile], tile)
        return value + jnp.where(low_half, other, 0.0)

    def put_inverse(layer, tile, diag):
        store(inv, layer, tile, jnp.where(diag > 0.0, (2.0 / DELTA) / diag, 0.0))

    def diagonal(layer, tiles):
        coef_v = column(visc, layer)
        coef_m = column(mass, layer)
        for tile in tiles:
            diag = xy_sum(coef_v * table(1, tile) + coef_m * table(0, tile))
            if tile in (0, 3):
                store(tmp, layer, tile, diag)
            else:
                put_inverse(layer, tile, diag)

    diagonal(0, (3,))
    over(1, 11, lambda layer: diagonal(layer, every))
    diagonal(11, (3,))

    def diagonal_faces(layer):
        for tile in (0, 3):
            put_inverse(layer, tile, face_sum(tmp, layer, tile))

    over(1, 11, diagonal_faces)

    def first_value(layer, tile, force):
        value = force * load(inv, layer, tile) * (0.5 * DELTA)
        store(v0, layer, tile, value)
        return value

    def put_first(layer, pair, forces):
        values = [
            first_value(layer, tile, force) for tile, force in zip((pair, 3 - pair), forces)
        ]
        store_lhs(lhs0, layer, pair, *values)

    def assemble(layer, tiles, scale):
        sums = []
        for tile in tiles:
            force = load(raw, layer, tile)
            if scale is not None:
                force = force * scale
            force = xy_sum(force)
            if tile in (0, 3):
                store(tmp, layer, tile, force)
            else:
                sums.append(force)
        if sums:
            put_first(layer, 1, sums)

    over(4, 8, lambda layer: assemble(layer, every, None))
    for copy in load_mats:
        copy.wait()
    def multiply(lhs, low, high, which, target, first=0):
        for part in range(2):
            target[:, first + part * 256 : first + part * 256 + 256] = jnp.dot(
                lhs[low * LAYER : high * LAYER, part * 768 : part * 768 + 768],
                weights[2 * which + part],
                preferred_element_type=F32,
            )

    def advance(step, layer, pair, totals):
        values = []
        for tile, total in zip((pair, 3 - pair), totals):
            value = total * load(inv, layer, tile)
            current = load(basis[step], layer, tile)
            if step == 0:
                value = 0.5 * value - (THETA / DELTA) * current
            else:
                value = value - (2.0 * THETA / DELTA) * current
                value = value - load(basis[step - 1], layer, tile)
            store(basis[step + 1], layer, tile, value)
            values.append(value)
        store_lhs(lefts[step + 1], layer, pair, *values)

    def apply(step, layer, tiles, sums, going):
        coef_v = column(visc, layer)
        coef_m = column(mass, layer)
        for pair in (1, 0):
            if pair not in tiles and 3 - pair not in tiles:
                continue
            even = load(tmp, layer, pair)
            uneven = load(tmp, layer, 2 + pair)
            images = []
            for tile, product in ((pair, even + uneven), (3 - pair, even - uneven)):
                if tile not in tiles:
                    continue
                value = load(basis[step], layer, tile)
                weighted = coef_m * table(0, tile)
                image = coef_v * product + weighted * value
                if sums is not None:
                    diag = coef_v * table(1, tile) + weighted
                    sums = (
                        sums[0] + jnp.sum(value * image, axis=0),
                        sums[1] + jnp.sum(value * value * diag, axis=0),
                    )
                if going:
                    image = xy_sum(image)
                    if pair == 0:
                        store(tmp, layer, tile, image)
                    else:
                        images.append(image)
            if images:
                advance(step, layer, 1, images)
        return sums

    def faces(step, layer):
        advance(step, layer, 0, [face_sum(tmp, layer, tile) for tile in (0, 3)])

    blank_sums = (jnp.zeros((8, 128), F32), jnp.zeros((8, 128), F32))

    def own_apply(step, going):
        sums = blank_sums
        for layer in range(4, 8):
            sums = apply(step, layer, every, sums, going)
        moments[step : step + 1, :] = jnp.sum(sums[0], axis=0, keepdims=True)
        moments[4 + step : 5 + step, :] = jnp.sum(sums[1], axis=0, keepdims=True)

    def first_faces(layer):
        put_first(layer, 0, [face_sum(tmp, layer, tile) for tile in (0, 3)])

    for copy in near_copies:
        copy.wait()
    assemble(2, (3,), has_down)
    assemble(3, every, has_down)
    assemble(8, every, has_up)
    assemble(9, (3,), has_up)
    over(3, 9, first_faces)
    for layer in (2, 9):
        first_value(layer, 3, face_sum(tmp, layer, 3))
    multiply(lhs0, 3, 6, 0, tmp.at[3 * LAYER : 6 * LAYER])
    multiply(lhs0, 6, 9, 0, tmp.at[6 * LAYER : 9 * LAYER])
    own_apply(0, True)
    for layer in (3, 8):
        apply(0, layer, every, None, True)

    for copy in far_copies:
        copy.wait()
    assemble(0, (3,), has_down)
    assemble(1, every, has_down)
    assemble(2, (0, 1, 2), has_down)
    assemble(9, (0, 1, 2), has_up)
    assemble(10, every, has_up)
    assemble(11, (3,), has_up)
    for layer in (1, 10):
        first_faces(layer)
    for layer in (2, 9):
        value = first_value(layer, 0, face_sum(tmp, layer, 0))
        store_lhs(lhs0, layer, 0, value, load(v0, layer, 3))
    far_rows = (slice(1 * LAYER, 3 * LAYER), slice(9 * LAYER, 11 * LAYER))
    for part in range(2):
        product = jnp.dot(
            jnp.concatenate(
                [lhs0[rows, part * 768 : part * 768 + 768] for rows in far_rows], 0
            ),
            weights[part],
            preferred_element_type=F32,
        )
        for side, rows in enumerate(far_rows):
            tmp[rows, part * 256 : part * 256 + 256] = product[
                side * 2 * LAYER : (side + 1) * 2 * LAYER
            ]
    apply(0, 1, (0,), None, True)
    apply(0, 2, every, None, True)
    apply(0, 9, every, None, True)
    apply(0, 10, (0,), None, True)
    over(2, 10, lambda layer: faces(0, layer))

    for step in range(1, ITERS):
        low, high = 1 + step, 11 - step
        going = step + 1 < ITERS
        multiply(lefts[step], low, 6, 0, tmp.at[low * LAYER : 6 * LAYER])
        multiply(lefts[step], 6, high, 0, tmp.at[6 * LAYER : high * LAYER])
        own_apply(step, going)
        if going:
            inward = 0 if low % 2 else 3
            apply(step, low, (inward,), None, True)
            over(low + 1, 4, lambda layer: apply(step, layer, every, None, True))
            over(8, high - 1, lambda layer: apply(step, layer, every, None, True))
            apply(step, high - 1, (inward,), None, True)
            over(low + 1, high - 1, lambda layer: faces(step, layer))

    red[0] = moments[...]
    for offset, peer in peers:
        remote(moments, red.at[offset], rsend, rrecv, (grp, peer)).start()

    def end_face(ref, layer):
        total = load(ref, layer, 0) * table(2, 0)
        for tile in (1, 2, 3):
            total = total + load(ref, layer, tile) * table(2, tile)
        total = total + rotated(total, 64, 2)
        return -total if layer % 2 else total

    fsend[0] = end_face(v3, 7).reshape(LAYER, 128)
    fsend[1] = end_face(v3, 4).reshape(LAYER, 128)
    face_copies = [
        remote(fsend.at[0], frecv.at[0], f3send.at[0], f3recv.at[0], (grp, up)),
        remote(fsend.at[1], frecv.at[1], f3send.at[1], f3recv.at[1], (grp, down)),
    ]
    for copy in face_copies:
        copy.start()

    own_rows = slice(4 * LAYER, 8 * LAYER)
    for index in range(ITERS):
        left = jnp.concatenate(
            [
                jnp.concatenate(
                    [
                        lefts[index][own_rows, start + part * 256 : start + part * 256 + 128]
                        for part in range(3)
                    ],
                    1,
                )
                for start in (0, 128, 768, 896)
            ],
            0,
        )
        both = jnp.dot(left, flat[0:384, 0:256], preferred_element_type=F32)
        for part in range(4):
            rows = slice(part * CELLS, part * CELLS + CELLS)
            grads[index, :, part * 128 : part * 128 + 128] = both[rows, 0:128]
            grads[index, :, NODES + part * 128 : NODES + part * 128 + 128] = both[rows, 128:256]
        multiply(lefts[index], 4, 8, 1, grads.at[index], 2 * NODES)
        if index < 3:
            fghost[index, 0] = end_face(basis[index], 3).reshape(LAYER, 128)
            fghost[index, 1] = end_face(basis[index], 8).reshape(LAYER, 128)

    for copy in face_copies:
        copy.wait()
    for side in range(2):
        fghost[3, side] = frecv[side]

    whole = remote(red.at[1:DOMS], red.at[1:DOMS], rsend, rrecv, (grp, up))
    whole.wait_send()
    whole.wait_recv()

    total = jnp.sum(red[...], axis=0)
    total = jnp.broadcast_to(jnp.sum(total, axis=1, keepdims=True), (8, 128))
    moments[...] = total

    def scalar(row):
        return jnp.broadcast_to(moments[row : row + 1, :], (8, 128))

    alpha = [scalar(row) for row in range(4)]
    beta = [scalar(4 + row) for row in range(4)]
    gamma = [(alpha[k] - THETA * beta[k]) * (1.0 / DELTA) for k in range(4)]
    mu = [beta[0], gamma[0]]
    ahead = gamma[0]
    for k in range(1, 4):
        ahead = 2.0 * gamma[k] - ahead
        mu.append(2.0 * beta[k] - mu[0])
        mu.append(2.0 * ahead - mu[1])

    def inner(i, j):
        return 0.5 * (mu[i + j] + mu[abs(i - j)])

    gram = [
        [
            DELTA * 0.5 * (inner(i, j + 1) + inner(i, abs(j - 1))) + THETA * inner(i, j)
            for j in range(4)
        ]
        for i in range(4)
    ]
    right = [mu[k] for k in range(4)]
    pivots = []
    for k in range(4):
        original = DELTA * 0.5 * (inner(k, k + 1) + inner(k, abs(k - 1))) + THETA * inner(k, k)
        pivot = gram[k][k]
        good = pivot > 1e-7 * original
        inverse = jnp.where(good, 1.0 / jnp.where(good, pivot, 1.0), 0.0)
        pivots.append(inverse)
        for i in range(k + 1, 4):
            factor = gram[i][k] * inverse
            for j in range(k + 1, 4):
                gram[i][j] = gram[i][j] - factor * gram[k][j]
            right[i] = right[i] - factor * right[k]
    coef = [None] * 4
    for k in (3, 2, 1, 0):
        value = right[k]
        for j in range(k + 1, 4):
            value = value - gram[k][j] * coef[j]
        coef[k] = value * pivots[k]

    coef8 = [(value * (1.0 / NP)).reshape(1, 8, 128) for value in coef]
    coef16 = [0.5 * value for value in coef8]
    x_sign = jnp.where(odd, -1.0, 1.0).reshape(1, 8, 128)
    x_scale = jnp.where(take_up | take_down, 0.5, 1.0).reshape(1, 8, 128) * x_sign
    y_half = jnp.where((node_j == 7) | (node_j == 0), 0.5, 1.0).reshape(1, 8, 128)
    y_end = jnp.where(node_j == 7, 0.5, 1.0).reshape(1, 8, 128)
    y_scale = jnp.concatenate(
        [y_end, -y_half, y_half, -y_half, y_half, -y_half, y_half, -y_end], 0
    )

    def combined(layer, direction, pair):
        parts_of = []
        scale = coef8 if direction == 2 else coef16
        for start in (0, 256):
            start = start + direction * NODES + pair * 128
            value = None
            for k in range(4):
                term = scale[k] * grads[k, rows_of(layer), start : start + 128].reshape(8, 8, 128)
                value = term if value is None else value + term
            parts_of.append(value)
        even, uneven = parts_of
        if direction == 2:
            return even + uneven, uneven - even
        return even + uneven, even - uneven

    def put_grad(layer, direction, tile, value):
        start = direction * NODES + tile * 128
        gcells[rows_of(layer), start : start + 128] = value.reshape(LAYER, 128).astype(BF16)

    def pack(direction):
        cols = slice(direction * NODES, direction * NODES + NODES)
        packed[:, cols] = jnp.dot(
            gpack[...], gcells[:, cols], preferred_element_type=F32
        ).astype(BF16)

    for direction, scale, others in ((0, x_scale, x_others), (1, y_scale, y_others)):
        for layer in range(4):
            for pair in (0, 1):
                for tile, value in zip((pair, 3 - pair), combined(layer, direction, pair)):
                    put_grad(layer, direction, tile, scale * (value - others(value)))
        pack(direction)

    for layer in range(4):
        z_sign = -1.0 if layer % 2 else 1.0
        for tile, value in zip((1, 2), combined(layer, 2, 1)):
            put_grad(layer, 2, tile, z_sign * value)
        for tile, value in zip((0, 3), combined(layer, 2, 0)):
            store(xstd, layer, tile, z_sign * value)

    def mean_face(layer, tile, other, there):
        value = load(xstd, layer, tile)
        put_grad(layer, 2, tile, value + jnp.where(low_half, there * (other - value), 0.0))

    for layer in range(4):
        mean_face(layer, 3, load(xstd, layer ^ 1, 3), 0.5)
        if layer in (1, 2):
            mean_face(layer, 0, load(xstd, 3 - layer, 0), 0.5)
        else:
            side = 0 if layer == 0 else 1
            other = None
            for k in range(4):
                term = coef8[k] * fghost[k, side].reshape(8, 8, 128)
                other = term if other is None else other + term
            mean_face(layer, 0, other, 0.5 * (has_up if side else has_down))

    def by_row(values):
        picked = values[3]
        for row in (2, 1, 0):
            picked = jnp.where(grp == row, values[row], picked)
        return picked

    own_first = by_row([first * CHUNK for first in FIRSTS])
    own_count = by_row(COUNTS)

    pack(2)

    def chunk_rows(chunk, base=0):
        return pl.ds(pl.multiple_of(base + chunk * CHUNK, CHUNK), CHUNK)

    def turn(step, count):
        return lax.rem(dom + step, count)

    def piece_copy(step, target, slot):
        chunk = turn(step, COUNTS[target])
        return remote(
            packed.at[chunk_rows(chunk, FIRSTS[target] * CHUNK)],
            recv.at[comp, chunk_rows(chunk)],
            asend.at[slot, step], arecv.at[comp, chunk], (target, dom),
        )

    def each_send(action):
        for row, targets in enumerate(((2, 1, 3), (3, 2, 0), (1,), (0,))):

            @pl.when(grp == row)
            def _():
                for step in range(MOST):
                    for slot, target in enumerate(targets):
                        if step < COUNTS[target]:
                            action(piece_copy(step, target, slot))

    each_send(lambda copy: copy.start())
    for row in range(4):

        @pl.when(grp == row)
        def _():
            slots = COUNTS[row] * CHUNK
            first = FIRSTS[row] * CHUNK
            recv[min(row, 2), 0:slots] = packed[first : first + slots, :]

    wide8 = [value.reshape(1, 8, 128) for value in coef]

    @pl.when(grp < 3)
    def _():
        def solve_layer(layer):
            for tile in every:
                value = wide8[0] * load(v0, layer, tile)
                for k in range(1, 4):
                    value = value + wide8[k] * load(basis[k], layer, tile)
                store(xs, layer - 4, tile, value)

        over(4, 8, solve_layer)
        for tile in every:
            mirror_layers(xs[:, tile * 128 : tile * 128 + 128], tile, xstd, 0, True)
        high, low = split(xstd[...])
        parts[0:CELLS, :] = high
        parts[CELLS : 2 * CELLS, :] = low
        out[...] = jnp.dot(ptr[...], parts[...], preferred_element_type=F32)

    def lambda_rows(block, carry):
        rows = pl.ds(pl.multiple_of(block * 16, 16), 16)
        jac = [
            [recv[c, rows, d * NODES : d * NODES + NODES].astype(F32) for d in range(3)]
            for c in range(3)
        ]
        lam[rows, :] = lambda_two(jac)
        return carry

    def natural_order(chunk):
        rows = chunk_rows(chunk)
        slots = pl.ds(pl.multiple_of(own_first + chunk * CHUNK, CHUNK), CHUNK)
        odd_x, odd_y, odd_z = [
            classes[slots, k * 128 : k * 128 + 128] > 0.5 for k in range(3)
        ]
        values = [lam[rows, tile * 128 : tile * 128 + 128] for tile in every]
        flipped = reversals(jnp.concatenate(values, 0))
        turned = []
        for tile in every:
            rev_x, rev_y, rev_xy = [
                part[tile * CHUNK : tile * CHUNK + CHUNK] for part in flipped
            ]
            turned.append(
                jnp.where(
                    odd_x,
                    jnp.where(odd_y, rev_xy, rev_x),
                    jnp.where(odd_y, rev_y, values[tile]),
                )
            )
        for tile in every:
            value = jnp.where(odd_z, turned[3 - tile], turned[tile])
            if tile >= 2:
                value = rotated(value, 64, 1)
            lam[rows, tile * 128 : tile * 128 + 128] = value

    here = pl.ds(pl.multiple_of(dom * 8, 8), 8)

    def each_owner(chunk, action, local):
        piece = lax.div(own_first, CHUNK) + chunk
        four = lax.div(piece, 2)
        for part in range(2):
            place = lax.rem(piece, 2) * 2 + part
            owner = place * 8 + lax.rem(place + lax.div(four, 2), 4) * 2 + lax.rem(four, 2)
            rows = pl.ds(pl.multiple_of(chunk * CHUNK + part * 8, 8), 8)
            own = (grp == 3) & (owner == dom)

            @pl.when(jnp.logical_not(own))
            def _():
                action(
                    remote(
                        lam.at[rows], lamrecv.at[here], osend.at[chunk * 2 + part], orecv,
                        (3, owner),
                    )
                )

            if local:

                @pl.when(own)
                def _():
                    lamrecv[here, :] = lam[rows, :]

    def analyse(chunk):
        for step in (1, 2):
            other = lax.rem(comp + step, 3)
            piece = recv.at[other, chunk_rows(chunk)]
            remote(
                piece, piece, asend.at[0, 0], arecv.at[other, chunk], (lax.rem(grp + 1, 4), dom)
            ).wait_recv()
        lambda_rows(chunk, 0)
        natural_order(chunk)
        each_owner(chunk, lambda copy: copy.start(), True)

    over(0, own_count, lambda step: analyse(turn(step, own_count)))
    over(
        0,
        own_count,
        lambda step: each_owner(turn(step, own_count), lambda copy: copy.wait_send(), False),
    )
    each_send(lambda copy: copy.wait_send())

    def wait_rows(count):
        piece = lamrecv.at[0 : 8 * count]
        remote(piece, piece, osend.at[0], orecv, (lax.rem(grp + 1, 4), dom)).wait_recv()

    four = lax.rem(lax.div(lax.rem(dom, 8), 2) - lax.div(dom, 8) + 4, 4) * 2 + lax.rem(dom, 2)
    to_itself = four * 2 + lax.div(dom, 16) >= FIRSTS[3]

    @pl.when((grp == 3) & to_itself)
    def _():
        wait_rows(31)

    @pl.when((grp == 3) & jnp.logical_not(to_itself))
    def _():
        wait_rows(32)

    @pl.when(grp == 3)
    def _():
        out[...] = lamrecv[...]


def lambda_two(jac):
    strain = [[0.5 * (jac[a][b] + jac[b][a]) for b in range(3)] for a in range(3)]
    spin = [[0.5 * (jac[a][b] - jac[b][a]) for b in range(3)] for a in range(3)]
    m = [[None] * 3 for _ in range(3)]
    for a in range(3):
        for b in range(a, 3):
            value = strain[a][0] * strain[0][b] + spin[a][0] * spin[0][b]
            for k in (1, 2):
                value = value + strain[a][k] * strain[k][b] + spin[a][k] * spin[k][b]
            m[a][b] = value
            m[b][a] = value
    for sweep in range(SWEEPS):
        for p, q, r in ((0, 1, 2), (0, 2, 1), (1, 2, 0)):
            last = sweep == SWEEPS - 1
            twice = 2.0 * m[p][q]
            gap = m[p][p] - m[q][q]
            square = twice * twice + gap * gap
            inverse = lax.rsqrt(jnp.maximum(square, 1e-36))
            length = square * inverse
            mean = 0.5 * (m[p][p] + m[q][q])
            m[p][p] = mean + 0.5 * length
            m[q][q] = mean - 0.5 * length
            if last and (p, q) == (1, 2):
                continue
            none = square < 1e-36
            cosine2 = jnp.where(none, 1.0, jnp.abs(gap) * inverse)
            sine2 = jnp.where(none, 0.0, twice * inverse)
            larger = 0.5 + 0.5 * cosine2
            root = lax.rsqrt(larger)
            big = larger * root
            small = 0.5 * sine2 * root
            flip = gap < 0.0
            sine_big = jnp.where(sine2 < 0.0, -big, big)
            cosine = jnp.where(flip, jnp.abs(small), big)
            sine = jnp.where(flip, sine_big, small)
            side_p = m[r][p]
            side_q = m[r][q]
            m[r][p] = m[p][r] = cosine * side_p + sine * side_q
            m[r][q] = m[q][r] = cosine * side_q - sine * side_p
            m[p][q] = m[q][p] = jnp.zeros_like(side_p)
    diagonal = [m[0][0], m[1][1], m[2][2]]
    largest = jnp.maximum(jnp.maximum(diagonal[0], diagonal[1]), diagonal[2])
    smallest = jnp.minimum(jnp.minimum(diagonal[0], diagonal[1]), diagonal[2])
    return diagonal[0] + diagonal[1] + diagonal[2] - largest - smallest


def per_device(forcing, viscosity, mass_coef, element_order, owner):
    mats, flat, lanes = tables()
    vmem = pl.BlockSpec(memory_space=pltpu.VMEM)
    hbm = pl.BlockSpec(memory_space=pltpu.HBM)
    wide = (12 * LAYER, NODES)
    own = (CELLS, NODES)
    dma = pltpu.SemaphoreType.DMA
    result = pl.pallas_call(
        kernel,
        out_shape=pltpu.VMEM(own, F32),
        in_specs=[hbm] * 8,
        out_specs=vmem,
        scratch_shapes=[
            pltpu.VMEM(own, F32),
            pltpu.VMEM((8, NODES), F32),
            pltpu.VMEM((640, 384), BF16),
            pltpu.VMEM((1, CELLS), jnp.int32),
            pltpu.VMEM((1, CELLS), jnp.int32),
            pltpu.VMEM((4, 768, 256), BF16),
            pltpu.VMEM((8, CELLS), F32),
            pltpu.VMEM((2, 8, CELLS), F32),
            pltpu.VMEM((CELLS, 2 * CELLS), BF16),
            pltpu.VMEM((CELLS, 2 * CELLS), BF16),
            pltpu.VMEM((2 * CELLS, NODES), BF16),
            pltpu.VMEM((12 * LAYER, 128), F32),
            pltpu.VMEM((12 * LAYER, 128), F32),
            pltpu.VMEM(wide, F32),
            pltpu.VMEM(wide, F32),
            pltpu.VMEM(wide, F32),
            pltpu.VMEM((12 * LAYER, 3 * NODES), BF16),
            pltpu.VMEM((12 * LAYER, 3 * NODES), BF16),
            pltpu.VMEM((12 * LAYER, 3 * NODES), BF16),
            pltpu.VMEM((12 * LAYER, 3 * NODES), BF16),
            pltpu.VMEM(wide, F32),
            pltpu.VMEM(wide, F32),
            pltpu.VMEM(wide, F32),
            pltpu.VMEM(wide, F32),
            pltpu.VMEM(own, F32),
            pltpu.VMEM(own, F32),
            pltpu.VMEM((4, CELLS, 3 * NODES), F32),
            pltpu.VMEM((CELLS, CELLS), BF16),
            pltpu.VMEM((CELLS, 384), F32),
            pltpu.VMEM((CELLS, 3 * NODES), BF16),
            pltpu.VMEM((2, LAYER, 128), F32),
            pltpu.VMEM((2, LAYER, 128), F32),
            pltpu.VMEM((4, 2, LAYER, 128), F32),
            pltpu.VMEM((8, 128), F32),
            pltpu.VMEM((DOMS, 8, 128), F32),
            pltpu.VMEM((CELLS, 3 * NODES), BF16),
            pltpu.VMEM((3, MOST * CHUNK, 3 * NODES), BF16),
            pltpu.VMEM((MOST * CHUNK, NODES), F32),
            pltpu.VMEM(own, F32),
            dma((6,)), dma((12,)), dma, dma((2,)), dma((2,)), dma((10,)), dma((10,)), dma((2,)),
            dma((2,)), dma, dma, dma((3, MOST)), dma((3, MOST)), dma((2 * MOST,)), dma,
        ],
        compiler_params=pltpu.CompilerParams(
            collective_id=0, has_side_effects=True, vmem_limit_bytes=60 * 1024 * 1024
        ),
        name="solve_and_analyse",
    )(
        forcing, viscosity[None], mass_coef[None], element_order, owner,
        jnp.asarray(lanes), jnp.asarray(flat), jnp.asarray(mats),
    )
    return result[None]


def solution(mesh):
    in_specs = (P(None, "dom", None), P("dom"), P("dom"), P("dom", None), P("dom", None))
    out_specs = P("grp", "dom", None)
    return jax.shard_map(
        per_device, mesh=mesh, in_specs=in_specs, out_specs=out_specs, check_vma=False
    )
```
